32 devices in a mesh: seq: 8 (over z, y), ctx: 4 (over x, core).
Axes of the slice: x: 2, y: 2, z: 4, core: 2. Of those that a mesh axis runs over, the one named last changes fastest.
Arguments:
- inputs: bfloat16 [8, 1024, 1536], P('seq', 'ctx'), may hold values from -6 to 6
- cotangent: bfloat16 [8, 1024, 1536], P('seq', 'ctx'), may hold values from -6 to 6
- segment_ids: int32 [8, 1024], P('seq'), may hold values from 0 to 2, never falling along the last dimension, each value on 1 to 512 neighbouring positions
- expert_ids: int32 [8, 1024, 8], P('seq', 'ctx'), may hold values from 0 to 15, all different within a row; in each aligned block of 256 rows (0 to 255, 256 to 511, ..., all dimensions but the last counted through in order) at most 128 rows name the same one
- adapter_ids: int32 [8], replicated, may hold values from 0 to 7
- gain_one: float32 [1536], replicated, may hold values from 0.25 to 1.75
- w_qkv: bfloat16 [1536, 2560], P('seq'), may hold values from -0.21875 to 0.21875
- w_out: bfloat16 [1536, 1536], P('seq'), may hold values from -0.625 to 0.625
- gain_two: float32 [1536], replicated, may hold values from 0.25 to 1.75
- router: bfloat16 [1536, 16], replicated, may hold values from -0.078125 to 0.078125
- w_gate_up: bfloat16 [16, 1536, 1024], P('seq'), may hold values from -0.15625 to 0.15625
- w_down: bfloat16 [16, 512, 1536], P('seq'), may hold values from -1 to 1
- qkv_down: bfloat16 [8, 1536, 48], replicated, may hold values from -0.15625 to 0.15625
- qkv_up: bfloat16 [8, 16, 2560], replicated, may hold values from -0.75 to 0.75
- out_down: bfloat16 [8, 1536, 16], replicated, may hold values from -0.15625 to 0.15625
- out_up: bfloat16 [8, 16, 1536], replicated, may hold values from -1.5 to 1.5
- gu_down: bfloat16 [8, 1536, 32], replicated, may hold values from -0.15625 to 0.15625
- gu_up: bfloat16 [8, 2, 16, 512], replicated, may hold values from -0.75 to 0.75
- down_a: bfloat16 [8, 512, 16], replicated, may hold values from -0.25 to 0.25
- down_b: bfloat16 [8, 16, 1536], replicated, may hold values from -1.5 to 1.5
Outputs:
- layer_output: bfloat16 [8, 1024, 1536], P('seq', 'ctx')
- input_grad: float32 [8, 1024, 1536], P('seq', 'ctx')
- grad_qkv_down: float32 [8, 1536, 48], replicated
- grad_qkv_up: float32 [8, 16, 2560], replicated
- grad_out_down: float32 [8, 1536, 16], replicated
- grad_out_up: float32 [8, 16, 1536], replicated
- grad_gu_down: float32 [8, 1536, 32], replicated
- grad_gu_up: float32 [8, 2, 16, 512], replicated
- grad_down_a: float32 [8, 512, 16], replicated
- grad_down_b: float32 [8, 16, 1536], replicated
The draws below stay inside these ranges and needn't reach their ends.
Inputs may be any that keep to these rules, and one draw needn't show every extreme that they name: `expert_ids`: each token names 8 different experts; in the rows of one device no expert is named more than 128 times, a bound that some block reaches. `segment_ids`: along each sequence the ids never fall; a document has at most min(2000, 512) positions, and one has exactly that many.
All inputs are finite; a program needn't handle non-finite values.
Results may differ from the reference program's by a relative error of at most 0.02.
Values may be sent and summed in bfloat16 or wider, within the bound.
No kernel may reach another device: no remote copies, remote signals or barrier semaphores. Data moves between devices by JAX's collectives and lax.ppermute only.
A program may use at most 256 MiB of HBM per device.

```python
import math
import jax
import jax.numpy as jnp
import numpy as np
from jax import lax

D = 1536
HEADS = 24
KV_HEADS = 8
HEAD_DIM = 64
FF = 512
TOPK = 8
RANK = 16
ADAPT = 8
TOK_DEV = 256
CAP = 128
LENGTH = 1024
SEQS = 8
EXPERTS = 16
QW = 1536
KVW = 512
N_CTX = 4


def place_ends(drawn, own_key, smallest, top_value):
    spot = [jax.random.randint(jax.random.fold_in(own_key, axis), (), 0, length) for axis, length in enumerate(drawn.shape)]
    widest = drawn.shape.index(max(drawn.shape))
    next_to = spot[:widest] + [(spot[widest] + 1) % drawn.shape[widest]] + spot[widest + 1:]
    return drawn.at[tuple(spot)].set(smallest).at[tuple(next_to)].set(top_value)


def steps_of(rng, shape, cuts, smallest, high):
    factor_of = 1.0
    for dim, blocks in cuts:
        draws = jax.random.uniform(jax.random.fold_in(jax.random.fold_in(rng, 6), dim), (blocks,), jnp.float32, smallest / len(cuts), high / len(cuts))
        factor_of = factor_of * jnp.repeat(jnp.exp(draws), shape[dim] // blocks).reshape((-1,) + (1,) * (len(shape) - 1 - dim))
    return factor_of


def length_profile(number_of, total, reach, slope):
    loads = [(1 << 20) // math.isqrt(grade ** slope) + 1 for grade in range(2, number_of + 1)]
    spare, holding = total - reach - (number_of - 1), [1] * (number_of - 1)
    while spare > 0:
        free = [i for i in range(number_of - 1) if holding[i] < reach]
        mass, remaining = sum([loads[i] for i in free]), spare
        for i in free:
            extra = min(reach - holding[i], max(1, remaining * loads[i] // mass), spare)
            holding[i] = holding[i] + extra
            spare = spare - extra
    return np.array([reach] + holding)


def uneven_parts(rng, number_of, total, reach, skew):
    if number_of == 2:
        one = jax.random.randint(rng, (), max(1, total - reach), min(reach, total - 1) + 1)
        return jnp.stack([one, total - one])
    sizes = jnp.asarray(length_profile(number_of, total, reach, skew), jnp.int32)
    couples = (number_of - 1) // 2
    donor, taker = sizes[1:1 + 2 * couples:2], sizes[2:2 + 2 * couples:2]
    margin = jnp.minimum(donor - 1, reach - taker)
    passed = jax.random.randint(jax.random.fold_in(rng, 1), (couples,), 0, 1 << 20) % (margin + 1)
    sizes = sizes.at[1:1 + 2 * couples:2].set(donor - passed).at[2:2 + 2 * couples:2].set(taker + passed)
    return sizes[jax.random.permutation(jax.random.fold_in(rng, 2), number_of)]


def routed_block(own_key, own, number, rows, amount, top, reach, lean):
    order = jax.random.permutation(own_key, amount)
    crowded, ordinary = load_shares(amount, rows * top, reach, lean, True), load_shares(amount, rows * top, reach, lean, False)
    places = jnp.arange(amount)

    def named(lengths, turn):
        used = int((lengths > 0).sum())
        fixed = max(1, used // 4)
        passed = fixed + (places - fixed + turn * (used - fixed)) % max(1, amount - fixed)
        return jnp.zeros((amount,), jnp.int32).at[order[jnp.where(places < fixed, places, passed)]].set(jnp.asarray(lengths, jnp.int32))

    lengths = jnp.where(number % 4 == 0, named(crowded, number // 4), named(ordinary, number - number // 4 - 1))
    mixed = jax.random.permutation(jax.random.fold_in(own, 3), amount)
    source_of, taker = mixed[0:amount // 2 * 2:2], mixed[1:amount // 2 * 2:2]
    slack = jnp.minimum(lengths[source_of] - 1, reach - lengths[taker]) // 2
    slack = jnp.where((source_of == order[0]) | (taker == order[0]) | (lengths[taker] == 0), 0, jnp.maximum(slack, 0))
    passed = jax.random.randint(jax.random.fold_in(own, 4), (amount // 2,), 0, 1 << 20) % (slack + 1)
    lengths = lengths.at[source_of].add(-passed).at[taker].add(passed)
    labels = jnp.searchsorted(jnp.cumsum(lengths), jnp.arange(rows * top), side="right").astype(jnp.int32)
    listing = labels.reshape(top, rows).T
    listing = listing[jax.random.permutation(jax.random.fold_in(own, 1), rows)]
    turn = jax.random.randint(jax.random.fold_in(own, 2), (rows, 1), 0, top)
    return jnp.take_along_axis(listing, (jnp.arange(top)[None, :] + turn) % top, axis=1)


def load_shares(number_of, total, bound, slope, full):
    weights = [(1 << 20) // math.isqrt(rank ** slope) + 1 for rank in range(1, number_of + 1)]
    largest = bound if full else min(bound, max(-(-total // number_of), total * weights[0] // sum(weights)))
    least = 1 if total - largest >= number_of - 1 else 0
    holding, surplus = [largest] + [least] * (number_of - 1), total - largest - least * (number_of - 1)
    while surplus > 0:
        free = [i for i in range(1, number_of) if holding[i] < largest] or [i for i in range(1, number_of) if holding[i] < bound]
        whole, left = sum([weights[i] for i in free]), surplus
        for i in free:
            more = min(bound - holding[i], max(1, left * weights[i] // whole), surplus)
            holding[i] = holding[i] + more
            surplus = surplus - more
    return np.array(holding)


def gaussian(own_key, dims, scale, limit, shards=(), dtype=jnp.bfloat16):
    values = jax.random.normal(own_key, dims, jnp.float32) * scale
    if len(shards) > 0:
        values = steps_of(own_key, dims, shards, -0.22, 0.18) * values
    return jnp.clip(values, min=-limit, max=limit).astype(dtype)


def setup_inputs(seed: int = 0) -> dict:
    streams_of = jax.random.split(jax.random.key(seed), 21)
    inputs = gaussian(streams_of[0], (SEQS, LENGTH, D), 1.0, 6.0, ((0, 8), (1, 4)))
    cotangent = gaussian(streams_of[1], (SEQS, LENGTH, D), 1.0, 6.0, ((0, 8), (1, 4)))
    segment_ids = jax.vmap(lambda own: jnp.searchsorted(jnp.cumsum(uneven_parts(own, max(3, LENGTH // 640 + 1), LENGTH, min(2000, LENGTH // 2), 1)), jnp.arange(LENGTH), side="right"))(jax.random.split(streams_of[2], SEQS)).reshape((SEQS, LENGTH)).astype(jnp.int32)
    expert_ids_keys = jax.random.split(jax.random.fold_in(streams_of[3], 1), SEQS * LENGTH // TOK_DEV)
    expert_ids_turns = jax.random.permutation(jax.random.fold_in(streams_of[3], 3), SEQS * LENGTH // TOK_DEV)
    expert_ids = jax.vmap(lambda own, number: routed_block(jax.random.fold_in(streams_of[3], 2), own, number, TOK_DEV, EXPERTS, TOPK, CAP, 1))(expert_ids_keys, expert_ids_turns).reshape((SEQS, LENGTH, TOPK))
    adapter_ids = place_ends(jax.random.randint(streams_of[4], (SEQS,), 0, ADAPT), jax.random.fold_in(streams_of[4], 1), 0, ADAPT - 1).astype(jnp.int32)
    gain_one = jnp.clip(1.0 + 0.15 * jax.random.normal(streams_of[5], (D,), jnp.float32), 0.25, 1.75)
    w_qkv = gaussian(streams_of[6], (D, QW + 2 * KVW), (D // 2) ** -0.5, 0.21875, ((0, 8),))
    w_out = gaussian(streams_of[7], (QW, D), (QW // 16) ** -0.5, 0.625, ((0, 8),))
    gain_two = jnp.clip(1.0 + 0.15 * jax.random.normal(streams_of[8], (D,), jnp.float32), 0.25, 1.75)
    router = gaussian(streams_of[9], (D, EXPERTS), (4 * D) ** -0.5, 0.078125)
    w_gate_up = gaussian(streams_of[10], (EXPERTS, D, 2 * FF), D ** -0.5, 0.15625, ((0, 8),))
    w_down = gaussian(streams_of[11], (EXPERTS, FF, D), (FF // 16) ** -0.5, 1.0, ((0, 8),))
    qkv_down = gaussian(streams_of[12], (ADAPT, D, 3 * RANK), D ** -0.5, 0.15625)
    qkv_up = gaussian(streams_of[13], (ADAPT, RANK, QW + 2 * KVW), (4 * RANK) ** -0.5, 0.75)
    out_down = gaussian(streams_of[14], (ADAPT, QW, RANK), QW ** -0.5, 0.15625)
    out_up = gaussian(streams_of[15], (ADAPT, RANK, D), RANK ** -0.5, 1.5)
    gu_down = gaussian(streams_of[16], (ADAPT, D, 2 * RANK), D ** -0.5, 0.15625)
    gu_up = gaussian(streams_of[17], (ADAPT, 2, RANK, FF), (4 * RANK) ** -0.5, 0.75)
    down_a = gaussian(streams_of[18], (ADAPT, FF, RANK), FF ** -0.5, 0.25)
    down_b = gaussian(streams_of[19], (ADAPT, RANK, D), RANK ** -0.5, 1.5)
    return {"inputs": inputs, "cotangent": cotangent, "segment_ids": segment_ids, "expert_ids": expert_ids, "adapter_ids": adapter_ids, "gain_one": gain_one, "w_qkv": w_qkv, "w_out": w_out, "gain_two": gain_two, "router": router, "w_gate_up": w_gate_up, "w_down": w_down, "qkv_down": qkv_down, "qkv_up": qkv_up, "out_down": out_down, "out_up": out_up, "gu_down": gu_down, "gu_up": gu_up, "down_a": down_a, "down_b": down_b}


@jax.custom_vjp
def low(v):
    return lax.optimization_barrier(v.astype(jnp.bfloat16)).astype(jnp.float32)

@jax.custom_vjp
def low_back(v):
    return v

def low_keep(v):
    return (low(v), None)

def low_pass(kept, grad):
    return (grad,)

def back_keep(v):
    return (v, None)

def back_low(kept, grad):
    return (low(grad),)
low.defvjp(low_keep, low_pass)
low_back.defvjp(back_keep, back_low)
NORM_EPS = 1e-05
HIGHEST_PREC = lax.Precision.HIGHEST

def matmul(left_arr, right_arr):
    return jnp.dot(left_arr, right_arr, precision=HIGHEST_PREC)

def rms_norm(values, gain_vec):
    return values * lax.rsqrt(lax.optimization_barrier(jnp.mean(values * values, axis=-1, keepdims=True)) + NORM_EPS) * gain_vec

def rotary(values, offsets, direction):
    half_dim = values.shape[-1] // 2
    frequency = 10000.0 ** (-2.0 * jnp.arange(half_dim).astype(jnp.float32) / values.shape[-1])
    angles = offsets.astype(jnp.float32)[:, None] * frequency[None, :]
    cosine = jnp.cos(angles)[:, None, :]
    sine_part = direction * jnp.sin(angles)[:, None, :]
    first_half = values[..., :half_dim]
    second_half = values[..., half_dim:]
    return jnp.concatenate([first_half * cosine - second_half * sine_part, second_half * cosine + first_half * sine_part], axis=-1)

def storage_positions(ctx_count, tok_count):
    half_len = tok_count // 2
    row_index = jnp.arange(tok_count * ctx_count)
    device_of = row_index // tok_count
    within = row_index % tok_count
    which_block = jnp.where(within < half_len, device_of, 2 * ctx_count - 1 - device_of)
    return (which_block * half_len + within % half_len).astype(jnp.int32)

def document_offsets(seg_row):
    row_index = jnp.arange(seg_row.shape[0])
    change = jnp.concatenate([jnp.ones((1,), jnp.bool_), seg_row[1:] != seg_row[:-1]])
    starts = lax.cummax(jnp.where(change, row_index, 0), axis=0)
    return (row_index - starts).astype(jnp.int32)

def sequence_forward(tokens, tables, frozen, context):
    qkv_down, qkv_up, out_down, out_up, gu_down, gu_up, down_a, down_b = tables
    gain_one, w_qkv, w_out, gain_two, router, w_gate_up, w_down = frozen
    position, offset, segment, chosen, adapter = context
    group_size = HEADS // KV_HEADS
    qkv_sel = qkv_down[adapter]
    up_sel = qkv_up[adapter]
    h_one = low(rms_norm(tokens, gain_one))
    rank_qkv = low(low_back(matmul(h_one, qkv_sel)))
    main_proj = matmul(h_one, w_qkv)
    q_pre = low_back(main_proj[:, :QW] + matmul(rank_qkv[:, :RANK], up_sel[:, :QW]))
    k_pre = low_back(main_proj[:, QW:QW + KVW] + matmul(rank_qkv[:, RANK:2 * RANK], up_sel[:, QW:QW + KVW]))
    v_pre = low_back(main_proj[:, QW + KVW:] + matmul(rank_qkv[:, 2 * RANK:], up_sel[:, QW + KVW:]))
    queries = low(rotary(q_pre.reshape(LENGTH, HEADS, HEAD_DIM), offset, 1.0)).reshape(LENGTH, KV_HEADS, group_size, HEAD_DIM)
    keys_all = low(rotary(k_pre.reshape(LENGTH, KV_HEADS, HEAD_DIM), offset, 1.0))
    values_all = low(v_pre.reshape(LENGTH, KV_HEADS, HEAD_DIM))
    block_len = min(512, LENGTH)

    def attend(start_row):
        query_block = lax.dynamic_slice_in_dim(queries, start_row, block_len, 0)
        scores = low_back(jnp.einsum('tgrd,kgd->grtk', query_block, keys_all, precision=HIGHEST_PREC) * 0.125)
        query_pos = lax.dynamic_slice_in_dim(position, start_row, block_len, 0)
        query_seg = lax.dynamic_slice_in_dim(segment, start_row, block_len, 0)
        allowed = (query_seg[:, None] == segment[None, :]) & (position[None, :] <= query_pos[:, None])
        scores = jnp.where(allowed, scores, -1e+30)
        peak_val = lax.optimization_barrier(jnp.max(scores, axis=-1, keepdims=True))
        expo_val = jnp.exp(scores - peak_val)
        prob_vals = expo_val / lax.optimization_barrier(jnp.sum(expo_val, axis=-1, keepdims=True))
        return jnp.einsum('grtk,kgd->tgrd', low(prob_vals), values_all, precision=HIGHEST_PREC).reshape(block_len, QW)
    starts = (jnp.arange(LENGTH // block_len) * block_len).astype(jnp.int32)
    attended = lax.map(jax.checkpoint(attend), starts).reshape(LENGTH, QW)
    out_heads = low(low_back(attended))
    rank_out = low(low_back(matmul(out_heads, out_down[adapter])))
    y_one = tokens + low_back(matmul(out_heads, w_out) + matmul(rank_out, out_up[adapter]))
    h_two = low(rms_norm(y_one, gain_two))
    logits = low_back(matmul(h_two, router))
    picked = jnp.take_along_axis(logits, chosen, axis=1)
    top_val = lax.optimization_barrier(jnp.max(picked, axis=-1, keepdims=True))
    weights = jnp.exp(picked - top_val)
    gate_vals = weights / lax.optimization_barrier(jnp.sum(weights, axis=-1, keepdims=True))
    rank_gu = low(low_back(matmul(h_two, gu_down[adapter])))
    expert_total = router.shape[1]
    seq_cap = LENGTH // TOK_DEV * CAP
    flat_expert = chosen.reshape(-1)
    flat_token = (jnp.arange(LENGTH * TOPK) // TOPK).astype(jnp.int32)
    onehot = (flat_expert[:, None] == jnp.arange(expert_total)[None, :]).astype(jnp.int32)
    rank_of = lax.optimization_barrier(jnp.sum(jnp.cumsum(onehot, axis=0) * onehot, axis=1)) - 1
    slot_of = (flat_expert * seq_cap + rank_of).astype(jnp.int32)
    slot_token = jnp.zeros((expert_total * seq_cap,), jnp.int32).at[slot_of].set(flat_token)
    slot_live = jnp.zeros((expert_total * seq_cap,), jnp.float32).at[slot_of].set(1.0)
    rows_in = low_back(h_two[slot_token] * slot_live[:, None]).reshape(expert_total, seq_cap, D)
    rank_in = low_back(rank_gu[slot_token] * slot_live[:, None]).reshape(expert_total, seq_cap, 2 * RANK)
    gu_sel = gu_up[adapter]
    both_pre = jnp.einsum('ecd,edf->ecf', rows_in, w_gate_up, precision=HIGHEST_PREC)
    gate_pre = low_back(both_pre[..., :FF] + jnp.einsum('ecr,rf->ecf', rank_in[..., :RANK], gu_sel[0], precision=HIGHEST_PREC))
    up_pre = low_back(both_pre[..., FF:] + jnp.einsum('ecr,rf->ecf', rank_in[..., RANK:], gu_sel[1], precision=HIGHEST_PREC))
    activated = low(jax.nn.silu(gate_pre) * up_pre)
    rank_down = low(low_back(jnp.einsum('ecf,fr->ecr', activated, down_a[adapter], precision=HIGHEST_PREC)))
    slot_outs = low(low_back(jnp.einsum('ecf,efd->ecd', activated, w_down, precision=HIGHEST_PREC) + jnp.einsum('ecr,rd->ecd', rank_down, down_b[adapter], precision=HIGHEST_PREC)))
    gathered = slot_outs.reshape(expert_total * seq_cap, D)[slot_of].reshape(LENGTH, TOPK, D)
    return y_one + lax.optimization_barrier(jnp.sum(gate_vals[..., None] * gathered, axis=1))

def reference(inputs, cotangent, segment_ids, expert_ids, adapter_ids, gain_one, w_qkv, w_out, gain_two, router, w_gate_up, w_down, qkv_down, qkv_up, out_down, out_up, gu_down, gu_up, down_a, down_b):
    frozen = (gain_one.astype(jnp.float32), w_qkv.astype(jnp.float32), w_out.astype(jnp.float32), gain_two.astype(jnp.float32), router.astype(jnp.float32), w_gate_up.astype(jnp.float32), w_down.astype(jnp.float32))
    tables = (qkv_down.astype(jnp.float32), qkv_up.astype(jnp.float32), out_down.astype(jnp.float32), out_up.astype(jnp.float32), gu_down.astype(jnp.float32), gu_up.astype(jnp.float32), down_a.astype(jnp.float32), down_b.astype(jnp.float32))
    position = storage_positions(N_CTX, TOK_DEV)

    def one_sequence(totals, seq_item):
        tokens, grad_out, seg_row, chosen, adapter = seq_item
        offset = document_offsets(seg_row)[position]
        segment = seg_row[position]
        context = (position, offset, segment, chosen, adapter)

        def forward(tok_arr, *table_args):
            return sequence_forward(tok_arr, table_args, frozen, context)
        result, pullback = jax.vjp(forward, tokens.astype(jnp.float32), *tables)
        gradients = pullback(grad_out.astype(jnp.float32))
        totals = tuple((running + fresh for running, fresh in zip(totals, gradients[1:])))
        return (totals, (result.astype(jnp.bfloat16), gradients[0]))
    zero_tables = tuple((jnp.zeros(table_arg.shape, jnp.float32) for table_arg in tables))
    totals, (outputs, input_grads) = lax.scan(one_sequence, zero_tables, (inputs, cotangent, segment_ids, expert_ids, adapter_ids))
    grad_qkv_down, grad_qkv_up, grad_out_down, grad_out_up, grad_gu_down, grad_gu_up, grad_down_a, grad_down_b = totals
    return (outputs, input_grads, grad_qkv_down, grad_qkv_up, grad_out_down, grad_out_up, grad_gu_down, grad_gu_up, grad_down_a, grad_down_b)
```

```python
import functools

import jax
import jax.numpy as jnp
from jax import lax
from jax.experimental import pallas as pl
from jax.experimental.pallas import tpu as pltpu
from jax.sharding import PartitionSpec as P

D = 1536
HEADS = 24
KV_HEADS = 8
HEAD_DIM = 64
FF = 512
RANK = 16
ADAPT = 8
E_DEV = 2
CAP = 128
QW = 1536
KVW = 512
NORM_EPS = 1e-05

GROUPS = KV_HEADS // 2
PAIRS = HEADS // KV_HEADS
QG = QW // GROUPS
KG = KVW // GROUPS
LOCAL = QG + 2 * KG
PAIR_ORDER = (0, 3, 1, 4, 2, 5)
BLK = 256
LANES = 128
EXP_AT = 2 * RANK
GATE_AT = 96
EXT = D + LANES
NEG = -1e30

BF = jnp.bfloat16
F32 = jnp.float32
NT = (((1,), (1,)), ((), ()))
TN = (((0,), (0,)), ((), ()))


def dot(left_arr, right_arr):
    return jnp.dot(left_arr, right_arr, preferred_element_type=F32)


def dot_nt(left_arr, right_arr):
    return lax.dot_general(left_arr, right_arr, NT, preferred_element_type=F32)


def dot_tn(left_arr, right_arr):
    return lax.dot_general(left_arr, right_arr, TN, preferred_element_type=F32)


def swap(block, axis, mask):
    count = lax.axis_size(axis)
    return lax.ppermute(block, axis, [(i, i ^ mask) for i in range(count)])


def gather_slots(block, axis, masks):
    slots = {0: block}
    for mask in masks:
        for have in list(slots):
            slots[have ^ mask] = swap(slots[have], axis, mask)
    return [slots[m] for m in range(len(slots))]


def gather_seq(block):
    count = lax.axis_size("seq")
    if count != 8:
        return gather_slots(block, "seq", doublings(count))
    even = [block] + [swap(block, "seq", m) for m in (2, 4, 6)]
    odd = [swap(item, "seq", 1) for item in even]
    return [item for both in zip(even, odd) for item in both]


def doublings(count):
    return [1 << bit for bit in range(count.bit_length() - 1)]


def add_low(left_arr, right_arr):
    return (left_arr.astype(F32) + right_arr.astype(F32)).astype(BF)


def reduce_slots(parts, axis, masks):
    parts = dict(enumerate(parts))
    for step, mask in enumerate(masks):
        last = step == len(masks) - 1
        for m in [m for m in parts if m & mask]:
            arrived = swap(parts.pop(m), axis, mask)
            mine = parts[m ^ mask]
            parts[m ^ mask] = (
                mine.astype(F32) + arrived.astype(F32) if last else add_low(mine, arrived)
            )
    return parts[0]


def reduce_seq(parts):
    count = lax.axis_size("seq")
    if count != 8:
        return reduce_slots(parts, "seq", doublings(count))
    total = None
    for m in (6, 4, 2, 0):
        arrived = swap(parts[m + 1], "seq", 1)
        if m:
            arrived = swap(add_low(parts[m], arrived), "seq", m)
        else:
            arrived = arrived.astype(F32) + parts[0].astype(F32)
        arrived = arrived.astype(F32)
        total = arrived if total is None else total + arrived
    return total


def rotate(values, cosine, sine, sign):
    lane = lax.broadcasted_iota(jnp.int32, values.shape, 1)
    ahead = pltpu.roll(values, LANES - HEAD_DIM // 2, 1)
    behind = pltpu.roll(values, HEAD_DIM // 2, 1)
    other = jnp.where(lane % HEAD_DIM < HEAD_DIM // 2, ahead, behind)
    return values * cosine + (sign * other) * sine


def project_kernel(order_ref, h_ref, t_ref, up_ref, cos_ref, sin_ref, *rest):
    shards = rest[:-3]
    qkv_ref, full_ref, w_ref = rest[-3:]
    rows = shards[0].shape[0]

    @pl.when(pl.program_id(0) == 0)
    def _():
        for m, shard in enumerate(shards):
            start = pl.multiple_of(order_ref[m] * rows, rows)
            w_ref[pl.ds(start, rows), :] = shard[...]
        full_ref[...] = w_ref[...]

    pre = dot(h_ref[...], w_ref[...]) + dot(t_ref[...], up_ref[...])
    cosine, sine = cos_ref[...], sin_ref[...]
    for j in range(LOCAL // LANES):
        part = pre[:, j * LANES : (j + 1) * LANES]
        if j <= PAIRS:
            part = rotate(part, cosine, sine, 1.0)
        if j < PAIRS:
            part = part * 0.125
        qkv_ref[:, j * LANES : (j + 1) * LANES] = part.astype(BF)


def project(order, h_one, rank_qkv, up_diag, cosine, sine, shards):
    length = h_one.shape[0]
    rows = shards[0].shape[0]
    per_block = lambda width: pl.BlockSpec((BLK, width), lambda i, order: (i, 0))
    whole = lambda shape: pl.BlockSpec(shape, lambda i, order: (0, 0))
    return pl.pallas_call(
        project_kernel,
        grid_spec=pltpu.PrefetchScalarGridSpec(
            num_scalar_prefetch=1,
            grid=(length // BLK,),
            in_specs=[
                per_block(D),
                per_block(3 * RANK),
                whole((3 * RANK, LOCAL)),
                per_block(LANES),
                per_block(LANES),
            ]
            + [whole((rows, LOCAL))] * len(shards),
            out_specs=[per_block(LOCAL), whole((D, LOCAL))],
            scratch_shapes=[pltpu.VMEM((D, LOCAL), BF)],
        ),
        out_shape=[
            jax.ShapeDtypeStruct((length, LOCAL), BF),
            jax.ShapeDtypeStruct((D, LOCAL), BF),
        ],
        cost_estimate=pl.CostEstimate(
            flops=2 * length * D * LOCAL, bytes_accessed=2 * length * (D + LOCAL), transcendentals=0
        ),
        name="project",
    )(order, h_one, rank_qkv, up_diag, cosine, sine, *shards)


def half_mask(shape, half):
    lane = lax.broadcasted_iota(jnp.int32, shape, 1)
    return (lane < HEAD_DIM) if half == 0 else (lane >= HEAD_DIM)


def stack_rows(place_ref, source_ref, target_ref, first_lane):
    half = BLK // 2
    for b in range(source_ref.shape[0] // half):
        rows = pl.ds(pl.multiple_of(place_ref[b] * half, half), half)
        for pair in range(PAIRS):
            at = (b // 2) * PAIRS * BLK + pair * BLK + (b % 2) * half
            lanes = slice(first_lane + pair * LANES, first_lane + (pair + 1) * LANES)
            target_ref[at : at + half, :] = source_ref[rows, lanes]


def split_keys(place_ref, qkv_ref, first_lane, target_ref, ones):
    half = BLK // 2
    for b in range(qkv_ref.shape[0] // half):
        rows = pl.ds(pl.multiple_of(place_ref[b] * half, half), half)
        both = qkv_ref[rows, first_lane : first_lane + LANES]
        for side in range(2):
            other = jnp.zeros_like(both)
            if ones:
                lane = lax.broadcasted_iota(jnp.int32, both.shape, 1)
                spare = HEAD_DIM if side == 0 else 0
                other = jnp.where(lane == spare, 1.0, 0.0).astype(BF)
            target_ref[side, b * half : (b + 1) * half, :] = jnp.where(
                half_mask(both.shape, side), both, other
            )


def tile_bias(start_col, q_first, k_first):
    shape = (BLK, BLK)
    key = k_first + lax.broadcasted_iota(jnp.int32, shape, 1)
    query = q_first + lax.broadcasted_iota(jnp.int32, shape, 0)
    bias = jnp.where((key >= start_col) & (key <= query), 0.0, NEG)
    return jnp.concatenate([bias] * PAIRS, axis=0)


def attend_kernel(place_ref, first_ref, qkv_ref, start_ref, o_ref, lse_ref, q_s, k_s, v_s, m_s, acc_s):
    stack_rows(place_ref, qkv_ref, q_s, 0)
    split_keys(place_ref, qkv_ref, QG, k_s, False)
    split_keys(place_ref, qkv_ref, QG + KG, v_s, True)
    half = BLK // 2
    tall = PAIRS * BLK

    def query_block(qb, unused):
        q_first = pl.multiple_of(qb * BLK, BLK)
        q_rows = pl.ds(pl.multiple_of(qb * tall, tall), tall)
        start_col = start_ref[pl.ds(q_first, BLK), :]
        m_s[...] = jnp.full(m_s.shape, NEG, F32)
        acc_s[...] = jnp.zeros(acc_s.shape, F32)

        def key_block(kb, unused):
            k_first = pl.multiple_of(kb * BLK, BLK)
            bias = tile_bias(start_col, q_first, k_first)
            queries = q_s[q_rows, :]
            for side in range(2):
                scores = dot_nt(queries, k_s[side, pl.ds(k_first, BLK), :]) + bias
                old = m_s[side]
                new = jnp.maximum(old, jnp.max(scores, axis=1, keepdims=True))
                prob = jnp.exp(scores - new)
                m_s[side] = new
                acc_s[side] = acc_s[side] * jnp.exp(old - new) + dot(
                    prob.astype(BF), v_s[side, pl.ds(k_first, BLK), :]
                )
            return unused

        lax.fori_loop(first_ref[qb], qb + 1, key_block, 0)
        low, high = acc_s[0], acc_s[1]
        low_sum = low[:, HEAD_DIM : HEAD_DIM + 1]
        high_sum = high[:, 0:1]
        is_low = half_mask(low.shape, 0)
        out = jnp.where(is_low, low / low_sum, high / high_sum).astype(BF)
        lse_ref[q_rows, :] = jnp.where(
            is_low, m_s[0] + jnp.log(low_sum), m_s[1] + jnp.log(high_sum)
        )
        for i in range(2):
            rows = pl.ds(pl.multiple_of(place_ref[2 * qb + i] * half, half), half)
            for pair in range(PAIRS):
                at = pair * BLK + i * half
                o_ref[rows, pair * LANES : (pair + 1) * LANES] = out[at : at + half, :]
        return unused

    lax.fori_loop(0, qkv_ref.shape[0] // BLK, query_block, 0)


SMEM_SPEC = pl.BlockSpec(memory_space=pltpu.SMEM)
VMEM_SPEC = pl.BlockSpec(memory_space=pltpu.VMEM)


def attend(place, first, qkv, start_col):
    length = qkv.shape[0]
    tall = PAIRS * BLK
    return pl.pallas_call(
        attend_kernel,
        in_specs=[SMEM_SPEC, SMEM_SPEC, VMEM_SPEC, VMEM_SPEC],
        out_specs=[VMEM_SPEC, VMEM_SPEC],
        out_shape=[
            jax.ShapeDtypeStruct((length, QG), BF),
            jax.ShapeDtypeStruct((PAIRS * length, LANES), F32),
        ],
        scratch_shapes=[
            pltpu.VMEM((PAIRS * length, LANES), BF),
            pltpu.VMEM((2, length, LANES), BF),
            pltpu.VMEM((2, length, LANES), BF),
            pltpu.VMEM((2, tall, 1), F32),
            pltpu.VMEM((2, tall, LANES), F32),
        ],
        cost_estimate=pl.CostEstimate(
            flops=4 * length * length * QG, bytes_accessed=8 * length * QG, transcendentals=0
        ),
        name="attend",
    )(place, first, qkv, start_col)


def attend_back_kernel(
    place_ref,
    first_ref,
    qkv_ref,
    start_ref,
    o_ref,
    lse_ref,
    do_ref,
    cos_ref,
    sin_ref,
    dqkv_ref,
    q_s,
    o_s,
    do_s,
    k_s,
    v_s,
    dk_s,
    dv_s,
    dq_s,
):
    stack_rows(place_ref, qkv_ref, q_s, 0)
    stack_rows(place_ref, o_ref, o_s, 0)
    stack_rows(place_ref, do_ref, do_s, 0)
    split_keys(place_ref, qkv_ref, QG, k_s, False)
    split_keys(place_ref, qkv_ref, QG + KG, v_s, False)
    dk_s[...] = jnp.zeros(dk_s.shape, F32)
    dv_s[...] = jnp.zeros(dv_s.shape, F32)
    half = BLK // 2
    tall = PAIRS * BLK

    def query_block(qb, unused):
        q_first = pl.multiple_of(qb * BLK, BLK)
        q_rows = pl.ds(pl.multiple_of(qb * tall, tall), tall)
        start_col = start_ref[pl.ds(q_first, BLK), :]
        dq_s[...] = jnp.zeros(dq_s.shape, F32)
        product = do_s[q_rows, :].astype(F32) * o_s[q_rows, :].astype(F32)
        lse = lse_ref[q_rows, :]
        lse_of = (lse[:, 0:1], lse[:, HEAD_DIM : HEAD_DIM + 1])
        delta_of = [
            jnp.sum(jnp.where(half_mask(product.shape, side), product, 0.0), axis=1, keepdims=True)
            for side in range(2)
        ]

        def key_block(kb, unused):
            k_first = pl.multiple_of(kb * BLK, BLK)
            k_rows = pl.ds(k_first, BLK)
            bias = tile_bias(start_col, q_first, k_first)
            queries = q_s[q_rows, :]
            d_out = do_s[q_rows, :]
            for side in range(2):
                keys = k_s[side, k_rows, :]
                scores = dot_nt(queries, keys) + bias
                prob = jnp.exp(scores - lse_of[side])
                d_prob = dot_nt(d_out, v_s[side, k_rows, :])
                d_score = (prob * (d_prob - delta_of[side])).astype(BF)
                dv_s[side, k_rows, :] += dot_tn(prob.astype(BF), d_out)
                dk_s[side, k_rows, :] += dot_tn(d_score, queries)
                dq_s[...] += dot(d_score, keys)
            return unused

        lax.fori_loop(first_ref[qb], qb + 1, key_block, 0)
        for i in range(2):
            rows = pl.ds(pl.multiple_of(place_ref[2 * qb + i] * half, half), half)
            cosine, sine = cos_ref[rows, :], sin_ref[rows, :]
            for pair in range(PAIRS):
                at = pair * BLK + i * half
                back = rotate(dq_s[at : at + half, :] * 0.125, cosine, sine, -1.0)
                dqkv_ref[rows, pair * LANES : (pair + 1) * LANES] = back.astype(BF)
        return unused

    lax.fori_loop(0, qkv_ref.shape[0] // BLK, query_block, 0)
    for b in range(qkv_ref.shape[0] // half):
        rows = pl.ds(pl.multiple_of(place_ref[b] * half, half), half)
        at = slice(b * half, (b + 1) * half)
        is_low = half_mask((half, LANES), 0)
        back = jnp.where(is_low, dk_s[0, at, :], dk_s[1, at, :])
        back = rotate(back, cos_ref[rows, :], sin_ref[rows, :], -1.0)
        dqkv_ref[rows, QG : QG + KG] = back.astype(BF)
        dqkv_ref[rows, QG + KG : LOCAL] = jnp.where(is_low, dv_s[0, at, :], dv_s[1, at, :]).astype(BF)


def attend_back(place, first, qkv, start_col, out, lse, d_out, cosine, sine):
    length = qkv.shape[0]
    tall = PAIRS * BLK
    stacked = pltpu.VMEM((PAIRS * length, LANES), BF)
    return pl.pallas_call(
        attend_back_kernel,
        in_specs=[SMEM_SPEC, SMEM_SPEC] + [VMEM_SPEC] * 7,
        out_specs=VMEM_SPEC,
        out_shape=jax.ShapeDtypeStruct((length, LOCAL), BF),
        scratch_shapes=[
            stacked,
            stacked,
            stacked,
            pltpu.VMEM((2, length, LANES), BF),
            pltpu.VMEM((2, length, LANES), BF),
            pltpu.VMEM((2, length, LANES), F32),
            pltpu.VMEM((2, length, LANES), F32),
            pltpu.VMEM((tall, LANES), F32),
        ],
        cost_estimate=pl.CostEstimate(
            flops=10 * length * length * QG, bytes_accessed=16 * length * QG, transcendentals=0
        ),
        name="attend_back",
    )(place, first, qkv, start_col, out, lse, d_out, cosine, sine)


def expert_kernel(ids_ref, h_refs, p_refs, wgu_ref, wd_ref, tables, y_refs, d_refs, scratch):
    aux_w, gu_refs, da_refs, db_refs = tables
    aux_s, gu_s, sel_s, yrow_s, drow_s, grad_s = scratch
    step = pl.program_id(0)
    wide = lax.broadcasted_iota(jnp.int32, (h_refs[0].shape[0], LANES), 1)
    count = len(h_refs)
    lane = EXP_AT + ids_ref[count] + step

    @pl.when(step == 0)
    def _():
        grad_s[...] = jnp.zeros(grad_s.shape, F32)
        gu_s[...] = jnp.zeros(gu_s.shape, BF)
        for j in range(count):
            gu_s[j, 0, 0:RANK, :] = gu_refs[j][0, 0]
            gu_s[j, 1, RANK : 2 * RANK, :] = gu_refs[j][0, 1]
            both = dot_nt(h_refs[j][...], aux_w[j][0])
            chosen = p_refs[j][:, D:EXT].astype(F32) > 0.0
            picked = jnp.where(chosen, both, NEG)
            weights = jnp.exp(picked - jnp.max(picked, axis=1, keepdims=True))
            gates = weights / jnp.sum(weights, axis=1, keepdims=True)
            aux_s[j] = jnp.where(wide < EXP_AT, both, gates)

    rows, extra, upstream = [], [], []
    for j in range(count):
        ranks = p_refs[j][:, D:EXT].astype(F32)
        column = jnp.sum(jnp.where(wide == lane, ranks, 0.0), axis=1, keepdims=True)
        tall = ranks.T
        which = lax.broadcasted_iota(jnp.int32, tall.shape, 0)
        row = jnp.sum(jnp.where(which == lane, tall, 0.0), axis=0, keepdims=True)
        slot = lax.broadcasted_iota(jnp.int32, (CAP, tall.shape[1]), 0).astype(F32) + 1.0
        take = jnp.where(slot == row, 1.0, 0.0).astype(BF)
        sel_s[j, step] = jnp.where(wide.astype(F32) + 1.0 == column, 1.0, 0.0).astype(BF)
        aux = aux_s[j]
        gate = jnp.sum(jnp.where(wide == lane, aux, 0.0), axis=1, keepdims=True)
        gate_one = gate.astype(BF).astype(F32)
        gate_two = (gate - gate_one).astype(BF).astype(F32)
        gate_three = gate - gate_one - gate_two
        aux = jnp.where(wide < EXP_AT, aux, 0.0)
        aux = jnp.where(wide == GATE_AT, gate_one, aux)
        aux = jnp.where(wide == GATE_AT + 1, gate_two, aux)
        aux = jnp.where(wide == GATE_AT + 2, gate_three, aux)
        rows.append(dot(take, h_refs[j][...]).astype(BF))
        extra.append(dot(take, aux.astype(BF)))
        upstream.append(dot(take, p_refs[j][:, :D]))

    def each(make):
        return jnp.concatenate([make(j) for j in range(count)], axis=0)

    part = lambda arr, j: arr[j * CAP : (j + 1) * CAP]
    low_extra = [item.astype(BF) for item in extra]
    narrow = lax.broadcasted_iota(jnp.int32, (CAP, LANES), 1)
    gate = each(
        lambda j: jnp.sum(
            jnp.where((narrow >= GATE_AT) & (narrow < GATE_AT + 3), extra[j], 0.0),
            axis=1,
            keepdims=True,
        )
    )
    both = dot(jnp.concatenate(rows, axis=0), wgu_ref[0])
    gate_pre = both[:, :FF] + each(lambda j: dot(low_extra[j], gu_s[j, 0]))
    up_pre = both[:, FF:] + each(lambda j: dot(low_extra[j], gu_s[j, 1]))
    sigmoid = jax.nn.sigmoid(gate_pre)
    silu = gate_pre * sigmoid
    active = (silu * up_pre).astype(BF)
    down = [dot_nt(part(active, j), da_refs[j][0]).astype(BF) for j in range(count)]
    result = dot(active, wd_ref[0]) + each(lambda j: dot(down[j], db_refs[j][0]))
    result = result.astype(BF).astype(F32)
    grad_in = jnp.concatenate(upstream, axis=0)
    d_gate_val = jnp.sum(grad_in * result, axis=1, keepdims=True)
    weighted = (gate * result).astype(BF)
    d_result = (gate * grad_in).astype(BF)
    d_down = [dot_nt(part(d_result, j), db_refs[j][0]).astype(BF) for j in range(count)]
    d_active = dot_nt(d_result, wd_ref[0]) + each(lambda j: dot(d_down[j], da_refs[j][0]))
    d_gate = (d_active * up_pre * sigmoid * (1.0 + gate_pre * (1.0 - sigmoid))).astype(BF)
    d_up = (d_active * silu).astype(BF)
    d_rows = dot_nt(jnp.concatenate([d_gate, d_up], axis=1), wgu_ref[0]).astype(BF)
    for j in range(count):
        at = pl.ds(pl.multiple_of(step * CAP, CAP), CAP)
        yrow_s[j, at, :] = part(weighted, j)
        drow_s[j, at, :D] = part(d_rows, j)
        d_extra = dot_nt(part(d_gate, j), gu_s[j, 0]) + dot_nt(part(d_up, j), gu_s[j, 1])
        d_extra = d_extra + jnp.where(narrow == lane, part(d_gate_val, j), 0.0)
        drow_s[j, at, D:] = d_extra.astype(BF)
        grad_s[j, 0:RANK, 0:FF] += dot_tn(low_extra[j], part(d_gate, j))[0:RANK]
        grad_s[j, 0:RANK, FF : 2 * FF] += dot_tn(low_extra[j], part(d_up, j))[RANK : 2 * RANK]
        grad_s[j, 0:RANK, 2 * FF :] += dot_tn(d_down[j], part(active, j))
        grad_s[j, RANK:, :] += dot_tn(down[j], part(d_result, j))

    @pl.when(step == E_DEV - 1)
    def _():
        for j in range(count):
            tokens = h_refs[j].shape[0]
            put = jnp.concatenate([sel_s[j, e] for e in range(E_DEV)], axis=1)
            y_refs[j][:tokens, :] = dot(put, yrow_s[j]).astype(BF)
            y_refs[j][tokens:, :] = grad_s[j].astype(BF)
            d_refs[j][...] = dot(put, drow_s[j]).astype(BF)


def experts(adapters, base, rows, packs, w_gate_up, w_down, aux_w, gu_up, down_a, down_b):
    count = len(rows)
    tokens = rows[0].shape[0]
    whole = lambda width: pl.BlockSpec((tokens, width), lambda e, ids: (0, 0))

    def table(shape, j):
        return pl.BlockSpec((1,) + shape, lambda e, ids: (ids[j],) + (0,) * len(shape))

    def body(ids_ref, *refs):
        refs = list(refs)
        take = lambda n: [refs.pop(0) for _ in range(n)]
        h_refs, p_refs = take(count), take(count)
        wgu_ref, wd_ref = take(2)
        tables = [take(count) for _ in range(4)]
        y_refs, d_refs = take(count), take(count)
        expert_kernel(ids_ref, h_refs, p_refs, wgu_ref, wd_ref, tables, y_refs, d_refs, refs)

    picked = [(LANES, D), (2, RANK, FF), (RANK, FF), (RANK, D)]
    shapes = [(tokens + 2 * RANK, D)] * count + [(tokens, EXT)] * count
    outs = pl.pallas_call(
        body,
        grid_spec=pltpu.PrefetchScalarGridSpec(
            num_scalar_prefetch=1,
            grid=(E_DEV,),
            in_specs=[whole(D)] * count
            + [whole(EXT)] * count
            + [
                pl.BlockSpec((1, D, 2 * FF), lambda e, ids: (e, 0, 0)),
                pl.BlockSpec((1, FF, D), lambda e, ids: (e, 0, 0)),
            ]
            + [table(shape, j) for shape in picked for j in range(count)],
            out_specs=[pl.BlockSpec(shape, lambda e, ids: (0, 0)) for shape in shapes],
            scratch_shapes=[
                pltpu.VMEM((count, tokens, LANES), F32),
                pltpu.VMEM((count, 2, LANES, FF), BF),
                pltpu.VMEM((count, E_DEV, tokens, CAP), BF),
                pltpu.VMEM((count, E_DEV * CAP, D), BF),
                pltpu.VMEM((count, E_DEV * CAP, EXT), BF),
                pltpu.VMEM((count, 2 * RANK, D), F32),
            ],
        ),
        out_shape=[jax.ShapeDtypeStruct(shape, BF) for shape in shapes],
        cost_estimate=pl.CostEstimate(
            flops=16 * count * E_DEV * CAP * D * FF,
            bytes_accessed=2 * E_DEV * 3 * D * FF + 8 * count * tokens * D,
            transcendentals=0,
        ),
        name="experts",
    )(
        jnp.concatenate([adapters, base[None]]).astype(jnp.int32),
        *rows,
        *packs,
        w_gate_up,
        w_down,
        *([aux_w] * count),
        *([gu_up] * count),
        *([down_a] * count),
        *([down_b] * count),
    )
    return outs[:count], outs[count:]


def norm_backward(values, inverse, gain_vec, upstream):
    scaled = gain_vec * upstream
    return inverse * scaled - values * inverse**3 * jnp.mean(
        values * scaled, axis=-1, keepdims=True
    )


def pair_columns(columns):
    lead = columns.shape[:-1]
    heads = columns.reshape(lead + (2 * PAIRS, HEAD_DIM))
    return heads[..., jnp.array(PAIR_ORDER), :].reshape(lead + (QG,))


def local_columns(table, group):
    lead = table.shape[:-1]
    cut = lambda first, width: lax.dynamic_slice_in_dim(
        table, first + group * width, width, table.ndim - 1
    )
    return cut(0, QG), cut(QW, KG), cut(QW + KVW, KG)


def on_device(
    inputs,
    cotangent,
    segment_ids,
    expert_ids,
    adapter_ids,
    gain_one,
    w_qkv,
    w_out,
    gain_two,
    router,
    w_gate_up,
    w_down,
    qkv_down,
    qkv_up,
    out_down,
    out_up,
    gu_down,
    gu_up,
    down_a,
    down_b,
):
    ctx_count = lax.axis_size("ctx")
    seq_count = lax.axis_size("seq")
    ctx_index = lax.axis_index("ctx")
    seq_index = lax.axis_index("seq")
    tokens = inputs.shape[1]
    length = tokens * ctx_count
    experts_all = router.shape[1]
    copies = ctx_count // GROUPS
    group = ctx_index // copies
    half = tokens // 2
    ctx_masks = doublings(ctx_count)[::-1]
    seq_slots = seq_index ^ jnp.arange(seq_count)
    ctx_slots = ctx_index ^ jnp.arange(ctx_count)
    group_slots = group ^ jnp.arange(GROUPS)
    own_rows = inputs[0]

    row_slots = gather_slots(own_rows, "ctx", ctx_masks)
    own_q, own_k, own_v = local_columns(w_qkv, group)
    own_cols = jnp.concatenate([pair_columns(own_q), own_k, own_v], axis=1)
    col_slots = gather_seq(own_cols)
    chosen = expert_ids[0]
    hot = jnp.any(chosen[:, :, None] == jnp.arange(experts_all)[None, None, :], axis=1)
    hot_low = hot.astype(BF)
    before = (jnp.arange(tokens)[:, None] >= jnp.arange(tokens)[None, :]).astype(BF)
    ranks = dot(before, hot_low).astype(BF) * hot_low
    ranks = jnp.pad(ranks, ((0, 0), (EXP_AT, LANES - EXP_AT - experts_all)))
    pack_slots = gather_seq(jnp.concatenate([cotangent[0], ranks], axis=1))
    out_part = D // ctx_count
    own_out = lax.dynamic_slice_in_dim(w_out, ctx_index * out_part, out_part, 1)
    out_slots = jnp.stack(gather_seq(own_out))[seq_slots].reshape(QW, out_part)
    out_all = jnp.stack(gather_slots(out_slots, "ctx", ctx_masks))[ctx_slots]
    out_all = jnp.transpose(out_all, (1, 0, 2)).reshape(GROUPS, 2, PAIRS, HEAD_DIM, D)
    out_all = jnp.transpose(out_all, (0, 2, 1, 3, 4)).reshape(GROUPS, QG, D)[group_slots]
    out_all = out_all.reshape(QW, D)

    seg_row = segment_ids[0]
    position = jnp.arange(length)
    start = jnp.sum((seg_row[None, :] < seg_row[:, None]).astype(jnp.int32), axis=1)
    block_id = jnp.stack([ctx_slots, 2 * ctx_count - 1 - ctx_slots], axis=1).reshape(-1)
    block_of = jnp.arange(2 * ctx_count)
    owner = jnp.minimum(block_of, 2 * ctx_count - 1 - block_of)
    place = (2 * (owner ^ ctx_index) + (block_of >= ctx_count)).astype(jnp.int32)
    first = (start[::BLK] // BLK).astype(jnp.int32)
    offset = (position - start).reshape(2 * ctx_count, half)[block_id].reshape(-1)
    frequency = 10000.0 ** (
        -2.0 * jnp.arange(HEAD_DIM // 2).astype(F32) / HEAD_DIM
    )
    angles = offset.astype(F32)[:, None] * frequency[None, :]
    cosine, sine = jnp.cos(angles), jnp.sin(angles)
    cosine = jnp.concatenate([cosine] * 4, axis=1)
    sine = jnp.concatenate([-sine, sine, -sine, sine], axis=1)
    start_col = start[:, None]
    adapter = adapter_ids[seq_index]
    slot_adapters = adapter_ids[seq_slots]

    def pick(table):
        return lax.dynamic_index_in_dim(table, adapter, 0, keepdims=False)

    qkv_down_sel = pick(qkv_down)
    up_q, up_k, up_v = local_columns(pick(qkv_up), group)
    up_q = pair_columns(up_q)
    up_diag = jnp.concatenate(
        [
            jnp.pad(up_q, ((0, 0), (0, 2 * KG))),
            jnp.pad(up_k, ((0, 0), (QG, KG))),
            jnp.pad(up_v, ((0, 0), (QG + KG, 0))),
        ],
        axis=0,
    )
    out_down_sel = pick(out_down).reshape(GROUPS, 2, PAIRS, HEAD_DIM, RANK)
    out_down_sel = jnp.transpose(out_down_sel, (0, 2, 1, 3, 4)).reshape(GROUPS, QG, RANK)
    out_down_sel = out_down_sel[group_slots].reshape(QW, RANK)
    out_up_sel = pick(out_up)
    gu_down_sel = pick(gu_down)
    aux_w = jnp.concatenate(
        [
            jnp.swapaxes(gu_down, 1, 2),
            jnp.broadcast_to(router.T[None], (ADAPT, experts_all, D)),
            jnp.zeros((ADAPT, LANES - 2 * RANK - experts_all, D), BF),
        ],
        axis=1,
    )
    down_a_t = jnp.swapaxes(down_a, 1, 2)

    features = own_rows.astype(F32)
    inv_one = lax.rsqrt(jnp.mean(features * features, axis=-1, keepdims=True) + NORM_EPS)
    all_rows = jnp.concatenate(row_slots, axis=0).astype(F32)
    inv_all = lax.rsqrt(jnp.mean(all_rows * all_rows, axis=-1, keepdims=True) + NORM_EPS)
    h_one = (all_rows * inv_all * gain_one).astype(BF)
    rank_qkv = dot(h_one, qkv_down_sel).astype(BF)
    qkv, cols_all = project(
        seq_slots.astype(jnp.int32), h_one, rank_qkv, up_diag, cosine, sine, col_slots
    )
    heads_out, lse = attend(place, first, qkv, start_col)

    def to_tokens(by_slot):
        parts = by_slot.reshape(ctx_count, tokens, QG)
        got = [
            swap(parts[j * copies], "ctx", j * copies) if j else parts[0] for j in range(GROUPS)
        ]
        return jnp.concatenate(got, axis=1)

    def to_heads(by_group):
        got = []
        for m in range(ctx_count):
            piece = by_group[:, (m // copies) * QG : (m // copies + 1) * QG]
            got.append(swap(piece, "ctx", m) if m else piece)
        return jnp.concatenate(got, axis=0)

    attended = to_tokens(heads_out)
    rank_out = dot(attended, out_down_sel).astype(BF)
    y_one = features + dot(attended, out_all) + dot(rank_out, out_up_sel)
    inv_two = lax.rsqrt(jnp.mean(y_one * y_one, axis=-1, keepdims=True) + NORM_EPS)
    h_two = (y_one * inv_two * gain_two).astype(BF)

    h_slots = gather_seq(h_two)
    y_parts, d_parts = [], []
    for m in range(0, seq_count, 2):
        y_pair, d_pair = experts(
            slot_adapters[m : m + 2],
            E_DEV * seq_index,
            h_slots[m : m + 2],
            pack_slots[m : m + 2],
            w_gate_up,
            w_down,
            aux_w,
            gu_up,
            down_a_t,
            down_b,
        )
        y_parts += y_pair
        d_parts += d_pair
    d_sum = reduce_seq(d_parts)
    y_sum = reduce_seq(y_parts)
    layer_output = (y_one + y_sum[:tokens]).astype(BF)[None]

    grad_two = cotangent[0].astype(F32)
    logits = dot(h_two, router)
    picked = jnp.where(hot, logits, NEG)
    weights = jnp.exp(picked - jnp.max(picked, axis=-1, keepdims=True))
    gates = weights / jnp.sum(weights, axis=-1, keepdims=True)
    d_gates = d_sum[:, D + EXP_AT : D + EXP_AT + experts_all]
    d_logits = (gates * (d_gates - jnp.sum(gates * d_gates, axis=-1, keepdims=True))).astype(BF)
    d_rank_gu = d_sum[:, D : D + 2 * RANK].astype(BF)
    d_h_two = d_sum[:, :D] + dot(d_logits, router.T) + dot(d_rank_gu, gu_down_sel.T)
    d_y_one = grad_two + norm_backward(y_one, inv_two, gain_two, d_h_two)
    d_attn = d_y_one.astype(BF)
    d_rank_out = dot(d_attn, out_up_sel.T).astype(BF)
    d_attended = (dot(d_attn, out_all.T) + dot(d_rank_out, out_down_sel.T)).astype(BF)
    d_heads = to_heads(d_attended)

    grad_out_down = dot(d_rank_out.T, attended).reshape(RANK, GROUPS, QG)[:, group_slots]
    grad_out_down = grad_out_down.reshape(RANK, GROUPS, PAIRS, 2, HEAD_DIM)
    grad_out_down = jnp.transpose(grad_out_down, (0, 1, 3, 2, 4)).reshape(RANK, QW)
    early = jnp.concatenate(
        [
            y_sum[tokens:],
            grad_out_down,
            dot(rank_out.T, d_attn),
            dot(d_rank_gu.T, h_two),
        ],
        axis=0,
    ).astype(BF)
    early_rows = early.shape[0]
    early = early.reshape(ctx_count, early_rows // ctx_count, D)[ctx_slots]
    early = reduce_slots([early[m] for m in range(ctx_count)], "ctx", ctx_masks[::-1]).astype(BF)
    early = jnp.stack(gather_seq(early))
    early = jnp.stack(gather_slots(early, "ctx", ctx_masks))[ctx_slots]

    d_qkv = attend_back(place, first, qkv, start_col, heads_out, lse, d_heads, cosine, sine)
    d_rows = dot_nt(d_qkv, cols_all).astype(BF).reshape(ctx_count, tokens, D)
    live = [m for m in range(ctx_count) if m % copies == 0]
    d_rank_qkv = dot_nt(d_qkv, up_diag)
    for mask in [copies * m for m in doublings(GROUPS)]:
        low = d_rank_qkv.astype(BF)
        arrived = swap(low, "ctx", mask).reshape(ctx_count, tokens, 3 * RANK)
        arrived = arrived[jnp.arange(ctx_count) ^ mask].reshape(length, 3 * RANK)
        d_rank_qkv = low.astype(F32) + arrived.astype(F32)
    d_rank_qkv = d_rank_qkv.astype(BF)
    d_h_one = reduce_ctx(d_rows, copies) + dot_nt(d_rank_qkv[:tokens], qkv_down_sel)
    input_grad = (d_y_one + norm_backward(features, inv_one, gain_one, d_h_one))[None]

    slice_width = D // ctx_count
    h_slice = lax.dynamic_slice_in_dim(h_one, ctx_index * slice_width, slice_width, 1)
    down_grad = dot(d_rank_qkv.T, h_slice).reshape(3, RANK, slice_width)
    late = jnp.concatenate(
        [
            dot(rank_qkv[:, :RANK].T, d_qkv[:, :QG]),
            dot(rank_qkv[:, RANK : 2 * RANK].T, d_qkv[:, QG : QG + KG]),
            dot(rank_qkv[:, 2 * RANK :].T, d_qkv[:, QG + KG :]),
            down_grad[0],
            down_grad[1],
            down_grad[2],
        ],
        axis=1,
    ).astype(BF)
    late = jnp.stack(gather_seq(late))
    late = jnp.stack(gather_slots(late, "ctx", ctx_masks))[ctx_slots]

    source_hot = (slot_adapters[:, None] == jnp.arange(ADAPT)[None, :]).astype(BF)

    def by_adapter(values):
        return jnp.einsum("sa,csrd->acrd", source_hot, values, preferred_element_type=F32)

    early = by_adapter(early).reshape(ADAPT, early_rows, D)
    grad_gate = early[:, :RANK, :FF]
    grad_up = early[:, :RANK, FF : 2 * FF]
    grad_gu_up = jnp.stack([grad_gate, grad_up], axis=1)
    grad_down_a = jnp.swapaxes(early[:, :RANK, 2 * FF :], 1, 2)
    grad_down_b = early[:, RANK : 2 * RANK]
    grad_out_down = jnp.swapaxes(early[:, 2 * RANK : 3 * RANK], 1, 2)
    grad_out_up = early[:, 3 * RANK : 4 * RANK]
    grad_gu_down = jnp.swapaxes(early[:, 4 * RANK :], 1, 2)
    late = by_adapter(late)
    heads_late = late[:, ::copies]
    grad_q = heads_late[..., :QG].reshape(ADAPT, GROUPS, RANK, PAIRS, 2, HEAD_DIM)
    grad_q = jnp.transpose(grad_q, (0, 2, 1, 4, 3, 5)).reshape(ADAPT, RANK, QW)
    merge = lambda part: jnp.transpose(part, (0, 2, 1, 3)).reshape(ADAPT, RANK, -1)
    grad_qkv_up = jnp.concatenate(
        [grad_q, merge(heads_late[..., QG : QG + KG]), merge(heads_late[..., QG + KG : LOCAL])],
        axis=2,
    )
    down_part = late[..., LOCAL:].reshape(ADAPT, ctx_count, RANK, 3, slice_width)
    grad_qkv_down = jnp.transpose(down_part, (0, 1, 4, 3, 2)).reshape(ADAPT, D, 3 * RANK)
    return (
        layer_output,
        input_grad,
        grad_qkv_down,
        grad_qkv_up,
        grad_out_down,
        grad_out_up,
        grad_gu_down,
        grad_gu_up,
        grad_down_a,
        grad_down_b,
    )


def reduce_ctx(parts, copies):
    parts = dict(enumerate(parts))
    masks = doublings(len(parts))
    for mask in masks:
        for m in [m for m in parts if m & mask]:
            sent = parts.pop(m)
            if mask >= copies:
                parts[m ^ mask] = add_low(parts[m ^ mask], swap(sent, "ctx", mask))
    return parts[0].astype(F32)


def solution(mesh):
    over_seq = P("seq", None)
    placed = (
        P("seq", "ctx", None),
        P("seq", "ctx", None),
        over_seq,
        P("seq", "ctx", None),
        P(),
        P(),
        over_seq,
        over_seq,
        P(),
        P(),
        P("seq", None, None),
        P("seq", None, None),
    ) + (P(),) * 8
    return jax.shard_map(
        on_device,
        mesh=mesh,
        in_specs=placed,
        out_specs=(P("seq", "ctx", None), P("seq", "ctx", None)) + (P(),) * 8,
        check_vma=False,
    )
```

```python
import functools

import jax
import jax.numpy as jnp
from jax import lax
from jax.experimental import pallas as pl
from jax.experimental.pallas import tpu as pltpu
from jax.sharding import PartitionSpec as P

D = 1536
HEADS = 24
KV_HEADS = 8
HEAD_DIM = 64
FF = 512
RANK = 16
ADAPT = 8
E_DEV = 2
CAP = 128
QW = 1536
KVW = 512
NORM_EPS = 1e-05

GROUPS = KV_HEADS // 2
PAIRS = HEADS // KV_HEADS
QG = QW // GROUPS
KG = KVW // GROUPS
LOCAL = QG + 2 * KG
PAIR_ORDER = (0, 3, 1, 4, 2, 5)
BLK = 256
LANES = 128
EXP_AT = 2 * RANK
GATE_AT = 96
EXT = D + LANES
NEG = -1e30

BF = jnp.bfloat16
F32 = jnp.float32
NT = (((1,), (1,)), ((), ()))
TN = (((0,), (0,)), ((), ()))


def dot(left_arr, right_arr):
    return jnp.dot(left_arr, right_arr, preferred_element_type=F32)


def dot_nt(left_arr, right_arr):
    return lax.dot_general(left_arr, right_arr, NT, preferred_element_type=F32)


def dot_tn(left_arr, right_arr):
    return lax.dot_general(left_arr, right_arr, TN, preferred_element_type=F32)


def swap(block, axis, mask):
    count = lax.axis_size(axis)
    return lax.ppermute(block, axis, [(i, i ^ mask) for i in range(count)])


def gather_slots(block, axis, masks):
    slots = {0: block}
    for mask in masks:
        for have in list(slots):
            slots[have ^ mask] = swap(slots[have], axis, mask)
    return [slots[m] for m in sorted(slots)]


def together(*arrays):
    return lax.optimization_barrier(arrays)


def line_swap(block, pairs):
    return lax.ppermute(block, "seq", [(2 * i + j, 2 * k + j) for i, k in pairs for j in (0, 1)])


def outward(block):
    return line_swap(block, [(1, 0), (2, 3)])


def inward(block):
    return line_swap(block, [(0, 1), (3, 2)])


def middle(block):
    return line_swap(block, [(1, 2), (2, 1)])


class Steps:
    def __init__(self, work):
        self.work = work
        self.moving = self.result = None
        self.resume(None)

    def resume(self, arrived):
        try:
            self.moving = self.work.send(arrived)
        except StopIteration as end:
            self.moving, self.result = None, end.value

    def beside(self, *others):
        if self.moving is None:
            return others
        arrived, others = lax.optimization_barrier((tuple(self.moving), others))
        self.resume(arrived)
        return others

    def finish(self):
        while self.moving is not None:
            self.beside()
        return self.result


def gather_line(block, slots):
    count = lax.axis_size("seq")
    if count != 8:
        slots += gather_slots(block, "seq", doublings(count))
        return slots
    two, six, one = yield swap(block, "seq", 2), middle(block), swap(block, "seq", 1)
    slots += [block, one]
    four, far, three = yield middle(two), outward(six), swap(two, "seq", 1)
    slots += [two, three]
    four = four + far
    far, five = yield outward(four), swap(four, "seq", 1)
    slots += [four, five]
    six = six + far
    (seven,) = yield (swap(six, "seq", 1),)
    slots += [six, seven]
    return slots


def gather_seq(block):
    return Steps(gather_line(block, [])).finish()


def reduce_line(parts, one=None):
    count = lax.axis_size("seq")
    if count != 8:
        return [reduce_slots(parts, "seq", doublings(count))]
    (seven,) = yield (swap(parts[7], "seq", 1),)
    six = add_low(parts[6], seven)
    near, five = yield inward(six), swap(parts[5], "seq", 1)
    four = add_low(parts[4], five, near)
    near, far, three = yield inward(four), middle(four), swap(parts[3], "seq", 1)
    six = add_low(six, near)
    two = add_low(parts[2], three, far)
    last = [swap(two, "seq", 2), middle(six)]
    if one is None:
        last.append(swap(parts[1], "seq", 1))
    last = yield last
    return [parts[0], *last] + ([] if one is None else [one])


def exchange_experts(block, packs, pack_slots, compute):
    count = lax.axis_size("seq")
    slots, y_parts, d_parts = [], [], []
    rows = Steps(gather_line(block, slots))

    def pair(m):
        y_pair, d_pair = compute(m, slots[m : m + 2])
        return [*y_pair, *d_pair]

    def keep(done):
        y_parts.extend(done[:2])
        d_parts.extend(done[2:])

    if count != 8:
        packs.finish()
        for m in range(0, count, 2):
            keep(pair(m))
        return y_parts, Steps(reduce_line(d_parts)).finish()
    packs.beside(*rows.beside())
    for m in (0, 2, 4):
        done = pair(m)
        keep(packs.beside(*rows.beside(*done)))
    one = swap(d_parts[1], "seq", 1)
    *done, one = lax.optimization_barrier((*pair(6), one))
    keep(done)
    return y_parts, Steps(reduce_line(d_parts, one)).finish()


def doublings(count):
    return [1 << bit for bit in range(count.bit_length() - 1)]


def add_low(*terms):
    total = terms[0].astype(F32)
    for term in terms[1:]:
        total = total + term.astype(F32)
    return lax.optimization_barrier(total.astype(BF))


def gather_groups(block, copies):
    return gather_slots(block, "ctx", [copies * m for m in doublings(GROUPS)[::-1]])


def reduce_groups(parts, copies, whole):
    parts = dict(enumerate(parts))
    for mask in doublings(GROUPS):
        for m in [m for m in parts if m & mask]:
            parts[m ^ mask] = add_low(parts[m ^ mask], swap(parts.pop(m), "ctx", copies * mask))
    total = parts[0]
    for mask in doublings(copies) if whole else []:
        total = add_low(total, swap(total, "ctx", mask))
    return total


def reduce_slots(parts, axis, masks):
    parts = dict(enumerate(parts))
    for step, mask in enumerate(masks):
        last = step == len(masks) - 1
        for m in [m for m in parts if m & mask]:
            arrived = swap(parts.pop(m), axis, mask)
            mine = parts[m ^ mask]
            parts[m ^ mask] = (
                mine.astype(F32) + arrived.astype(F32) if last else add_low(mine, arrived)
            )
    return parts[0]


def rotate(values, cosine, sine, sign):
    lane = lax.broadcasted_iota(jnp.int32, values.shape, 1)
    ahead = pltpu.roll(values, LANES - HEAD_DIM // 2, 1)
    behind = pltpu.roll(values, HEAD_DIM // 2, 1)
    other = jnp.where(lane % HEAD_DIM < HEAD_DIM // 2, ahead, behind)
    return values * cosine + (sign * other) * sine


def project_kernel(order_ref, h_ref, t_ref, up_ref, cos_ref, sin_ref, *rest):
    shards = rest[:-3]
    qkv_ref, full_ref, w_ref = rest[-3:]
    rows = shards[0].shape[0]

    @pl.when(pl.program_id(0) == 0)
    def _():
        for m, shard in enumerate(shards):
            start = pl.multiple_of(order_ref[m] * rows, rows)
            w_ref[pl.ds(start, rows), :] = shard[:, :LOCAL]
        full_ref[...] = w_ref[...]

    pre = dot(h_ref[...], w_ref[...]) + dot(t_ref[...], up_ref[...])
    cosine, sine = cos_ref[...], sin_ref[...]
    for j in range(LOCAL // LANES):
        part = pre[:, j * LANES : (j + 1) * LANES]
        if j <= PAIRS:
            part = rotate(part, cosine, sine, 1.0)
        if j < PAIRS:
            part = part * 0.125
        qkv_ref[:, j * LANES : (j + 1) * LANES] = part.astype(BF)


def project(order, h_one, rank_qkv, up_diag, cosine, sine, shards):
    length = h_one.shape[0]
    rows = shards[0].shape[0]
    per_block = lambda width: pl.BlockSpec((BLK, width), lambda i, order: (i, 0))
    whole = lambda shape: pl.BlockSpec(shape, lambda i, order: (0, 0))
    return pl.pallas_call(
        project_kernel,
        grid_spec=pltpu.PrefetchScalarGridSpec(
            num_scalar_prefetch=1,
            grid=(length // BLK,),
            in_specs=[
                per_block(D),
                per_block(3 * RANK),
                whole((3 * RANK, LOCAL)),
                per_block(LANES),
                per_block(LANES),
            ]
            + [whole((rows, LOCAL + QG))] * len(shards),
            out_specs=[per_block(LOCAL), whole((D, LOCAL))],
            scratch_shapes=[pltpu.VMEM((D, LOCAL), BF)],
        ),
        out_shape=[
            jax.ShapeDtypeStruct((length, LOCAL), BF),
            jax.ShapeDtypeStruct((D, LOCAL), BF),
        ],
        cost_estimate=pl.CostEstimate(
            flops=2 * length * D * LOCAL, bytes_accessed=2 * length * (D + LOCAL), transcendentals=0
        ),
        name="project",
    )(order, h_one, rank_qkv, up_diag, cosine, sine, *shards)


def half_mask(shape, half):
    lane = lax.broadcasted_iota(jnp.int32, shape, 1)
    return (lane < HEAD_DIM) if half == 0 else (lane >= HEAD_DIM)


def stack_rows(place_ref, source_ref, target_ref, first_lane):
    half = BLK // 2
    for b in range(source_ref.shape[0] // half):
        rows = pl.ds(pl.multiple_of(place_ref[b] * half, half), half)
        for pair in range(PAIRS):
            at = (b // 2) * PAIRS * BLK + pair * BLK + (b % 2) * half
            lanes = slice(first_lane + pair * LANES, first_lane + (pair + 1) * LANES)
            target_ref[at : at + half, :] = source_ref[rows, lanes]


def split_keys(place_ref, qkv_ref, first_lane, target_ref, ones):
    half = BLK // 2
    for b in range(qkv_ref.shape[0] // half):
        rows = pl.ds(pl.multiple_of(place_ref[b] * half, half), half)
        both = qkv_ref[rows, first_lane : first_lane + LANES]
        for side in range(2):
            other = jnp.zeros_like(both)
            if ones:
                lane = lax.broadcasted_iota(jnp.int32, both.shape, 1)
                spare = HEAD_DIM if side == 0 else 0
                other = jnp.where(lane == spare, 1.0, 0.0).astype(BF)
            target_ref[side, b * half : (b + 1) * half, :] = jnp.where(
                half_mask(both.shape, side), both, other
            )


def tile_bias(start_col, q_first, k_first):
    shape = (BLK, BLK)
    key = k_first + lax.broadcasted_iota(jnp.int32, shape, 1)
    query = q_first + lax.broadcasted_iota(jnp.int32, shape, 0)
    bias = jnp.where((key >= start_col) & (key <= query), 0.0, NEG)
    return jnp.concatenate([bias] * PAIRS, axis=0)


def attend_kernel(copies, place_ref, first_ref, qkv_ref, start_ref, o_ref, lse_ref, *refs):
    piece_refs, (q_s, k_s, v_s, score_s, m_s, acc_s) = refs[:GROUPS], refs[GROUPS:]
    stack_rows(place_ref, qkv_ref, q_s, 0)
    split_keys(place_ref, qkv_ref, QG, k_s, False)
    split_keys(place_ref, qkv_ref, QG + KG, v_s, True)
    half = BLK // 2
    tall = PAIRS * BLK

    def query_block(qb, unused):
        q_first = pl.multiple_of(qb * BLK, BLK)
        q_rows = pl.ds(pl.multiple_of(qb * tall, tall), tall)
        start_col = start_ref[pl.ds(q_first, BLK), :]
        queries = q_s[q_rows, :]
        m_s[...] = jnp.full(m_s.shape, NEG, F32)
        acc_s[...] = jnp.zeros(acc_s.shape, F32)

        def score_block(kb, unused):
            k_first = pl.multiple_of(kb * BLK, BLK)
            bias = tile_bias(start_col, q_first, k_first)
            for side in range(2):
                scores = dot_nt(queries, k_s[side, pl.ds(k_first, BLK), :]) + bias
                score_s[kb, side] = scores
                m_s[side] = jnp.maximum(
                    m_s[side], jnp.maximum(scores[:, :LANES], scores[:, LANES:])
                )
            return unused

        lax.fori_loop(first_ref[qb], qb + 1, score_block, 0)
        peaks = [jnp.max(m_s[side], axis=1, keepdims=True) for side in range(2)]

        def value_block(kb, unused):
            k_first = pl.multiple_of(kb * BLK, BLK)
            for side in range(2):
                prob = jnp.exp(score_s[kb, side] - peaks[side]).astype(BF)
                acc_s[side] += dot(prob, v_s[side, pl.ds(k_first, BLK), :])
            return unused

        lax.fori_loop(first_ref[qb], qb + 1, value_block, 0)
        low, high = acc_s[0], acc_s[1]
        low_sum = low[:, HEAD_DIM : HEAD_DIM + 1]
        high_sum = high[:, 0:1]
        is_low = half_mask(low.shape, 0)
        out = jnp.where(is_low, low / low_sum, high / high_sum).astype(BF)
        lse_ref[q_rows, :] = jnp.where(
            is_low, peaks[0] + jnp.log(low_sum), peaks[1] + jnp.log(high_sum)
        )
        for i in range(2):
            rows = pl.ds(pl.multiple_of(place_ref[2 * qb + i] * half, half), half)
            for pair in range(PAIRS):
                at = pair * BLK + i * half
                o_ref[rows, pair * LANES : (pair + 1) * LANES] = out[at : at + half, :]
        return unused

    lax.fori_loop(0, qkv_ref.shape[0] // BLK, query_block, 0)
    for j, piece in enumerate(piece_refs):
        tokens = piece.shape[0]
        piece[...] = o_ref[j * copies * tokens : (j * copies + 1) * tokens, :]


SMEM_SPEC = pl.BlockSpec(memory_space=pltpu.SMEM)
VMEM_SPEC = pl.BlockSpec(memory_space=pltpu.VMEM)


def attend(place, first, qkv, start_col, copies):
    length = qkv.shape[0]
    tall = PAIRS * BLK
    return pl.pallas_call(
        functools.partial(attend_kernel, copies),
        in_specs=[SMEM_SPEC, SMEM_SPEC, VMEM_SPEC, VMEM_SPEC],
        out_specs=[VMEM_SPEC] * (2 + GROUPS),
        out_shape=[
            jax.ShapeDtypeStruct((length, QG), BF),
            jax.ShapeDtypeStruct((PAIRS * length, LANES), F32),
        ]
        + [jax.ShapeDtypeStruct((length // (GROUPS * copies), QG), BF)] * GROUPS,
        scratch_shapes=[
            pltpu.VMEM((PAIRS * length, LANES), BF),
            pltpu.VMEM((2, length, LANES), BF),
            pltpu.VMEM((2, length, LANES), BF),
            pltpu.VMEM((length // BLK, 2, tall, BLK), F32),
            pltpu.VMEM((2, tall, LANES), F32),
            pltpu.VMEM((2, tall, LANES), F32),
        ],
        cost_estimate=pl.CostEstimate(
            flops=4 * length * length * QG, bytes_accessed=8 * length * QG, transcendentals=0
        ),
        name="attend",
    )(place, first, qkv, start_col)


def attend_back_kernel(
    place_ref,
    first_ref,
    qkv_ref,
    start_ref,
    o_ref,
    lse_ref,
    cos_ref,
    sin_ref,
    *refs,
):
    do_refs = refs[:-10]
    dqkv_ref, join_s, q_s, o_s, do_s, k_s, v_s, dk_s, dv_s, dq_s = refs[-10:]
    for m, piece in enumerate(do_refs):
        join_s[m * piece.shape[0] : (m + 1) * piece.shape[0], :] = piece[...]
    stack_rows(place_ref, qkv_ref, q_s, 0)
    stack_rows(place_ref, o_ref, o_s, 0)
    stack_rows(place_ref, join_s, do_s, 0)
    split_keys(place_ref, qkv_ref, QG, k_s, False)
    split_keys(place_ref, qkv_ref, QG + KG, v_s, False)
    dk_s[...] = jnp.zeros(dk_s.shape, F32)
    dv_s[...] = jnp.zeros(dv_s.shape, F32)
    half = BLK // 2
    tall = PAIRS * BLK

    def query_block(qb, unused):
        q_first = pl.multiple_of(qb * BLK, BLK)
        q_rows = pl.ds(pl.multiple_of(qb * tall, tall), tall)
        start_col = start_ref[pl.ds(q_first, BLK), :]
        dq_s[...] = jnp.zeros(dq_s.shape, F32)
        product = do_s[q_rows, :].astype(F32) * o_s[q_rows, :].astype(F32)
        lse = lse_ref[q_rows, :]
        lse_of = (lse[:, 0:1], lse[:, HEAD_DIM : HEAD_DIM + 1])
        delta_of = [
            jnp.sum(jnp.where(half_mask(product.shape, side), product, 0.0), axis=1, keepdims=True)
            for side in range(2)
        ]

        def key_block(kb, unused):
            k_first = pl.multiple_of(kb * BLK, BLK)
            k_rows = pl.ds(k_first, BLK)
            bias = tile_bias(start_col, q_first, k_first)
            queries = q_s[q_rows, :]
            d_out = do_s[q_rows, :]
            for side in range(2):
                keys = k_s[side, k_rows, :]
                scores = dot_nt(queries, keys) + bias
                prob = jnp.exp(scores - lse_of[side])
                d_prob = dot_nt(d_out, v_s[side, k_rows, :])
                d_score = (prob * (d_prob - delta_of[side])).astype(BF)
                dv_s[side, k_rows, :] += dot_tn(prob.astype(BF), d_out)
                dk_s[side, k_rows, :] += dot_tn(d_score, queries)
                dq_s[...] += dot(d_score, keys)
            return unused

        lax.fori_loop(first_ref[qb], qb + 1, key_block, 0)
        for i in range(2):
            rows = pl.ds(pl.multiple_of(place_ref[2 * qb + i] * half, half), half)
            cosine, sine = cos_ref[rows, :], sin_ref[rows, :]
            for pair in range(PAIRS):
                at = pair * BLK + i * half
                back = rotate(dq_s[at : at + half, :] * 0.125, cosine, sine, -1.0)
                dqkv_ref[rows, pair * LANES : (pair + 1) * LANES] = back.astype(BF)
        return unused

    lax.fori_loop(0, qkv_ref.shape[0] // BLK, query_block, 0)
    for b in range(qkv_ref.shape[0] // half):
        rows = pl.ds(pl.multiple_of(place_ref[b] * half, half), half)
        at = slice(b * half, (b + 1) * half)
        is_low = half_mask((half, LANES), 0)
        back = jnp.where(is_low, dk_s[0, at, :], dk_s[1, at, :])
        back = rotate(back, cos_ref[rows, :], sin_ref[rows, :], -1.0)
        dqkv_ref[rows, QG : QG + KG] = back.astype(BF)
        dqkv_ref[rows, QG + KG : LOCAL] = jnp.where(is_low, dv_s[0, at, :], dv_s[1, at, :]).astype(BF)


def attend_back(place, first, qkv, start_col, out, lse, cosine, sine, d_out):
    length = qkv.shape[0]
    tall = PAIRS * BLK
    stacked = pltpu.VMEM((PAIRS * length, LANES), BF)
    return pl.pallas_call(
        attend_back_kernel,
        in_specs=[SMEM_SPEC, SMEM_SPEC] + [VMEM_SPEC] * (6 + len(d_out)),
        out_specs=VMEM_SPEC,
        out_shape=jax.ShapeDtypeStruct((length, LOCAL), BF),
        scratch_shapes=[
            pltpu.VMEM((length, QG), BF),
            stacked,
            stacked,
            stacked,
            pltpu.VMEM((2, length, LANES), BF),
            pltpu.VMEM((2, length, LANES), BF),
            pltpu.VMEM((2, length, LANES), F32),
            pltpu.VMEM((2, length, LANES), F32),
            pltpu.VMEM((tall, LANES), F32),
        ],
        cost_estimate=pl.CostEstimate(
            flops=10 * length * length * QG, bytes_accessed=16 * length * QG, transcendentals=0
        ),
        name="attend_back",
    )(place, first, qkv, start_col, out, lse, cosine, sine, *d_out)


def expert_kernel(ids_ref, h_refs, p_refs, wgu_ref, wd_ref, tables, y_refs, d_refs, scratch):
    aux_w, gu_refs, da_refs, db_refs = tables
    aux_s, gu_s, sel_s, yrow_s, drow_s, grad_s = scratch
    step = pl.program_id(0)
    wide = lax.broadcasted_iota(jnp.int32, (h_refs[0].shape[0], LANES), 1)
    count = len(h_refs)
    lane = EXP_AT + ids_ref[count] + step

    @pl.when(step == 0)
    def _():
        grad_s[...] = jnp.zeros(grad_s.shape, F32)
        gu_s[...] = jnp.zeros(gu_s.shape, BF)
        for j in range(count):
            gu_s[j, 0, 0:RANK, :] = gu_refs[j][0, 0]
            gu_s[j, 1, RANK : 2 * RANK, :] = gu_refs[j][0, 1]
            both = dot_nt(h_refs[j][...], aux_w[j][0])
            chosen = p_refs[j][:, D:EXT].astype(F32) > 0.0
            picked = jnp.where(chosen, both, NEG)
            weights = jnp.exp(picked - jnp.max(picked, axis=1, keepdims=True))
            gates = weights / jnp.sum(weights, axis=1, keepdims=True)
            aux_s[j] = jnp.where(wide < EXP_AT, both, gates)

    rows, extra, upstream = [], [], []
    for j in range(count):
        ranks = p_refs[j][:, D:EXT].astype(F32)
        column = jnp.sum(jnp.where(wide == lane, ranks, 0.0), axis=1, keepdims=True)
        tall = ranks.T
        which = lax.broadcasted_iota(jnp.int32, tall.shape, 0)
        row = jnp.sum(jnp.where(which == lane, tall, 0.0), axis=0, keepdims=True)
        slot = lax.broadcasted_iota(jnp.int32, (CAP, tall.shape[1]), 0).astype(F32) + 1.0
        take = jnp.where(slot == row, 1.0, 0.0).astype(BF)
        sel_s[j, step] = jnp.where(wide.astype(F32) + 1.0 == column, 1.0, 0.0).astype(BF)
        aux = aux_s[j]
        gate = jnp.sum(jnp.where(wide == lane, aux, 0.0), axis=1, keepdims=True)
        gate_one = gate.astype(BF).astype(F32)
        gate_two = (gate - gate_one).astype(BF).astype(F32)
        gate_three = gate - gate_one - gate_two
        aux = jnp.where(wide < EXP_AT, aux, 0.0)
        aux = jnp.where(wide == GATE_AT, gate_one, aux)
        aux = jnp.where(wide == GATE_AT + 1, gate_two, aux)
        aux = jnp.where(wide == GATE_AT + 2, gate_three, aux)
        rows.append(dot(take, h_refs[j][...]).astype(BF))
        extra.append(dot(take, aux.astype(BF)))
        upstream.append(dot(take, p_refs[j][:, :D]))

    def each(make):
        return jnp.concatenate([make(j) for j in range(count)], axis=0)

    part = lambda arr, j: arr[j * CAP : (j + 1) * CAP]
    low_extra = [item.astype(BF) for item in extra]
    narrow = lax.broadcasted_iota(jnp.int32, (CAP, LANES), 1)
    gate = each(
        lambda j: jnp.sum(
            jnp.where((narrow >= GATE_AT) & (narrow < GATE_AT + 3), extra[j], 0.0),
            axis=1,
            keepdims=True,
        )
    )
    both = dot(jnp.concatenate(rows, axis=0), wgu_ref[0])
    gate_pre = both[:, :FF] + each(lambda j: dot(low_extra[j], gu_s[j, 0]))
    up_pre = both[:, FF:] + each(lambda j: dot(low_extra[j], gu_s[j, 1]))
    sigmoid = jax.nn.sigmoid(gate_pre)
    silu = gate_pre * sigmoid
    active = (silu * up_pre).astype(BF)
    down = [dot_nt(part(active, j), da_refs[j][0]).astype(BF) for j in range(count)]
    result = dot(active, wd_ref[0]) + each(lambda j: dot(down[j], db_refs[j][0]))
    result = result.astype(BF).astype(F32)
    grad_in = jnp.concatenate(upstream, axis=0)
    d_gate_val = jnp.sum(grad_in * result, axis=1, keepdims=True)
    weighted = (gate * result).astype(BF)
    d_result = (gate * grad_in).astype(BF)
    d_down = [dot_nt(part(d_result, j), db_refs[j][0]).astype(BF) for j in range(count)]
    d_active = dot_nt(d_result, wd_ref[0]) + each(lambda j: dot(d_down[j], da_refs[j][0]))
    d_gate = (d_active * up_pre * sigmoid * (1.0 + gate_pre * (1.0 - sigmoid))).astype(BF)
    d_up = (d_active * silu).astype(BF)
    d_rows = dot_nt(jnp.concatenate([d_gate, d_up], axis=1), wgu_ref[0]).astype(BF)
    for j in range(count):
        at = pl.ds(pl.multiple_of(step * CAP, CAP), CAP)
        yrow_s[j, at, :] = part(weighted, j)
        drow_s[j, at, :D] = part(d_rows, j)
        d_extra = dot_nt(part(d_gate, j), gu_s[j, 0]) + dot_nt(part(d_up, j), gu_s[j, 1])
        d_extra = d_extra + jnp.where(narrow == lane, part(d_gate_val, j), 0.0)
        drow_s[j, at, D:] = d_extra.astype(BF)
        grad_s[j, 0:RANK, 0:FF] += dot_tn(low_extra[j], part(d_gate, j))[0:RANK]
        grad_s[j, 0:RANK, FF : 2 * FF] += dot_tn(low_extra[j], part(d_up, j))[RANK : 2 * RANK]
        grad_s[j, 0:RANK, 2 * FF :] += dot_tn(d_down[j], part(active, j))
        grad_s[j, RANK:, :] += dot_tn(down[j], part(d_result, j))

    @pl.when(step == E_DEV - 1)
    def _():
        for j in range(count):
            tokens = h_refs[j].shape[0]
            put = jnp.concatenate([sel_s[j, e] for e in range(E_DEV)], axis=1)
            y_refs[j][...] = dot(put, yrow_s[j]).astype(BF)
            d_refs[j][:tokens, :] = dot(put, drow_s[j]).astype(BF)
            d_refs[j][tokens:, :D] = grad_s[j].astype(BF)
            d_refs[j][tokens:, D:] = jnp.zeros((2 * RANK, LANES), BF)


def experts(adapters, base, rows, packs, w_gate_up, w_down, aux_w, gu_up, down_a, down_b):
    count = len(rows)
    tokens = rows[0].shape[0]
    whole = lambda width: pl.BlockSpec((tokens, width), lambda e, ids: (0, 0))

    def table(shape, j):
        return pl.BlockSpec((1,) + shape, lambda e, ids: (ids[j],) + (0,) * len(shape))

    def body(ids_ref, *refs):
        refs = list(refs)
        take = lambda n: [refs.pop(0) for _ in range(n)]
        h_refs, p_refs = take(count), take(count)
        wgu_ref, wd_ref = take(2)
        tables = [take(count) for _ in range(4)]
        y_refs, d_refs = take(count), take(count)
        expert_kernel(ids_ref, h_refs, p_refs, wgu_ref, wd_ref, tables, y_refs, d_refs, refs)

    picked = [(LANES, D), (2, RANK, FF), (RANK, FF), (RANK, D)]
    shapes = [(tokens, D)] * count + [(tokens + 2 * RANK, EXT)] * count
    outs = pl.pallas_call(
        body,
        grid_spec=pltpu.PrefetchScalarGridSpec(
            num_scalar_prefetch=1,
            grid=(E_DEV,),
            in_specs=[whole(D)] * count
            + [whole(EXT)] * count
            + [
                pl.BlockSpec((1, D, 2 * FF), lambda e, ids: (e, 0, 0)),
                pl.BlockSpec((1, FF, D), lambda e, ids: (e, 0, 0)),
            ]
            + [table(shape, j) for shape in picked for j in range(count)],
            out_specs=[pl.BlockSpec(shape, lambda e, ids: (0, 0)) for shape in shapes],
            scratch_shapes=[
                pltpu.VMEM((count, tokens, LANES), F32),
                pltpu.VMEM((count, 2, LANES, FF), BF),
                pltpu.VMEM((count, E_DEV, tokens, CAP), BF),
                pltpu.VMEM((count, E_DEV * CAP, D), BF),
                pltpu.VMEM((count, E_DEV * CAP, EXT), BF),
                pltpu.VMEM((count, 2 * RANK, D), F32),
            ],
        ),
        out_shape=[jax.ShapeDtypeStruct(shape, BF) for shape in shapes],
        cost_estimate=pl.CostEstimate(
            flops=16 * count * E_DEV * CAP * D * FF,
            bytes_accessed=2 * E_DEV * 3 * D * FF + 8 * count * tokens * D,
            transcendentals=0,
        ),
        name="experts",
    )(
        jnp.concatenate([adapters, base[None]]).astype(jnp.int32),
        *rows,
        *packs,
        w_gate_up,
        w_down,
        *([aux_w] * count),
        *([gu_up] * count),
        *([down_a] * count),
        *([down_b] * count),
    )
    return list(outs[:count]), list(outs[count:])


def join_kernel(*refs):
    parts, out_ref = refs[:-1], refs[-1]
    for m, part in enumerate(parts):
        out_ref[m] = part[...]


def join(parts):
    return pl.pallas_call(
        join_kernel,
        in_specs=[VMEM_SPEC] * len(parts),
        out_specs=VMEM_SPEC,
        out_shape=jax.ShapeDtypeStruct((len(parts),) + parts[0].shape, parts[0].dtype),
        name="join",
    )(*parts)


def order_rows_kernel(order_ref, *refs):
    parts, out_ref = refs[:-1], refs[-1]
    rows = parts[0].shape[0]
    step = HEAD_DIM // 2
    for m, part in enumerate(parts):
        for i in range(rows // step):
            first = order_ref[m] * rows + i * step
            head = first // HEAD_DIM
            key, pair = head // PAIRS, head % PAIRS
            at = (key // 2) * QG + pair * LANES + (key % 2) * HEAD_DIM + first % HEAD_DIM
            at = pl.multiple_of(at, step)
            out_ref[pl.ds(at, step), :] = part[i * step : (i + 1) * step, LOCAL:]


def order_rows(order, parts):
    return pl.pallas_call(
        order_rows_kernel,
        in_specs=[SMEM_SPEC] + [VMEM_SPEC] * len(parts),
        out_specs=VMEM_SPEC,
        out_shape=jax.ShapeDtypeStruct((QW, QG), BF),
        name="order_rows",
    )(order, *parts)


def lanes_of(index):
    return pl.ds(pl.multiple_of(index * QG, LANES), QG)


def out_kernel(group_ref, x_ref, gain_ref, down_ref, up_ref, *refs):
    o_refs, w_refs = refs[:GROUPS], refs[GROUPS : 2 * GROUPS]
    att_ref, rank_ref, y_ref, h_ref = refs[2 * GROUPS :]
    group = group_ref[0]
    for j in range(GROUPS):
        att_ref[:, lanes_of(group ^ j)] = o_refs[j][...]
    attended = att_ref[...]
    for j in range(GROUPS):
        y_ref[:, lanes_of(group ^ j)] = dot(attended, w_refs[j][...])
    rank_out = dot_nt(attended, down_ref[...]).astype(BF)
    rank_ref[...] = rank_out
    y_one = x_ref[...].astype(F32) + y_ref[...] + dot(rank_out, up_ref[...])
    y_ref[...] = y_one
    inverse = lax.rsqrt(jnp.mean(y_one * y_one, axis=1, keepdims=True) + NORM_EPS)
    h_ref[...] = (y_one * inverse * gain_ref[...]).astype(BF)


def project_out(group, rows, gain, down_t, up, outs, w_parts):
    tokens = rows.shape[0]
    return pl.pallas_call(
        out_kernel,
        in_specs=[SMEM_SPEC] + [VMEM_SPEC] * (4 + 2 * GROUPS),
        out_specs=[VMEM_SPEC] * 4,
        out_shape=[
            jax.ShapeDtypeStruct((tokens, QW), BF),
            jax.ShapeDtypeStruct((tokens, RANK), BF),
            jax.ShapeDtypeStruct((tokens, D), F32),
            jax.ShapeDtypeStruct((tokens, D), BF),
        ],
        cost_estimate=pl.CostEstimate(
            flops=2 * tokens * QW * D, bytes_accessed=2 * QW * D + 12 * tokens * D, transcendentals=0
        ),
        name="project_out",
    )(group, rows, gain, down_t, up, *outs, *w_parts)


def natural_heads(tiles):
    is_low = half_mask(tiles[0].shape, 0)
    turn = lambda tile: pltpu.roll(tile, HEAD_DIM, 1)
    return [
        jnp.where(is_low, tiles[0], turn(tiles[1])),
        jnp.where(is_low, tiles[2], tiles[0]),
        jnp.where(is_low, turn(tiles[1]), tiles[2]),
    ]


def middle_kernel(count, terms, info_ref, *refs):
    refs = list(refs)
    take = lambda n: [refs.pop(0) for _ in range(n)]
    d_refs = take(terms)
    pack_ref, y_ref, h_ref, gain_ref, aux_ref, att_ref, rank_ref, down_ref, up_ref = take(9)
    w_refs = take(GROUPS)
    (dy_ref,) = take(1)
    do_refs, early_refs = take(count), take(GROUPS)
    do_s, early_s = refs
    group, ctx_index, copies = info_ref[0], info_ref[1], count // GROUPS
    tokens = y_ref.shape[0]
    d_sum = d_refs[0][...].astype(F32)
    for ref in d_refs[1:]:
        d_sum = d_sum + ref[...].astype(F32)
    early_s[0 : 2 * RANK, :] = d_sum[tokens:, :D]
    d_ext = d_sum[:tokens, D:]
    h_two = h_ref[...]
    lane = lax.broadcasted_iota(jnp.int32, (tokens, LANES), 1)
    chosen = pack_ref[:, D:EXT].astype(F32) > 0.0
    picked = jnp.where(chosen, dot_nt(h_two, aux_ref[...]), NEG)
    weights = jnp.exp(picked - jnp.max(picked, axis=1, keepdims=True))
    gates = weights / jnp.sum(weights, axis=1, keepdims=True)
    mixed = jnp.sum(jnp.where(chosen, gates * d_ext, 0.0), axis=1, keepdims=True)
    d_logits = jnp.where(chosen, gates * (d_ext - mixed), 0.0)
    d_ext = jnp.where(lane < EXP_AT, d_ext, d_logits).astype(BF)
    d_h = d_sum[:tokens, :D] + dot(d_ext, aux_ref[...])
    y_one = y_ref[...]
    inverse = lax.rsqrt(jnp.mean(y_one * y_one, axis=1, keepdims=True) + NORM_EPS)
    scaled = gain_ref[...] * d_h
    d_y = pack_ref[:, :D].astype(F32) + inverse * scaled
    d_y = d_y - y_one * inverse**3 * jnp.mean(y_one * scaled, axis=1, keepdims=True)
    dy_ref[...] = d_y
    d_attn = d_y.astype(BF)
    d_rank = dot_nt(d_attn, up_ref[...]).astype(BF)
    do_s[...] = dot(d_rank, down_ref[...])
    for j in range(GROUPS):
        at = lanes_of(group ^ j)
        early_s[3 * RANK : 4 * RANK, at] = dot_tn(rank_ref[...], dy_ref[:, at].astype(BF))
        do_s[...] += dot_nt(dy_ref[:, at].astype(BF), w_refs[j][...])
    for m in range(count):
        do_refs[m][...] = do_s[:, lanes_of((ctx_index ^ m) // copies)].astype(BF)
    down_grad = dot_tn(d_rank, att_ref[...])
    for g in range(GROUPS):
        tiles = [down_grad[:, g * QG + i * LANES : g * QG + (i + 1) * LANES] for i in range(PAIRS)]
        for i, tile in enumerate(natural_heads(tiles)):
            early_s[2 * RANK : 3 * RANK, g * QG + i * LANES : g * QG + (i + 1) * LANES] = tile
    early_s[4 * RANK :, :] = dot_tn(d_ext, h_two)[: 2 * RANK]
    for j in range(GROUPS):
        early_refs[j][...] = early_s[:, lanes_of(group ^ j)].astype(BF)


def middle_back(info, count, terms, pack, y_one, h_two, gain, aux, attended, rank_out, down_t, up, w_parts):
    tokens = y_one.shape[0]
    outs = pl.pallas_call(
        functools.partial(middle_kernel, count, len(terms)),
        in_specs=[SMEM_SPEC] + [VMEM_SPEC] * (len(terms) + 9 + GROUPS),
        out_specs=[VMEM_SPEC] * (1 + count + GROUPS),
        out_shape=[jax.ShapeDtypeStruct((tokens, D), F32)]
        + [jax.ShapeDtypeStruct((tokens, QG), BF)] * count
        + [jax.ShapeDtypeStruct((6 * RANK, QG), BF)] * GROUPS,
        scratch_shapes=[pltpu.VMEM((tokens, QW), F32), pltpu.VMEM((6 * RANK, D), F32)],
        cost_estimate=pl.CostEstimate(
            flops=2 * tokens * QW * D, bytes_accessed=2 * QW * D + 20 * tokens * D, transcendentals=0
        ),
        name="middle_back",
    )(info, *terms, pack, y_one, h_two, gain, aux, attended, rank_out, down_t, up, *w_parts)
    return outs[0], list(outs[1 : 1 + count]), list(outs[1 + count :])


def inputs_kernel(group_ref, dqkv_ref, w_ref, up_ref, down_ref, t_ref, h_ref, *refs):
    count = len(refs) - 3 - GROUPS
    rows_refs, grad_ref, piece_refs = refs[:count], refs[count], refs[count + 1 : -2]
    grad_s, down_s = refs[-2:]
    step = pl.program_id(0)

    @pl.when(step == 0)
    def _():
        grad_s[...] = jnp.zeros(grad_s.shape, F32)
        down_s[...] = jnp.zeros(down_s.shape, F32)

    d_qkv = dqkv_ref[...]
    d_rank = dot_nt(d_qkv, up_ref[...]).astype(BF)
    rows = (dot_nt(d_qkv, w_ref[...]) + dot_nt(d_rank, down_ref[...])).astype(BF)
    for m in range(count):

        @pl.when(step == m)
        def _():
            rows_refs[m][...] = rows

    ranks = t_ref[...]
    grad_s[...] += dot_tn(ranks, d_qkv)
    down_s[...] += dot_tn(d_rank, h_ref[...])

    @pl.when(step == count - 1)
    def _():
        tiles = [grad_s[:RANK, i * LANES : (i + 1) * LANES] for i in range(PAIRS)]
        for i, tile in enumerate(natural_heads(tiles)):
            grad_ref[:, i * LANES : (i + 1) * LANES] = tile.astype(BF)
        keys = slice(QG, QG + KG)
        grad_ref[:, keys] = grad_s[RANK : 2 * RANK, keys].astype(BF)
        grad_ref[:, QG + KG :] = grad_s[2 * RANK :, QG + KG :].astype(BF)
        for j in range(GROUPS):
            piece = down_s[:, lanes_of(group_ref[0] ^ j)].astype(BF)
            for i in range(3):
                piece_refs[j][:, i * QG : (i + 1) * QG] = piece[i * RANK : (i + 1) * RANK]


def inputs_back(group, count, d_qkv, cols_all, up_diag, down_sel, rank_qkv, h_one):
    length = d_qkv.shape[0]
    tokens = length // count
    per_block = lambda width: pl.BlockSpec((tokens, width), lambda i: (i, 0))
    whole = lambda shape: pl.BlockSpec(shape, lambda i: (0, 0))
    shapes = [(tokens, D)] * count + [(RANK, LOCAL)] + [(RANK, 3 * QG)] * GROUPS
    outs = pl.pallas_call(
        inputs_kernel,
        grid=(count,),
        in_specs=[
            SMEM_SPEC,
            per_block(LOCAL),
            whole((D, LOCAL)),
            whole((3 * RANK, LOCAL)),
            whole((D, 3 * RANK)),
            per_block(3 * RANK),
            per_block(D),
        ],
        out_specs=[whole(shape) for shape in shapes],
        out_shape=[jax.ShapeDtypeStruct(shape, BF) for shape in shapes],
        scratch_shapes=[pltpu.VMEM((3 * RANK, LOCAL), F32), pltpu.VMEM((3 * RANK, D), F32)],
        cost_estimate=pl.CostEstimate(
            flops=2 * length * D * LOCAL, bytes_accessed=4 * length * (D + LOCAL), transcendentals=0
        ),
        name="inputs_back",
    )(group, d_qkv, cols_all, up_diag, down_sel, rank_qkv, h_one)
    return list(outs[:count]), outs[count], list(outs[count + 1 :])


def place_kernel(ids_ref, *refs):
    parts = refs[:2]
    up_ref, down_ref, gu_ref, da_ref, db_ref, od_ref, ou_ref, gd_ref, sum_s = refs[2:]
    sources = parts[0].shape[0]
    up_ref[...] = jnp.zeros(up_ref.shape, F32)
    down_ref[...] = jnp.zeros(down_ref.shape, F32)
    sum_s[...] = jnp.zeros(sum_s.shape, F32)
    for j in range(GROUPS):
        group = ids_ref[sources] ^ j
        keys = lambda first: pl.ds(pl.multiple_of(first + group * KG, LANES), KG)
        rows = slice((j // 2) * RANK, (j // 2 + 1) * RANK)
        for m in range(sources):
            a = ids_ref[m]
            take = lambda first, width: parts[j % 2][m, rows, first : first + width].astype(F32)
            up_ref[a, :, lanes_of(group)] += take(0, QG)
            up_ref[a, :, keys(QW)] += take(QG, KG)
            up_ref[a, :, keys(QW + KVW)] += take(QG + KG, KG)
            for i in range(3):
                at = slice(i * RANK, (i + 1) * RANK)
                down_ref[a, at, lanes_of(group)] += take(LOCAL + i * QG, QG)
            for i in range(6):
                at = slice(i * RANK, (i + 1) * RANK)
                sum_s[a, at, lanes_of(group)] += take(LOCAL + (3 + i) * QG, QG)
    for a in range(ADAPT):
        gu_ref[a, 0] = sum_s[a, :RANK, :FF]
        gu_ref[a, 1] = sum_s[a, :RANK, FF : 2 * FF]
        da_ref[a] = sum_s[a, :RANK, 2 * FF :]
        db_ref[a] = sum_s[a, RANK : 2 * RANK]
        od_ref[a] = sum_s[a, 2 * RANK : 3 * RANK]
        ou_ref[a] = sum_s[a, 3 * RANK : 4 * RANK]
        gd_ref[a] = sum_s[a, 4 * RANK :]


def place_grads(ids, near, far):
    shapes = [(RANK, QW + 2 * KVW), (3 * RANK, D), (2, RANK, FF), (RANK, FF), (RANK, D)]
    shapes += [(RANK, QW), (RANK, D), (2 * RANK, D)]
    return pl.pallas_call(
        place_kernel,
        in_specs=[SMEM_SPEC] + [VMEM_SPEC] * 2,
        out_specs=[VMEM_SPEC] * len(shapes),
        out_shape=[jax.ShapeDtypeStruct((ADAPT,) + shape, F32) for shape in shapes],
        scratch_shapes=[pltpu.VMEM((ADAPT, 6 * RANK, D), F32)],
        name="place_grads",
    )(ids, near, far)


def norm_backward(values, inverse, gain_vec, upstream):
    scaled = gain_vec * upstream
    return inverse * scaled - values * inverse**3 * jnp.mean(
        values * scaled, axis=-1, keepdims=True
    )


def pair_columns(columns):
    lead = columns.shape[:-1]
    heads = columns.reshape(lead + (2 * PAIRS, HEAD_DIM))
    return heads[..., jnp.array(PAIR_ORDER), :].reshape(lead + (QG,))


def local_columns(table, group):
    lead = table.shape[:-1]
    cut = lambda first, width: lax.dynamic_slice_in_dim(
        table, first + group * width, width, table.ndim - 1
    )
    return cut(0, QG), cut(QW, KG), cut(QW + KVW, KG)


def on_device(
    inputs,
    cotangent,
    segment_ids,
    expert_ids,
    adapter_ids,
    gain_one,
    w_qkv,
    w_out,
    gain_two,
    router,
    w_gate_up,
    w_down,
    qkv_down,
    qkv_up,
    out_down,
    out_up,
    gu_down,
    gu_up,
    down_a,
    down_b,
):
    ctx_count = lax.axis_size("ctx")
    seq_count = lax.axis_size("seq")
    ctx_index = lax.axis_index("ctx")
    seq_index = lax.axis_index("seq")
    tokens = inputs.shape[1]
    length = tokens * ctx_count
    experts_all = router.shape[1]
    copies = ctx_count // GROUPS
    group = ctx_index // copies
    half = tokens // 2
    ctx_masks = doublings(ctx_count)[::-1]
    seq_slots = (seq_index ^ jnp.arange(seq_count)).astype(jnp.int32)
    ctx_slots = ctx_index ^ jnp.arange(ctx_count)
    own_rows = inputs[0]

    row_slots = gather_slots(own_rows, "ctx", ctx_masks)
    own_q, own_k, own_v = local_columns(w_qkv, group)
    own_out = lax.dynamic_slice_in_dim(w_out, group * QG, QG, 1)
    col_slots = gather_seq(jnp.concatenate([pair_columns(own_q), own_k, own_v, own_out], axis=1))
    chosen = expert_ids[0]
    hot = jnp.any(chosen[:, :, None] == jnp.arange(experts_all)[None, None, :], axis=1)
    hot_low = hot.astype(BF)
    before = (jnp.arange(tokens)[:, None] >= jnp.arange(tokens)[None, :]).astype(BF)
    ranks = dot(before, hot_low).astype(BF) * hot_low
    ranks = jnp.pad(ranks, ((0, 0), (EXP_AT, LANES - EXP_AT - experts_all)))
    pack = jnp.concatenate([cotangent[0], ranks], axis=1)
    pack, *col_slots = together(pack, *col_slots)
    pack_slots = []
    packs = Steps(gather_line(pack, pack_slots))
    out_parts = gather_groups(order_rows(seq_slots, col_slots), copies)

    seg_row = segment_ids[0]
    position = jnp.arange(length)
    start = jnp.sum((seg_row[None, :] < seg_row[:, None]).astype(jnp.int32), axis=1)
    block_id = jnp.stack([ctx_slots, 2 * ctx_count - 1 - ctx_slots], axis=1).reshape(-1)
    block_of = jnp.arange(2 * ctx_count)
    owner = jnp.minimum(block_of, 2 * ctx_count - 1 - block_of)
    place = (2 * (owner ^ ctx_index) + (block_of >= ctx_count)).astype(jnp.int32)
    first = (start[::BLK] // BLK).astype(jnp.int32)
    offset = (position - start).reshape(2 * ctx_count, half)[block_id].reshape(-1)
    frequency = 10000.0 ** (-2.0 * jnp.arange(HEAD_DIM // 2).astype(F32) / HEAD_DIM)
    angles = offset.astype(F32)[:, None] * frequency[None, :]
    cosine, sine = jnp.cos(angles), jnp.sin(angles)
    cosine = jnp.concatenate([cosine] * 4, axis=1)
    sine = jnp.concatenate([-sine, sine, -sine, sine], axis=1)
    start_col = start[:, None]
    adapter = adapter_ids[seq_index]
    slot_adapters = adapter_ids[seq_slots]
    slots_and_group = jnp.concatenate([slot_adapters, group[None]]).astype(jnp.int32)
    group_info = group[None].astype(jnp.int32)

    def pick(table):
        return lax.dynamic_index_in_dim(table, adapter, 0, keepdims=False)

    qkv_down_sel = pick(qkv_down)
    up_q, up_k, up_v = local_columns(pick(qkv_up), group)
    up_diag = jnp.concatenate(
        [
            jnp.pad(pair_columns(up_q), ((0, 0), (0, 2 * KG))),
            jnp.pad(up_k, ((0, 0), (QG, KG))),
            jnp.pad(up_v, ((0, 0), (QG + KG, 0))),
        ],
        axis=0,
    )
    out_down_sel = pick(out_down).T.reshape(RANK, GROUPS, 2, PAIRS, HEAD_DIM)
    out_down_sel = jnp.transpose(out_down_sel, (0, 1, 3, 2, 4)).reshape(RANK, QW)
    out_up_sel = pick(out_up)
    aux_w = jnp.concatenate(
        [
            jnp.swapaxes(gu_down, 1, 2),
            jnp.broadcast_to(router.T[None], (ADAPT, experts_all, D)),
            jnp.zeros((ADAPT, LANES - 2 * RANK - experts_all, D), BF),
        ],
        axis=1,
    )
    down_a_t = jnp.swapaxes(down_a, 1, 2)

    all_rows = jnp.concatenate(row_slots, axis=0).astype(F32)
    inv_all = lax.rsqrt(jnp.mean(all_rows * all_rows, axis=-1, keepdims=True) + NORM_EPS)
    h_one = (all_rows * inv_all * gain_one).astype(BF)
    rank_qkv = dot(h_one, qkv_down_sel).astype(BF)
    qkv, cols_all = project(seq_slots, h_one, rank_qkv, up_diag, cosine, sine, col_slots)
    heads_out, lse, *pieces = packs.beside(*attend(place, first, qkv, start_col, copies))
    heads_here = [
        swap(piece, "ctx", j * copies) if j else piece for j, piece in enumerate(pieces)
    ]
    attended, rank_out, y_one, h_two = project_out(
        group_info, own_rows, gain_two[None], out_down_sel, out_up_sel, heads_here, out_parts
    )
    attended, rank_out, y_one, h_two = packs.beside(attended, rank_out, y_one, h_two)

    def compute(m, rows):
        return experts(
            slot_adapters[m : m + 2],
            E_DEV * seq_index,
            rows,
            pack_slots[m : m + 2],
            w_gate_up,
            w_down,
            aux_w,
            gu_up,
            down_a_t,
            down_b,
        )

    y_parts, d_terms = exchange_experts(h_two, packs, pack_slots, compute)
    d_terms, y_parts = lax.optimization_barrier((d_terms, y_parts))
    y_sums = Steps(reduce_line(y_parts))

    d_y_one, d_heads, early = middle_back(
        jnp.stack([group, ctx_index]).astype(jnp.int32),
        ctx_count,
        d_terms,
        pack,
        y_one,
        h_two,
        gain_two[None],
        pick(aux_w),
        attended,
        rank_out,
        out_down_sel,
        out_up_sel,
        out_parts,
    )
    d_heads = [swap(piece, "ctx", m) if m else piece for m, piece in enumerate(d_heads)]
    d_y_one, *d_heads = y_sums.beside(d_y_one, *d_heads)

    (d_qkv,) = y_sums.beside(
        attend_back(place, first, qkv, start_col, heads_out, lse, cosine, sine, d_heads)
    )
    d_rows, late, late_down = inputs_back(
        group_info, ctx_count, d_qkv, cols_all, up_diag, qkv_down_sel, rank_qkv, h_one
    )

    early = reduce_groups(early, copies, True)
    late_down = reduce_groups(late_down, copies, False)
    early, late, late_down = y_sums.beside(early, late, late_down)
    grads = jnp.concatenate(
        [late, late_down] + [early[i * RANK : (i + 1) * RANK] for i in range(6)], axis=1
    )
    grads = jnp.concatenate([grads, swap(grads, "ctx", 2 * copies)], axis=0)
    grads = join(gather_seq(grads))
    (
        grad_qkv_up,
        grad_qkv_down,
        grad_gu_up,
        grad_down_a,
        grad_down_b,
        grad_out_down,
        grad_out_up,
        grad_gu_down,
    ) = place_grads(slots_and_group, grads, swap(grads, "ctx", copies))

    layer_output = y_one
    for term in y_sums.finish():
        layer_output = layer_output + term.astype(F32)

    d_h_one = reduce_ctx(d_rows, copies)
    features = own_rows.astype(F32)
    inv_one = lax.rsqrt(jnp.mean(features * features, axis=-1, keepdims=True) + NORM_EPS)
    input_grad = d_y_one + norm_backward(features, inv_one, gain_one, d_h_one)
    return (
        layer_output.astype(BF)[None],
        input_grad[None],
        jnp.swapaxes(grad_qkv_down, 1, 2),
        grad_qkv_up,
        jnp.swapaxes(grad_out_down, 1, 2),
        grad_out_up,
        jnp.swapaxes(grad_gu_down, 1, 2),
        grad_gu_up,
        jnp.swapaxes(grad_down_a, 1, 2),
        grad_down_b,
    )


def reduce_ctx(parts, copies):
    parts = dict(enumerate(parts))
    masks = doublings(len(parts))
    for mask in masks:
        for m in [m for m in parts if m & mask]:
            sent = parts.pop(m)
            if mask >= copies:
                parts[m ^ mask] = add_low(parts[m ^ mask], swap(sent, "ctx", mask))
    return parts[0].astype(F32)


def solution(mesh):
    over_seq = P("seq", None)
    placed = (
        P("seq", "ctx", None),
        P("seq", "ctx", None),
        over_seq,
        P("seq", "ctx", None),
        P(),
        P(),
        over_seq,
        over_seq,
        P(),
        P(),
        P("seq", None, None),
        P("seq", None, None),
    ) + (P(),) * 8
    return jax.shard_map(
        on_device,
        mesh=mesh,
        in_specs=placed,
        out_specs=(P("seq", "ctx", None), P("seq", "ctx", None)) + (P(),) * 8,
        check_vma=False,
    )
```

```python
import functools

import jax
import jax.numpy as jnp
from jax import lax
from jax.experimental import pallas as pl
from jax.experimental.pallas import tpu as pltpu
from jax.sharding import PartitionSpec as P

D = 1536
HEADS = 24
KV_HEADS = 8
HEAD_DIM = 64
FF = 512
RANK = 16
ADAPT = 8
E_DEV = 2
CAP = 128
QW = 1536
KVW = 512
NORM_EPS = 1e-05

GROUPS = KV_HEADS // 2
PAIRS = HEADS // KV_HEADS
QG = QW // GROUPS
KG = KVW // GROUPS
LOCAL = QG + 2 * KG
BLK = 256
LANES = 128
EXP_AT = 2 * RANK
GATE_AT = 96
EXT = D + LANES
NEG = -1e30

BF = jnp.bfloat16
F32 = jnp.float32
NT = (((1,), (1,)), ((), ()))
TN = (((0,), (0,)), ((), ()))


def dot(left_arr, right_arr):
    return jnp.dot(left_arr, right_arr, preferred_element_type=F32)


def dot_nt(left_arr, right_arr):
    return lax.dot_general(left_arr, right_arr, NT, preferred_element_type=F32)


def dot_tn(left_arr, right_arr):
    return lax.dot_general(left_arr, right_arr, TN, preferred_element_type=F32)


def swap(block, axis, mask):
    count = lax.axis_size(axis)
    return lax.ppermute(block, axis, [(i, i ^ mask) for i in range(count)])


def gather_slots(block, axis, masks):
    slots = {0: block}
    for mask in masks:
        for have in list(slots):
            slots[have ^ mask] = swap(slots[have], axis, mask)
    return [slots[m] for m in sorted(slots)]


def together(*arrays):
    return lax.optimization_barrier(arrays)


def gather_rest(block, arrived, masks):
    slots = {0: block}
    for mask, first in zip(masks, arrived):
        for have in list(slots):
            slots[have ^ mask] = swap(slots[have], "ctx", mask) if have else first
    return [slots[m] for m in sorted(slots)]


def line_swap(block, pairs):
    return lax.ppermute(block, "seq", [(2 * i + j, 2 * k + j) for i, k in pairs for j in (0, 1)])


def outward(block):
    return line_swap(block, [(1, 0), (2, 3)])


def inward(block):
    return line_swap(block, [(0, 1), (3, 2)])


def middle(block):
    return line_swap(block, [(1, 2), (2, 1)])


class Steps:
    def __init__(self, work):
        self.work = work
        self.moving = self.result = None
        self.resume(None)

    def resume(self, arrived):
        try:
            self.moving = self.work.send(arrived)
        except StopIteration as end:
            self.moving, self.result = None, end.value

    def beside(self, *others):
        if self.moving is None:
            return others
        arrived, others = lax.optimization_barrier((tuple(self.moving), others))
        self.resume(arrived)
        return others

    def join(self, other, *others):
        if self.moving is None or other.moving is None:
            return self.beside(*other.beside(*others))
        mine, theirs, others = lax.optimization_barrier(
            (tuple(self.moving), tuple(other.moving), others)
        )
        self.resume(mine)
        other.resume(theirs)
        return others

    def finish(self):
        while self.moving is not None:
            self.beside()
        return self.result


def gather_line(block, slots):
    count = lax.axis_size("seq")
    if count != 8:
        slots += gather_slots(block, "seq", doublings(count))
        return slots
    slots.append(block)
    two, six, one = yield swap(block, "seq", 2), middle(block), swap(block, "seq", 1)
    slots += [one, two]
    four, far, three = yield middle(two), outward(six), swap(two, "seq", 1)
    four = four + far
    slots += [three, four]
    far, five = yield outward(four), swap(four, "seq", 1)
    six = six + far
    slots += [five, six]
    (seven,) = yield (swap(six, "seq", 1),)
    slots.append(seven)
    return slots


def gather_seq(block):
    return Steps(gather_line(block, [])).finish()


def reduce_line(parts, one=None):
    count = lax.axis_size("seq")
    if count != 8:
        return [reduce_slots(parts, "seq", doublings(count))]
    (seven,) = yield (swap(parts[7], "seq", 1),)
    six = add_low(parts[6], seven)
    near, five = yield inward(six), swap(parts[5], "seq", 1)
    four = add_low(parts[4], five, near)
    near, far, three = yield inward(four), middle(four), swap(parts[3], "seq", 1)
    six = add_low(six, near)
    two = add_low(parts[2], three, far)
    last = [swap(two, "seq", 2), middle(six)]
    if one is None:
        last.append(swap(parts[1], "seq", 1))
    last = yield last
    return [parts[0], *last] + ([] if one is None else [one])


def exchange_experts(block, packs, compute):
    count = lax.axis_size("seq")
    slots, y_parts, d_parts = [], [], []
    rows = Steps(gather_line(block, slots))

    def slots_of(m, some):
        some_y, some_d = compute(m, slots[m : m + some])
        return [*some_y, *some_d]

    def keep(done, some):
        y_parts.extend(done[:some])
        d_parts.extend(done[some:])

    if count != 8:
        packs.finish()
        for m in range(0, count, 2):
            keep(slots_of(m, 2), 2)
        return Steps(reduce_line(y_parts)), Steps(reduce_line(d_parts)).finish()
    keep(rows.join(packs, *slots_of(0, 1)), 1)
    for m in (1, 3, 5):
        keep(rows.beside(*slots_of(m, 2)), 2)
    one = swap(d_parts[1], "seq", 1)
    *done, one = lax.optimization_barrier((*slots_of(7, 1), one))
    keep(done, 1)
    terms = Steps(reduce_line(d_parts, one))
    terms.beside()
    terms.beside()
    y_sums = Steps(reduce_line(list(terms.beside(*y_parts))))
    return y_sums, terms.finish()


def doublings(count):
    return [1 << bit for bit in range(count.bit_length() - 1)]


def add_low(*terms):
    total = terms[0].astype(F32)
    for term in terms[1:]:
        total = total + term.astype(F32)
    return lax.optimization_barrier(total.astype(BF))


def gather_groups(block, copies):
    two, one = yield swap(block, "ctx", 2 * copies), swap(block, "ctx", copies)
    return [block, one, two, swap(two, "ctx", copies)]


def reduce_slots(parts, axis, masks):
    parts = dict(enumerate(parts))
    for step, mask in enumerate(masks):
        last = step == len(masks) - 1
        for m in [m for m in parts if m & mask]:
            arrived = swap(parts.pop(m), axis, mask)
            mine = parts[m ^ mask]
            parts[m ^ mask] = (
                mine.astype(F32) + arrived.astype(F32) if last else add_low(mine, arrived)
            )
    return parts[0]


def rotate(values, cosine, sine, sign):
    lane = lax.broadcasted_iota(jnp.int32, values.shape, 1)
    ahead = pltpu.roll(values, LANES - HEAD_DIM // 2, 1)
    behind = pltpu.roll(values, HEAD_DIM // 2, 1)
    other = jnp.where(lane % HEAD_DIM < HEAD_DIM // 2, ahead, behind)
    return values * cosine + (sign * other) * sine


def project_kernel(info_ref, h_ref, t_ref, table_ref, cos_ref, sin_ref, *rest):
    shards = rest[:-4]
    qkv_ref, full_ref, up_ref, w_ref = rest[-4:]
    rows = shards[0].shape[0]
    group = info_ref[len(shards) + 1]

    @pl.when(pl.program_id(0) == 0)
    def _():
        for m, shard in enumerate(shards):
            start = pl.multiple_of(info_ref[m] * rows, rows)
            w_ref[pl.ds(start, rows), :] = shard[:, :LOCAL]
        full_ref[...] = w_ref[...]
        up_ref[...] = jnp.zeros(up_ref.shape, BF)
        columns = lambda first, width: table_ref[
            0, :, pl.ds(pl.multiple_of(first + group * width, LANES), width)
        ]
        up_ref[:RANK, :QG] = columns(0, QG)
        up_ref[RANK : 2 * RANK, QG : QG + KG] = columns(QW, KG)
        up_ref[2 * RANK :, QG + KG :] = columns(QW + KVW, KG)

    pre = dot(h_ref[...], w_ref[...]) + dot(t_ref[...], up_ref[...])
    cosine, sine = cos_ref[...], sin_ref[...]
    tiles = [rotate(tile, cosine, sine, 1.0) * 0.125 for tile in lane_tiles(pre)]
    tiles = paired_heads(tiles)
    tiles.append(rotate(pre[:, QG : QG + KG], cosine, sine, 1.0))
    tiles.append(pre[:, QG + KG :])
    for j, tile in enumerate(tiles):
        qkv_ref[:, j * LANES : (j + 1) * LANES] = tile.astype(BF)


def project(order, adapter, group, h_one, rank_qkv, table, cosine, sine, shards):
    length = h_one.shape[0]
    rows = shards[0].shape[0]
    count = len(shards)
    per_block = lambda width: pl.BlockSpec((BLK, width), lambda i, info: (i, 0))
    whole = lambda shape: pl.BlockSpec(shape, lambda i, info: (0, 0))
    return pl.pallas_call(
        project_kernel,
        grid_spec=pltpu.PrefetchScalarGridSpec(
            num_scalar_prefetch=1,
            grid=(length // BLK,),
            in_specs=[
                per_block(D),
                per_block(3 * RANK),
                pl.BlockSpec((1,) + table.shape[1:], lambda i, info: (info[count], 0, 0)),
                per_block(LANES),
                per_block(LANES),
            ]
            + [whole((rows, LOCAL + QG))] * count,
            out_specs=[per_block(LOCAL), whole((D, LOCAL)), whole((3 * RANK, LOCAL))],
            scratch_shapes=[pltpu.VMEM((D, LOCAL), BF)],
        ),
        out_shape=[
            jax.ShapeDtypeStruct((length, LOCAL), BF),
            jax.ShapeDtypeStruct((D, LOCAL), BF),
            jax.ShapeDtypeStruct((3 * RANK, LOCAL), BF),
        ],
        cost_estimate=pl.CostEstimate(
            flops=2 * length * D * LOCAL, bytes_accessed=2 * length * (D + LOCAL), transcendentals=0
        ),
        name="project",
    )(
        jnp.concatenate([order, adapter[None], group[None]]).astype(jnp.int32),
        h_one,
        rank_qkv,
        table,
        cosine,
        sine,
        *shards,
    )


def half_mask(shape, half):
    lane = lax.broadcasted_iota(jnp.int32, shape, 1)
    return (lane < HEAD_DIM) if half == 0 else (lane >= HEAD_DIM)


def turned(tile):
    return pltpu.roll(tile.astype(F32), HEAD_DIM, 1).astype(tile.dtype)


def paired_heads(tiles):
    is_low = half_mask(tiles[0].shape, 0)
    return [
        jnp.where(is_low, tiles[0], tiles[1]),
        jnp.where(is_low, turned(tiles[0]), turned(tiles[2])),
        jnp.where(is_low, tiles[1], tiles[2]),
    ]


def natural_heads(tiles):
    is_low = half_mask(tiles[0].shape, 0)
    return [
        jnp.where(is_low, tiles[0], turned(tiles[1])),
        jnp.where(is_low, tiles[2], tiles[0]),
        jnp.where(is_low, turned(tiles[1]), tiles[2]),
    ]


def lane_tiles(block):
    return [block[:, i * LANES : (i + 1) * LANES] for i in range(PAIRS)]


def stack_rows(place_ref, source_ref, target_ref, paired):
    half = BLK // 2
    for b in range(source_ref.shape[0] // half):
        rows = pl.ds(pl.multiple_of(place_ref[b] * half, half), half)
        tiles = lane_tiles(source_ref[rows, :QG])
        for pair, tile in enumerate(tiles if paired else paired_heads(tiles)):
            at = (b // 2) * PAIRS * BLK + pair * BLK + (b % 2) * half
            target_ref[at : at + half, :] = tile


def split_keys(place_ref, qkv_ref, first_lane, target_ref, ones):
    half = BLK // 2
    for b in range(qkv_ref.shape[0] // half):
        rows = pl.ds(pl.multiple_of(place_ref[b] * half, half), half)
        both = qkv_ref[rows, first_lane : first_lane + LANES]
        for side in range(2):
            other = jnp.zeros_like(both)
            if ones:
                lane = lax.broadcasted_iota(jnp.int32, both.shape, 1)
                spare = HEAD_DIM if side == 0 else 0
                other = jnp.where(lane == spare, 1.0, 0.0).astype(BF)
            target_ref[side, b * half : (b + 1) * half, :] = jnp.where(
                half_mask(both.shape, side), both, other
            )


def tile_bias(start_col, q_first, k_first):
    shape = (BLK, BLK)
    key = k_first + lax.broadcasted_iota(jnp.int32, shape, 1)
    query = q_first + lax.broadcasted_iota(jnp.int32, shape, 0)
    bias = jnp.where((key >= start_col) & (key <= query), 0.0, NEG)
    return jnp.concatenate([bias] * PAIRS, axis=0)


def attend_kernel(copies, place_ref, first_ref, qkv_ref, start_ref, o_ref, lse_ref, *refs):
    piece_refs, (q_s, k_s, v_s, score_s, m_s, acc_s) = refs[:GROUPS], refs[GROUPS:]
    stack_rows(place_ref, qkv_ref, q_s, True)
    split_keys(place_ref, qkv_ref, QG, k_s, False)
    split_keys(place_ref, qkv_ref, QG + KG, v_s, True)
    half = BLK // 2
    tall = PAIRS * BLK

    def query_block(qb, unused):
        q_first = pl.multiple_of(qb * BLK, BLK)
        q_rows = pl.ds(pl.multiple_of(qb * tall, tall), tall)
        start_col = start_ref[pl.ds(q_first, BLK), :]
        queries = q_s[q_rows, :]
        m_s[...] = jnp.full(m_s.shape, NEG, F32)
        acc_s[...] = jnp.zeros(acc_s.shape, F32)

        def score_block(kb, unused):
            k_first = pl.multiple_of(kb * BLK, BLK)
            bias = tile_bias(start_col, q_first, k_first)
            for side in range(2):
                scores = dot_nt(queries, k_s[side, pl.ds(k_first, BLK), :]) + bias
                score_s[kb, side] = scores
                m_s[side] = jnp.maximum(
                    m_s[side], jnp.maximum(scores[:, :LANES], scores[:, LANES:])
                )
            return unused

        lax.fori_loop(first_ref[qb], qb + 1, score_block, 0)
        peaks = [jnp.max(m_s[side], axis=1, keepdims=True) for side in range(2)]

        def value_block(kb, unused):
            k_first = pl.multiple_of(kb * BLK, BLK)
            for side in range(2):
                prob = jnp.exp(score_s[kb, side] - peaks[side]).astype(BF)
                acc_s[side] += dot(prob, v_s[side, pl.ds(k_first, BLK), :])
            return unused

        lax.fori_loop(first_ref[qb], qb + 1, value_block, 0)
        low, high = acc_s[0], acc_s[1]
        low_sum = low[:, HEAD_DIM : HEAD_DIM + 1]
        high_sum = high[:, 0:1]
        is_low = half_mask(low.shape, 0)
        out = jnp.where(is_low, low / low_sum, high / high_sum).astype(BF)
        lse_ref[q_rows, :] = jnp.where(
            is_low, peaks[0] + jnp.log(low_sum), peaks[1] + jnp.log(high_sum)
        )
        for i in range(2):
            rows = pl.ds(pl.multiple_of(place_ref[2 * qb + i] * half, half), half)
            tiles = [out[pair * BLK + i * half :][:half] for pair in range(PAIRS)]
            for pair, tile in enumerate(natural_heads(tiles)):
                o_ref[rows, pair * LANES : (pair + 1) * LANES] = tile
        return unused

    lax.fori_loop(0, qkv_ref.shape[0] // BLK, query_block, 0)
    for j, piece in enumerate(piece_refs):
        tokens = piece.shape[0]
        piece[...] = o_ref[j * copies * tokens : (j * copies + 1) * tokens, :]


SMEM_SPEC = pl.BlockSpec(memory_space=pltpu.SMEM)
VMEM_SPEC = pl.BlockSpec(memory_space=pltpu.VMEM)


def attend(place, first, qkv, start_col, copies):
    length = qkv.shape[0]
    tall = PAIRS * BLK
    return pl.pallas_call(
        functools.partial(attend_kernel, copies),
        in_specs=[SMEM_SPEC, SMEM_SPEC, VMEM_SPEC, VMEM_SPEC],
        out_specs=[VMEM_SPEC] * (2 + GROUPS),
        out_shape=[
            jax.ShapeDtypeStruct((length, QG), BF),
            jax.ShapeDtypeStruct((PAIRS * length, LANES), F32),
        ]
        + [jax.ShapeDtypeStruct((length // (GROUPS * copies), QG), BF)] * GROUPS,
        scratch_shapes=[
            pltpu.VMEM((PAIRS * length, LANES), BF),
            pltpu.VMEM((2, length, LANES), BF),
            pltpu.VMEM((2, length, LANES), BF),
            pltpu.VMEM((length // BLK, 2, tall, BLK), F32),
            pltpu.VMEM((2, tall, LANES), F32),
            pltpu.VMEM((2, tall, LANES), F32),
        ],
        cost_estimate=pl.CostEstimate(
            flops=4 * length * length * QG, bytes_accessed=8 * length * QG, transcendentals=0
        ),
        name="attend",
    )(place, first, qkv, start_col)


def attend_back_kernel(
    place_ref,
    first_ref,
    qkv_ref,
    start_ref,
    o_ref,
    lse_ref,
    cos_ref,
    sin_ref,
    *refs,
):
    do_refs = refs[:-10]
    dqkv_ref, join_s, q_s, o_s, do_s, k_s, v_s, dk_s, dv_s, dq_s = refs[-10:]
    for m, piece in enumerate(do_refs):
        join_s[m * piece.shape[0] : (m + 1) * piece.shape[0], :] = piece[...]
    stack_rows(place_ref, qkv_ref, q_s, True)
    stack_rows(place_ref, o_ref, o_s, False)
    stack_rows(place_ref, join_s, do_s, False)
    split_keys(place_ref, qkv_ref, QG, k_s, False)
    split_keys(place_ref, qkv_ref, QG + KG, v_s, False)
    dk_s[...] = jnp.zeros(dk_s.shape, F32)
    dv_s[...] = jnp.zeros(dv_s.shape, F32)
    half = BLK // 2
    tall = PAIRS * BLK

    def query_block(qb, unused):
        q_first = pl.multiple_of(qb * BLK, BLK)
        q_rows = pl.ds(pl.multiple_of(qb * tall, tall), tall)
        start_col = start_ref[pl.ds(q_first, BLK), :]
        dq_s[...] = jnp.zeros(dq_s.shape, F32)
        product = do_s[q_rows, :].astype(F32) * o_s[q_rows, :].astype(F32)
        lse = lse_ref[q_rows, :]
        lse_of = (lse[:, 0:1], lse[:, HEAD_DIM : HEAD_DIM + 1])
        delta_of = [
            jnp.sum(jnp.where(half_mask(product.shape, side), product, 0.0), axis=1, keepdims=True)
            for side in range(2)
        ]

        def key_block(kb, unused):
            k_first = pl.multiple_of(kb * BLK, BLK)
            k_rows = pl.ds(k_first, BLK)
            bias = tile_bias(start_col, q_first, k_first)
            queries = q_s[q_rows, :]
            d_out = do_s[q_rows, :]
            for side in range(2):
                keys = k_s[side, k_rows, :]
                scores = dot_nt(queries, keys) + bias
                prob = jnp.exp(scores - lse_of[side])
                d_prob = dot_nt(d_out, v_s[side, k_rows, :])
                d_score = (prob * (d_prob - delta_of[side])).astype(BF)
                dv_s[side, k_rows, :] += dot_tn(prob.astype(BF), d_out)
                dk_s[side, k_rows, :] += dot_tn(d_score, queries)
                dq_s[...] += dot(d_score, keys)
            return unused

        lax.fori_loop(first_ref[qb], qb + 1, key_block, 0)
        for i in range(2):
            rows = pl.ds(pl.multiple_of(place_ref[2 * qb + i] * half, half), half)
            cosine, sine = cos_ref[rows, :], sin_ref[rows, :]
            tiles = []
            for pair in range(PAIRS):
                at = pair * BLK + i * half
                tiles.append(rotate(dq_s[at : at + half, :] * 0.125, cosine, sine, -1.0))
            for pair, tile in enumerate(natural_heads(tiles)):
                dqkv_ref[rows, pair * LANES : (pair + 1) * LANES] = tile.astype(BF)
        return unused

    lax.fori_loop(0, qkv_ref.shape[0] // BLK, query_block, 0)
    for b in range(qkv_ref.shape[0] // half):
        rows = pl.ds(pl.multiple_of(place_ref[b] * half, half), half)
        at = slice(b * half, (b + 1) * half)
        is_low = half_mask((half, LANES), 0)
        back = jnp.where(is_low, dk_s[0, at, :], dk_s[1, at, :])
        back = rotate(back, cos_ref[rows, :], sin_ref[rows, :], -1.0)
        dqkv_ref[rows, QG : QG + KG] = back.astype(BF)
        dqkv_ref[rows, QG + KG : LOCAL] = jnp.where(is_low, dv_s[0, at, :], dv_s[1, at, :]).astype(BF)


def attend_back(place, first, qkv, start_col, out, lse, cosine, sine, d_out):
    length = qkv.shape[0]
    tall = PAIRS * BLK
    stacked = pltpu.VMEM((PAIRS * length, LANES), BF)
    return pl.pallas_call(
        attend_back_kernel,
        in_specs=[SMEM_SPEC, SMEM_SPEC] + [VMEM_SPEC] * (6 + len(d_out)),
        out_specs=VMEM_SPEC,
        out_shape=jax.ShapeDtypeStruct((length, LOCAL), BF),
        scratch_shapes=[
            pltpu.VMEM((length, QG), BF),
            stacked,
            stacked,
            stacked,
            pltpu.VMEM((2, length, LANES), BF),
            pltpu.VMEM((2, length, LANES), BF),
            pltpu.VMEM((2, length, LANES), F32),
            pltpu.VMEM((2, length, LANES), F32),
            pltpu.VMEM((tall, LANES), F32),
        ],
        cost_estimate=pl.CostEstimate(
            flops=10 * length * length * QG, bytes_accessed=16 * length * QG, transcendentals=0
        ),
        name="attend_back",
    )(place, first, qkv, start_col, out, lse, cosine, sine, *d_out)


def expert_kernel(ids_ref, h_refs, p_refs, wgu_ref, wd_ref, tables, y_refs, d_refs, scratch):
    aux_w, gu_refs, da_refs, db_refs = tables
    wgu_s, wd_s, gu_s, put_s, x_s, g_s, extra_s, yrow_s, drow_s, grad_s, sems = scratch
    count = len(h_refs)
    tokens = h_refs[0].shape[0]

    def fetch(e):
        return [
            pltpu.make_async_copy(wgu_ref.at[e], wgu_s.at[e], sems.at[0, e]),
            pltpu.make_async_copy(wd_ref.at[e], wd_s.at[e], sems.at[1, e]),
        ]

    for e in range(E_DEV):
        for copy in fetch(e):
            copy.start()
    wide = lax.broadcasted_iota(jnp.int32, (tokens, LANES), 1)
    narrow = lax.broadcasted_iota(jnp.int32, (CAP, LANES), 1)
    base = EXP_AT + ids_ref[count]
    grad_s[...] = jnp.zeros(grad_s.shape, F32)
    gu_s[...] = jnp.zeros(gu_s.shape, BF)
    part = lambda arr, j: arr[j * CAP : (j + 1) * CAP]
    for j in range(count):
        gu_s[j, 0, 0:RANK, :] = gu_refs[j][0, 0]
        gu_s[j, 1, RANK : 2 * RANK, :] = gu_refs[j][0, 1]
        both = dot_nt(h_refs[j][...], aux_w[j][0])
        ranks = p_refs[j][:, D:EXT].astype(F32)
        chosen = ranks > 0.0
        picked = jnp.where(chosen, both, NEG)
        weights = jnp.exp(picked - jnp.max(picked, axis=1, keepdims=True))
        gates = weights / jnp.sum(weights, axis=1, keepdims=True)
        aux = jnp.where(wide < EXP_AT, both, 0.0)
        tall = ranks.T
        which = lax.broadcasted_iota(jnp.int32, tall.shape, 0)
        slot = lax.broadcasted_iota(jnp.int32, (CAP, tokens), 0).astype(F32) + 1.0
        takes = []
        for e in range(E_DEV):
            column = jnp.sum(jnp.where(wide == base + e, ranks, 0.0), axis=1, keepdims=True)
            row = jnp.sum(jnp.where(which == base + e, tall, 0.0), axis=0, keepdims=True)
            takes.append(jnp.where(slot == row, 1.0, 0.0).astype(BF))
            put_s[j, :, e * CAP : (e + 1) * CAP] = jnp.where(
                wide.astype(F32) + 1.0 == column, 1.0, 0.0
            ).astype(BF)
            gate = jnp.sum(jnp.where(wide == base + e, gates, 0.0), axis=1, keepdims=True)
            gate_one = gate.astype(BF).astype(F32)
            gate_two = (gate - gate_one).astype(BF).astype(F32)
            first = GATE_AT + 3 * e
            aux = jnp.where(wide == first, gate_one, aux)
            aux = jnp.where(wide == first + 1, gate_two, aux)
            aux = jnp.where(wide == first + 2, gate - gate_one - gate_two, aux)
        take = jnp.concatenate(takes, axis=0)
        at = slice(j * CAP, (j + 1) * CAP)
        rows = dot(take, h_refs[j][...]).astype(BF)
        upstream = dot(take, p_refs[j][:, :D]).astype(BF)
        extra = dot(take, aux.astype(BF))
        for e in range(E_DEV):
            x_s[e, at, :] = part(rows, e)
            g_s[e, at, :] = part(upstream, e)
            extra_s[e, at, :] = part(extra, e)

    def each(make):
        return jnp.concatenate([make(j) for j in range(count)], axis=0)

    def expert(e, unused):
        for copy in fetch(e):
            copy.wait()
        extra = extra_s[e]
        low_extra = extra.astype(BF)
        place = lax.broadcasted_iota(jnp.int32, extra.shape, 1) - (GATE_AT + 3 * e)
        gate = jnp.sum(jnp.where((place >= 0) & (place < 3), extra, 0.0), axis=1, keepdims=True)
        both = dot(x_s[e], wgu_s[e])
        gate_pre = both[:, :FF] + each(lambda j: dot(part(low_extra, j), gu_s[j, 0]))
        up_pre = both[:, FF:] + each(lambda j: dot(part(low_extra, j), gu_s[j, 1]))
        sigmoid = jax.nn.sigmoid(gate_pre)
        silu = gate_pre * sigmoid
        active = (silu * up_pre).astype(BF)
        down = [dot_nt(part(active, j), da_refs[j][0]).astype(BF) for j in range(count)]
        result = dot(active, wd_s[e]) + each(lambda j: dot(down[j], db_refs[j][0]))
        result = result.astype(BF).astype(F32)
        grad_in = g_s[e].astype(F32)
        d_gate_val = jnp.sum(grad_in * result, axis=1, keepdims=True)
        weighted = (gate * result).astype(BF)
        d_result = (gate * grad_in).astype(BF)
        d_down = [dot_nt(part(d_result, j), db_refs[j][0]).astype(BF) for j in range(count)]
        d_active = dot_nt(d_result, wd_s[e]) + each(lambda j: dot(d_down[j], da_refs[j][0]))
        d_gate = (d_active * up_pre * sigmoid * (1.0 + gate_pre * (1.0 - sigmoid))).astype(BF)
        d_up = (d_active * silu).astype(BF)
        d_rows = dot_nt(jnp.concatenate([d_gate, d_up], axis=1), wgu_s[e]).astype(BF)
        at = pl.ds(pl.multiple_of(e * CAP, CAP), CAP)
        for j in range(count):
            yrow_s[j, at, :] = part(weighted, j)
            drow_s[j, at, :D] = part(d_rows, j)
            d_extra = dot_nt(part(d_gate, j), gu_s[j, 0]) + dot_nt(part(d_up, j), gu_s[j, 1])
            d_extra = d_extra + jnp.where(narrow == base + e, part(d_gate_val, j), 0.0)
            drow_s[j, at, D:] = d_extra.astype(BF)
            ranks_in = part(low_extra, j)
            grad_s[j, 0:RANK, 0:FF] += dot_tn(ranks_in, part(d_gate, j))[0:RANK]
            grad_s[j, 0:RANK, FF : 2 * FF] += dot_tn(ranks_in, part(d_up, j))[RANK : 2 * RANK]
            grad_s[j, 0:RANK, 2 * FF :] += dot_tn(d_down[j], part(active, j))
            grad_s[j, RANK:, :] += dot_tn(down[j], part(d_result, j))
        return unused

    lax.fori_loop(0, E_DEV, expert, 0)
    for j in range(count):
        put = put_s[j]
        y_refs[j][...] = dot(put, yrow_s[j]).astype(BF)
        d_refs[j][:tokens, :] = dot(put, drow_s[j]).astype(BF)
        d_refs[j][tokens:, :D] = grad_s[j].astype(BF)
        d_refs[j][tokens:, D:] = jnp.zeros((2 * RANK, LANES), BF)


def experts(adapters, base, rows, packs, w_gate_up, w_down, aux_w, gu_up, down_a, down_b):
    count = len(rows)
    tokens = rows[0].shape[0]
    whole = lambda width: pl.BlockSpec((tokens, width), lambda e, ids: (0, 0))

    def table(shape, j):
        return pl.BlockSpec((1,) + shape, lambda e, ids: (ids[j],) + (0,) * len(shape))

    def body(ids_ref, *refs):
        refs = list(refs)
        take = lambda n: [refs.pop(0) for _ in range(n)]
        h_refs, p_refs = take(count), take(count)
        wgu_ref, wd_ref = take(2)
        tables = [take(count) for _ in range(4)]
        y_refs, d_refs = take(count), take(count)
        expert_kernel(ids_ref, h_refs, p_refs, wgu_ref, wd_ref, tables, y_refs, d_refs, refs)

    picked = [(LANES, D), (2, RANK, FF), (RANK, FF), (RANK, D)]
    shapes = [(tokens, D)] * count + [(tokens + 2 * RANK, EXT)] * count
    height = count * CAP
    outs = pl.pallas_call(
        body,
        grid_spec=pltpu.PrefetchScalarGridSpec(
            num_scalar_prefetch=1,
            grid=(1,),
            in_specs=[whole(D)] * count
            + [whole(EXT)] * count
            + [pl.BlockSpec(memory_space=pl.ANY)] * 2
            + [table(shape, j) for shape in picked for j in range(count)],
            out_specs=[pl.BlockSpec(shape, lambda e, ids: (0, 0)) for shape in shapes],
            scratch_shapes=[
                pltpu.VMEM((E_DEV, D, 2 * FF), BF),
                pltpu.VMEM((E_DEV, FF, D), BF),
                pltpu.VMEM((count, 2, LANES, FF), BF),
                pltpu.VMEM((count, tokens, E_DEV * CAP), BF),
                pltpu.VMEM((E_DEV, height, D), BF),
                pltpu.VMEM((E_DEV, height, D), BF),
                pltpu.VMEM((E_DEV, height, LANES), F32),
                pltpu.VMEM((count, E_DEV * CAP, D), BF),
                pltpu.VMEM((count, E_DEV * CAP, EXT), BF),
                pltpu.VMEM((count, 2 * RANK, D), F32),
                pltpu.SemaphoreType.DMA((2, E_DEV)),
            ],
        ),
        out_shape=[jax.ShapeDtypeStruct(shape, BF) for shape in shapes],
        cost_estimate=pl.CostEstimate(
            flops=16 * count * E_DEV * CAP * D * FF,
            bytes_accessed=2 * E_DEV * 3 * D * FF + 8 * count * tokens * D,
            transcendentals=0,
        ),
        name="experts",
    )(
        jnp.concatenate([adapters, base[None]]).astype(jnp.int32),
        *rows,
        *packs,
        w_gate_up,
        w_down,
        *([aux_w] * count),
        *([gu_up] * count),
        *([down_a] * count),
        *([down_b] * count),
    )
    return list(outs[:count]), list(outs[count:])


def join_kernel(*refs):
    parts, out_ref = refs[:-1], refs[-1]
    for m, part in enumerate(parts):
        out_ref[m] = part[...]


def join(parts):
    return pl.pallas_call(
        join_kernel,
        in_specs=[VMEM_SPEC] * len(parts),
        out_specs=VMEM_SPEC,
        out_shape=jax.ShapeDtypeStruct((len(parts),) + parts[0].shape, parts[0].dtype),
        name="join",
    )(*parts)


def order_rows_kernel(order_ref, *refs):
    parts, out_ref = refs[:-1], refs[-1]
    rows = parts[0].shape[0]
    for m, part in enumerate(parts):
        out_ref[pl.ds(pl.multiple_of(order_ref[m] * rows, rows), rows), :] = part[:, LOCAL:]


def order_rows(order, parts):
    return pl.pallas_call(
        order_rows_kernel,
        in_specs=[SMEM_SPEC] + [VMEM_SPEC] * len(parts),
        out_specs=VMEM_SPEC,
        out_shape=jax.ShapeDtypeStruct((QW, QG), BF),
        name="order_rows",
    )(order, *parts)


def lanes_of(index):
    return pl.ds(pl.multiple_of(index * QG, LANES), QG)


def by_adapter(table):
    return pl.BlockSpec((1,) + table.shape[1:], lambda i, info: (info[0], 0, 0))


def out_kernel(info_ref, x_ref, gain_ref, down_ref, up_ref, *refs):
    o_refs, w_refs = refs[:GROUPS], refs[GROUPS : 2 * GROUPS]
    att_ref, rank_ref, y_ref, h_ref = refs[2 * GROUPS :]
    group = info_ref[1]
    for j in range(GROUPS):
        att_ref[:, lanes_of(group ^ j)] = o_refs[j][...]
    attended = att_ref[...]
    for j in range(GROUPS):
        y_ref[:, lanes_of(group ^ j)] = dot(attended, w_refs[j][...])
    rank_out = dot_nt(attended, down_ref[0]).astype(BF)
    rank_ref[...] = rank_out
    y_one = x_ref[...].astype(F32) + y_ref[...] + dot(rank_out, up_ref[0])
    y_ref[...] = y_one
    inverse = lax.rsqrt(jnp.mean(y_one * y_one, axis=1, keepdims=True) + NORM_EPS)
    h_ref[...] = (y_one * inverse * gain_ref[...]).astype(BF)


def project_out(info, rows, gain, down_t, up, outs, w_parts):
    tokens = rows.shape[0]
    return pl.pallas_call(
        out_kernel,
        grid_spec=pltpu.PrefetchScalarGridSpec(
            num_scalar_prefetch=1,
            grid=(1,),
            in_specs=[VMEM_SPEC] * 2
            + [by_adapter(down_t), by_adapter(up)]
            + [VMEM_SPEC] * (2 * GROUPS),
            out_specs=[VMEM_SPEC] * 4,
        ),
        out_shape=[
            jax.ShapeDtypeStruct((tokens, QW), BF),
            jax.ShapeDtypeStruct((tokens, RANK), BF),
            jax.ShapeDtypeStruct((tokens, D), F32),
            jax.ShapeDtypeStruct((tokens, D), BF),
        ],
        cost_estimate=pl.CostEstimate(
            flops=2 * tokens * QW * D, bytes_accessed=2 * QW * D + 12 * tokens * D, transcendentals=0
        ),
        name="project_out",
    )(info, rows, gain, down_t, up, *outs, *w_parts)


def middle_kernel(count, terms, info_ref, *refs):
    refs = list(refs)
    take = lambda n: [refs.pop(0) for _ in range(n)]
    d_refs = take(terms)
    pack_ref, y_ref, h_ref, gain_ref, aux_ref, att_ref, rank_ref, down_ref, up_ref = take(9)
    w_refs = take(GROUPS)
    (dy_ref,) = take(1)
    do_refs, early_refs = take(count), take(GROUPS)
    do_s, early_s = refs
    group, ctx_index, copies = info_ref[1], info_ref[2], count // GROUPS
    tokens = y_ref.shape[0]
    d_sum = d_refs[0][...].astype(F32)
    for ref in d_refs[1:]:
        d_sum = d_sum + ref[...].astype(F32)
    early_s[0 : 2 * RANK, :] = d_sum[tokens:, :D]
    d_ext = d_sum[:tokens, D:]
    h_two = h_ref[...]
    lane = lax.broadcasted_iota(jnp.int32, (tokens, LANES), 1)
    chosen = pack_ref[:, D:EXT].astype(F32) > 0.0
    picked = jnp.where(chosen, dot_nt(h_two, aux_ref[0]), NEG)
    weights = jnp.exp(picked - jnp.max(picked, axis=1, keepdims=True))
    gates = weights / jnp.sum(weights, axis=1, keepdims=True)
    mixed = jnp.sum(jnp.where(chosen, gates * d_ext, 0.0), axis=1, keepdims=True)
    d_logits = jnp.where(chosen, gates * (d_ext - mixed), 0.0)
    d_ext = jnp.where(lane < EXP_AT, d_ext, d_logits).astype(BF)
    d_h = d_sum[:tokens, :D] + dot(d_ext, aux_ref[0])
    y_one = y_ref[...]
    inverse = lax.rsqrt(jnp.mean(y_one * y_one, axis=1, keepdims=True) + NORM_EPS)
    scaled = gain_ref[...] * d_h
    d_y = pack_ref[:, :D].astype(F32) + inverse * scaled
    d_y = d_y - y_one * inverse**3 * jnp.mean(y_one * scaled, axis=1, keepdims=True)
    dy_ref[...] = d_y
    d_attn = d_y.astype(BF)
    d_rank = dot_nt(d_attn, up_ref[0]).astype(BF)
    do_s[...] = dot(d_rank, down_ref[0])
    for j in range(GROUPS):
        at = lanes_of(group ^ j)
        early_s[3 * RANK : 4 * RANK, at] = dot_tn(rank_ref[...], dy_ref[:, at].astype(BF))
        do_s[...] += dot_nt(dy_ref[:, at].astype(BF), w_refs[j][...])
    for m in range(count):
        do_refs[m][...] = do_s[:, lanes_of((ctx_index ^ m) // copies)].astype(BF)
    early_s[2 * RANK : 3 * RANK, :] = dot_tn(d_rank, att_ref[...])
    early_s[4 * RANK :, :] = dot_tn(d_ext, h_two)[: 2 * RANK]
    for j in range(GROUPS):
        for i in range(6):
            block = early_s[i * RANK : (i + 1) * RANK, lanes_of(group ^ j)]
            early_refs[j][:, i * QG : (i + 1) * QG] = block.astype(BF)


def middle_back(info, count, terms, pack, y_one, h_two, gain, aux, attended, rank_out, down_t, up, w_parts):
    tokens = y_one.shape[0]
    outs = pl.pallas_call(
        functools.partial(middle_kernel, count, len(terms)),
        grid_spec=pltpu.PrefetchScalarGridSpec(
            num_scalar_prefetch=1,
            grid=(1,),
            in_specs=[VMEM_SPEC] * (len(terms) + 4)
            + [by_adapter(aux)]
            + [VMEM_SPEC] * 2
            + [by_adapter(down_t), by_adapter(up)]
            + [VMEM_SPEC] * GROUPS,
            out_specs=[VMEM_SPEC] * (1 + count + GROUPS),
            scratch_shapes=[pltpu.VMEM((tokens, QW), F32), pltpu.VMEM((6 * RANK, D), F32)],
        ),
        out_shape=[jax.ShapeDtypeStruct((tokens, D), F32)]
        + [jax.ShapeDtypeStruct((tokens, QG), BF)] * count
        + [jax.ShapeDtypeStruct((RANK, 6 * QG), BF)] * GROUPS,
        cost_estimate=pl.CostEstimate(
            flops=2 * tokens * QW * D, bytes_accessed=2 * QW * D + 20 * tokens * D, transcendentals=0
        ),
        name="middle_back",
    )(info, *terms, pack, y_one, h_two, gain, aux, attended, rank_out, down_t, up, *w_parts)
    return outs[0], list(outs[1 : 1 + count]), list(outs[1 + count :])


def ranks_kernel(group_ref, dqkv_ref, up_ref, t_ref, h_ref, *refs):
    early_refs, (rank_ref, keep_ref, send_ref) = refs[:GROUPS], refs[GROUPS:]
    d_qkv = dqkv_ref[...]
    d_rank = dot_nt(d_qkv, up_ref[...]).astype(BF)
    rank_ref[...] = d_rank
    grad = dot_tn(t_ref[...], d_qkv)
    keep_ref[:, :QG] = grad[:RANK, :QG].astype(BF)
    keep_ref[:, QG : QG + KG] = grad[RANK : 2 * RANK, QG : QG + KG].astype(BF)
    keep_ref[:, QG + KG : LOCAL] = grad[2 * RANK :, QG + KG :].astype(BF)
    send_ref[:, :LOCAL] = jnp.zeros((RANK, LOCAL), BF)
    for j in range(GROUPS):
        target = send_ref if j % 2 else keep_ref
        down = dot_tn(d_rank, h_ref[:, lanes_of(group_ref[0] ^ j)]).astype(BF)
        first = LOCAL + (j // 2) * 3 * QG
        for i in range(3):
            target[:, first + i * QG : first + (i + 1) * QG] = down[i * RANK : (i + 1) * RANK]
        first = LOCAL + 6 * QG + (j // 2) * 6 * QG
        target[:, first : first + 6 * QG] = early_refs[j][...]


HALF = LOCAL + 18 * QG
BOTH = HALF + LOCAL


def ranks_back(group, d_qkv, up_diag, rank_qkv, h_one, early):
    length = d_qkv.shape[0]
    return pl.pallas_call(
        ranks_kernel,
        in_specs=[SMEM_SPEC] + [VMEM_SPEC] * (4 + GROUPS),
        out_specs=[VMEM_SPEC] * 3,
        out_shape=[
            jax.ShapeDtypeStruct((length, 3 * RANK), BF),
            jax.ShapeDtypeStruct((RANK, HALF), BF),
            jax.ShapeDtypeStruct((RANK, HALF), BF),
        ],
        name="ranks_back",
    )(group, d_qkv, up_diag, rank_qkv, h_one, *early)


def mix_kernel(near_ref, far_ref, out_ref):
    out_ref[:, :LOCAL] = near_ref[:, :LOCAL]
    out_ref[:, LOCAL : 2 * LOCAL] = far_ref[:, :LOCAL]
    first = LOCAL
    for width in (3 * QG, 6 * QG):
        for mine, theirs in ((0, width), (width, 0)):
            total = near_ref[:, first + mine : first + mine + width].astype(F32)
            total = total + far_ref[:, first + theirs : first + theirs + width].astype(F32)
            at = LOCAL + first + mine
            out_ref[:, at : at + width] = total.astype(BF)
        first += 2 * width


def mix(near, far):
    return pl.pallas_call(
        mix_kernel,
        in_specs=[VMEM_SPEC] * 2,
        out_specs=VMEM_SPEC,
        out_shape=jax.ShapeDtypeStruct((RANK, BOTH), BF),
        name="mix",
    )(near, far)


def inputs_kernel(dqkv_ref, rank_ref, w_ref, down_ref, *rows_refs):
    rows = dot_nt(dqkv_ref[...], w_ref[...]) + dot_nt(rank_ref[...], down_ref[...])
    rows = rows.astype(BF)
    for m, ref in enumerate(rows_refs):

        @pl.when(pl.program_id(0) == m)
        def _():
            ref[...] = rows


def inputs_back(count, d_qkv, d_rank, cols_all, down_sel):
    length = d_qkv.shape[0]
    tokens = length // count
    per_block = lambda width: pl.BlockSpec((tokens, width), lambda i: (i, 0))
    whole = lambda shape: pl.BlockSpec(shape, lambda i: (0, 0))
    return pl.pallas_call(
        inputs_kernel,
        grid=(count,),
        in_specs=[
            per_block(LOCAL),
            per_block(3 * RANK),
            whole((D, LOCAL)),
            whole((D, 3 * RANK)),
        ],
        out_specs=[whole((tokens, D))] * count,
        out_shape=[jax.ShapeDtypeStruct((tokens, D), BF)] * count,
        cost_estimate=pl.CostEstimate(
            flops=2 * length * D * LOCAL, bytes_accessed=4 * length * (D + LOCAL), transcendentals=0
        ),
        name="inputs_back",
    )(d_qkv, d_rank, cols_all, down_sel)


def place_kernel(ids_ref, *refs):
    parts = refs[:2]
    up_ref, down_ref, gu_ref, da_ref, db_ref, od_ref, ou_ref, gd_ref, sum_s = refs[2:]
    sources = parts[0].shape[0]
    up_ref[...] = jnp.zeros(up_ref.shape, F32)
    down_ref[...] = jnp.zeros(down_ref.shape, F32)
    sum_s[...] = jnp.zeros(sum_s.shape, F32)
    for j in range(GROUPS):
        group = ids_ref[sources] ^ j
        keys = lambda first: pl.ds(pl.multiple_of(first + group * KG, LANES), KG)
        far = j // 2
        down_at = 2 * LOCAL + far * 3 * QG
        early_at = 2 * LOCAL + 6 * QG + far * 6 * QG
        for m in range(sources):
            a = ids_ref[m]
            take = lambda first, width: parts[j % 2][m, :, first : first + width].astype(F32)
            up_ref[a, :, lanes_of(group)] += take(far * LOCAL, QG)
            up_ref[a, :, keys(QW)] += take(far * LOCAL + QG, KG)
            up_ref[a, :, keys(QW + KVW)] += take(far * LOCAL + QG + KG, KG)
            for i in range(3):
                at = slice(i * RANK, (i + 1) * RANK)
                down_ref[a, at, lanes_of(group)] += take(down_at + i * QG, QG)
            for i in range(6):
                at = slice(i * RANK, (i + 1) * RANK)
                sum_s[a, at, lanes_of(group)] += take(early_at + i * QG, QG)
    for a in range(ADAPT):
        gu_ref[a, 0] = sum_s[a, :RANK, :FF]
        gu_ref[a, 1] = sum_s[a, :RANK, FF : 2 * FF]
        da_ref[a] = sum_s[a, :RANK, 2 * FF :]
        db_ref[a] = sum_s[a, RANK : 2 * RANK]
        od_ref[a] = sum_s[a, 2 * RANK : 3 * RANK]
        ou_ref[a] = sum_s[a, 3 * RANK : 4 * RANK]
        gd_ref[a] = sum_s[a, 4 * RANK :]


def place_grads(ids, near, far):
    shapes = [(RANK, QW + 2 * KVW), (3 * RANK, D), (2, RANK, FF), (RANK, FF), (RANK, D)]
    shapes += [(RANK, QW), (RANK, D), (2 * RANK, D)]
    return pl.pallas_call(
        place_kernel,
        in_specs=[SMEM_SPEC] + [VMEM_SPEC] * 2,
        out_specs=[VMEM_SPEC] * len(shapes),
        out_shape=[jax.ShapeDtypeStruct((ADAPT,) + shape, F32) for shape in shapes],
        scratch_shapes=[pltpu.VMEM((ADAPT, 6 * RANK, D), F32)],
        name="place_grads",
    )(ids, near, far)


def norm_backward(values, inverse, gain_vec, upstream):
    scaled = gain_vec * upstream
    return inverse * scaled - values * inverse**3 * jnp.mean(
        values * scaled, axis=-1, keepdims=True
    )


def local_columns(table, group):
    lead = table.shape[:-1]
    cut = lambda first, width: lax.dynamic_slice_in_dim(
        table, first + group * width, width, table.ndim - 1
    )
    return cut(0, QG), cut(QW, KG), cut(QW + KVW, KG)


def on_device(
    inputs,
    cotangent,
    segment_ids,
    expert_ids,
    adapter_ids,
    gain_one,
    w_qkv,
    w_out,
    gain_two,
    router,
    w_gate_up,
    w_down,
    qkv_down,
    qkv_up,
    out_down,
    out_up,
    gu_down,
    gu_up,
    down_a,
    down_b,
):
    ctx_count = lax.axis_size("ctx")
    seq_count = lax.axis_size("seq")
    ctx_index = lax.axis_index("ctx")
    seq_index = lax.axis_index("seq")
    tokens = inputs.shape[1]
    length = tokens * ctx_count
    experts_all = router.shape[1]
    copies = ctx_count // GROUPS
    group = ctx_index // copies
    half = tokens // 2
    ctx_masks = doublings(ctx_count)[::-1]
    seq_slots = (seq_index ^ jnp.arange(seq_count)).astype(jnp.int32)
    ctx_slots = ctx_index ^ jnp.arange(ctx_count)
    own_rows = inputs[0]

    moving_rows = [swap(own_rows, "ctx", mask) for mask in ctx_masks]
    own_q, own_k, own_v = local_columns(w_qkv, group)
    own_out = lax.dynamic_slice_in_dim(w_out, group * QG, QG, 1)
    col_slots = []
    cols = Steps(
        gather_line(
            jnp.concatenate([own_q, own_k, own_v, own_out], axis=1), col_slots
        )
    )
    chosen = expert_ids[0]
    hot = jnp.any(chosen[:, :, None] == jnp.arange(experts_all)[None, None, :], axis=1)
    hot_low = hot.astype(BF)
    before = (jnp.arange(tokens)[:, None] >= jnp.arange(tokens)[None, :]).astype(BF)
    ranks = dot(before, hot_low).astype(BF) * hot_low
    ranks = jnp.pad(ranks, ((0, 0), (EXP_AT, LANES - EXP_AT - experts_all)))
    pack = jnp.concatenate([cotangent[0], ranks], axis=1)
    cols.beside()
    seg_row = segment_ids[0]
    position = jnp.arange(length)
    start = jnp.sum((seg_row[None, :] < seg_row[:, None]).astype(jnp.int32), axis=1)
    block_id = jnp.stack([ctx_slots, 2 * ctx_count - 1 - ctx_slots], axis=1).reshape(-1)
    block_of = jnp.arange(2 * ctx_count)
    owner = jnp.minimum(block_of, 2 * ctx_count - 1 - block_of)
    place = (2 * (owner ^ ctx_index) + (block_of >= ctx_count)).astype(jnp.int32)
    first = (start[::BLK] // BLK).astype(jnp.int32)
    offset = (position - start).reshape(2 * ctx_count, half)[block_id].reshape(-1)
    lane = jnp.arange(LANES) % HEAD_DIM
    frequency = 10000.0 ** (-2.0 * (lane % (HEAD_DIM // 2)).astype(F32) / HEAD_DIM)
    angles = offset.astype(F32)[:, None] * frequency[None, :]
    cosine = jnp.cos(angles)
    sine = jnp.sin(angles) * jnp.where(lane < HEAD_DIM // 2, -1.0, 1.0)[None, :]
    start_col = start[:, None]
    adapter = adapter_ids[seq_index]
    slot_adapters = adapter_ids[seq_slots]
    slots_and_group = jnp.concatenate([slot_adapters, group[None]]).astype(jnp.int32)
    group_info = group[None].astype(jnp.int32)
    info = jnp.stack([adapter, group, ctx_index]).astype(jnp.int32)

    def pick(table):
        return lax.dynamic_index_in_dim(table, adapter, 0, keepdims=False)

    qkv_down_sel = pick(qkv_down)
    out_down_t = jnp.swapaxes(out_down, 1, 2)
    aux_w = jnp.concatenate(
        [
            jnp.swapaxes(gu_down, 1, 2),
            jnp.broadcast_to(router.T[None], (ADAPT, experts_all, D)),
            jnp.zeros((ADAPT, LANES - 2 * RANK - experts_all, D), BF),
        ],
        axis=1,
    )
    down_a_t = jnp.swapaxes(down_a, 1, 2)

    pack, start_col, cosine, sine, place, first, *moving_rows = cols.beside(
        pack, start_col, cosine, sine, place, first, *moving_rows
    )
    row_slots = gather_rest(own_rows, moving_rows, ctx_masks)
    all_rows = jnp.concatenate(row_slots, axis=0).astype(F32)
    inv_all = lax.rsqrt(jnp.mean(all_rows * all_rows, axis=-1, keepdims=True) + NORM_EPS)
    h_one = (all_rows * inv_all * gain_one).astype(BF)
    rank_qkv = dot(h_one, qkv_down_sel).astype(BF)
    h_one, rank_qkv, pack = cols.beside(h_one, rank_qkv, pack)
    pack_slots = []
    packs = Steps(gather_line(pack, pack_slots))
    cols.finish()
    outs = Steps(gather_groups(order_rows(seq_slots, col_slots), copies))
    qkv, cols_all, up_diag = packs.beside(
        *project(
            seq_slots, adapter, group, h_one, rank_qkv, qkv_up, cosine, sine, col_slots
        )
    )
    heads_out, lse, *pieces = packs.beside(
        *outs.beside(*attend(place, first, qkv, start_col, copies))
    )
    heads_here = packs.beside(
        *[swap(piece, "ctx", j * copies) if j else piece for j, piece in enumerate(pieces)]
    )
    out_parts = outs.finish()
    attended, rank_out, y_one, h_two = project_out(
        info, own_rows, gain_two[None], out_down_t, out_up, heads_here, out_parts
    )

    def compute(m, rows):
        return experts(
            slot_adapters[m : m + len(rows)],
            E_DEV * seq_index,
            rows,
            pack_slots[m : m + len(rows)],
            w_gate_up,
            w_down,
            aux_w,
            gu_up,
            down_a_t,
            down_b,
        )

    y_sums, d_terms = exchange_experts(h_two, packs, compute)

    d_y_one, d_heads, early = middle_back(
        info,
        ctx_count,
        d_terms,
        pack,
        y_one,
        h_two,
        gain_two[None],
        aux_w,
        attended,
        rank_out,
        out_down_t,
        out_up,
        out_parts,
    )
    (d_y_one,) = y_sums.beside(d_y_one)
    d_heads = [swap(piece, "ctx", m) if m else piece for m, piece in enumerate(d_heads)]
    d_heads = y_sums.beside(*d_heads)

    (d_qkv,) = y_sums.beside(
        attend_back(place, first, qkv, start_col, heads_out, lse, cosine, sine, d_heads)
    )
    d_rank_qkv, keep, sent = ranks_back(group_info, d_qkv, up_diag, rank_qkv, h_one, early)

    halves = add_low(keep, swap(sent, "ctx", copies))
    for mask in doublings(copies):
        shared = halves[:, HALF - 12 * QG :]
        shared = add_low(shared, swap(shared, "ctx", mask))
        halves = jnp.concatenate([halves[:, : HALF - 12 * QG], shared], axis=1)
    halves, d_rank_qkv = lax.optimization_barrier((halves, d_rank_qkv))
    arrived, *d_rows = together(
        swap(halves, "ctx", 2 * copies),
        *inputs_back(ctx_count, d_qkv, d_rank_qkv, cols_all, qkv_down_sel),
    )
    d_rows = d_rows[::copies]
    near = add_low(d_rows[0], swap(d_rows[1], "ctx", copies))
    far = add_low(d_rows[2], swap(d_rows[3], "ctx", copies))
    slots = []
    grads = Steps(gather_line(mix(halves, arrived), slots))
    near, far = grads.join(y_sums, near, far)
    d_h_one = near.astype(F32) + swap(far, "ctx", 2 * copies).astype(F32)
    features = own_rows.astype(F32)
    inv_one = lax.rsqrt(jnp.mean(features * features, axis=-1, keepdims=True) + NORM_EPS)
    input_grad = d_y_one + norm_backward(features, inv_one, gain_one, d_h_one)
    layer_output = y_one
    for term in y_sums.finish():
        layer_output = layer_output + term.astype(F32)
    layer_output = layer_output.astype(BF)
    grads.beside()
    grads.beside()
    input_grad, layer_output = grads.beside(input_grad, layer_output)
    grads.finish()
    grads = join(slots)
    (
        grad_qkv_up,
        grad_qkv_down,
        grad_gu_up,
        grad_down_a,
        grad_down_b,
        grad_out_down,
        grad_out_up,
        grad_gu_down,
    ) = place_grads(slots_and_group, grads, swap(grads, "ctx", copies))

    return (
        layer_output[None],
        input_grad[None],
        jnp.swapaxes(grad_qkv_down, 1, 2),
        grad_qkv_up,
        jnp.swapaxes(grad_out_down, 1, 2),
        grad_out_up,
        jnp.swapaxes(grad_gu_down, 1, 2),
        grad_gu_up,
        jnp.swapaxes(grad_down_a, 1, 2),
        grad_down_b,
    )


def solution(mesh):
    over_seq = P("seq", None)
    placed = (
        P("seq", "ctx", None),
        P("seq", "ctx", None),
        over_seq,
        P("seq", "ctx", None),
        P(),
        P(),
        over_seq,
        over_seq,
        P(),
        P(),
        P("seq", None, None),
        P("seq", None, None),
    ) + (P(),) * 8
    return jax.shard_map(
        on_device,
        mesh=mesh,
        in_specs=placed,
        out_specs=(P("seq", "ctx", None), P("seq", "ctx", None)) + (P(),) * 8,
        check_vma=False,
    )
```

```python
import functools

import jax
import jax.numpy as jnp
from jax import lax
from jax.experimental import pallas as pl
from jax.experimental.pallas import tpu as pltpu
from jax.sharding import PartitionSpec as P

D = 1536
HEADS = 24
KV_HEADS = 8
HEAD_DIM = 64
FF = 512
RANK = 16
ADAPT = 8
E_DEV = 2
CAP = 128
QW = 1536
KVW = 512
NORM_EPS = 1e-05

GROUPS = KV_HEADS // 2
PAIRS = HEADS // KV_HEADS
QG = QW // GROUPS
KG = KVW // GROUPS
LOCAL = QG + 2 * KG
BLK = 256
LANES = 128
EXP_AT = 2 * RANK
GATE_AT = 96
SLOTS_AT = 4
EXT = D + LANES
TURN = 8
NEG = -1e30

BF = jnp.bfloat16
F32 = jnp.float32
NT = (((1,), (1,)), ((), ()))
TN = (((0,), (0,)), ((), ()))


def turned_rows(columns, tokens):
    return TURN * -(-columns * tokens // (TURN * D))


def dot(left_arr, right_arr):
    return jnp.dot(left_arr, right_arr, preferred_element_type=F32)


def dot_nt(left_arr, right_arr):
    return lax.dot_general(left_arr, right_arr, NT, preferred_element_type=F32)


def dot_tn(left_arr, right_arr):
    return lax.dot_general(left_arr, right_arr, TN, preferred_element_type=F32)


def swap(block, axis, mask):
    count = lax.axis_size(axis)
    return lax.ppermute(block, axis, [(i, i ^ mask) for i in range(count)])


def gather_slots(block, axis, masks):
    slots = {0: block}
    for mask in masks:
        for have in list(slots):
            slots[have ^ mask] = swap(slots[have], axis, mask)
    return [slots[m] for m in sorted(slots)]


def together(*arrays):
    return lax.optimization_barrier(arrays)


def gather_rest(block, arrived, masks):
    slots = {0: block}
    for mask, first in zip(masks, arrived):
        for have in list(slots):
            slots[have ^ mask] = swap(slots[have], "ctx", mask) if have else first
    return [slots[m] for m in sorted(slots)]


def line_swap(block, pairs):
    return lax.ppermute(block, "seq", [(2 * i + j, 2 * k + j) for i, k in pairs for j in (0, 1)])


def outward(block):
    return line_swap(block, [(1, 0), (2, 3)])


def inward(block):
    return line_swap(block, [(0, 1), (3, 2)])


def middle(block):
    return line_swap(block, [(1, 2), (2, 1)])


class Steps:
    def __init__(self, work):
        self.work = work
        self.moving = self.result = None
        self.resume(None)

    def resume(self, arrived):
        try:
            self.moving = self.work.send(arrived)
        except StopIteration as end:
            self.moving, self.result = None, end.value

    def beside(self, *others):
        if self.moving is None:
            return others
        arrived, others = lax.optimization_barrier((tuple(self.moving), others))
        self.resume(arrived)
        return others

    def join(self, other, *others):
        if self.moving is None or other.moving is None:
            return self.beside(*other.beside(*others))
        mine, theirs, others = lax.optimization_barrier(
            (tuple(self.moving), tuple(other.moving), others)
        )
        self.resume(mine)
        other.resume(theirs)
        return others

    def finish(self):
        while self.moving is not None:
            self.beside()
        return self.result


def gather_line(block, slots):
    count = lax.axis_size("seq")
    if count != 8:
        slots += gather_slots(block, "seq", doublings(count))
        return slots
    slots.append(block)
    two, six, one = yield swap(block, "seq", 2), middle(block), swap(block, "seq", 1)
    slots += [one, two]
    four, far, three = yield middle(two), outward(six), swap(two, "seq", 1)
    four = four + far
    slots += [three, four]
    far, five = yield outward(four), swap(four, "seq", 1)
    six = six + far
    slots += [five, six]
    (seven,) = yield (swap(six, "seq", 1),)
    slots.append(seven)
    return slots


def gather_seq(block):
    return Steps(gather_line(block, [])).finish()


def reduce_line(parts, one=None):
    count = lax.axis_size("seq")
    if count != 8:
        return [reduce_slots(parts, "seq", doublings(count))]
    (seven,) = yield (swap(parts[7], "seq", 1),)
    six = add_low(parts[6], seven)
    near, five = yield inward(six), swap(parts[5], "seq", 1)
    four = add_low(parts[4], five, near)
    near, far, three = yield inward(four), middle(four), swap(parts[3], "seq", 1)
    six = add_low(six, near)
    two = add_low(parts[2], three, far)
    last = [swap(two, "seq", 2), middle(six)]
    if one is None:
        last.append(swap(parts[1], "seq", 1))
    last = yield last
    return [parts[0], *last] + ([] if one is None else [one])


def exchange_experts(block, packs, compute):
    count = lax.axis_size("seq")
    slots, y_parts, d_parts = [], [], []
    rows = Steps(gather_line(block, slots))

    def slots_of(m, some):
        some_y, some_d = compute(m, slots[m : m + some])
        return [*some_y, *some_d]

    def keep(done, some):
        y_parts.extend(done[:some])
        d_parts.extend(done[some:])

    if count != 8:
        packs.finish()
        for m in range(0, count, 2):
            keep(slots_of(m, 2), 2)
        return Steps(reduce_line(y_parts)), Steps(reduce_line(d_parts)).finish()
    keep(rows.join(packs, *slots_of(0, 1)), 1)
    for m in (1, 3, 5):
        keep(rows.beside(*slots_of(m, 2)), 2)
    one = swap(d_parts[1], "seq", 1)
    *done, one = lax.optimization_barrier((*slots_of(7, 1), one))
    keep(done, 1)
    terms = Steps(reduce_line(d_parts, one))
    terms.beside()
    terms.beside()
    y_sums = Steps(reduce_line(list(terms.beside(*y_parts))))
    return y_sums, terms.finish()


def doublings(count):
    return [1 << bit for bit in range(count.bit_length() - 1)]


def add_low(*terms):
    total = terms[0].astype(F32)
    for term in terms[1:]:
        total = total + term.astype(F32)
    return lax.optimization_barrier(total.astype(BF))


def gather_groups(block, copies):
    two, one = yield swap(block, "ctx", 2 * copies), swap(block, "ctx", copies)
    return [block, one, two, swap(two, "ctx", copies)]


def reduce_slots(parts, axis, masks):
    parts = dict(enumerate(parts))
    for step, mask in enumerate(masks):
        last = step == len(masks) - 1
        for m in [m for m in parts if m & mask]:
            arrived = swap(parts.pop(m), axis, mask)
            mine = parts[m ^ mask]
            parts[m ^ mask] = (
                mine.astype(F32) + arrived.astype(F32) if last else add_low(mine, arrived)
            )
    return parts[0]


def rotate(values, cosine, sine, sign):
    lane = lax.broadcasted_iota(jnp.int32, values.shape, 1)
    ahead = pltpu.roll(values, LANES - HEAD_DIM // 2, 1)
    behind = pltpu.roll(values, HEAD_DIM // 2, 1)
    other = jnp.where(lane % HEAD_DIM < HEAD_DIM // 2, ahead, behind)
    return values * cosine + (sign * other) * sine


def by_adapter(table):
    return pl.BlockSpec((1,) + table.shape[1:], lambda i, info: (info[0], 0, 0))


def project_kernel(info_ref, h_ref, t_ref, table_ref, cos_ref, sin_ref, *rest):
    shards = rest[:-4]
    qkv_ref, full_ref, up_ref, w_ref = rest[-4:]
    rows = shards[0].shape[0]
    group = info_ref[1]

    @pl.when(pl.program_id(0) == 0)
    def _():
        for m, shard in enumerate(shards):
            start = pl.multiple_of(info_ref[SLOTS_AT + m] * rows, rows)
            w_ref[pl.ds(start, rows), :] = shard[:, :LOCAL]
        full_ref[...] = w_ref[...]
        up_ref[...] = jnp.zeros(up_ref.shape, BF)
        columns = lambda first, width: table_ref[
            0, :, pl.ds(pl.multiple_of(first + group * width, LANES), width)
        ]
        up_ref[:RANK, :QG] = columns(0, QG)
        up_ref[RANK : 2 * RANK, QG : QG + KG] = columns(QW, KG)
        up_ref[2 * RANK :, QG + KG :] = columns(QW + KVW, KG)

    pre = dot(h_ref[...], w_ref[...]) + dot(t_ref[...], up_ref[...])
    cosine, sine = cos_ref[...], sin_ref[...]
    tiles = [rotate(tile, cosine, sine, 1.0) * 0.125 for tile in lane_tiles(pre)]
    tiles = paired_heads(tiles)
    tiles.append(rotate(pre[:, QG : QG + KG], cosine, sine, 1.0))
    tiles.append(pre[:, QG + KG :])
    for j, tile in enumerate(tiles):
        qkv_ref[:, j * LANES : (j + 1) * LANES] = tile.astype(BF)


def project(info, h_one, rank_qkv, table, cosine, sine, shards):
    length = h_one.shape[0]
    rows = shards[0].shape[0]
    count = len(shards)
    per_block = lambda width: pl.BlockSpec((BLK, width), lambda i, info: (i, 0))
    whole = lambda shape: pl.BlockSpec(shape, lambda i, info: (0, 0))
    return pl.pallas_call(
        project_kernel,
        grid_spec=pltpu.PrefetchScalarGridSpec(
            num_scalar_prefetch=1,
            grid=(length // BLK,),
            in_specs=[
                per_block(D),
                per_block(3 * RANK),
                by_adapter(table),
                per_block(LANES),
                per_block(LANES),
            ]
            + [whole((rows, LOCAL + QG))] * count,
            out_specs=[per_block(LOCAL), whole((D, LOCAL)), whole((3 * RANK, LOCAL))],
            scratch_shapes=[pltpu.VMEM((D, LOCAL), BF)],
        ),
        out_shape=[
            jax.ShapeDtypeStruct((length, LOCAL), BF),
            jax.ShapeDtypeStruct((D, LOCAL), BF),
            jax.ShapeDtypeStruct((3 * RANK, LOCAL), BF),
        ],
        cost_estimate=pl.CostEstimate(
            flops=2 * length * D * LOCAL, bytes_accessed=2 * length * (D + LOCAL), transcendentals=0
        ),
        name="project",
    )(info, h_one, rank_qkv, table, cosine, sine, *shards)


def half_mask(shape, half):
    lane = lax.broadcasted_iota(jnp.int32, shape, 1)
    return (lane < HEAD_DIM) if half == 0 else (lane >= HEAD_DIM)


def turned(tile):
    return pltpu.roll(tile.astype(F32), HEAD_DIM, 1).astype(tile.dtype)


def paired_heads(tiles):
    is_low = half_mask(tiles[0].shape, 0)
    return [
        jnp.where(is_low, tiles[0], tiles[1]),
        jnp.where(is_low, turned(tiles[0]), turned(tiles[2])),
        jnp.where(is_low, tiles[1], tiles[2]),
    ]


def natural_heads(tiles):
    is_low = half_mask(tiles[0].shape, 0)
    return [
        jnp.where(is_low, tiles[0], turned(tiles[1])),
        jnp.where(is_low, tiles[2], tiles[0]),
        jnp.where(is_low, turned(tiles[1]), tiles[2]),
    ]


def lane_tiles(block):
    return [block[:, i * LANES : (i + 1) * LANES] for i in range(PAIRS)]


def stack_rows(place_ref, source_ref, target_ref, paired):
    half = BLK // 2
    for b in range(source_ref.shape[0] // half):
        rows = pl.ds(pl.multiple_of(place_ref[b] * half, half), half)
        tiles = lane_tiles(source_ref[rows, :QG])
        for pair, tile in enumerate(tiles if paired else paired_heads(tiles)):
            at = (b // 2) * PAIRS * BLK + pair * BLK + (b % 2) * half
            target_ref[at : at + half, :] = tile


def read_turned(block, columns, tokens, first):
    per = D // tokens
    parts = []
    for b in range(columns // TURN):
        at = slice((b // per) * TURN, (b // per + 1) * TURN)
        parts.append(block[at, (b % per) * tokens : (b % per + 1) * tokens])
    before = [jnp.zeros((first, tokens), F32)] if first else []
    after = [jnp.zeros((LANES - first - columns, tokens), F32)]
    return jnp.concatenate(before + parts + after, axis=0)


def split_keys(place_ref, qkv_ref, first_lane, target_ref, ones):
    half = BLK // 2
    for b in range(qkv_ref.shape[0] // half):
        rows = pl.ds(pl.multiple_of(place_ref[b] * half, half), half)
        both = qkv_ref[rows, first_lane : first_lane + LANES]
        for side in range(2):
            other = jnp.zeros_like(both)
            if ones:
                lane = lax.broadcasted_iota(jnp.int32, both.shape, 1)
                spare = HEAD_DIM if side == 0 else 0
                other = jnp.where(lane == spare, 1.0, 0.0).astype(BF)
            target_ref[side, b * half : (b + 1) * half, :] = jnp.where(
                half_mask(both.shape, side), both, other
            )


def tile_bias(start_col, q_first, k_first):
    shape = (BLK, BLK)
    key = k_first + lax.broadcasted_iota(jnp.int32, shape, 1)
    query = q_first + lax.broadcasted_iota(jnp.int32, shape, 0)
    bias = jnp.where((key >= start_col) & (key <= query), 0.0, NEG)
    return jnp.concatenate([bias] * PAIRS, axis=0)


def attend_kernel(copies, place_ref, first_ref, qkv_ref, start_ref, o_ref, lse_ref, *refs):
    piece_refs, (q_s, k_s, v_s, score_s, m_s, acc_s) = refs[:GROUPS], refs[GROUPS:]
    stack_rows(place_ref, qkv_ref, q_s, True)
    split_keys(place_ref, qkv_ref, QG, k_s, False)
    split_keys(place_ref, qkv_ref, QG + KG, v_s, True)
    half = BLK // 2
    tall = PAIRS * BLK

    def query_block(qb, unused):
        q_first = pl.multiple_of(qb * BLK, BLK)
        q_rows = pl.ds(pl.multiple_of(qb * tall, tall), tall)
        start_col = start_ref[pl.ds(q_first, BLK), :]
        queries = q_s[q_rows, :]
        m_s[...] = jnp.full(m_s.shape, NEG, F32)
        acc_s[...] = jnp.zeros(acc_s.shape, F32)

        def score_block(kb, unused):
            k_first = pl.multiple_of(kb * BLK, BLK)
            bias = tile_bias(start_col, q_first, k_first)
            for side in range(2):
                scores = dot_nt(queries, k_s[side, pl.ds(k_first, BLK), :]) + bias
                score_s[kb, side] = scores
                m_s[side] = jnp.maximum(
                    m_s[side], jnp.maximum(scores[:, :LANES], scores[:, LANES:])
                )
            return unused

        lax.fori_loop(first_ref[qb], qb + 1, score_block, 0)
        peaks = [jnp.max(m_s[side], axis=1, keepdims=True) for side in range(2)]

        def value_block(kb, unused):
            k_first = pl.multiple_of(kb * BLK, BLK)
            for side in range(2):
                prob = jnp.exp(score_s[kb, side] - peaks[side]).astype(BF)
                acc_s[side] += dot(prob, v_s[side, pl.ds(k_first, BLK), :])
            return unused

        lax.fori_loop(first_ref[qb], qb + 1, value_block, 0)
        low, high = acc_s[0], acc_s[1]
        low_sum = low[:, HEAD_DIM : HEAD_DIM + 1]
        high_sum = high[:, 0:1]
        is_low = half_mask(low.shape, 0)
        out = jnp.where(is_low, low / low_sum, high / high_sum).astype(BF)
        lse_ref[q_rows, :] = jnp.where(
            is_low, peaks[0] + jnp.log(low_sum), peaks[1] + jnp.log(high_sum)
        )
        for i in range(2):
            rows = pl.ds(pl.multiple_of(place_ref[2 * qb + i] * half, half), half)
            tiles = [out[pair * BLK + i * half :][:half] for pair in range(PAIRS)]
            for pair, tile in enumerate(natural_heads(tiles)):
                o_ref[rows, pair * LANES : (pair + 1) * LANES] = tile
        return unused

    lax.fori_loop(0, qkv_ref.shape[0] // BLK, query_block, 0)
    for j, piece in enumerate(piece_refs):
        tokens = piece.shape[0]
        piece[...] = o_ref[j * copies * tokens : (j * copies + 1) * tokens, :]


SMEM_SPEC = pl.BlockSpec(memory_space=pltpu.SMEM)
VMEM_SPEC = pl.BlockSpec(memory_space=pltpu.VMEM)


def attend(place, first, qkv, start_col, copies):
    length = qkv.shape[0]
    tall = PAIRS * BLK
    return pl.pallas_call(
        functools.partial(attend_kernel, copies),
        in_specs=[SMEM_SPEC, SMEM_SPEC, VMEM_SPEC, VMEM_SPEC],
        out_specs=[VMEM_SPEC] * (2 + GROUPS),
        out_shape=[
            jax.ShapeDtypeStruct((length, QG), BF),
            jax.ShapeDtypeStruct((PAIRS * length, LANES), F32),
        ]
        + [jax.ShapeDtypeStruct((length // (GROUPS * copies), QG), BF)] * GROUPS,
        scratch_shapes=[
            pltpu.VMEM((PAIRS * length, LANES), BF),
            pltpu.VMEM((2, length, LANES), BF),
            pltpu.VMEM((2, length, LANES), BF),
            pltpu.VMEM((length // BLK, 2, tall, BLK), F32),
            pltpu.VMEM((2, tall, LANES), F32),
            pltpu.VMEM((2, tall, LANES), F32),
        ],
        cost_estimate=pl.CostEstimate(
            flops=4 * length * length * QG, bytes_accessed=8 * length * QG, transcendentals=0
        ),
        name="attend",
    )(place, first, qkv, start_col)


def attend_back_kernel(
    place_ref,
    first_ref,
    qkv_ref,
    start_ref,
    o_ref,
    lse_ref,
    cos_ref,
    sin_ref,
    *refs,
):
    do_refs = refs[:-10]
    dqkv_ref, join_s, q_s, o_s, do_s, k_s, v_s, dk_s, dv_s, dq_s = refs[-10:]
    for m, piece in enumerate(do_refs):
        join_s[m * piece.shape[0] : (m + 1) * piece.shape[0], :] = piece[...]
    stack_rows(place_ref, qkv_ref, q_s, True)
    stack_rows(place_ref, o_ref, o_s, False)
    stack_rows(place_ref, join_s, do_s, False)
    split_keys(place_ref, qkv_ref, QG, k_s, False)
    split_keys(place_ref, qkv_ref, QG + KG, v_s, False)
    dk_s[...] = jnp.zeros(dk_s.shape, F32)
    dv_s[...] = jnp.zeros(dv_s.shape, F32)
    half = BLK // 2
    tall = PAIRS * BLK

    def query_block(qb, unused):
        q_first = pl.multiple_of(qb * BLK, BLK)
        q_rows = pl.ds(pl.multiple_of(qb * tall, tall), tall)
        start_col = start_ref[pl.ds(q_first, BLK), :]
        dq_s[...] = jnp.zeros(dq_s.shape, F32)
        product = do_s[q_rows, :].astype(F32) * o_s[q_rows, :].astype(F32)
        lse = lse_ref[q_rows, :]
        lse_of = (lse[:, 0:1], lse[:, HEAD_DIM : HEAD_DIM + 1])
        delta_of = [
            jnp.sum(jnp.where(half_mask(product.shape, side), product, 0.0), axis=1, keepdims=True)
            for side in range(2)
        ]

        def key_block(kb, unused):
            k_first = pl.multiple_of(kb * BLK, BLK)
            k_rows = pl.ds(k_first, BLK)
            bias = tile_bias(start_col, q_first, k_first)
            queries = q_s[q_rows, :]
            d_out = do_s[q_rows, :]
            for side in range(2):
                keys = k_s[side, k_rows, :]
                scores = dot_nt(queries, keys) + bias
                prob = jnp.exp(scores - lse_of[side])
                d_prob = dot_nt(d_out, v_s[side, k_rows, :])
                d_score = (prob * (d_prob - delta_of[side])).astype(BF)
                dv_s[side, k_rows, :] += dot_tn(prob.astype(BF), d_out)
                dk_s[side, k_rows, :] += dot_tn(d_score, queries)
                dq_s[...] += dot(d_score, keys)
            return unused

        lax.fori_loop(first_ref[qb], qb + 1, key_block, 0)
        for i in range(2):
            rows = pl.ds(pl.multiple_of(place_ref[2 * qb + i] * half, half), half)
            cosine, sine = cos_ref[rows, :], sin_ref[rows, :]
            tiles = []
            for pair in range(PAIRS):
                at = pair * BLK + i * half
                tiles.append(rotate(dq_s[at : at + half, :] * 0.125, cosine, sine, -1.0))
            for pair, tile in enumerate(natural_heads(tiles)):
                dqkv_ref[rows, pair * LANES : (pair + 1) * LANES] = tile.astype(BF)
        return unused

    lax.fori_loop(0, qkv_ref.shape[0] // BLK, query_block, 0)
    for b in range(qkv_ref.shape[0] // half):
        rows = pl.ds(pl.multiple_of(place_ref[b] * half, half), half)
        at = slice(b * half, (b + 1) * half)
        is_low = half_mask((half, LANES), 0)
        back = jnp.where(is_low, dk_s[0, at, :], dk_s[1, at, :])
        back = rotate(back, cos_ref[rows, :], sin_ref[rows, :], -1.0)
        dqkv_ref[rows, QG : QG + KG] = back.astype(BF)
        dqkv_ref[rows, QG + KG : LOCAL] = jnp.where(is_low, dv_s[0, at, :], dv_s[1, at, :]).astype(BF)


def attend_back(place, first, qkv, start_col, out, lse, cosine, sine, d_out):
    length = qkv.shape[0]
    tall = PAIRS * BLK
    stacked = pltpu.VMEM((PAIRS * length, LANES), BF)
    return pl.pallas_call(
        attend_back_kernel,
        in_specs=[SMEM_SPEC, SMEM_SPEC] + [VMEM_SPEC] * (6 + len(d_out)),
        out_specs=VMEM_SPEC,
        out_shape=jax.ShapeDtypeStruct((length, LOCAL), BF),
        scratch_shapes=[
            pltpu.VMEM((length, QG), BF),
            stacked,
            stacked,
            stacked,
            pltpu.VMEM((2, length, LANES), BF),
            pltpu.VMEM((2, length, LANES), BF),
            pltpu.VMEM((2, length, LANES), F32),
            pltpu.VMEM((2, length, LANES), F32),
            pltpu.VMEM((tall, LANES), F32),
        ],
        cost_estimate=pl.CostEstimate(
            flops=10 * length * length * QG, bytes_accessed=16 * length * QG, transcendentals=0
        ),
        name="attend_back",
    )(place, first, qkv, start_col, out, lse, cosine, sine, *d_out)


def expert_kernel(experts_all, ids_ref, h_refs, p_refs, wgu_ref, wd_ref, tables, y_refs, d_refs, scratch):
    aux_w, gu_refs, da_refs, db_refs = tables
    wgu_s, wd_s, gu_s, put_s, x_s, g_s, extra_s, yrow_s, drow_s, grad_s, sems = scratch
    count = len(h_refs)
    tokens = h_refs[0].shape[0]

    def fetch(e):
        return [
            pltpu.make_async_copy(wgu_ref.at[e], wgu_s.at[e], sems.at[0, e]),
            pltpu.make_async_copy(wd_ref.at[e], wd_s.at[e], sems.at[1, e]),
        ]

    for e in range(E_DEV):
        for copy in fetch(e):
            copy.start()
    wide = lax.broadcasted_iota(jnp.int32, (tokens, LANES), 1)
    narrow = lax.broadcasted_iota(jnp.int32, (CAP, LANES), 1)
    base = EXP_AT + ids_ref[3]
    grad_s[...] = jnp.zeros(grad_s.shape, F32)
    gu_s[...] = jnp.zeros(gu_s.shape, BF)
    part = lambda arr, j: arr[j * CAP : (j + 1) * CAP]
    for j in range(count):
        gu_s[j, 0, 0:RANK, :] = gu_refs[j][0, 0]
        gu_s[j, 1, RANK : 2 * RANK, :] = gu_refs[j][0, 1]
        both = dot_nt(h_refs[j][...], aux_w[j][0])
        tall = read_turned(p_refs[j][tokens:, :].astype(F32), experts_all, tokens, EXP_AT)
        ranks = tall.T
        chosen = ranks > 0.0
        picked = jnp.where(chosen, both, NEG)
        weights = jnp.exp(picked - jnp.max(picked, axis=1, keepdims=True))
        gates = weights / jnp.sum(weights, axis=1, keepdims=True)
        aux = jnp.where(wide < EXP_AT, both, 0.0)
        which = lax.broadcasted_iota(jnp.int32, tall.shape, 0)
        slot = lax.broadcasted_iota(jnp.int32, (CAP, tokens), 0).astype(F32) + 1.0
        takes = []
        for e in range(E_DEV):
            column = jnp.sum(jnp.where(wide == base + e, ranks, 0.0), axis=1, keepdims=True)
            row = jnp.sum(jnp.where(which == base + e, tall, 0.0), axis=0, keepdims=True)
            takes.append(jnp.where(slot == row, 1.0, 0.0).astype(BF))
            put_s[j, :, e * CAP : (e + 1) * CAP] = jnp.where(
                wide.astype(F32) + 1.0 == column, 1.0, 0.0
            ).astype(BF)
            gate = jnp.sum(jnp.where(wide == base + e, gates, 0.0), axis=1, keepdims=True)
            gate_one = gate.astype(BF).astype(F32)
            gate_two = (gate - gate_one).astype(BF).astype(F32)
            first = GATE_AT + 3 * e
            aux = jnp.where(wide == first, gate_one, aux)
            aux = jnp.where(wide == first + 1, gate_two, aux)
            aux = jnp.where(wide == first + 2, gate - gate_one - gate_two, aux)
        take = jnp.concatenate(takes, axis=0)
        at = slice(j * CAP, (j + 1) * CAP)
        rows = dot(take, h_refs[j][...]).astype(BF)
        upstream = dot(take, p_refs[j][:tokens, :]).astype(BF)
        extra = dot(take, aux.astype(BF))
        for e in range(E_DEV):
            x_s[e, at, :] = part(rows, e)
            g_s[e, at, :] = part(upstream, e)
            extra_s[e, at, :] = part(extra, e)

    def each(make):
        return jnp.concatenate([make(j) for j in range(count)], axis=0)

    def expert(e, unused):
        for copy in fetch(e):
            copy.wait()
        extra = extra_s[e]
        low_extra = extra.astype(BF)
        place = lax.broadcasted_iota(jnp.int32, extra.shape, 1) - (GATE_AT + 3 * e)
        gate = jnp.sum(jnp.where((place >= 0) & (place < 3), extra, 0.0), axis=1, keepdims=True)
        both = dot(x_s[e], wgu_s[e])
        gate_pre = both[:, :FF] + each(lambda j: dot(part(low_extra, j), gu_s[j, 0]))
        up_pre = both[:, FF:] + each(lambda j: dot(part(low_extra, j), gu_s[j, 1]))
        sigmoid = jax.nn.sigmoid(gate_pre)
        silu = gate_pre * sigmoid
        active = (silu * up_pre).astype(BF)
        down = [dot_nt(part(active, j), da_refs[j][0]).astype(BF) for j in range(count)]
        result = dot(active, wd_s[e]) + each(lambda j: dot(down[j], db_refs[j][0]))
        result = result.astype(BF).astype(F32)
        grad_in = g_s[e].astype(F32)
        d_gate_val = jnp.sum(grad_in * result, axis=1, keepdims=True)
        weighted = (gate * result).astype(BF)
        d_result = (gate * grad_in).astype(BF)
        d_down = [dot_nt(part(d_result, j), db_refs[j][0]).astype(BF) for j in range(count)]
        d_active = dot_nt(d_result, wd_s[e]) + each(lambda j: dot(d_down[j], da_refs[j][0]))
        d_gate = (d_active * up_pre * sigmoid * (1.0 + gate_pre * (1.0 - sigmoid))).astype(BF)
        d_up = (d_active * silu).astype(BF)
        d_rows = dot_nt(jnp.concatenate([d_gate, d_up], axis=1), wgu_s[e]).astype(BF)
        at = pl.ds(pl.multiple_of(e * CAP, CAP), CAP)
        for j in range(count):
            yrow_s[j, at, :] = part(weighted, j)
            drow_s[j, at, :D] = part(d_rows, j)
            d_extra = dot_nt(part(d_gate, j), gu_s[j, 0]) + dot_nt(part(d_up, j), gu_s[j, 1])
            d_extra = d_extra + jnp.where(narrow == base + e, part(d_gate_val, j), 0.0)
            drow_s[j, at, D:] = d_extra.astype(BF)
            ranks_in = part(low_extra, j)
            grad_s[j, 0:RANK, 0:FF] += dot_tn(ranks_in, part(d_gate, j))[0:RANK]
            grad_s[j, 0:RANK, FF : 2 * FF] += dot_tn(ranks_in, part(d_up, j))[RANK : 2 * RANK]
            grad_s[j, 0:RANK, 2 * FF :] += dot_tn(d_down[j], part(active, j))
            grad_s[j, RANK:, :] += dot_tn(down[j], part(d_result, j))
        return unused

    lax.fori_loop(0, E_DEV, expert, 0)
    for j in range(count):
        put = put_s[j]
        y_refs[j][...] = dot(put, yrow_s[j]).astype(BF)
        d_refs[j][:tokens, :] = dot(put, drow_s[j, :, :D]).astype(BF)
        d_refs[j][tokens : tokens + 2 * RANK, :] = grad_s[j].astype(BF)
        turned_ext = dot(put, drow_s[j, :, D:]).T.astype(BF)
        per = D // tokens
        for b in range(-(-(EXP_AT + experts_all) // TURN)):
            at = tokens + 2 * RANK + (b // per) * TURN
            lanes = slice((b % per) * tokens, (b % per + 1) * tokens)
            d_refs[j][at : at + TURN, lanes] = turned_ext[b * TURN : (b + 1) * TURN]


def experts(experts_all, info, first, rows, packs, w_gate_up, w_down, aux_w, gu_up, down_a, down_b):
    count = len(rows)
    tokens = rows[0].shape[0]
    whole = lambda arr: pl.BlockSpec(arr.shape, lambda e, ids: (0, 0))
    d_rows = tokens + 2 * RANK + turned_rows(EXP_AT + experts_all, tokens)

    def table(shape, j):
        at = first + j
        return pl.BlockSpec((1,) + shape, lambda e, ids: (ids[at],) + (0,) * len(shape))

    def body(ids_ref, *refs):
        refs = list(refs)
        take = lambda n: [refs.pop(0) for _ in range(n)]
        h_refs, p_refs = take(count), take(count)
        wgu_ref, wd_ref = take(2)
        tables = [take(count) for _ in range(4)]
        y_refs, d_refs = take(count), take(count)
        expert_kernel(experts_all, ids_ref, h_refs, p_refs, wgu_ref, wd_ref, tables, y_refs, d_refs, refs)

    picked = [(LANES, D), (2, RANK, FF), (RANK, FF), (RANK, D)]
    shapes = [(tokens, D)] * count + [(d_rows, D)] * count
    height = count * CAP
    outs = pl.pallas_call(
        body,
        grid_spec=pltpu.PrefetchScalarGridSpec(
            num_scalar_prefetch=1,
            grid=(1,),
            in_specs=[whole(arr) for arr in [*rows, *packs]]
            + [pl.BlockSpec(memory_space=pl.ANY)] * 2
            + [table(shape, j) for shape in picked for j in range(count)],
            out_specs=[pl.BlockSpec(shape, lambda e, ids: (0, 0)) for shape in shapes],
            scratch_shapes=[
                pltpu.VMEM((E_DEV, D, 2 * FF), BF),
                pltpu.VMEM((E_DEV, FF, D), BF),
                pltpu.VMEM((count, 2, LANES, FF), BF),
                pltpu.VMEM((count, tokens, E_DEV * CAP), BF),
                pltpu.VMEM((E_DEV, height, D), BF),
                pltpu.VMEM((E_DEV, height, D), BF),
                pltpu.VMEM((E_DEV, height, LANES), F32),
                pltpu.VMEM((count, E_DEV * CAP, D), BF),
                pltpu.VMEM((count, E_DEV * CAP, EXT), BF),
                pltpu.VMEM((count, 2 * RANK, D), F32),
                pltpu.SemaphoreType.DMA((2, E_DEV)),
            ],
        ),
        out_shape=[jax.ShapeDtypeStruct(shape, BF) for shape in shapes],
        cost_estimate=pl.CostEstimate(
            flops=16 * count * E_DEV * CAP * D * FF,
            bytes_accessed=2 * E_DEV * 3 * D * FF + 8 * count * tokens * D,
            transcendentals=0,
        ),
        name="experts",
    )(
        info,
        *rows,
        *packs,
        w_gate_up,
        w_down,
        *([aux_w] * count),
        *([gu_up] * count),
        *([down_a] * count),
        *([down_b] * count),
    )
    return list(outs[:count]), list(outs[count:])


def join_kernel(*refs):
    parts, out_ref = refs[:-1], refs[-1]
    for m, part in enumerate(parts):
        out_ref[m] = part[...]


def join(parts):
    return pl.pallas_call(
        join_kernel,
        in_specs=[VMEM_SPEC] * len(parts),
        out_specs=VMEM_SPEC,
        out_shape=jax.ShapeDtypeStruct((len(parts),) + parts[0].shape, parts[0].dtype),
        name="join",
    )(*parts)


def order_rows_kernel(info_ref, *refs):
    parts, out_ref = refs[:-1], refs[-1]
    rows = parts[0].shape[0]
    for m, part in enumerate(parts):
        start = pl.multiple_of(info_ref[SLOTS_AT + m] * rows, rows)
        out_ref[pl.ds(start, rows), :] = part[:, LOCAL:]


def order_rows(order, parts):
    return pl.pallas_call(
        order_rows_kernel,
        in_specs=[SMEM_SPEC] + [VMEM_SPEC] * len(parts),
        out_specs=VMEM_SPEC,
        out_shape=jax.ShapeDtypeStruct((QW, QG), BF),
        name="order_rows",
    )(order, *parts)


def lanes_of(index):
    return pl.ds(pl.multiple_of(index * QG, LANES), QG)


def start_copies(sources, target, sems):
    copies = [
        pltpu.make_async_copy(source, target.at[j], sems.at[j]) for j, source in enumerate(sources)
    ]
    for copy in copies:
        copy.start()
    return copies


def out_kernel(info_ref, x_ref, gain_ref, down_ref, up_ref, *refs):
    o_refs, w_hbm = refs[:GROUPS], refs[GROUPS : 2 * GROUPS]
    att_ref, rank_ref, y_ref, h_ref, w_s, sems = refs[2 * GROUPS :]
    w_copies = start_copies(w_hbm, w_s, sems)
    group = info_ref[1]
    for j in range(GROUPS):
        att_ref[:, lanes_of(group ^ j)] = o_refs[j][...]
    attended = att_ref[...]
    for j in range(GROUPS):
        w_copies[j].wait()
        y_ref[:, lanes_of(group ^ j)] = dot(attended, w_s[j])
    rank_out = dot_nt(attended, down_ref[0]).astype(BF)
    rank_ref[...] = rank_out
    y_one = x_ref[...].astype(F32) + y_ref[...] + dot(rank_out, up_ref[0])
    y_ref[...] = y_one
    inverse = lax.rsqrt(jnp.mean(y_one * y_one, axis=1, keepdims=True) + NORM_EPS)
    h_ref[...] = (y_one * inverse * gain_ref[...]).astype(BF)


def project_out(info, rows, gain, down_t, up, outs, w_parts):
    tokens = rows.shape[0]
    return pl.pallas_call(
        out_kernel,
        grid_spec=pltpu.PrefetchScalarGridSpec(
            num_scalar_prefetch=1,
            grid=(1,),
            in_specs=[VMEM_SPEC] * 2
            + [by_adapter(down_t), by_adapter(up)]
            + [VMEM_SPEC] * GROUPS
            + [pl.BlockSpec(memory_space=pl.ANY)] * GROUPS,
            out_specs=[VMEM_SPEC] * 4,
            scratch_shapes=[
                pltpu.VMEM((GROUPS, QW, QG), BF),
                pltpu.SemaphoreType.DMA((GROUPS,)),
            ],
        ),
        out_shape=[
            jax.ShapeDtypeStruct((tokens, QW), BF),
            jax.ShapeDtypeStruct((tokens, RANK), BF),
            jax.ShapeDtypeStruct((tokens, D), F32),
            jax.ShapeDtypeStruct((tokens, D), BF),
        ],
        cost_estimate=pl.CostEstimate(
            flops=2 * tokens * QW * D, bytes_accessed=2 * QW * D + 12 * tokens * D, transcendentals=0
        ),
        name="project_out",
    )(info, rows, gain, down_t, up, *outs, *w_parts)


def middle_kernel(count, terms, experts_all, info_ref, *refs):
    refs = list(refs)
    take = lambda n: [refs.pop(0) for _ in range(n)]
    d_refs = take(terms)
    pack_ref, y_ref, h_ref, gain_ref, aux_ref, att_ref, rank_ref, down_ref, up_ref = take(9)
    w_hbm = take(GROUPS)
    (dy_ref,) = take(1)
    do_refs, early_refs = take(count), take(GROUPS)
    do_s, early_s, w_s, sems = refs
    w_refs = start_copies(w_hbm, w_s, sems)
    group, ctx_index, copies = info_ref[1], info_ref[2], count // GROUPS
    tokens = y_ref.shape[0]
    d_sum = d_refs[0][...].astype(F32)
    for ref in d_refs[1:]:
        d_sum = d_sum + ref[...].astype(F32)
    early_s[0 : 2 * RANK, :] = d_sum[tokens : tokens + 2 * RANK]
    d_ext = read_turned(d_sum[tokens + 2 * RANK :], EXP_AT + experts_all, tokens, 0).T
    h_two = h_ref[...]
    lane = lax.broadcasted_iota(jnp.int32, (tokens, LANES), 1)
    chosen = read_turned(pack_ref[tokens:, :].astype(F32), experts_all, tokens, EXP_AT).T > 0.0
    picked = jnp.where(chosen, dot_nt(h_two, aux_ref[0]), NEG)
    weights = jnp.exp(picked - jnp.max(picked, axis=1, keepdims=True))
    gates = weights / jnp.sum(weights, axis=1, keepdims=True)
    mixed = jnp.sum(jnp.where(chosen, gates * d_ext, 0.0), axis=1, keepdims=True)
    d_logits = jnp.where(chosen, gates * (d_ext - mixed), 0.0)
    d_ext = jnp.where(lane < EXP_AT, d_ext, d_logits).astype(BF)
    d_h = d_sum[:tokens] + dot(d_ext, aux_ref[0])
    y_one = y_ref[...]
    inverse = lax.rsqrt(jnp.mean(y_one * y_one, axis=1, keepdims=True) + NORM_EPS)
    scaled = gain_ref[...] * d_h
    d_y = pack_ref[:tokens, :].astype(F32) + inverse * scaled
    d_y = d_y - y_one * inverse**3 * jnp.mean(y_one * scaled, axis=1, keepdims=True)
    dy_ref[...] = d_y
    d_attn = d_y.astype(BF)
    d_rank = dot_nt(d_attn, up_ref[0]).astype(BF)
    do_s[...] = dot(d_rank, down_ref[0])
    for j in range(GROUPS):
        at = lanes_of(group ^ j)
        early_s[3 * RANK : 4 * RANK, at] = dot_tn(rank_ref[...], dy_ref[:, at].astype(BF))
        w_refs[j].wait()
        do_s[...] += dot_nt(dy_ref[:, at].astype(BF), w_s[j])
    for m in range(count):
        do_refs[m][...] = do_s[:, lanes_of((ctx_index ^ m) // copies)].astype(BF)
    early_s[2 * RANK : 3 * RANK, :] = dot_tn(d_rank, att_ref[...])
    early_s[4 * RANK :, :] = dot_tn(d_ext, h_two)[: 2 * RANK]
    for j in range(GROUPS):
        for i in range(6):
            block = early_s[i * RANK : (i + 1) * RANK, lanes_of(group ^ j)]
            early_refs[j][:, i * QG : (i + 1) * QG] = block.astype(BF)


def middle_back(info, count, experts_all, terms, pack, y_one, h_two, gain, aux, attended, rank_out, down_t, up, w_parts):
    tokens = y_one.shape[0]
    outs = pl.pallas_call(
        functools.partial(middle_kernel, count, len(terms), experts_all),
        grid_spec=pltpu.PrefetchScalarGridSpec(
            num_scalar_prefetch=1,
            grid=(1,),
            in_specs=[VMEM_SPEC] * (len(terms) + 4)
            + [by_adapter(aux)]
            + [VMEM_SPEC] * 2
            + [by_adapter(down_t), by_adapter(up)]
            + [pl.BlockSpec(memory_space=pl.ANY)] * GROUPS,
            out_specs=[VMEM_SPEC] * (1 + count + GROUPS),
            scratch_shapes=[
                pltpu.VMEM((tokens, QW), F32),
                pltpu.VMEM((6 * RANK, D), F32),
                pltpu.VMEM((GROUPS, QW, QG), BF),
                pltpu.SemaphoreType.DMA((GROUPS,)),
            ],
        ),
        out_shape=[jax.ShapeDtypeStruct((tokens, D), F32)]
        + [jax.ShapeDtypeStruct((tokens, QG), BF)] * count
        + [jax.ShapeDtypeStruct((RANK, 6 * QG), BF)] * GROUPS,
        cost_estimate=pl.CostEstimate(
            flops=2 * tokens * QW * D, bytes_accessed=2 * QW * D + 20 * tokens * D, transcendentals=0
        ),
        name="middle_back",
    )(info, *terms, pack, y_one, h_two, gain, aux, attended, rank_out, down_t, up, *w_parts)
    return outs[0], list(outs[1 : 1 + count]), list(outs[1 + count :])


def ranks_kernel(info_ref, dqkv_ref, up_ref, t_ref, h_ref, *refs):
    early_refs, (rank_ref, keep_ref, send_ref) = refs[:GROUPS], refs[GROUPS:]
    d_qkv = dqkv_ref[...]
    d_rank = dot_nt(d_qkv, up_ref[...]).astype(BF)
    rank_ref[...] = d_rank
    grad = dot_tn(t_ref[...], d_qkv)
    keep_ref[:, :QG] = grad[:RANK, :QG].astype(BF)
    keep_ref[:, QG : QG + KG] = grad[RANK : 2 * RANK, QG : QG + KG].astype(BF)
    keep_ref[:, QG + KG : LOCAL] = grad[2 * RANK :, QG + KG :].astype(BF)
    send_ref[:, :LOCAL] = jnp.zeros((RANK, LOCAL), BF)
    for j in range(GROUPS):
        target = send_ref if j % 2 else keep_ref
        down = dot_tn(d_rank, h_ref[:, lanes_of(info_ref[1] ^ j)]).astype(BF)
        first = LOCAL + (j // 2) * 3 * QG
        for i in range(3):
            target[:, first + i * QG : first + (i + 1) * QG] = down[i * RANK : (i + 1) * RANK]
        first = LOCAL + 6 * QG + (j // 2) * 6 * QG
        target[:, first : first + 6 * QG] = early_refs[j][...]


HALF = LOCAL + 18 * QG
BOTH = HALF + LOCAL


def ranks_back(info, d_qkv, up_diag, rank_qkv, h_one, early):
    length = d_qkv.shape[0]
    return pl.pallas_call(
        ranks_kernel,
        in_specs=[SMEM_SPEC] + [VMEM_SPEC] * (4 + GROUPS),
        out_specs=[VMEM_SPEC] * 3,
        out_shape=[
            jax.ShapeDtypeStruct((length, 3 * RANK), BF),
            jax.ShapeDtypeStruct((RANK, HALF), BF),
            jax.ShapeDtypeStruct((RANK, HALF), BF),
        ],
        name="ranks_back",
    )(info, d_qkv, up_diag, rank_qkv, h_one, *early)


def mix_kernel(near_ref, far_ref, out_ref):
    out_ref[:, :LOCAL] = near_ref[:, :LOCAL]
    out_ref[:, LOCAL : 2 * LOCAL] = far_ref[:, :LOCAL]
    first = LOCAL
    for width in (3 * QG, 6 * QG):
        for mine, theirs in ((0, width), (width, 0)):
            total = near_ref[:, first + mine : first + mine + width].astype(F32)
            total = total + far_ref[:, first + theirs : first + theirs + width].astype(F32)
            at = LOCAL + first + mine
            out_ref[:, at : at + width] = total.astype(BF)
        first += 2 * width


def mix(near, far):
    return pl.pallas_call(
        mix_kernel,
        in_specs=[VMEM_SPEC] * 2,
        out_specs=VMEM_SPEC,
        out_shape=jax.ShapeDtypeStruct((RANK, BOTH), BF),
        name="mix",
    )(near, far)


def inputs_kernel(dqkv_ref, rank_ref, w_ref, down_ref, *rows_refs):
    rows = dot_nt(dqkv_ref[...], w_ref[...]) + dot_nt(rank_ref[...], down_ref[...])
    rows = rows.astype(BF)
    for m, ref in enumerate(rows_refs):

        @pl.when(pl.program_id(0) == m)
        def _():
            ref[...] = rows


def inputs_back(count, d_qkv, d_rank, cols_all, down_sel):
    length = d_qkv.shape[0]
    tokens = length // count
    per_block = lambda width: pl.BlockSpec((tokens, width), lambda i: (i, 0))
    whole = lambda shape: pl.BlockSpec(shape, lambda i: (0, 0))
    return pl.pallas_call(
        inputs_kernel,
        grid=(count,),
        in_specs=[
            per_block(LOCAL),
            per_block(3 * RANK),
            whole((D, LOCAL)),
            whole((D, 3 * RANK)),
        ],
        out_specs=[whole((tokens, D))] * count,
        out_shape=[jax.ShapeDtypeStruct((tokens, D), BF)] * count,
        cost_estimate=pl.CostEstimate(
            flops=2 * length * D * LOCAL, bytes_accessed=4 * length * (D + LOCAL), transcendentals=0
        ),
        name="inputs_back",
    )(d_qkv, d_rank, cols_all, down_sel)


def place_kernel(info_ref, *refs):
    parts = refs[:2]
    up_ref, down_ref, gu_ref, da_ref, db_ref, od_ref, ou_ref, gd_ref, sum_s = refs[2:]
    sources = parts[0].shape[0]
    up_ref[...] = jnp.zeros(up_ref.shape, F32)
    down_ref[...] = jnp.zeros(down_ref.shape, F32)
    sum_s[...] = jnp.zeros(sum_s.shape, F32)
    for j in range(GROUPS):
        group = info_ref[1] ^ j
        keys = lambda first: pl.ds(pl.multiple_of(first + group * KG, LANES), KG)
        far = j // 2
        down_at = 2 * LOCAL + far * 3 * QG
        early_at = 2 * LOCAL + 6 * QG + far * 6 * QG
        for m in range(sources):
            a = info_ref[SLOTS_AT + sources + m]
            take = lambda first, width: parts[j % 2][m, :, first : first + width].astype(F32)
            up_ref[a, :, lanes_of(group)] += take(far * LOCAL, QG)
            up_ref[a, :, keys(QW)] += take(far * LOCAL + QG, KG)
            up_ref[a, :, keys(QW + KVW)] += take(far * LOCAL + QG + KG, KG)
            for i in range(3):
                at = slice(i * RANK, (i + 1) * RANK)
                down_ref[a, at, lanes_of(group)] += take(down_at + i * QG, QG)
            for i in range(6):
                at = slice(i * RANK, (i + 1) * RANK)
                sum_s[a, at, lanes_of(group)] += take(early_at + i * QG, QG)
    for a in range(ADAPT):
        gu_ref[a, 0] = sum_s[a, :RANK, :FF]
        gu_ref[a, 1] = sum_s[a, :RANK, FF : 2 * FF]
        da_ref[a] = sum_s[a, :RANK, 2 * FF :]
        db_ref[a] = sum_s[a, RANK : 2 * RANK]
        od_ref[a] = sum_s[a, 2 * RANK : 3 * RANK]
        ou_ref[a] = sum_s[a, 3 * RANK : 4 * RANK]
        gd_ref[a] = sum_s[a, 4 * RANK :]


def place_grads(info, near, far):
    shapes = [(RANK, QW + 2 * KVW), (3 * RANK, D), (2, RANK, FF), (RANK, FF), (RANK, D)]
    shapes += [(RANK, QW), (RANK, D), (2 * RANK, D)]
    return pl.pallas_call(
        place_kernel,
        in_specs=[SMEM_SPEC] + [VMEM_SPEC] * 2,
        out_specs=[VMEM_SPEC] * len(shapes),
        out_shape=[jax.ShapeDtypeStruct((ADAPT,) + shape, F32) for shape in shapes],
        scratch_shapes=[pltpu.VMEM((ADAPT, 6 * RANK, D), F32)],
        name="place_grads",
    )(info, near, far)


def norm_backward(values, inverse, gain_vec, upstream):
    scaled = gain_vec * upstream
    return inverse * scaled - values * inverse**3 * jnp.mean(
        values * scaled, axis=-1, keepdims=True
    )


def local_columns(table, group):
    lead = table.shape[:-1]
    cut = lambda first, width: lax.dynamic_slice_in_dim(
        table, first + group * width, width, table.ndim - 1
    )
    return cut(0, QG), cut(QW, KG), cut(QW + KVW, KG)


def on_device(
    inputs,
    cotangent,
    segment_ids,
    expert_ids,
    adapter_ids,
    gain_one,
    w_qkv,
    w_out,
    gain_two,
    router,
    w_gate_up,
    w_down,
    qkv_down,
    qkv_up,
    out_down,
    out_up,
    gu_down,
    gu_up,
    down_a,
    down_b,
):
    ctx_count = lax.axis_size("ctx")
    seq_count = lax.axis_size("seq")
    ctx_index = lax.axis_index("ctx")
    seq_index = lax.axis_index("seq")
    tokens = inputs.shape[1]
    length = tokens * ctx_count
    experts_all = router.shape[1]
    copies = ctx_count // GROUPS
    group = ctx_index // copies
    half = tokens // 2
    ctx_masks = doublings(ctx_count)[::-1]
    seq_slots = (seq_index ^ jnp.arange(seq_count)).astype(jnp.int32)
    ctx_slots = ctx_index ^ jnp.arange(ctx_count)
    own_rows = inputs[0]

    moving_rows = [swap(own_rows, "ctx", mask) for mask in ctx_masks]
    own_q, own_k, own_v = local_columns(w_qkv, group)
    own_out = lax.dynamic_slice_in_dim(w_out, group * QG, QG, 1)
    col_slots = []
    cols = Steps(
        gather_line(
            jnp.concatenate([own_q, own_k, own_v, own_out], axis=1), col_slots
        )
    )
    chosen = expert_ids[0]
    hot = jnp.any(chosen[:, :, None] == jnp.arange(experts_all)[None, None, :], axis=1)
    hot_low = hot.astype(BF).T
    before = (jnp.arange(tokens)[:, None] <= jnp.arange(tokens)[None, :]).astype(BF)
    ranks = dot(hot_low, before).astype(BF) * hot_low
    per = D // tokens
    rank_rows = turned_rows(experts_all, tokens)
    ranks = jnp.pad(ranks, ((0, rank_rows * per - experts_all), (0, 0)))
    ranks = ranks.reshape(rank_rows // TURN, per, TURN, tokens)
    ranks = jnp.transpose(ranks, (0, 2, 1, 3)).reshape(rank_rows, D)
    pack = jnp.concatenate([cotangent[0], ranks], axis=0)
    cols.beside()
    seg_row = segment_ids[0]
    position = jnp.arange(length)
    start = jnp.sum((seg_row[None, :] < seg_row[:, None]).astype(jnp.int32), axis=1)
    block_id = jnp.stack([ctx_slots, 2 * ctx_count - 1 - ctx_slots], axis=1).reshape(-1)
    block_of = jnp.arange(2 * ctx_count)
    owner = jnp.minimum(block_of, 2 * ctx_count - 1 - block_of)
    place = (2 * (owner ^ ctx_index) + (block_of >= ctx_count)).astype(jnp.int32)
    first = (start[::BLK] // BLK).astype(jnp.int32)
    offset = (position - start).reshape(2 * ctx_count, half)[block_id].reshape(-1)
    lane = jnp.arange(LANES) % HEAD_DIM
    frequency = 10000.0 ** (-2.0 * (lane % (HEAD_DIM // 2)).astype(F32) / HEAD_DIM)
    angles = offset.astype(F32)[:, None] * frequency[None, :]
    cosine = jnp.cos(angles)
    sine = jnp.sin(angles) * jnp.where(lane < HEAD_DIM // 2, -1.0, 1.0)[None, :]
    start_col = start[:, None]
    adapter = adapter_ids[seq_index]
    slot_adapters = adapter_ids[seq_slots]
    info = jnp.concatenate(
        [jnp.stack([adapter, group, ctx_index, E_DEV * seq_index]), seq_slots, slot_adapters]
    ).astype(jnp.int32)

    def pick(table):
        return lax.dynamic_index_in_dim(table, adapter, 0, keepdims=False)

    qkv_down_sel = pick(qkv_down)
    out_down_t = jnp.swapaxes(out_down, 1, 2)
    aux_w = jnp.concatenate(
        [
            jnp.swapaxes(gu_down, 1, 2),
            jnp.broadcast_to(router.T[None], (ADAPT, experts_all, D)),
            jnp.zeros((ADAPT, LANES - 2 * RANK - experts_all, D), BF),
        ],
        axis=1,
    )
    down_a_t = jnp.swapaxes(down_a, 1, 2)

    pack, start_col, cosine, sine, place, first, info, *moving_rows = cols.beside(
        pack, start_col, cosine, sine, place, first, info, *moving_rows
    )
    row_slots = gather_rest(own_rows, moving_rows, ctx_masks)
    all_rows = jnp.concatenate(row_slots, axis=0).astype(F32)
    inv_all = lax.rsqrt(jnp.mean(all_rows * all_rows, axis=-1, keepdims=True) + NORM_EPS)
    h_one = (all_rows * inv_all * gain_one).astype(BF)
    rank_qkv = dot(h_one, qkv_down_sel).astype(BF)
    h_one, rank_qkv, pack = cols.beside(h_one, rank_qkv, pack)
    pack_slots = []
    packs = Steps(gather_line(pack, pack_slots))
    cols.finish()
    outs = Steps(gather_groups(order_rows(info, col_slots), copies))
    qkv, cols_all, up_diag = packs.beside(
        *project(info, h_one, rank_qkv, qkv_up, cosine, sine, col_slots)
    )
    heads_out, lse, *pieces = packs.beside(
        *outs.beside(*attend(place, first, qkv, start_col, copies))
    )
    heads_here = packs.beside(
        *[swap(piece, "ctx", j * copies) if j else piece for j, piece in enumerate(pieces)]
    )
    out_parts = outs.finish()
    attended, rank_out, y_one, h_two = project_out(
        info, own_rows, gain_two[None], out_down_t, out_up, heads_here, out_parts
    )

    def compute(m, rows):
        return experts(
            experts_all,
            info,
            SLOTS_AT + seq_count + m,
            rows,
            pack_slots[m : m + len(rows)],
            w_gate_up,
            w_down,
            aux_w,
            gu_up,
            down_a_t,
            down_b,
        )

    y_sums, d_terms = exchange_experts(h_two, packs, compute)

    d_y_one, d_heads, early = middle_back(
        info,
        ctx_count,
        experts_all,
        d_terms,
        pack,
        y_one,
        h_two,
        gain_two[None],
        aux_w,
        attended,
        rank_out,
        out_down_t,
        out_up,
        out_parts,
    )
    (d_y_one,) = y_sums.beside(d_y_one)
    d_heads = [swap(piece, "ctx", m) if m else piece for m, piece in enumerate(d_heads)]
    d_heads = y_sums.beside(*d_heads)

    (d_qkv,) = y_sums.beside(
        attend_back(place, first, qkv, start_col, heads_out, lse, cosine, sine, d_heads)
    )
    d_rank_qkv, keep, sent = ranks_back(info, d_qkv, up_diag, rank_qkv, h_one, early)

    halves = add_low(keep, swap(sent, "ctx", copies))
    for mask in doublings(copies):
        shared = halves[:, HALF - 12 * QG :]
        shared = add_low(shared, swap(shared, "ctx", mask))
        halves = jnp.concatenate([halves[:, : HALF - 12 * QG], shared], axis=1)
    halves, d_rank_qkv = lax.optimization_barrier((halves, d_rank_qkv))
    arrived, *d_rows = together(
        swap(halves, "ctx", 2 * copies),
        *inputs_back(ctx_count, d_qkv, d_rank_qkv, cols_all, qkv_down_sel),
    )
    d_rows = d_rows[::copies]
    near = add_low(d_rows[0], swap(d_rows[1], "ctx", copies))
    far = add_low(d_rows[2], swap(d_rows[3], "ctx", copies))
    slots = []
    grads = Steps(gather_line(mix(halves, arrived), slots))
    near, far = grads.join(y_sums, near, far)
    d_h_one = near.astype(F32) + swap(far, "ctx", 2 * copies).astype(F32)
    features = own_rows.astype(F32)
    inv_one = lax.rsqrt(jnp.mean(features * features, axis=-1, keepdims=True) + NORM_EPS)
    input_grad = d_y_one + norm_backward(features, inv_one, gain_one, d_h_one)
    layer_output = y_one
    for term in y_sums.finish():
        layer_output = layer_output + term.astype(F32)
    layer_output = layer_output.astype(BF)
    grads.beside()
    grads.beside()
    input_grad, layer_output = grads.beside(input_grad, layer_output)
    grads.finish()
    grads = join(slots)
    (
        grad_qkv_up,
        grad_qkv_down,
        grad_gu_up,
        grad_down_a,
        grad_down_b,
        grad_out_down,
        grad_out_up,
        grad_gu_down,
    ) = place_grads(info, grads, swap(grads, "ctx", copies))

    return (
        layer_output[None],
        input_grad[None],
        jnp.swapaxes(grad_qkv_down, 1, 2),
        grad_qkv_up,
        jnp.swapaxes(grad_out_down, 1, 2),
        grad_out_up,
        jnp.swapaxes(grad_gu_down, 1, 2),
        grad_gu_up,
        jnp.swapaxes(grad_down_a, 1, 2),
        grad_down_b,
    )


def solution(mesh):
    over_seq = P("seq", None)
    placed = (
        P("seq", "ctx", None),
        P("seq", "ctx", None),
        over_seq,
        P("seq", "ctx", None),
        P(),
        P(),
        over_seq,
        over_seq,
        P(),
        P(),
        P("seq", None, None),
        P("seq", None, None),
    ) + (P(),) * 8
    return jax.shard_map(
        on_device,
        mesh=mesh,
        in_specs=placed,
        out_specs=(P("seq", "ctx", None), P("seq", "ctx", None)) + (P(),) * 8,
        check_vma=False,
    )
```

```python
import functools

import jax
import jax.numpy as jnp
from jax import lax
from jax.experimental import pallas as pl
from jax.experimental.pallas import tpu as pltpu
from jax.sharding import PartitionSpec as P

D = 1536
HEADS = 24
KV_HEADS = 8
HEAD_DIM = 64
FF = 512
RANK = 16
ADAPT = 8
E_DEV = 2
CAP = 128
QW = 1536
KVW = 512
NORM_EPS = 1e-05

GROUPS = KV_HEADS // 2
PAIRS = HEADS // KV_HEADS
QG = QW // GROUPS
KG = KVW // GROUPS
LOCAL = QG + 2 * KG
BLK = 256
LANES = 128
EXP_AT = 2 * RANK
GATE_AT = 96
SLOTS_AT = 4
EXT = D + LANES
TURN = 8
NEG = -1e30

BF = jnp.bfloat16
F32 = jnp.float32
NT = (((1,), (1,)), ((), ()))
TN = (((0,), (0,)), ((), ()))


def turned_rows(columns, tokens):
    return TURN * -(-columns * tokens // (TURN * D))


def dot(left_arr, right_arr):
    return jnp.dot(left_arr, right_arr, preferred_element_type=F32)


def dot_nt(left_arr, right_arr):
    return lax.dot_general(left_arr, right_arr, NT, preferred_element_type=F32)


def dot_tn(left_arr, right_arr):
    return lax.dot_general(left_arr, right_arr, TN, preferred_element_type=F32)


def swap(block, axis, mask):
    count = lax.axis_size(axis)
    return lax.ppermute(block, axis, [(i, i ^ mask) for i in range(count)])


def gather_slots(block, axis, masks):
    slots = {0: block}
    for mask in masks:
        for have in list(slots):
            slots[have ^ mask] = swap(slots[have], axis, mask)
    return [slots[m] for m in sorted(slots)]


def together(*arrays):
    return lax.optimization_barrier(arrays)


def gather_rest(block, arrived, masks):
    slots = {0: block}
    for mask, first in zip(masks, arrived):
        for have in list(slots):
            slots[have ^ mask] = swap(slots[have], "ctx", mask) if have else first
    return [slots[m] for m in sorted(slots)]


def line_swap(block, pairs):
    return lax.ppermute(block, "seq", [(2 * i + j, 2 * k + j) for i, k in pairs for j in (0, 1)])


def outward(block):
    return line_swap(block, [(1, 0), (2, 3)])


def inward(block):
    return line_swap(block, [(0, 1), (3, 2)])


def middle(block):
    return line_swap(block, [(1, 2), (2, 1)])


class Steps:
    def __init__(self, work):
        self.work = work
        self.moving = self.result = None
        self.resume(None)

    def resume(self, arrived):
        try:
            self.moving = self.work.send(arrived)
        except StopIteration as end:
            self.moving, self.result = None, end.value

    def beside(self, *others):
        if self.moving is None:
            return others
        arrived, others = lax.optimization_barrier((tuple(self.moving), others))
        self.resume(arrived)
        return others

    def join(self, other, *others):
        if self.moving is None or other.moving is None:
            return self.beside(*other.beside(*others))
        mine, theirs, others = lax.optimization_barrier(
            (tuple(self.moving), tuple(other.moving), others)
        )
        self.resume(mine)
        other.resume(theirs)
        return others

    def finish(self):
        while self.moving is not None:
            self.beside()
        return self.result


def gather_line(block, slots):
    count = lax.axis_size("seq")
    if count != 8:
        slots += gather_slots(block, "seq", doublings(count))
        return slots
    slots.append(block)
    two, six, one = yield swap(block, "seq", 2), middle(block), swap(block, "seq", 1)
    slots += [one, two]
    four, far, three = yield middle(two), outward(six), swap(two, "seq", 1)
    four = four + far
    slots += [three, four]
    far, five = yield outward(four), swap(four, "seq", 1)
    six = six + far
    slots += [five, six]
    (seven,) = yield (swap(six, "seq", 1),)
    slots.append(seven)
    return slots


def gather_seq(block):
    return Steps(gather_line(block, [])).finish()


def reduce_line(parts, one=None):
    count = lax.axis_size("seq")
    if count != 8:
        return [reduce_slots(parts, "seq", doublings(count))]
    (seven,) = yield (swap(parts[7], "seq", 1),)
    six = add_low(parts[6], seven)
    near, five = yield inward(six), swap(parts[5], "seq", 1)
    four = add_low(parts[4], five, near)
    near, far, three = yield inward(four), middle(four), swap(parts[3], "seq", 1)
    six = add_low(six, near)
    two = add_low(parts[2], three, far)
    last = [swap(two, "seq", 2), middle(six)]
    if one is None:
        last.append(swap(parts[1], "seq", 1))
    last = yield last
    return [parts[0], *last] + ([] if one is None else [one])


def exchange_experts(block, packs, compute):
    count = lax.axis_size("seq")
    slots, y_parts, d_parts = [], [], []
    rows = Steps(gather_line(block, slots))

    def slots_of(m, some):
        some_y, some_d = compute(m, slots[m : m + some])
        return [*some_y, *some_d]

    def keep(done, some):
        y_parts.extend(done[:some])
        d_parts.extend(done[some:])

    if count != 8:
        packs.finish()
        for m in range(0, count, 2):
            keep(slots_of(m, 2), 2)
        return Steps(reduce_line(y_parts)), Steps(reduce_line(d_parts)).finish()
    keep(rows.join(packs, *slots_of(0, 1)), 1)
    for m in (1, 3, 5):
        keep(rows.beside(*slots_of(m, 2)), 2)
    one = swap(d_parts[1], "seq", 1)
    *done, one = lax.optimization_barrier((*slots_of(7, 1), one))
    keep(done, 1)
    terms = Steps(reduce_line(d_parts, one))
    terms.beside()
    terms.beside()
    y_sums = Steps(reduce_line(list(terms.beside(*y_parts))))
    return y_sums, terms.finish()


def doublings(count):
    return [1 << bit for bit in range(count.bit_length() - 1)]


def add_low(*terms):
    total = terms[0].astype(F32)
    for term in terms[1:]:
        total = total + term.astype(F32)
    return lax.optimization_barrier(total.astype(BF))


def gather_groups(block, copies):
    two, one = yield swap(block, "ctx", 2 * copies), swap(block, "ctx", copies)
    return [block, one, two, swap(two, "ctx", copies)]


def reduce_slots(parts, axis, masks):
    parts = dict(enumerate(parts))
    for step, mask in enumerate(masks):
        last = step == len(masks) - 1
        for m in [m for m in parts if m & mask]:
            arrived = swap(parts.pop(m), axis, mask)
            mine = parts[m ^ mask]
            parts[m ^ mask] = (
                mine.astype(F32) + arrived.astype(F32) if last else add_low(mine, arrived)
            )
    return parts[0]


def rotate(values, cosine, sine, sign):
    lane = lax.broadcasted_iota(jnp.int32, values.shape, 1)
    ahead = pltpu.roll(values, LANES - HEAD_DIM // 2, 1)
    behind = pltpu.roll(values, HEAD_DIM // 2, 1)
    other = jnp.where(lane % HEAD_DIM < HEAD_DIM // 2, ahead, behind)
    return values * cosine + (sign * other) * sine


def by_adapter(table):
    return pl.BlockSpec((1,) + table.shape[1:], lambda i, info: (info[0], 0, 0))


def project_kernel(info_ref, h_ref, t_ref, table_ref, cos_ref, sin_ref, *rest):
    shards = rest[:-3]
    qkv_ref, w_ref, up_ref = rest[-3:]
    rows = shards[0].shape[0]
    group = info_ref[1]

    @pl.when(pl.program_id(0) == 0)
    def _():
        for m, shard in enumerate(shards):
            start = pl.multiple_of(info_ref[SLOTS_AT + m] * rows, rows)
            w_ref[pl.ds(start, rows), :] = shard[:, :LOCAL]
        up_ref[...] = jnp.zeros(up_ref.shape, BF)
        columns = lambda first, width: table_ref[
            0, :, pl.ds(pl.multiple_of(first + group * width, LANES), width)
        ]
        up_ref[:RANK, :QG] = columns(0, QG)
        up_ref[RANK : 2 * RANK, QG : QG + KG] = columns(QW, KG)
        up_ref[2 * RANK :, QG + KG :] = columns(QW + KVW, KG)

    pre = dot(h_ref[...], w_ref[...]) + dot(t_ref[...], up_ref[...])
    cosine, sine = cos_ref[...], sin_ref[...]
    tiles = [rotate(tile, cosine, sine, 1.0) * 0.125 for tile in lane_tiles(pre)]
    tiles = paired_heads(tiles)
    tiles.append(rotate(pre[:, QG : QG + KG], cosine, sine, 1.0))
    tiles.append(pre[:, QG + KG :])
    for j, tile in enumerate(tiles):
        qkv_ref[:, j * LANES : (j + 1) * LANES] = tile.astype(BF)


def project(info, h_one, rank_qkv, table, cosine, sine, shards):
    length = h_one.shape[0]
    rows = shards[0].shape[0]
    count = len(shards)
    per_block = lambda width: pl.BlockSpec((BLK, width), lambda i, info: (i, 0))
    whole = lambda shape: pl.BlockSpec(shape, lambda i, info: (0, 0))
    return pl.pallas_call(
        project_kernel,
        grid_spec=pltpu.PrefetchScalarGridSpec(
            num_scalar_prefetch=1,
            grid=(length // BLK,),
            in_specs=[
                per_block(D),
                per_block(3 * RANK),
                by_adapter(table),
                per_block(LANES),
                per_block(LANES),
            ]
            + [whole((rows, LOCAL + QG))] * count,
            out_specs=[per_block(LOCAL), whole((D, LOCAL)), whole((3 * RANK, LOCAL))],
        ),
        out_shape=[
            jax.ShapeDtypeStruct((length, LOCAL), BF),
            jax.ShapeDtypeStruct((D, LOCAL), BF),
            jax.ShapeDtypeStruct((3 * RANK, LOCAL), BF),
        ],
        cost_estimate=pl.CostEstimate(
            flops=2 * length * D * LOCAL, bytes_accessed=2 * length * (D + LOCAL), transcendentals=0
        ),
        name="project",
    )(info, h_one, rank_qkv, table, cosine, sine, *shards)


def half_mask(shape, half):
    lane = lax.broadcasted_iota(jnp.int32, shape, 1)
    return (lane < HEAD_DIM) if half == 0 else (lane >= HEAD_DIM)


def turned(tile):
    return pltpu.roll(tile.astype(F32), HEAD_DIM, 1).astype(tile.dtype)


def paired_heads(tiles):
    is_low = half_mask(tiles[0].shape, 0)
    return [
        jnp.where(is_low, tiles[0], tiles[1]),
        jnp.where(is_low, turned(tiles[0]), turned(tiles[2])),
        jnp.where(is_low, tiles[1], tiles[2]),
    ]


def natural_heads(tiles):
    is_low = half_mask(tiles[0].shape, 0)
    return [
        jnp.where(is_low, tiles[0], turned(tiles[1])),
        jnp.where(is_low, tiles[2], tiles[0]),
        jnp.where(is_low, turned(tiles[1]), tiles[2]),
    ]


def lane_tiles(block):
    return [block[:, i * LANES : (i + 1) * LANES] for i in range(PAIRS)]


def stack_rows(place_ref, source_ref, target_ref, paired):
    half = BLK // 2
    for b in range(source_ref.shape[0] // half):
        rows = pl.ds(pl.multiple_of(place_ref[b] * half, half), half)
        tiles = lane_tiles(source_ref[rows, :QG])
        for pair, tile in enumerate(tiles if paired else paired_heads(tiles)):
            at = (b // 2) * PAIRS * BLK + pair * BLK + (b % 2) * half
            target_ref[at : at + half, :] = tile


def read_turned(block, columns, tokens, first):
    per = D // tokens
    parts = []
    for b in range(columns // TURN):
        at = slice((b // per) * TURN, (b // per + 1) * TURN)
        parts.append(block[at, (b % per) * tokens : (b % per + 1) * tokens])
    before = [jnp.zeros((first, tokens), F32)] if first else []
    after = [jnp.zeros((LANES - first - columns, tokens), F32)]
    return jnp.concatenate(before + parts + after, axis=0)


def split_keys(place_ref, qkv_ref, first_lane, target_ref, ones):
    half = BLK // 2
    for b in range(qkv_ref.shape[0] // half):
        rows = pl.ds(pl.multiple_of(place_ref[b] * half, half), half)
        both = qkv_ref[rows, first_lane : first_lane + LANES]
        for side in range(2):
            other = jnp.zeros_like(both)
            if ones:
                lane = lax.broadcasted_iota(jnp.int32, both.shape, 1)
                spare = HEAD_DIM if side == 0 else 0
                other = jnp.where(lane == spare, 1.0, 0.0).astype(BF)
            target_ref[side, b * half : (b + 1) * half, :] = jnp.where(
                half_mask(both.shape, side), both, other
            )


def as_column(row):
    return jnp.broadcast_to(row.astype(F32), (TURN, row.shape[1])).T[:, :1].astype(jnp.int32)


def tile_bias(start_col, q_first, k_first):
    shape = (BLK, BLK)
    key = k_first + lax.broadcasted_iota(jnp.int32, shape, 1)
    query = q_first + lax.broadcasted_iota(jnp.int32, shape, 0)
    bias = jnp.where((key >= start_col) & (key <= query), 0.0, NEG)
    return jnp.concatenate([bias] * PAIRS, axis=0)


def attend_kernel(copies, place_ref, first_ref, qkv_ref, start_ref, o_ref, lse_ref, *refs):
    piece_refs, (q_s, k_s, v_s, score_s, m_s, acc_s) = refs[:GROUPS], refs[GROUPS:]
    stack_rows(place_ref, qkv_ref, q_s, True)
    split_keys(place_ref, qkv_ref, QG, k_s, False)
    split_keys(place_ref, qkv_ref, QG + KG, v_s, True)
    half = BLK // 2
    tall = PAIRS * BLK

    def query_block(qb, unused):
        q_first = pl.multiple_of(qb * BLK, BLK)
        q_rows = pl.ds(pl.multiple_of(qb * tall, tall), tall)
        start_col = as_column(start_ref[:, pl.ds(q_first, BLK)])
        queries = q_s[q_rows, :]
        m_s[...] = jnp.full(m_s.shape, NEG, F32)
        acc_s[...] = jnp.zeros(acc_s.shape, F32)

        def score_block(kb, unused):
            k_first = pl.multiple_of(kb * BLK, BLK)
            bias = tile_bias(start_col, q_first, k_first)
            for side in range(2):
                scores = dot_nt(queries, k_s[side, pl.ds(k_first, BLK), :]) + bias
                score_s[kb, side] = scores
                m_s[side] = jnp.maximum(
                    m_s[side], jnp.maximum(scores[:, :LANES], scores[:, LANES:])
                )
            return unused

        lax.fori_loop(first_ref[qb], qb + 1, score_block, 0)
        peaks = [jnp.max(m_s[side], axis=1, keepdims=True) for side in range(2)]

        def value_block(kb, unused):
            k_first = pl.multiple_of(kb * BLK, BLK)
            for side in range(2):
                prob = jnp.exp(score_s[kb, side] - peaks[side]).astype(BF)
                acc_s[side] += dot(prob, v_s[side, pl.ds(k_first, BLK), :])
            return unused

        lax.fori_loop(first_ref[qb], qb + 1, value_block, 0)
        low, high = acc_s[0], acc_s[1]
        low_sum = low[:, HEAD_DIM : HEAD_DIM + 1]
        high_sum = high[:, 0:1]
        is_low = half_mask(low.shape, 0)
        out = jnp.where(is_low, low / low_sum, high / high_sum).astype(BF)
        lse_ref[q_rows, :] = jnp.where(
            is_low, peaks[0] + jnp.log(low_sum), peaks[1] + jnp.log(high_sum)
        )
        for i in range(2):
            rows = pl.ds(pl.multiple_of(place_ref[2 * qb + i] * half, half), half)
            tiles = [out[pair * BLK + i * half :][:half] for pair in range(PAIRS)]
            for pair, tile in enumerate(natural_heads(tiles)):
                o_ref[rows, pair * LANES : (pair + 1) * LANES] = tile
        return unused

    lax.fori_loop(0, qkv_ref.shape[0] // BLK, query_block, 0)
    for j, piece in enumerate(piece_refs):
        tokens = piece.shape[0]
        piece[...] = o_ref[j * copies * tokens : (j * copies + 1) * tokens, :]


SMEM_SPEC = pl.BlockSpec(memory_space=pltpu.SMEM)
VMEM_SPEC = pl.BlockSpec(memory_space=pltpu.VMEM)


def attend(place, first, qkv, start_row, copies):
    length = qkv.shape[0]
    tall = PAIRS * BLK
    return pl.pallas_call(
        functools.partial(attend_kernel, copies),
        in_specs=[SMEM_SPEC, SMEM_SPEC, VMEM_SPEC, VMEM_SPEC],
        out_specs=[VMEM_SPEC] * (2 + GROUPS),
        out_shape=[
            jax.ShapeDtypeStruct((length, QG), BF),
            jax.ShapeDtypeStruct((PAIRS * length, LANES), F32),
        ]
        + [jax.ShapeDtypeStruct((length // (GROUPS * copies), QG), BF)] * GROUPS,
        scratch_shapes=[
            pltpu.VMEM((PAIRS * length, LANES), BF),
            pltpu.VMEM((2, length, LANES), BF),
            pltpu.VMEM((2, length, LANES), BF),
            pltpu.VMEM((length // BLK, 2, tall, BLK), F32),
            pltpu.VMEM((2, tall, LANES), F32),
            pltpu.VMEM((2, tall, LANES), F32),
        ],
        cost_estimate=pl.CostEstimate(
            flops=4 * length * length * QG, bytes_accessed=8 * length * QG, transcendentals=0
        ),
        name="attend",
    )(place, first, qkv, start_row)


def attend_back_kernel(
    place_ref,
    first_ref,
    qkv_ref,
    start_ref,
    o_ref,
    lse_ref,
    cos_ref,
    sin_ref,
    *refs,
):
    do_refs = refs[:-10]
    dqkv_ref, join_s, q_s, o_s, do_s, k_s, v_s, dk_s, dv_s, dq_s = refs[-10:]
    for m, piece in enumerate(do_refs):
        join_s[m * piece.shape[0] : (m + 1) * piece.shape[0], :] = piece[...]
    stack_rows(place_ref, qkv_ref, q_s, True)
    stack_rows(place_ref, o_ref, o_s, False)
    stack_rows(place_ref, join_s, do_s, False)
    split_keys(place_ref, qkv_ref, QG, k_s, False)
    split_keys(place_ref, qkv_ref, QG + KG, v_s, False)
    dk_s[...] = jnp.zeros(dk_s.shape, F32)
    dv_s[...] = jnp.zeros(dv_s.shape, F32)
    half = BLK // 2
    tall = PAIRS * BLK

    def query_block(qb, unused):
        q_first = pl.multiple_of(qb * BLK, BLK)
        q_rows = pl.ds(pl.multiple_of(qb * tall, tall), tall)
        start_col = as_column(start_ref[:, pl.ds(q_first, BLK)])
        dq_s[...] = jnp.zeros(dq_s.shape, F32)
        product = do_s[q_rows, :].astype(F32) * o_s[q_rows, :].astype(F32)
        lse = lse_ref[q_rows, :]
        lse_of = (lse[:, 0:1], lse[:, HEAD_DIM : HEAD_DIM + 1])
        delta_of = [
            jnp.sum(jnp.where(half_mask(product.shape, side), product, 0.0), axis=1, keepdims=True)
            for side in range(2)
        ]

        def key_block(kb, unused):
            k_first = pl.multiple_of(kb * BLK, BLK)
            k_rows = pl.ds(k_first, BLK)
            bias = tile_bias(start_col, q_first, k_first)
            queries = q_s[q_rows, :]
            d_out = do_s[q_rows, :]
            for side in range(2):
                keys = k_s[side, k_rows, :]
                scores = dot_nt(queries, keys) + bias
                prob = jnp.exp(scores - lse_of[side])
                d_prob = dot_nt(d_out, v_s[side, k_rows, :])
                d_score = (prob * (d_prob - delta_of[side])).astype(BF)
                dv_s[side, k_rows, :] += dot_tn(prob.astype(BF), d_out)
                dk_s[side, k_rows, :] += dot_tn(d_score, queries)
                dq_s[...] += dot(d_score, keys)
            return unused

        lax.fori_loop(first_ref[qb], qb + 1, key_block, 0)
        for i in range(2):
            rows = pl.ds(pl.multiple_of(place_ref[2 * qb + i] * half, half), half)
            cosine, sine = cos_ref[rows, :], sin_ref[rows, :]
            tiles = []
            for pair in range(PAIRS):
                at = pair * BLK + i * half
                tiles.append(rotate(dq_s[at : at + half, :] * 0.125, cosine, sine, -1.0))
            for pair, tile in enumerate(natural_heads(tiles)):
                dqkv_ref[rows, pair * LANES : (pair + 1) * LANES] = tile.astype(BF)
        return unused

    lax.fori_loop(0, qkv_ref.shape[0] // BLK, query_block, 0)
    for b in range(qkv_ref.shape[0] // half):
        rows = pl.ds(pl.multiple_of(place_ref[b] * half, half), half)
        at = slice(b * half, (b + 1) * half)
        is_low = half_mask((half, LANES), 0)
        back = jnp.where(is_low, dk_s[0, at, :], dk_s[1, at, :])
        back = rotate(back, cos_ref[rows, :], sin_ref[rows, :], -1.0)
        dqkv_ref[rows, QG : QG + KG] = back.astype(BF)
        dqkv_ref[rows, QG + KG : LOCAL] = jnp.where(is_low, dv_s[0, at, :], dv_s[1, at, :]).astype(BF)


def attend_back(place, first, qkv, start_row, out, lse, cosine, sine, d_out):
    length = qkv.shape[0]
    tall = PAIRS * BLK
    stacked = pltpu.VMEM((PAIRS * length, LANES), BF)
    return pl.pallas_call(
        attend_back_kernel,
        in_specs=[SMEM_SPEC, SMEM_SPEC] + [VMEM_SPEC] * (6 + len(d_out)),
        out_specs=VMEM_SPEC,
        out_shape=jax.ShapeDtypeStruct((length, LOCAL), BF),
        scratch_shapes=[
            pltpu.VMEM((length, QG), BF),
            stacked,
            stacked,
            stacked,
            pltpu.VMEM((2, length, LANES), BF),
            pltpu.VMEM((2, length, LANES), BF),
            pltpu.VMEM((2, length, LANES), F32),
            pltpu.VMEM((2, length, LANES), F32),
            pltpu.VMEM((tall, LANES), F32),
        ],
        cost_estimate=pl.CostEstimate(
            flops=10 * length * length * QG, bytes_accessed=16 * length * QG, transcendentals=0
        ),
        name="attend_back",
    )(place, first, qkv, start_row, out, lse, cosine, sine, *d_out)


def expert_kernel(experts_all, ids_ref, h_refs, p_refs, wgu_ref, wd_ref, tables, y_refs, d_refs, scratch):
    aux_w, gu_refs, da_refs, db_refs = tables
    wgu_s, wd_s, gu_s, put_s, x_s, g_s, extra_s, yrow_s, drow_s, grad_s, sems = scratch
    count = len(h_refs)
    tokens = h_refs[0].shape[0]

    def fetch(e):
        return [
            pltpu.make_async_copy(wgu_ref.at[e], wgu_s.at[e], sems.at[0, e]),
            pltpu.make_async_copy(wd_ref.at[e], wd_s.at[e], sems.at[1, e]),
        ]

    for e in range(E_DEV):
        for copy in fetch(e):
            copy.start()
    wide = lax.broadcasted_iota(jnp.int32, (tokens, LANES), 1)
    narrow = lax.broadcasted_iota(jnp.int32, (CAP, LANES), 1)
    base = EXP_AT + ids_ref[3]
    grad_s[...] = jnp.zeros(grad_s.shape, F32)
    gu_s[...] = jnp.zeros(gu_s.shape, BF)
    part = lambda arr, j: arr[j * CAP : (j + 1) * CAP]
    for j in range(count):
        gu_s[j, 0, 0:RANK, :] = gu_refs[j][0, 0]
        gu_s[j, 1, RANK : 2 * RANK, :] = gu_refs[j][0, 1]
        both = dot_nt(h_refs[j][...], aux_w[j][0])
        tall = read_turned(p_refs[j][tokens:, :].astype(F32), experts_all, tokens, EXP_AT)
        ranks = tall.T
        chosen = ranks > 0.0
        picked = jnp.where(chosen, both, NEG)
        weights = jnp.exp(picked - jnp.max(picked, axis=1, keepdims=True))
        gates = weights / jnp.sum(weights, axis=1, keepdims=True)
        aux = jnp.where(wide < EXP_AT, both, 0.0)
        which = lax.broadcasted_iota(jnp.int32, tall.shape, 0)
        slot = lax.broadcasted_iota(jnp.int32, (CAP, tokens), 0).astype(F32) + 1.0
        takes = []
        for e in range(E_DEV):
            column = jnp.sum(jnp.where(wide == base + e, ranks, 0.0), axis=1, keepdims=True)
            row = jnp.sum(jnp.where(which == base + e, tall, 0.0), axis=0, keepdims=True)
            takes.append(jnp.where(slot == row, 1.0, 0.0).astype(BF))
            put_s[j, :, e * CAP : (e + 1) * CAP] = jnp.where(
                wide.astype(F32) + 1.0 == column, 1.0, 0.0
            ).astype(BF)
            gate = jnp.sum(jnp.where(wide == base + e, gates, 0.0), axis=1, keepdims=True)
            gate_one = gate.astype(BF).astype(F32)
            gate_two = (gate - gate_one).astype(BF).astype(F32)
            first = GATE_AT + 3 * e
            aux = jnp.where(wide == first, gate_one, aux)
            aux = jnp.where(wide == first + 1, gate_two, aux)
            aux = jnp.where(wide == first + 2, gate - gate_one - gate_two, aux)
        take = jnp.concatenate(takes, axis=0)
        at = slice(j * CAP, (j + 1) * CAP)
        rows = dot(take, h_refs[j][...]).astype(BF)
        upstream = dot(take, p_refs[j][:tokens, :]).astype(BF)
        extra = dot(take, aux.astype(BF))
        for e in range(E_DEV):
            x_s[e, at, :] = part(rows, e)
            g_s[e, at, :] = part(upstream, e)
            extra_s[e, at, :] = part(extra, e)

    def each(make):
        return jnp.concatenate([make(j) for j in range(count)], axis=0)

    def expert(e, unused):
        for copy in fetch(e):
            copy.wait()
        extra = extra_s[e]
        low_extra = extra.astype(BF)
        place = lax.broadcasted_iota(jnp.int32, extra.shape, 1) - (GATE_AT + 3 * e)
        gate = jnp.sum(jnp.where((place >= 0) & (place < 3), extra, 0.0), axis=1, keepdims=True)
        both = dot(x_s[e], wgu_s[e])
        gate_pre = both[:, :FF] + each(lambda j: dot(part(low_extra, j), gu_s[j, 0]))
        up_pre = both[:, FF:] + each(lambda j: dot(part(low_extra, j), gu_s[j, 1]))
        sigmoid = jax.nn.sigmoid(gate_pre)
        silu = gate_pre * sigmoid
        active = (silu * up_pre).astype(BF)
        down = [dot_nt(part(active, j), da_refs[j][0]).astype(BF) for j in range(count)]
        result = dot(active, wd_s[e]) + each(lambda j: dot(down[j], db_refs[j][0]))
        result = result.astype(BF).astype(F32)
        grad_in = g_s[e].astype(F32)
        d_gate_val = jnp.sum(grad_in * result, axis=1, keepdims=True)
        weighted = (gate * result).astype(BF)
        d_result = (gate * grad_in).astype(BF)
        d_down = [dot_nt(part(d_result, j), db_refs[j][0]).astype(BF) for j in range(count)]
        d_active = dot_nt(d_result, wd_s[e]) + each(lambda j: dot(d_down[j], da_refs[j][0]))
        d_gate = (d_active * up_pre * sigmoid * (1.0 + gate_pre * (1.0 - sigmoid))).astype(BF)
        d_up = (d_active * silu).astype(BF)
        d_rows = dot_nt(jnp.concatenate([d_gate, d_up], axis=1), wgu_s[e]).astype(BF)
        at = pl.ds(pl.multiple_of(e * CAP, CAP), CAP)
        for j in range(count):
            yrow_s[j, at, :] = part(weighted, j)
            drow_s[j, at, :D] = part(d_rows, j)
            d_extra = dot_nt(part(d_gate, j), gu_s[j, 0]) + dot_nt(part(d_up, j), gu_s[j, 1])
            d_extra = d_extra + jnp.where(narrow == base + e, part(d_gate_val, j), 0.0)
            drow_s[j, at, D:] = d_extra.astype(BF)
            ranks_in = part(low_extra, j)
            grad_s[j, 0:RANK, 0:FF] += dot_tn(ranks_in, part(d_gate, j))[0:RANK]
            grad_s[j, 0:RANK, FF : 2 * FF] += dot_tn(ranks_in, part(d_up, j))[RANK : 2 * RANK]
            grad_s[j, 0:RANK, 2 * FF :] += dot_tn(d_down[j], part(active, j))
            grad_s[j, RANK:, :] += dot_tn(down[j], part(d_result, j))
        return unused

    lax.fori_loop(0, E_DEV, expert, 0)
    for j in range(count):
        put = put_s[j]
        y_refs[j][...] = dot(put, yrow_s[j]).astype(BF)
        d_refs[j][:tokens, :] = dot(put, drow_s[j, :, :D]).astype(BF)
        d_refs[j][tokens : tokens + 2 * RANK, :] = grad_s[j].astype(BF)
        turned_ext = dot(put, drow_s[j, :, D:]).T.astype(BF)
        per = D // tokens
        for b in range(-(-(EXP_AT + experts_all) // TURN)):
            at = tokens + 2 * RANK + (b // per) * TURN
            lanes = slice((b % per) * tokens, (b % per + 1) * tokens)
            d_refs[j][at : at + TURN, lanes] = turned_ext[b * TURN : (b + 1) * TURN]


def experts(experts_all, info, first, rows, packs, w_gate_up, w_down, aux_w, gu_up, down_a, down_b):
    count = len(rows)
    tokens = rows[0].shape[0]
    whole = lambda arr: pl.BlockSpec(arr.shape, lambda e, ids: (0, 0))
    d_rows = tokens + 2 * RANK + turned_rows(EXP_AT + experts_all, tokens)

    def table(shape, j):
        at = first + j
        return pl.BlockSpec((1,) + shape, lambda e, ids: (ids[at],) + (0,) * len(shape))

    def body(ids_ref, *refs):
        refs = list(refs)
        take = lambda n: [refs.pop(0) for _ in range(n)]
        h_refs, p_refs = take(count), take(count)
        wgu_ref, wd_ref = take(2)
        tables = [take(count) for _ in range(4)]
        y_refs, d_refs = take(count), take(count)
        expert_kernel(experts_all, ids_ref, h_refs, p_refs, wgu_ref, wd_ref, tables, y_refs, d_refs, refs)

    picked = [(LANES, D), (2, RANK, FF), (RANK, FF), (RANK, D)]
    shapes = [(tokens, D)] * count + [(d_rows, D)] * count
    height = count * CAP
    outs = pl.pallas_call(
        body,
        grid_spec=pltpu.PrefetchScalarGridSpec(
            num_scalar_prefetch=1,
            grid=(1,),
            in_specs=[whole(arr) for arr in [*rows, *packs]]
            + [pl.BlockSpec(memory_space=pl.ANY)] * 2
            + [table(shape, j) for shape in picked for j in range(count)],
            out_specs=[pl.BlockSpec(shape, lambda e, ids: (0, 0)) for shape in shapes],
            scratch_shapes=[
                pltpu.VMEM((E_DEV, D, 2 * FF), BF),
                pltpu.VMEM((E_DEV, FF, D), BF),
                pltpu.VMEM((count, 2, LANES, FF), BF),
                pltpu.VMEM((count, tokens, E_DEV * CAP), BF),
                pltpu.VMEM((E_DEV, height, D), BF),
                pltpu.VMEM((E_DEV, height, D), BF),
                pltpu.VMEM((E_DEV, height, LANES), F32),
                pltpu.VMEM((count, E_DEV * CAP, D), BF),
                pltpu.VMEM((count, E_DEV * CAP, EXT), BF),
                pltpu.VMEM((count, 2 * RANK, D), F32),
                pltpu.SemaphoreType.DMA((2, E_DEV)),
            ],
        ),
        out_shape=[jax.ShapeDtypeStruct(shape, BF) for shape in shapes],
        cost_estimate=pl.CostEstimate(
            flops=16 * count * E_DEV * CAP * D * FF,
            bytes_accessed=2 * E_DEV * 3 * D * FF + 8 * count * tokens * D,
            transcendentals=0,
        ),
        name="experts",
    )(
        info,
        *rows,
        *packs,
        w_gate_up,
        w_down,
        *([aux_w] * count),
        *([gu_up] * count),
        *([down_a] * count),
        *([down_b] * count),
    )
    return list(outs[:count]), list(outs[count:])


def join_kernel(*refs):
    parts, out_ref = refs[:-1], refs[-1]
    for m, part in enumerate(parts):
        out_ref[m] = part[...]


def join(parts):
    return pl.pallas_call(
        join_kernel,
        in_specs=[VMEM_SPEC] * len(parts),
        out_specs=VMEM_SPEC,
        out_shape=jax.ShapeDtypeStruct((len(parts),) + parts[0].shape, parts[0].dtype),
        name="join",
    )(*parts)


def order_rows_kernel(info_ref, *refs):
    parts, out_ref = refs[:-1], refs[-1]
    rows = parts[0].shape[0]
    for m, part in enumerate(parts):
        start = pl.multiple_of(info_ref[SLOTS_AT + m] * rows, rows)
        out_ref[pl.ds(start, rows), :] = part[:, LOCAL:]


def order_rows(order, parts):
    return pl.pallas_call(
        order_rows_kernel,
        in_specs=[SMEM_SPEC] + [VMEM_SPEC] * len(parts),
        out_specs=VMEM_SPEC,
        out_shape=jax.ShapeDtypeStruct((QW, QG), BF),
        name="order_rows",
    )(order, *parts)


def lanes_of(index):
    return pl.ds(pl.multiple_of(index * QG, LANES), QG)


def start_copies(sources, target, sems):
    copies = [
        pltpu.make_async_copy(source, target.at[j], sems.at[j]) for j, source in enumerate(sources)
    ]
    for copy in copies:
        copy.start()
    return copies


def out_kernel(info_ref, x_ref, gain_ref, down_ref, up_ref, *refs):
    o_refs, w_hbm = refs[:GROUPS], refs[GROUPS : 2 * GROUPS]
    att_ref, rank_ref, y_ref, h_ref, w_s, sems = refs[2 * GROUPS :]
    w_copies = start_copies(w_hbm, w_s, sems)
    group = info_ref[1]
    for j in range(GROUPS):
        att_ref[:, lanes_of(group ^ j)] = o_refs[j][...]
    attended = att_ref[...]
    for j in range(GROUPS):
        w_copies[j].wait()
        y_ref[:, lanes_of(group ^ j)] = dot(attended, w_s[j])
    rank_out = dot_nt(attended, down_ref[0]).astype(BF)
    rank_ref[...] = rank_out
    y_one = x_ref[...].astype(F32) + y_ref[...] + dot(rank_out, up_ref[0])
    y_ref[...] = y_one
    inverse = lax.rsqrt(jnp.mean(y_one * y_one, axis=1, keepdims=True) + NORM_EPS)
    h_ref[...] = (y_one * inverse * gain_ref[...]).astype(BF)


def project_out(info, rows, gain, down_t, up, outs, w_parts):
    tokens = rows.shape[0]
    return pl.pallas_call(
        out_kernel,
        grid_spec=pltpu.PrefetchScalarGridSpec(
            num_scalar_prefetch=1,
            grid=(1,),
            in_specs=[VMEM_SPEC] * 2
            + [by_adapter(down_t), by_adapter(up)]
            + [VMEM_SPEC] * GROUPS
            + [pl.BlockSpec(memory_space=pl.ANY)] * GROUPS,
            out_specs=[VMEM_SPEC] * 4,
            scratch_shapes=[
                pltpu.VMEM((GROUPS, QW, QG), BF),
                pltpu.SemaphoreType.DMA((GROUPS,)),
            ],
        ),
        out_shape=[
            jax.ShapeDtypeStruct((tokens, QW), BF),
            jax.ShapeDtypeStruct((tokens, RANK), BF),
            jax.ShapeDtypeStruct((tokens, D), F32),
            jax.ShapeDtypeStruct((tokens, D), BF),
        ],
        cost_estimate=pl.CostEstimate(
            flops=2 * tokens * QW * D, bytes_accessed=2 * QW * D + 12 * tokens * D, transcendentals=0
        ),
        name="project_out",
    )(info, rows, gain, down_t, up, *outs, *w_parts)


def middle_kernel(count, terms, experts_all, info_ref, *refs):
    refs = list(refs)
    take = lambda n: [refs.pop(0) for _ in range(n)]
    d_refs = take(terms)
    pack_ref, y_ref, h_ref, gain_ref, aux_ref, att_ref, rank_ref, down_ref, up_ref = take(9)
    w_hbm = take(GROUPS)
    (dy_ref,) = take(1)
    do_refs, early_refs = take(count), take(GROUPS)
    do_s, early_s, w_s, sems = refs
    w_refs = start_copies(w_hbm, w_s, sems)
    group, ctx_index, copies = info_ref[1], info_ref[2], count // GROUPS
    tokens = y_ref.shape[0]
    d_sum = d_refs[0][...].astype(F32)
    for ref in d_refs[1:]:
        d_sum = d_sum + ref[...].astype(F32)
    early_s[0 : 2 * RANK, :] = d_sum[tokens : tokens + 2 * RANK]
    d_ext = read_turned(d_sum[tokens + 2 * RANK :], EXP_AT + experts_all, tokens, 0).T
    h_two = h_ref[...]
    lane = lax.broadcasted_iota(jnp.int32, (tokens, LANES), 1)
    chosen = read_turned(pack_ref[tokens:, :].astype(F32), experts_all, tokens, EXP_AT).T > 0.0
    picked = jnp.where(chosen, dot_nt(h_two, aux_ref[0]), NEG)
    weights = jnp.exp(picked - jnp.max(picked, axis=1, keepdims=True))
    gates = weights / jnp.sum(weights, axis=1, keepdims=True)
    mixed = jnp.sum(jnp.where(chosen, gates * d_ext, 0.0), axis=1, keepdims=True)
    d_logits = jnp.where(chosen, gates * (d_ext - mixed), 0.0)
    d_ext = jnp.where(lane < EXP_AT, d_ext, d_logits).astype(BF)
    d_h = d_sum[:tokens] + dot(d_ext, aux_ref[0])
    y_one = y_ref[...]
    inverse = lax.rsqrt(jnp.mean(y_one * y_one, axis=1, keepdims=True) + NORM_EPS)
    scaled = gain_ref[...] * d_h
    d_y = pack_ref[:tokens, :].astype(F32) + inverse * scaled
    d_y = d_y - y_one * inverse**3 * jnp.mean(y_one * scaled, axis=1, keepdims=True)
    dy_ref[...] = d_y
    d_attn = d_y.astype(BF)
    d_rank = dot_nt(d_attn, up_ref[0]).astype(BF)
    do_s[...] = dot(d_rank, down_ref[0])
    for j in range(GROUPS):
        at = lanes_of(group ^ j)
        early_s[3 * RANK : 4 * RANK, at] = dot_tn(rank_ref[...], dy_ref[:, at].astype(BF))
        w_refs[j].wait()
        do_s[...] += dot_nt(dy_ref[:, at].astype(BF), w_s[j])
    for m in range(count):
        do_refs[m][...] = do_s[:, lanes_of((ctx_index ^ m) // copies)].astype(BF)
    early_s[2 * RANK : 3 * RANK, :] = dot_tn(d_rank, att_ref[...])
    early_s[4 * RANK :, :] = dot_tn(d_ext, h_two)[: 2 * RANK]
    for j in range(GROUPS):
        for i in range(6):
            block = early_s[i * RANK : (i + 1) * RANK, lanes_of(group ^ j)]
            early_refs[j][:, i * QG : (i + 1) * QG] = block.astype(BF)


def middle_back(info, count, experts_all, terms, pack, y_one, h_two, gain, aux, attended, rank_out, down_t, up, w_parts):
    tokens = y_one.shape[0]
    outs = pl.pallas_call(
        functools.partial(middle_kernel, count, len(terms), experts_all),
        grid_spec=pltpu.PrefetchScalarGridSpec(
            num_scalar_prefetch=1,
            grid=(1,),
            in_specs=[VMEM_SPEC] * (len(terms) + 4)
            + [by_adapter(aux)]
            + [VMEM_SPEC] * 2
            + [by_adapter(down_t), by_adapter(up)]
            + [pl.BlockSpec(memory_space=pl.ANY)] * GROUPS,
            out_specs=[VMEM_SPEC] * (1 + count + GROUPS),
            scratch_shapes=[
                pltpu.VMEM((tokens, QW), F32),
                pltpu.VMEM((6 * RANK, D), F32),
                pltpu.VMEM((GROUPS, QW, QG), BF),
                pltpu.SemaphoreType.DMA((GROUPS,)),
            ],
        ),
        out_shape=[jax.ShapeDtypeStruct((tokens, D), F32)]
        + [jax.ShapeDtypeStruct((tokens, QG), BF)] * count
        + [jax.ShapeDtypeStruct((RANK, 6 * QG), BF)] * GROUPS,
        cost_estimate=pl.CostEstimate(
            flops=2 * tokens * QW * D, bytes_accessed=2 * QW * D + 20 * tokens * D, transcendentals=0
        ),
        name="middle_back",
    )(info, *terms, pack, y_one, h_two, gain, aux, attended, rank_out, down_t, up, *w_parts)
    return outs[0], list(outs[1 : 1 + count]), list(outs[1 + count :])


def ranks_kernel(info_ref, dqkv_ref, up_ref, t_ref, h_ref, *refs):
    early_refs, (rank_ref, keep_ref, send_ref) = refs[:GROUPS], refs[GROUPS:]
    d_qkv = dqkv_ref[...]
    d_rank = dot_nt(d_qkv, up_ref[...]).astype(BF)
    rank_ref[...] = d_rank
    grad = dot_tn(t_ref[...], d_qkv)
    keep_ref[:, :QG] = grad[:RANK, :QG].astype(BF)
    keep_ref[:, QG : QG + KG] = grad[RANK : 2 * RANK, QG : QG + KG].astype(BF)
    keep_ref[:, QG + KG : LOCAL] = grad[2 * RANK :, QG + KG :].astype(BF)
    send_ref[:, :LOCAL] = jnp.zeros((RANK, LOCAL), BF)
    for j in range(GROUPS):
        target = send_ref if j % 2 else keep_ref
        down = dot_tn(d_rank, h_ref[:, lanes_of(info_ref[1] ^ j)]).astype(BF)
        first = LOCAL + (j // 2) * 3 * QG
        for i in range(3):
            target[:, first + i * QG : first + (i + 1) * QG] = down[i * RANK : (i + 1) * RANK]
        first = LOCAL + 6 * QG + (j // 2) * 6 * QG
        target[:, first : first + 6 * QG] = early_refs[j][...]


HALF = LOCAL + 18 * QG
BOTH = HALF + LOCAL


def ranks_back(info, d_qkv, up_diag, rank_qkv, h_one, early):
    length = d_qkv.shape[0]
    return pl.pallas_call(
        ranks_kernel,
        in_specs=[SMEM_SPEC] + [VMEM_SPEC] * (4 + GROUPS),
        out_specs=[VMEM_SPEC] * 3,
        out_shape=[
            jax.ShapeDtypeStruct((length, 3 * RANK), BF),
            jax.ShapeDtypeStruct((RANK, HALF), BF),
            jax.ShapeDtypeStruct((RANK, HALF), BF),
        ],
        name="ranks_back",
    )(info, d_qkv, up_diag, rank_qkv, h_one, *early)


def mix_kernel(near_ref, far_ref, out_ref):
    out_ref[:, :LOCAL] = near_ref[:, :LOCAL]
    out_ref[:, LOCAL : 2 * LOCAL] = far_ref[:, :LOCAL]
    first = LOCAL
    for width in (3 * QG, 6 * QG):
        for mine, theirs in ((0, width), (width, 0)):
            total = near_ref[:, first + mine : first + mine + width].astype(F32)
            total = total + far_ref[:, first + theirs : first + theirs + width].astype(F32)
            at = LOCAL + first + mine
            out_ref[:, at : at + width] = total.astype(BF)
        first += 2 * width


def mix(near, far):
    return pl.pallas_call(
        mix_kernel,
        in_specs=[VMEM_SPEC] * 2,
        out_specs=VMEM_SPEC,
        out_shape=jax.ShapeDtypeStruct((RANK, BOTH), BF),
        name="mix",
    )(near, far)


def inputs_kernel(dqkv_ref, rank_ref, w_ref, down_ref, *rows_refs):
    rows = dot_nt(dqkv_ref[...], w_ref[...]) + dot_nt(rank_ref[...], down_ref[...])
    rows = rows.astype(BF)
    for m, ref in enumerate(rows_refs):

        @pl.when(pl.program_id(0) == m)
        def _():
            ref[...] = rows


def inputs_back(count, d_qkv, d_rank, cols_all, down_sel):
    length = d_qkv.shape[0]
    tokens = length // count
    per_block = lambda width: pl.BlockSpec((tokens, width), lambda i: (i, 0))
    whole = lambda shape: pl.BlockSpec(shape, lambda i: (0, 0))
    return pl.pallas_call(
        inputs_kernel,
        grid=(count,),
        in_specs=[
            per_block(LOCAL),
            per_block(3 * RANK),
            whole((D, LOCAL)),
            whole((D, 3 * RANK)),
        ],
        out_specs=[whole((tokens, D))] * count,
        out_shape=[jax.ShapeDtypeStruct((tokens, D), BF)] * count,
        cost_estimate=pl.CostEstimate(
            flops=2 * length * D * LOCAL, bytes_accessed=4 * length * (D + LOCAL), transcendentals=0
        ),
        name="inputs_back",
    )(d_qkv, d_rank, cols_all, down_sel)


def place_kernel(info_ref, *refs):
    up_ref, down_ref, gu_ref, da_ref, db_ref, od_ref, ou_ref, gd_ref, sum_s, parts, sems = refs[2:]
    sources = parts.shape[1]
    copies = start_copies(refs[:2], parts, sems)
    up_ref[...] = jnp.zeros(up_ref.shape, F32)
    down_ref[...] = jnp.zeros(down_ref.shape, F32)
    sum_s[...] = jnp.zeros(sum_s.shape, F32)
    for copy in copies:
        copy.wait()
    for j in range(GROUPS):
        group = info_ref[1] ^ j
        keys = lambda first: pl.ds(pl.multiple_of(first + group * KG, LANES), KG)
        far = j // 2
        down_at = 2 * LOCAL + far * 3 * QG
        early_at = 2 * LOCAL + 6 * QG + far * 6 * QG
        for m in range(sources):
            a = info_ref[SLOTS_AT + sources + m]
            take = lambda first, width: parts[j % 2, m, :, first : first + width].astype(F32)
            up_ref[a, :, lanes_of(group)] += take(far * LOCAL, QG)
            up_ref[a, :, keys(QW)] += take(far * LOCAL + QG, KG)
            up_ref[a, :, keys(QW + KVW)] += take(far * LOCAL + QG + KG, KG)
            for i in range(3):
                at = slice(i * RANK, (i + 1) * RANK)
                down_ref[a, at, lanes_of(group)] += take(down_at + i * QG, QG)
            for i in range(6):
                at = slice(i * RANK, (i + 1) * RANK)
                sum_s[a, at, lanes_of(group)] += take(early_at + i * QG, QG)
    for a in range(ADAPT):
        gu_ref[a, 0] = sum_s[a, :RANK, :FF]
        gu_ref[a, 1] = sum_s[a, :RANK, FF : 2 * FF]
        da_ref[a] = sum_s[a, :RANK, 2 * FF :]
        db_ref[a] = sum_s[a, RANK : 2 * RANK]
        od_ref[a] = sum_s[a, 2 * RANK : 3 * RANK]
        ou_ref[a] = sum_s[a, 3 * RANK : 4 * RANK]
        gd_ref[a] = sum_s[a, 4 * RANK :]


def place_grads(info, near, far):
    shapes = [(RANK, QW + 2 * KVW), (3 * RANK, D), (2, RANK, FF), (RANK, FF), (RANK, D)]
    shapes += [(RANK, QW), (RANK, D), (2 * RANK, D)]
    return pl.pallas_call(
        place_kernel,
        in_specs=[SMEM_SPEC] + [pl.BlockSpec(memory_space=pl.ANY)] * 2,
        out_specs=[VMEM_SPEC] * len(shapes),
        out_shape=[jax.ShapeDtypeStruct((ADAPT,) + shape, F32) for shape in shapes],
        scratch_shapes=[
            pltpu.VMEM((ADAPT, 6 * RANK, D), F32),
            pltpu.VMEM((2,) + near.shape, BF),
            pltpu.SemaphoreType.DMA((2,)),
        ],
        name="place_grads",
    )(info, near, far)


def norm_backward(values, inverse, gain_vec, upstream):
    scaled = gain_vec * upstream
    return inverse * scaled - values * inverse**3 * jnp.mean(
        values * scaled, axis=-1, keepdims=True
    )


def local_columns(table, group):
    lead = table.shape[:-1]
    cut = lambda first, width: lax.dynamic_slice_in_dim(
        table, first + group * width, width, table.ndim - 1
    )
    return cut(0, QG), cut(QW, KG), cut(QW + KVW, KG)


def on_device(
    inputs,
    cotangent,
    segment_ids,
    expert_ids,
    adapter_ids,
    gain_one,
    w_qkv,
    w_out,
    gain_two,
    router,
    w_gate_up,
    w_down,
    qkv_down,
    qkv_up,
    out_down,
    out_up,
    gu_down,
    gu_up,
    down_a,
    down_b,
):
    ctx_count = lax.axis_size("ctx")
    seq_count = lax.axis_size("seq")
    ctx_index = lax.axis_index("ctx")
    seq_index = lax.axis_index("seq")
    tokens = inputs.shape[1]
    length = tokens * ctx_count
    experts_all = router.shape[1]
    copies = ctx_count // GROUPS
    group = ctx_index // copies
    half = tokens // 2
    ctx_masks = doublings(ctx_count)[::-1]
    seq_slots = (seq_index ^ jnp.arange(seq_count)).astype(jnp.int32)
    ctx_slots = ctx_index ^ jnp.arange(ctx_count)
    own_rows = inputs[0]

    moving_rows = [swap(own_rows, "ctx", mask) for mask in ctx_masks]
    own_q, own_k, own_v = local_columns(w_qkv, group)
    own_out = lax.dynamic_slice_in_dim(w_out, group * QG, QG, 1)
    col_slots = []
    cols = Steps(
        gather_line(
            jnp.concatenate([own_q, own_k, own_v, own_out], axis=1), col_slots
        )
    )
    chosen = expert_ids[0]
    hot = jnp.any(chosen[:, :, None] == jnp.arange(experts_all)[None, None, :], axis=1)
    hot_low = hot.astype(BF).T
    before = (jnp.arange(tokens)[:, None] <= jnp.arange(tokens)[None, :]).astype(BF)
    ranks = dot(hot_low, before).astype(BF) * hot_low
    per = D // tokens
    rank_rows = turned_rows(experts_all, tokens)
    ranks = jnp.pad(ranks, ((0, rank_rows * per - experts_all), (0, 0)))
    ranks = ranks.reshape(rank_rows // TURN, per, TURN, tokens)
    ranks = jnp.transpose(ranks, (0, 2, 1, 3)).reshape(rank_rows, D)
    pack = jnp.concatenate([cotangent[0], ranks], axis=0)
    cols.beside()
    seg_row = segment_ids[0]
    position = jnp.arange(length)
    start = jnp.sum((seg_row[None, :] < seg_row[:, None]).astype(jnp.int32), axis=1)
    block_id = jnp.stack([ctx_slots, 2 * ctx_count - 1 - ctx_slots], axis=1).reshape(-1)
    block_of = jnp.arange(2 * ctx_count)
    owner = jnp.minimum(block_of, 2 * ctx_count - 1 - block_of)
    place = (2 * (owner ^ ctx_index) + (block_of >= ctx_count)).astype(jnp.int32)
    first = (start[::BLK] // BLK).astype(jnp.int32)
    offset = (position - start).reshape(2 * ctx_count, half)[block_id].reshape(-1)
    lane = jnp.arange(LANES) % HEAD_DIM
    frequency = 10000.0 ** (-2.0 * (lane % (HEAD_DIM // 2)).astype(F32) / HEAD_DIM)
    angles = offset.astype(F32)[:, None] * frequency[None, :]
    cosine = jnp.cos(angles)
    sine = jnp.sin(angles) * jnp.where(lane < HEAD_DIM // 2, -1.0, 1.0)[None, :]
    start_row = start[None, :]
    adapter = adapter_ids[seq_index]
    slot_adapters = adapter_ids[seq_slots]
    info = jnp.concatenate(
        [jnp.stack([adapter, group, ctx_index, E_DEV * seq_index]), seq_slots, slot_adapters]
    ).astype(jnp.int32)

    def pick(table):
        return lax.dynamic_index_in_dim(table, adapter, 0, keepdims=False)

    qkv_down_sel = pick(qkv_down)
    out_down_t = jnp.swapaxes(out_down, 1, 2)
    aux_w = jnp.concatenate(
        [
            jnp.swapaxes(gu_down, 1, 2),
            jnp.broadcast_to(router.T[None], (ADAPT, experts_all, D)),
            jnp.zeros((ADAPT, LANES - 2 * RANK - experts_all, D), BF),
        ],
        axis=1,
    )
    down_a_t = jnp.swapaxes(down_a, 1, 2)

    pack, start_row, cosine, sine, place, first, info, *moving_rows = cols.beside(
        pack, start_row, cosine, sine, place, first, info, *moving_rows
    )
    row_slots = gather_rest(own_rows, moving_rows, ctx_masks)
    all_rows = jnp.concatenate(row_slots, axis=0).astype(F32)
    inv_all = lax.rsqrt(jnp.mean(all_rows * all_rows, axis=-1, keepdims=True) + NORM_EPS)
    h_one = (all_rows * inv_all * gain_one).astype(BF)
    rank_qkv = dot(h_one, qkv_down_sel).astype(BF)
    h_one, rank_qkv, pack = cols.beside(h_one, rank_qkv, pack)
    pack_slots = []
    packs = Steps(gather_line(pack, pack_slots))
    cols.finish()
    outs = Steps(gather_groups(order_rows(info, col_slots), copies))
    qkv, cols_all, up_diag = packs.beside(
        *project(info, h_one, rank_qkv, qkv_up, cosine, sine, col_slots)
    )
    heads_out, lse, *pieces = packs.beside(
        *outs.beside(*attend(place, first, qkv, start_row, copies))
    )
    heads_here = packs.beside(
        *[swap(piece, "ctx", j * copies) if j else piece for j, piece in enumerate(pieces)]
    )
    out_parts = outs.finish()
    attended, rank_out, y_one, h_two = project_out(
        info, own_rows, gain_two[None], out_down_t, out_up, heads_here, out_parts
    )

    def compute(m, rows):
        return experts(
            experts_all,
            info,
            SLOTS_AT + seq_count + m,
            rows,
            pack_slots[m : m + len(rows)],
            w_gate_up,
            w_down,
            aux_w,
            gu_up,
            down_a_t,
            down_b,
        )

    y_sums, d_terms = exchange_experts(h_two, packs, compute)

    d_y_one, d_heads, early = middle_back(
        info,
        ctx_count,
        experts_all,
        d_terms,
        pack,
        y_one,
        h_two,
        gain_two[None],
        aux_w,
        attended,
        rank_out,
        out_down_t,
        out_up,
        out_parts,
    )
    (d_y_one,) = y_sums.beside(d_y_one)
    d_heads = [swap(piece, "ctx", m) if m else piece for m, piece in enumerate(d_heads)]
    d_heads = y_sums.beside(*d_heads)

    (d_qkv,) = y_sums.beside(
        attend_back(place, first, qkv, start_row, heads_out, lse, cosine, sine, d_heads)
    )
    d_rank_qkv, keep, sent = ranks_back(info, d_qkv, up_diag, rank_qkv, h_one, early)

    halves = add_low(keep, swap(sent, "ctx", copies))
    for mask in doublings(copies):
        shared = halves[:, HALF - 12 * QG :]
        shared = add_low(shared, swap(shared, "ctx", mask))
        halves = jnp.concatenate([halves[:, : HALF - 12 * QG], shared], axis=1)
    halves, d_rank_qkv = lax.optimization_barrier((halves, d_rank_qkv))
    arrived, *d_rows = y_sums.beside(
        swap(halves, "ctx", 2 * copies),
        *inputs_back(ctx_count, d_qkv, d_rank_qkv, cols_all, qkv_down_sel),
    )
    d_rows = d_rows[::copies]
    near = add_low(d_rows[0], swap(d_rows[1], "ctx", copies))
    far = add_low(d_rows[2], swap(d_rows[3], "ctx", copies))
    slots = []
    grads = Steps(gather_line(mix(halves, arrived), slots))
    near, far = grads.beside(near, far)
    d_h_one = near.astype(F32) + swap(far, "ctx", 2 * copies).astype(F32)
    features = own_rows.astype(F32)
    inv_one = lax.rsqrt(jnp.mean(features * features, axis=-1, keepdims=True) + NORM_EPS)
    input_grad = d_y_one + norm_backward(features, inv_one, gain_one, d_h_one)
    layer_output = y_one
    for term in y_sums.finish():
        layer_output = layer_output + term.astype(F32)
    layer_output = layer_output.astype(BF)
    grads.beside()
    grads.beside()
    input_grad, layer_output = grads.beside(input_grad, layer_output)
    grads.finish()
    grads = join(slots)
    (
        grad_qkv_up,
        grad_qkv_down,
        grad_gu_up,
        grad_down_a,
        grad_down_b,
        grad_out_down,
        grad_out_up,
        grad_gu_down,
    ) = place_grads(info, grads, swap(grads, "ctx", copies))

    return (
        layer_output[None],
        input_grad[None],
        jnp.swapaxes(grad_qkv_down, 1, 2),
        grad_qkv_up,
        jnp.swapaxes(grad_out_down, 1, 2),
        grad_out_up,
        jnp.swapaxes(grad_gu_down, 1, 2),
        grad_gu_up,
        jnp.swapaxes(grad_down_a, 1, 2),
        grad_down_b,
    )


def solution(mesh):
    over_seq = P("seq", None)
    placed = (
        P("seq", "ctx", None),
        P("seq", "ctx", None),
        over_seq,
        P("seq", "ctx", None),
        P(),
        P(),
        over_seq,
        over_seq,
        P(),
        P(),
        P("seq", None, None),
        P("seq", None, None),
    ) + (P(),) * 8
    return jax.shard_map(
        on_device,
        mesh=mesh,
        in_specs=placed,
        out_specs=(P("seq", "ctx", None), P("seq", "ctx", None)) + (P(),) * 8,
        check_vma=False,
    )
```

```python
import functools

import jax
import jax.numpy as jnp
from jax import lax
from jax.experimental import pallas as pl
from jax.experimental.pallas import tpu as pltpu
from jax.sharding import PartitionSpec as P

D = 1536
HEADS = 24
KV_HEADS = 8
HEAD_DIM = 64
FF = 512
RANK = 16
ADAPT = 8
E_DEV = 2
CAP = 128
QW = 1536
KVW = 512
NORM_EPS = 1e-05

GROUPS = KV_HEADS // 2
PAIRS = HEADS // KV_HEADS
QG = QW // GROUPS
KG = KVW // GROUPS
LOCAL = QG + 2 * KG
BLK = 256
LANES = 128
EXP_AT = 2 * RANK
GATE_AT = 96
SLOTS_AT = 4
EXT = D + LANES
TURN = 8
NEG = -1e30

BF = jnp.bfloat16
F32 = jnp.float32
NT = (((1,), (1,)), ((), ()))
TN = (((0,), (0,)), ((), ()))


def turned_rows(columns, tokens):
    return TURN * -(-columns * tokens // (TURN * D))


def dot(left_arr, right_arr):
    return jnp.dot(left_arr, right_arr, preferred_element_type=F32)


def dot_nt(left_arr, right_arr):
    return lax.dot_general(left_arr, right_arr, NT, preferred_element_type=F32)


def dot_tn(left_arr, right_arr):
    return lax.dot_general(left_arr, right_arr, TN, preferred_element_type=F32)


def swap(block, axis, mask):
    count = lax.axis_size(axis)
    return lax.ppermute(block, axis, [(i, i ^ mask) for i in range(count)])


def gather_slots(block, axis, masks):
    slots = {0: block}
    for mask in masks:
        for have in list(slots):
            slots[have ^ mask] = swap(slots[have], axis, mask)
    return [slots[m] for m in sorted(slots)]


def together(*arrays):
    return lax.optimization_barrier(arrays)


def gather_rest(block, arrived, masks):
    slots = {0: block}
    for mask, first in zip(masks, arrived):
        for have in list(slots):
            slots[have ^ mask] = swap(slots[have], "ctx", mask) if have else first
    return [slots[m] for m in sorted(slots)]


def line_swap(block, pairs):
    return lax.ppermute(block, "seq", [(2 * i + j, 2 * k + j) for i, k in pairs for j in (0, 1)])


def outward(block):
    return line_swap(block, [(1, 0), (2, 3)])


def inward(block):
    return line_swap(block, [(0, 1), (3, 2)])


def middle(block):
    return line_swap(block, [(1, 2), (2, 1)])


class Steps:
    def __init__(self, work):
        self.work = work
        self.moving = self.result = None
        self.resume(None)

    def resume(self, arrived):
        try:
            self.moving = self.work.send(arrived)
        except StopIteration as end:
            self.moving, self.result = None, end.value

    def beside(self, *others):
        if self.moving is None:
            return others
        arrived, others = lax.optimization_barrier((tuple(self.moving), others))
        self.resume(arrived)
        return others

    def join(self, other, *others):
        if self.moving is None or other.moving is None:
            return self.beside(*other.beside(*others))
        mine, theirs, others = lax.optimization_barrier(
            (tuple(self.moving), tuple(other.moving), others)
        )
        self.resume(mine)
        other.resume(theirs)
        return others

    def finish(self):
        while self.moving is not None:
            self.beside()
        return self.result


def gather_line(block, slots):
    count = lax.axis_size("seq")
    if count != 8:
        slots += gather_slots(block, "seq", doublings(count))
        return slots
    slots.append(block)
    two, six, one = yield swap(block, "seq", 2), middle(block), swap(block, "seq", 1)
    slots += [one, two]
    four, far, three = yield middle(two), outward(six), swap(two, "seq", 1)
    four = four + far
    slots += [three, four]
    far, five = yield outward(four), swap(four, "seq", 1)
    six = six + far
    slots += [five, six]
    (seven,) = yield (swap(six, "seq", 1),)
    slots.append(seven)
    return slots


def gather_seq(block):
    return Steps(gather_line(block, [])).finish()


def reduce_line(parts, one=None):
    count = lax.axis_size("seq")
    if count != 8:
        return [reduce_slots(parts, "seq", doublings(count))]
    (seven,) = yield (swap(parts[7], "seq", 1),)
    six = add_low(parts[6], seven)
    near, five = yield inward(six), swap(parts[5], "seq", 1)
    four = add_low(parts[4], five, near)
    near, far, three = yield inward(four), middle(four), swap(parts[3], "seq", 1)
    six = add_low(six, near)
    two = add_low(parts[2], three, far)
    last = [swap(two, "seq", 2), middle(six)]
    if one is None:
        last.append(swap(parts[1], "seq", 1))
    last = yield last
    return [parts[0], *last] + ([] if one is None else [one])


def exchange_experts(block, packs, compute):
    count = lax.axis_size("seq")
    slots, y_parts, d_parts = [], [], []
    rows = Steps(gather_line(block, slots))

    def slots_of(m, some):
        some_y, some_d = compute(m, slots[m : m + some])
        return [*some_y, *some_d]

    def keep(done, some):
        y_parts.extend(done[:some])
        d_parts.extend(done[some:])

    if count != 8:
        packs.finish()
        for m in range(0, count, 2):
            keep(slots_of(m, 2), 2)
        return Steps(reduce_line(y_parts)), Steps(reduce_line(d_parts)).finish()
    keep(rows.join(packs, *slots_of(0, 1)), 1)
    for m in (1, 3, 5):
        keep(rows.beside(*slots_of(m, 2)), 2)
    one = swap(d_parts[1], "seq", 1)
    *done, one = lax.optimization_barrier((*slots_of(7, 1), one))
    keep(done, 1)
    terms = Steps(reduce_line(d_parts, one))
    terms.beside()
    terms.beside()
    y_sums = Steps(reduce_line(list(terms.beside(*y_parts))))
    return y_sums, terms.finish()


def doublings(count):
    return [1 << bit for bit in range(count.bit_length() - 1)]


def add_low(*terms):
    total = terms[0].astype(F32)
    for term in terms[1:]:
        total = total + term.astype(F32)
    return lax.optimization_barrier(total.astype(BF))


def gather_groups(block, copies):
    two, one = yield swap(block, "ctx", 2 * copies), swap(block, "ctx", copies)
    return [block, one, two, swap(two, "ctx", copies)]


def reduce_slots(parts, axis, masks):
    parts = dict(enumerate(parts))
    for step, mask in enumerate(masks):
        last = step == len(masks) - 1
        for m in [m for m in parts if m & mask]:
            arrived = swap(parts.pop(m), axis, mask)
            mine = parts[m ^ mask]
            parts[m ^ mask] = (
                mine.astype(F32) + arrived.astype(F32) if last else add_low(mine, arrived)
            )
    return parts[0]


def rotate(values, cosine, sine, sign):
    lane = lax.broadcasted_iota(jnp.int32, values.shape, 1)
    ahead = pltpu.roll(values, LANES - HEAD_DIM // 2, 1)
    behind = pltpu.roll(values, HEAD_DIM // 2, 1)
    other = jnp.where(lane % HEAD_DIM < HEAD_DIM // 2, ahead, behind)
    return values * cosine + (sign * other) * sine


def by_adapter(table):
    return pl.BlockSpec((1,) + table.shape[1:], lambda i, info: (info[0], 0, 0))


def project_kernel(info_ref, h_ref, t_ref, table_ref, cos_ref, sin_ref, *rest):
    shards = rest[:-3]
    qkv_ref, w_ref, up_ref = rest[-3:]
    rows = shards[0].shape[0]
    group = info_ref[1]

    @pl.when(pl.program_id(0) == 0)
    def _():
        for m, shard in enumerate(shards):
            start = pl.multiple_of(info_ref[SLOTS_AT + m] * rows, rows)
            w_ref[pl.ds(start, rows), :] = shard[:, :LOCAL]
        up_ref[...] = jnp.zeros(up_ref.shape, BF)
        columns = lambda first, width: table_ref[
            0, :, pl.ds(pl.multiple_of(first + group * width, LANES), width)
        ]
        up_ref[:RANK, :QG] = columns(0, QG)
        up_ref[RANK : 2 * RANK, QG : QG + KG] = columns(QW, KG)
        up_ref[2 * RANK :, QG + KG :] = columns(QW + KVW, KG)

    pre = dot(h_ref[...], w_ref[...]) + dot(t_ref[...], up_ref[...])
    cosine, sine = cos_ref[...], sin_ref[...]
    tiles = [rotate(tile, cosine, sine, 1.0) * 0.125 for tile in lane_tiles(pre)]
    tiles = paired_heads(tiles)
    tiles.append(rotate(pre[:, QG : QG + KG], cosine, sine, 1.0))
    tiles.append(pre[:, QG + KG :])
    for j, tile in enumerate(tiles):
        qkv_ref[:, j * LANES : (j + 1) * LANES] = tile.astype(BF)


def project(info, h_one, rank_qkv, table, cosine, sine, shards):
    length = h_one.shape[0]
    rows = shards[0].shape[0]
    count = len(shards)
    per_block = lambda width: pl.BlockSpec((BLK, width), lambda i, info: (i, 0))
    whole = lambda shape: pl.BlockSpec(shape, lambda i, info: (0, 0))
    return pl.pallas_call(
        project_kernel,
        grid_spec=pltpu.PrefetchScalarGridSpec(
            num_scalar_prefetch=1,
            grid=(length // BLK,),
            in_specs=[
                per_block(D),
                per_block(3 * RANK),
                by_adapter(table),
                per_block(LANES),
                per_block(LANES),
            ]
            + [whole((rows, LOCAL + QG))] * count,
            out_specs=[per_block(LOCAL), whole((D, LOCAL)), whole((3 * RANK, LOCAL))],
        ),
        out_shape=[
            jax.ShapeDtypeStruct((length, LOCAL), BF),
            jax.ShapeDtypeStruct((D, LOCAL), BF),
            jax.ShapeDtypeStruct((3 * RANK, LOCAL), BF),
        ],
        cost_estimate=pl.CostEstimate(
            flops=2 * length * D * LOCAL, bytes_accessed=2 * length * (D + LOCAL), transcendentals=0
        ),
        name="project",
    )(info, h_one, rank_qkv, table, cosine, sine, *shards)


def half_mask(shape, half):
    lane = lax.broadcasted_iota(jnp.int32, shape, 1)
    return (lane < HEAD_DIM) if half == 0 else (lane >= HEAD_DIM)


def turned(tile):
    return pltpu.roll(tile.astype(F32), HEAD_DIM, 1).astype(tile.dtype)


def paired_heads(tiles):
    is_low = half_mask(tiles[0].shape, 0)
    return [
        jnp.where(is_low, tiles[0], tiles[1]),
        jnp.where(is_low, turned(tiles[0]), turned(tiles[2])),
        jnp.where(is_low, tiles[1], tiles[2]),
    ]


def natural_heads(tiles):
    is_low = half_mask(tiles[0].shape, 0)
    return [
        jnp.where(is_low, tiles[0], turned(tiles[1])),
        jnp.where(is_low, tiles[2], tiles[0]),
        jnp.where(is_low, turned(tiles[1]), tiles[2]),
    ]


def lane_tiles(block):
    return [block[:, i * LANES : (i + 1) * LANES] for i in range(PAIRS)]


def stack_rows(place_ref, source_ref, target_ref, paired):
    half = BLK // 2
    for b in range(source_ref.shape[0] // half):
        rows = pl.ds(pl.multiple_of(place_ref[b] * half, half), half)
        tiles = lane_tiles(source_ref[rows, :QG])
        for pair, tile in enumerate(tiles if paired else paired_heads(tiles)):
            at = (b // 2) * PAIRS * BLK + pair * BLK + (b % 2) * half
            target_ref[at : at + half, :] = tile


def read_turned(block, columns, tokens, first):
    per = D // tokens
    parts = []
    for b in range(columns // TURN):
        at = slice((b // per) * TURN, (b // per + 1) * TURN)
        parts.append(block[at, (b % per) * tokens : (b % per + 1) * tokens])
    before = [jnp.zeros((first, tokens), F32)] if first else []
    after = [jnp.zeros((LANES - first - columns, tokens), F32)]
    return jnp.concatenate(before + parts + after, axis=0)


def split_keys(place_ref, qkv_ref, first_lane, target_ref, ones):
    half = BLK // 2
    for b in range(qkv_ref.shape[0] // half):
        rows = pl.ds(pl.multiple_of(place_ref[b] * half, half), half)
        both = qkv_ref[rows, first_lane : first_lane + LANES]
        for side in range(2):
            other = jnp.zeros_like(both)
            if ones:
                lane = lax.broadcasted_iota(jnp.int32, both.shape, 1)
                spare = HEAD_DIM if side == 0 else 0
                other = jnp.where(lane == spare, 1.0, 0.0).astype(BF)
            target_ref[side, b * half : (b + 1) * half, :] = jnp.where(
                half_mask(both.shape, side), both, other
            )


def as_column(row):
    return jnp.broadcast_to(row.astype(F32), (TURN, row.shape[1])).T[:, :1].astype(jnp.int32)


def tile_bias(start_col, q_first, k_first):
    shape = (BLK, BLK)
    key = k_first + lax.broadcasted_iota(jnp.int32, shape, 1)
    query = q_first + lax.broadcasted_iota(jnp.int32, shape, 0)
    bias = jnp.where((key >= start_col) & (key <= query), 0.0, NEG)
    return jnp.concatenate([bias] * PAIRS, axis=0)


def attend_kernel(copies, place_ref, first_ref, qkv_ref, start_ref, o_ref, lse_ref, *refs):
    piece_refs, (q_s, k_s, v_s, score_s, m_s, acc_s) = refs[:GROUPS], refs[GROUPS:]
    stack_rows(place_ref, qkv_ref, q_s, True)
    split_keys(place_ref, qkv_ref, QG, k_s, False)
    split_keys(place_ref, qkv_ref, QG + KG, v_s, True)
    half = BLK // 2
    tall = PAIRS * BLK

    def query_block(qb, unused):
        q_first = pl.multiple_of(qb * BLK, BLK)
        q_rows = pl.ds(pl.multiple_of(qb * tall, tall), tall)
        start_col = as_column(start_ref[:, pl.ds(q_first, BLK)])
        queries = q_s[q_rows, :]
        m_s[...] = jnp.full(m_s.shape, NEG, F32)
        acc_s[...] = jnp.zeros(acc_s.shape, F32)

        def score_block(kb, unused):
            k_first = pl.multiple_of(kb * BLK, BLK)
            bias = tile_bias(start_col, q_first, k_first)
            for side in range(2):
                scores = dot_nt(queries, k_s[side, pl.ds(k_first, BLK), :]) + bias
                score_s[kb, side] = scores
                m_s[side] = jnp.maximum(
                    m_s[side], jnp.maximum(scores[:, :LANES], scores[:, LANES:])
                )
            return unused

        lax.fori_loop(first_ref[qb], qb + 1, score_block, 0)
        peaks = [jnp.max(m_s[side], axis=1, keepdims=True) for side in range(2)]

        def value_block(kb, unused):
            k_first = pl.multiple_of(kb * BLK, BLK)
            for side in range(2):
                prob = jnp.exp(score_s[kb, side] - peaks[side]).astype(BF)
                acc_s[side] += dot(prob, v_s[side, pl.ds(k_first, BLK), :])
            return unused

        lax.fori_loop(first_ref[qb], qb + 1, value_block, 0)
        low, high = acc_s[0], acc_s[1]
        low_sum = low[:, HEAD_DIM : HEAD_DIM + 1]
        high_sum = high[:, 0:1]
        is_low = half_mask(low.shape, 0)
        out = jnp.where(is_low, low / low_sum, high / high_sum).astype(BF)
        lse_ref[q_rows, :] = jnp.where(
            is_low, peaks[0] + jnp.log(low_sum), peaks[1] + jnp.log(high_sum)
        )
        for i in range(2):
            rows = pl.ds(pl.multiple_of(place_ref[2 * qb + i] * half, half), half)
            tiles = [out[pair * BLK + i * half :][:half] for pair in range(PAIRS)]
            for pair, tile in enumerate(natural_heads(tiles)):
                o_ref[rows, pair * LANES : (pair + 1) * LANES] = tile
        return unused

    lax.fori_loop(0, qkv_ref.shape[0] // BLK, query_block, 0)
    for j, piece in enumerate(piece_refs):
        tokens = piece.shape[0]
        piece[...] = o_ref[j * copies * tokens : (j * copies + 1) * tokens, :]


SMEM_SPEC = pl.BlockSpec(memory_space=pltpu.SMEM)
VMEM_SPEC = pl.BlockSpec(memory_space=pltpu.VMEM)


def attend(place, first, qkv, start_row, copies):
    length = qkv.shape[0]
    tall = PAIRS * BLK
    return pl.pallas_call(
        functools.partial(attend_kernel, copies),
        in_specs=[SMEM_SPEC, SMEM_SPEC, VMEM_SPEC, VMEM_SPEC],
        out_specs=[VMEM_SPEC] * (2 + GROUPS),
        out_shape=[
            jax.ShapeDtypeStruct((length, QG), BF),
            jax.ShapeDtypeStruct((PAIRS * length, LANES), F32),
        ]
        + [jax.ShapeDtypeStruct((length // (GROUPS * copies), QG), BF)] * GROUPS,
        scratch_shapes=[
            pltpu.VMEM((PAIRS * length, LANES), BF),
            pltpu.VMEM((2, length, LANES), BF),
            pltpu.VMEM((2, length, LANES), BF),
            pltpu.VMEM((length // BLK, 2, tall, BLK), F32),
            pltpu.VMEM((2, tall, LANES), F32),
            pltpu.VMEM((2, tall, LANES), F32),
        ],
        cost_estimate=pl.CostEstimate(
            flops=4 * length * length * QG, bytes_accessed=8 * length * QG, transcendentals=0
        ),
        name="attend",
    )(place, first, qkv, start_row)


def attend_back_kernel(
    place_ref,
    first_ref,
    qkv_ref,
    start_ref,
    o_ref,
    lse_ref,
    cos_ref,
    sin_ref,
    *refs,
):
    do_refs = refs[:-10]
    dqkv_ref, join_s, q_s, o_s, do_s, k_s, v_s, dk_s, dv_s, dq_s = refs[-10:]
    for m, piece in enumerate(do_refs):
        join_s[m * piece.shape[0] : (m + 1) * piece.shape[0], :] = piece[...]
    stack_rows(place_ref, qkv_ref, q_s, True)
    stack_rows(place_ref, o_ref, o_s, False)
    stack_rows(place_ref, join_s, do_s, False)
    split_keys(place_ref, qkv_ref, QG, k_s, False)
    split_keys(place_ref, qkv_ref, QG + KG, v_s, False)
    dk_s[...] = jnp.zeros(dk_s.shape, F32)
    dv_s[...] = jnp.zeros(dv_s.shape, F32)
    half = BLK // 2
    tall = PAIRS * BLK

    def query_block(qb, unused):
        q_first = pl.multiple_of(qb * BLK, BLK)
        q_rows = pl.ds(pl.multiple_of(qb * tall, tall), tall)
        start_col = as_column(start_ref[:, pl.ds(q_first, BLK)])
        dq_s[...] = jnp.zeros(dq_s.shape, F32)
        product = do_s[q_rows, :].astype(F32) * o_s[q_rows, :].astype(F32)
        lse = lse_ref[q_rows, :]
        lse_of = (lse[:, 0:1], lse[:, HEAD_DIM : HEAD_DIM + 1])
        delta_of = [
            jnp.sum(jnp.where(half_mask(product.shape, side), product, 0.0), axis=1, keepdims=True)
            for side in range(2)
        ]

        def key_block(kb, unused):
            k_first = pl.multiple_of(kb * BLK, BLK)
            k_rows = pl.ds(k_first, BLK)
            bias = tile_bias(start_col, q_first, k_first)
            queries = q_s[q_rows, :]
            d_out = do_s[q_rows, :]
            for side in range(2):
                keys = k_s[side, k_rows, :]
                scores = dot_nt(queries, keys) + bias
                prob = jnp.exp(scores - lse_of[side])
                d_prob = dot_nt(d_out, v_s[side, k_rows, :])
                d_score = (prob * (d_prob - delta_of[side])).astype(BF)
                dv_s[side, k_rows, :] += dot_tn(prob.astype(BF), d_out)
                dk_s[side, k_rows, :] += dot_tn(d_score, queries)
                dq_s[...] += dot(d_score, keys)
            return unused

        lax.fori_loop(first_ref[qb], qb + 1, key_block, 0)
        for i in range(2):
            rows = pl.ds(pl.multiple_of(place_ref[2 * qb + i] * half, half), half)
            cosine, sine = cos_ref[rows, :], sin_ref[rows, :]
            tiles = []
            for pair in range(PAIRS):
                at = pair * BLK + i * half
                tiles.append(rotate(dq_s[at : at + half, :] * 0.125, cosine, sine, -1.0))
            for pair, tile in enumerate(natural_heads(tiles)):
                dqkv_ref[rows, pair * LANES : (pair + 1) * LANES] = tile.astype(BF)
        return unused

    lax.fori_loop(0, qkv_ref.shape[0] // BLK, query_block, 0)
    for b in range(qkv_ref.shape[0] // half):
        rows = pl.ds(pl.multiple_of(place_ref[b] * half, half), half)
        at = slice(b * half, (b + 1) * half)
        is_low = half_mask((half, LANES), 0)
        back = jnp.where(is_low, dk_s[0, at, :], dk_s[1, at, :])
        back = rotate(back, cos_ref[rows, :], sin_ref[rows, :], -1.0)
        dqkv_ref[rows, QG : QG + KG] = back.astype(BF)
        dqkv_ref[rows, QG + KG : LOCAL] = jnp.where(is_low, dv_s[0, at, :], dv_s[1, at, :]).astype(BF)


def attend_back(place, first, qkv, start_row, out, lse, cosine, sine, d_out):
    length = qkv.shape[0]
    tall = PAIRS * BLK
    stacked = pltpu.VMEM((PAIRS * length, LANES), BF)
    return pl.pallas_call(
        attend_back_kernel,
        in_specs=[SMEM_SPEC, SMEM_SPEC] + [VMEM_SPEC] * (6 + len(d_out)),
        out_specs=VMEM_SPEC,
        out_shape=jax.ShapeDtypeStruct((length, LOCAL), BF),
        scratch_shapes=[
            pltpu.VMEM((length, QG), BF),
            stacked,
            stacked,
            stacked,
            pltpu.VMEM((2, length, LANES), BF),
            pltpu.VMEM((2, length, LANES), BF),
            pltpu.VMEM((2, length, LANES), F32),
            pltpu.VMEM((2, length, LANES), F32),
            pltpu.VMEM((tall, LANES), F32),
        ],
        cost_estimate=pl.CostEstimate(
            flops=10 * length * length * QG, bytes_accessed=16 * length * QG, transcendentals=0
        ),
        name="attend_back",
    )(place, first, qkv, start_row, out, lse, cosine, sine, *d_out)


def expert_kernel(experts_all, ids_ref, h_refs, p_refs, wgu_ref, wd_ref, tables, y_refs, d_refs, scratch):
    aux_w, gu_refs, da_refs, db_refs = tables
    wgu_s, wd_s, gu_s, put_s, x_s, g_s, extra_s, yrow_s, drow_s, grad_s, sems = scratch
    count = len(h_refs)
    tokens = h_refs[0].shape[0]

    def fetch(e):
        return [
            pltpu.make_async_copy(wgu_ref.at[e], wgu_s.at[e], sems.at[0, e]),
            pltpu.make_async_copy(wd_ref.at[e], wd_s.at[e], sems.at[1, e]),
        ]

    for e in range(E_DEV):
        for copy in fetch(e):
            copy.start()
    wide = lax.broadcasted_iota(jnp.int32, (tokens, LANES), 1)
    narrow = lax.broadcasted_iota(jnp.int32, (CAP, LANES), 1)
    base = EXP_AT + ids_ref[3]
    grad_s[...] = jnp.zeros(grad_s.shape, F32)
    gu_s[...] = jnp.zeros(gu_s.shape, BF)
    part = lambda arr, j: arr[j * CAP : (j + 1) * CAP]
    for j in range(count):
        gu_s[j, 0, 0:RANK, :] = gu_refs[j][0, 0]
        gu_s[j, 1, RANK : 2 * RANK, :] = gu_refs[j][0, 1]
        both = dot_nt(h_refs[j][...], aux_w[j][0])
        tall = read_turned(p_refs[j][tokens:, :].astype(F32), experts_all, tokens, EXP_AT)
        ranks = tall.T
        chosen = ranks > 0.0
        picked = jnp.where(chosen, both, NEG)
        weights = jnp.exp(picked - jnp.max(picked, axis=1, keepdims=True))
        gates = weights / jnp.sum(weights, axis=1, keepdims=True)
        aux = jnp.where(wide < EXP_AT, both, 0.0)
        which = lax.broadcasted_iota(jnp.int32, tall.shape, 0)
        slot = lax.broadcasted_iota(jnp.int32, (CAP, tokens), 0).astype(F32) + 1.0
        takes = []
        for e in range(E_DEV):
            column = jnp.sum(jnp.where(wide == base + e, ranks, 0.0), axis=1, keepdims=True)
            row = jnp.sum(jnp.where(which == base + e, tall, 0.0), axis=0, keepdims=True)
            takes.append(jnp.where(slot == row, 1.0, 0.0).astype(BF))
            put_s[j, :, e * CAP : (e + 1) * CAP] = jnp.where(
                wide.astype(F32) + 1.0 == column, 1.0, 0.0
            ).astype(BF)
            gate = jnp.sum(jnp.where(wide == base + e, gates, 0.0), axis=1, keepdims=True)
            gate_one = gate.astype(BF).astype(F32)
            gate_two = (gate - gate_one).astype(BF).astype(F32)
            first = GATE_AT + 3 * e
            aux = jnp.where(wide == first, gate_one, aux)
            aux = jnp.where(wide == first + 1, gate_two, aux)
            aux = jnp.where(wide == first + 2, gate - gate_one - gate_two, aux)
        take = jnp.concatenate(takes, axis=0)
        at = slice(j * CAP, (j + 1) * CAP)
        rows = dot(take, h_refs[j][...]).astype(BF)
        upstream = dot(take, p_refs[j][:tokens, :]).astype(BF)
        extra = dot(take, aux.astype(BF))
        for e in range(E_DEV):
            x_s[e, at, :] = part(rows, e)
            g_s[e, at, :] = part(upstream, e)
            extra_s[e, at, :] = part(extra, e)

    def each(make):
        return jnp.concatenate([make(j) for j in range(count)], axis=0)

    def expert(e, unused):
        for copy in fetch(e):
            copy.wait()
        extra = extra_s[e]
        low_extra = extra.astype(BF)
        place = lax.broadcasted_iota(jnp.int32, extra.shape, 1) - (GATE_AT + 3 * e)
        gate = jnp.sum(jnp.where((place >= 0) & (place < 3), extra, 0.0), axis=1, keepdims=True)
        both = dot(x_s[e], wgu_s[e])
        gate_pre = both[:, :FF] + each(lambda j: dot(part(low_extra, j), gu_s[j, 0]))
        up_pre = both[:, FF:] + each(lambda j: dot(part(low_extra, j), gu_s[j, 1]))
        sigmoid = jax.nn.sigmoid(gate_pre)
        silu = gate_pre * sigmoid
        active = (silu * up_pre).astype(BF)
        down = [dot_nt(part(active, j), da_refs[j][0]).astype(BF) for j in range(count)]
        result = dot(active, wd_s[e]) + each(lambda j: dot(down[j], db_refs[j][0]))
        result = result.astype(BF).astype(F32)
        grad_in = g_s[e].astype(F32)
        d_gate_val = jnp.sum(grad_in * result, axis=1, keepdims=True)
        weighted = (gate * result).astype(BF)
        d_result = (gate * grad_in).astype(BF)
        d_down = [dot_nt(part(d_result, j), db_refs[j][0]).astype(BF) for j in range(count)]
        d_active = dot_nt(d_result, wd_s[e]) + each(lambda j: dot(d_down[j], da_refs[j][0]))
        d_gate = (d_active * up_pre * sigmoid * (1.0 + gate_pre * (1.0 - sigmoid))).astype(BF)
        d_up = (d_active * silu).astype(BF)
        d_rows = dot_nt(jnp.concatenate([d_gate, d_up], axis=1), wgu_s[e]).astype(BF)
        at = pl.ds(pl.multiple_of(e * CAP, CAP), CAP)
        for j in range(count):
            yrow_s[j, at, :] = part(weighted, j)
            drow_s[j, at, :D] = part(d_rows, j)
            d_extra = dot_nt(part(d_gate, j), gu_s[j, 0]) + dot_nt(part(d_up, j), gu_s[j, 1])
            d_extra = d_extra + jnp.where(narrow == base + e, part(d_gate_val, j), 0.0)
            drow_s[j, at, D:] = d_extra.astype(BF)
            ranks_in = part(low_extra, j)
            grad_s[j, 0:RANK, 0:FF] += dot_tn(ranks_in, part(d_gate, j))[0:RANK]
            grad_s[j, 0:RANK, FF : 2 * FF] += dot_tn(ranks_in, part(d_up, j))[RANK : 2 * RANK]
            grad_s[j, 0:RANK, 2 * FF :] += dot_tn(d_down[j], part(active, j))
            grad_s[j, RANK:, :] += dot_tn(down[j], part(d_result, j))
        return unused

    lax.fori_loop(0, E_DEV, expert, 0)
    for j in range(count):
        put = put_s[j]
        y_refs[j][...] = dot(put, yrow_s[j]).astype(BF)
        d_refs[j][:tokens, :] = dot(put, drow_s[j, :, :D]).astype(BF)
        d_refs[j][tokens : tokens + 2 * RANK, :] = grad_s[j].astype(BF)
        turned_ext = dot(put, drow_s[j, :, D:]).T.astype(BF)
        per = D // tokens
        for b in range(-(-(EXP_AT + experts_all) // TURN)):
            at = tokens + 2 * RANK + (b // per) * TURN
            lanes = slice((b % per) * tokens, (b % per + 1) * tokens)
            d_refs[j][at : at + TURN, lanes] = turned_ext[b * TURN : (b + 1) * TURN]


def experts(experts_all, info, first, rows, packs, w_gate_up, w_down, aux_w, gu_up, down_a, down_b):
    count = len(rows)
    tokens = rows[0].shape[0]
    whole = lambda arr: pl.BlockSpec(arr.shape, lambda e, ids: (0, 0))
    d_rows = tokens + 2 * RANK + turned_rows(EXP_AT + experts_all, tokens)

    def table(shape, j):
        at = first + j
        return pl.BlockSpec((1,) + shape, lambda e, ids: (ids[at],) + (0,) * len(shape))

    def body(ids_ref, *refs):
        refs = list(refs)
        take = lambda n: [refs.pop(0) for _ in range(n)]
        h_refs, p_refs = take(count), take(count)
        wgu_ref, wd_ref = take(2)
        tables = [take(count) for _ in range(4)]
        y_refs, d_refs = take(count), take(count)
        expert_kernel(experts_all, ids_ref, h_refs, p_refs, wgu_ref, wd_ref, tables, y_refs, d_refs, refs)

    picked = [(LANES, D), (2, RANK, FF), (RANK, FF), (RANK, D)]
    shapes = [(tokens, D)] * count + [(d_rows, D)] * count
    height = count * CAP
    outs = pl.pallas_call(
        body,
        grid_spec=pltpu.PrefetchScalarGridSpec(
            num_scalar_prefetch=1,
            grid=(1,),
            in_specs=[whole(arr) for arr in [*rows, *packs]]
            + [pl.BlockSpec(memory_space=pl.ANY)] * 2
            + [table(shape, j) for shape in picked for j in range(count)],
            out_specs=[pl.BlockSpec(shape, lambda e, ids: (0, 0)) for shape in shapes],
            scratch_shapes=[
                pltpu.VMEM((E_DEV, D, 2 * FF), BF),
                pltpu.VMEM((E_DEV, FF, D), BF),
                pltpu.VMEM((count, 2, LANES, FF), BF),
                pltpu.VMEM((count, tokens, E_DEV * CAP), BF),
                pltpu.VMEM((E_DEV, height, D), BF),
                pltpu.VMEM((E_DEV, height, D), BF),
                pltpu.VMEM((E_DEV, height, LANES), F32),
                pltpu.VMEM((count, E_DEV * CAP, D), BF),
                pltpu.VMEM((count, E_DEV * CAP, EXT), BF),
                pltpu.VMEM((count, 2 * RANK, D), F32),
                pltpu.SemaphoreType.DMA((2, E_DEV)),
            ],
        ),
        out_shape=[jax.ShapeDtypeStruct(shape, BF) for shape in shapes],
        cost_estimate=pl.CostEstimate(
            flops=16 * count * E_DEV * CAP * D * FF,
            bytes_accessed=2 * E_DEV * 3 * D * FF + 8 * count * tokens * D,
            transcendentals=0,
        ),
        name="experts",
    )(
        info,
        *rows,
        *packs,
        w_gate_up,
        w_down,
        *([aux_w] * count),
        *([gu_up] * count),
        *([down_a] * count),
        *([down_b] * count),
    )
    return list(outs[:count]), list(outs[count:])


def join_kernel(*refs):
    parts, (out_ref, sems) = refs[:-2], refs[-2:]
    for copy in start_copies(parts, out_ref, sems):
        copy.wait()


def join(parts):
    return pl.pallas_call(
        join_kernel,
        in_specs=[pl.BlockSpec(memory_space=pl.ANY)] * len(parts),
        out_specs=VMEM_SPEC,
        out_shape=jax.ShapeDtypeStruct((len(parts),) + parts[0].shape, parts[0].dtype),
        scratch_shapes=[pltpu.SemaphoreType.DMA((len(parts),))],
        name="join",
    )(*parts)


def order_rows_kernel(info_ref, *refs):
    parts, out_ref = refs[:-1], refs[-1]
    rows = parts[0].shape[0]
    for m, part in enumerate(parts):
        start = pl.multiple_of(info_ref[SLOTS_AT + m] * rows, rows)
        out_ref[pl.ds(start, rows), :] = part[:, LOCAL:]


def order_rows(order, parts):
    return pl.pallas_call(
        order_rows_kernel,
        in_specs=[SMEM_SPEC] + [VMEM_SPEC] * len(parts),
        out_specs=VMEM_SPEC,
        out_shape=jax.ShapeDtypeStruct((QW, QG), BF),
        name="order_rows",
    )(order, *parts)


def lanes_of(index):
    return pl.ds(pl.multiple_of(index * QG, LANES), QG)


def start_copies(sources, target, sems):
    copies = [
        pltpu.make_async_copy(source, target.at[j], sems.at[j]) for j, source in enumerate(sources)
    ]
    for copy in copies:
        copy.start()
    return copies


def out_kernel(info_ref, x_ref, gain_ref, down_ref, up_ref, *refs):
    o_refs, w_hbm = refs[:GROUPS], refs[GROUPS : 2 * GROUPS]
    att_ref, rank_ref, y_ref, h_ref, w_s, sems = refs[2 * GROUPS :]
    w_copies = start_copies(w_hbm, w_s, sems)
    group = info_ref[1]
    for j in range(GROUPS):
        att_ref[:, lanes_of(group ^ j)] = o_refs[j][...]
    attended = att_ref[...]
    for j in range(GROUPS):
        w_copies[j].wait()
        y_ref[:, lanes_of(group ^ j)] = dot(attended, w_s[j])
    rank_out = dot_nt(attended, down_ref[0]).astype(BF)
    rank_ref[...] = rank_out
    y_one = x_ref[...].astype(F32) + y_ref[...] + dot(rank_out, up_ref[0])
    y_ref[...] = y_one
    inverse = lax.rsqrt(jnp.mean(y_one * y_one, axis=1, keepdims=True) + NORM_EPS)
    h_ref[...] = (y_one * inverse * gain_ref[...]).astype(BF)


def project_out(info, rows, gain, down_t, up, outs, w_parts):
    tokens = rows.shape[0]
    return pl.pallas_call(
        out_kernel,
        grid_spec=pltpu.PrefetchScalarGridSpec(
            num_scalar_prefetch=1,
            grid=(1,),
            in_specs=[VMEM_SPEC] * 2
            + [by_adapter(down_t), by_adapter(up)]
            + [VMEM_SPEC] * GROUPS
            + [pl.BlockSpec(memory_space=pl.ANY)] * GROUPS,
            out_specs=[VMEM_SPEC] * 4,
            scratch_shapes=[
                pltpu.VMEM((GROUPS, QW, QG), BF),
                pltpu.SemaphoreType.DMA((GROUPS,)),
            ],
        ),
        out_shape=[
            jax.ShapeDtypeStruct((tokens, QW), BF),
            jax.ShapeDtypeStruct((tokens, RANK), BF),
            jax.ShapeDtypeStruct((tokens, D), F32),
            jax.ShapeDtypeStruct((tokens, D), BF),
        ],
        cost_estimate=pl.CostEstimate(
            flops=2 * tokens * QW * D, bytes_accessed=2 * QW * D + 12 * tokens * D, transcendentals=0
        ),
        name="project_out",
    )(info, rows, gain, down_t, up, *outs, *w_parts)


def middle_kernel(count, terms, experts_all, info_ref, *refs):
    refs = list(refs)
    take = lambda n: [refs.pop(0) for _ in range(n)]
    d_refs = take(terms)
    pack_ref, y_ref, h_ref, gain_ref, aux_ref, att_ref, rank_ref, down_ref, up_ref = take(9)
    w_hbm = take(GROUPS)
    (dy_ref,) = take(1)
    do_refs, early_refs = take(count), take(GROUPS)
    do_s, early_s, w_s, sems = refs
    w_refs = start_copies(w_hbm, w_s, sems)
    group, ctx_index, copies = info_ref[1], info_ref[2], count // GROUPS
    tokens = y_ref.shape[0]
    d_sum = d_refs[0][...].astype(F32)
    for ref in d_refs[1:]:
        d_sum = d_sum + ref[...].astype(F32)
    early_s[0 : 2 * RANK, :] = d_sum[tokens : tokens + 2 * RANK]
    d_ext = read_turned(d_sum[tokens + 2 * RANK :], EXP_AT + experts_all, tokens, 0).T
    h_two = h_ref[...]
    lane = lax.broadcasted_iota(jnp.int32, (tokens, LANES), 1)
    chosen = read_turned(pack_ref[tokens:, :].astype(F32), experts_all, tokens, EXP_AT).T > 0.0
    picked = jnp.where(chosen, dot_nt(h_two, aux_ref[0]), NEG)
    weights = jnp.exp(picked - jnp.max(picked, axis=1, keepdims=True))
    gates = weights / jnp.sum(weights, axis=1, keepdims=True)
    mixed = jnp.sum(jnp.where(chosen, gates * d_ext, 0.0), axis=1, keepdims=True)
    d_logits = jnp.where(chosen, gates * (d_ext - mixed), 0.0)
    d_ext = jnp.where(lane < EXP_AT, d_ext, d_logits).astype(BF)
    d_h = d_sum[:tokens] + dot(d_ext, aux_ref[0])
    y_one = y_ref[...]
    inverse = lax.rsqrt(jnp.mean(y_one * y_one, axis=1, keepdims=True) + NORM_EPS)
    scaled = gain_ref[...] * d_h
    d_y = pack_ref[:tokens, :].astype(F32) + inverse * scaled
    d_y = d_y - y_one * inverse**3 * jnp.mean(y_one * scaled, axis=1, keepdims=True)
    dy_ref[...] = d_y
    d_attn = d_y.astype(BF)
    d_rank = dot_nt(d_attn, up_ref[0]).astype(BF)
    do_s[...] = dot(d_rank, down_ref[0])
    for j in range(GROUPS):
        at = lanes_of(group ^ j)
        early_s[3 * RANK : 4 * RANK, at] = dot_tn(rank_ref[...], dy_ref[:, at].astype(BF))
        w_refs[j].wait()
        do_s[...] += dot_nt(dy_ref[:, at].astype(BF), w_s[j])
    for m in range(count):
        do_refs[m][...] = do_s[:, lanes_of((ctx_index ^ m) // copies)].astype(BF)
    early_s[2 * RANK : 3 * RANK, :] = dot_tn(d_rank, att_ref[...])
    early_s[4 * RANK :, :] = dot_tn(d_ext, h_two)[: 2 * RANK]
    for j in range(GROUPS):
        for i in range(6):
            block = early_s[i * RANK : (i + 1) * RANK, lanes_of(group ^ j)]
            early_refs[j][:, i * QG : (i + 1) * QG] = block.astype(BF)


def middle_back(info, count, experts_all, terms, pack, y_one, h_two, gain, aux, attended, rank_out, down_t, up, w_parts):
    tokens = y_one.shape[0]
    outs = pl.pallas_call(
        functools.partial(middle_kernel, count, len(terms), experts_all),
        grid_spec=pltpu.PrefetchScalarGridSpec(
            num_scalar_prefetch=1,
            grid=(1,),
            in_specs=[VMEM_SPEC] * (len(terms) + 4)
            + [by_adapter(aux)]
            + [VMEM_SPEC] * 2
            + [by_adapter(down_t), by_adapter(up)]
            + [pl.BlockSpec(memory_space=pl.ANY)] * GROUPS,
            out_specs=[VMEM_SPEC] * (1 + count + GROUPS),
            scratch_shapes=[
                pltpu.VMEM((tokens, QW), F32),
                pltpu.VMEM((6 * RANK, D), F32),
                pltpu.VMEM((GROUPS, QW, QG), BF),
                pltpu.SemaphoreType.DMA((GROUPS,)),
            ],
        ),
        out_shape=[jax.ShapeDtypeStruct((tokens, D), F32)]
        + [jax.ShapeDtypeStruct((tokens, QG), BF)] * count
        + [jax.ShapeDtypeStruct((RANK, 6 * QG), BF)] * GROUPS,
        cost_estimate=pl.CostEstimate(
            flops=2 * tokens * QW * D, bytes_accessed=2 * QW * D + 20 * tokens * D, transcendentals=0
        ),
        name="middle_back",
    )(info, *terms, pack, y_one, h_two, gain, aux, attended, rank_out, down_t, up, *w_parts)
    return outs[0], list(outs[1 : 1 + count]), list(outs[1 + count :])


def ranks_kernel(info_ref, dqkv_ref, up_ref, t_ref, h_ref, *refs):
    early_refs, (rank_ref, keep_ref, send_ref, h_s, sems) = refs[:GROUPS], refs[GROUPS:]
    (rows,) = start_copies([h_ref], h_s, sems)
    d_qkv = dqkv_ref[...]
    d_rank = dot_nt(d_qkv, up_ref[...]).astype(BF)
    rank_ref[...] = d_rank
    grad = dot_tn(t_ref[...], d_qkv)
    keep_ref[:, :QG] = grad[:RANK, :QG].astype(BF)
    keep_ref[:, QG : QG + KG] = grad[RANK : 2 * RANK, QG : QG + KG].astype(BF)
    keep_ref[:, QG + KG : LOCAL] = grad[2 * RANK :, QG + KG :].astype(BF)
    send_ref[:, :LOCAL] = jnp.zeros((RANK, LOCAL), BF)
    rows.wait()
    for j in range(GROUPS):
        target = send_ref if j % 2 else keep_ref
        down = dot_tn(d_rank, h_s[0, :, lanes_of(info_ref[1] ^ j)]).astype(BF)
        first = LOCAL + (j // 2) * 3 * QG
        for i in range(3):
            target[:, first + i * QG : first + (i + 1) * QG] = down[i * RANK : (i + 1) * RANK]
        first = LOCAL + 6 * QG + (j // 2) * 6 * QG
        target[:, first : first + 6 * QG] = early_refs[j][...]


HALF = LOCAL + 18 * QG
BOTH = HALF + LOCAL


def ranks_back(info, d_qkv, up_diag, rank_qkv, h_one, early):
    length = d_qkv.shape[0]
    return pl.pallas_call(
        ranks_kernel,
        in_specs=[SMEM_SPEC]
        + [VMEM_SPEC] * 3
        + [pl.BlockSpec(memory_space=pl.ANY)]
        + [VMEM_SPEC] * GROUPS,
        out_specs=[VMEM_SPEC] * 3,
        scratch_shapes=[pltpu.VMEM((1,) + h_one.shape, BF), pltpu.SemaphoreType.DMA((1,))],
        out_shape=[
            jax.ShapeDtypeStruct((length, 3 * RANK), BF),
            jax.ShapeDtypeStruct((RANK, HALF), BF),
            jax.ShapeDtypeStruct((RANK, HALF), BF),
        ],
        name="ranks_back",
    )(info, d_qkv, up_diag, rank_qkv, h_one, *early)


def mix_kernel(near_ref, far_ref, out_ref):
    out_ref[:, :LOCAL] = near_ref[:, :LOCAL]
    out_ref[:, LOCAL : 2 * LOCAL] = far_ref[:, :LOCAL]
    first = LOCAL
    for width in (3 * QG, 6 * QG):
        for mine, theirs in ((0, width), (width, 0)):
            total = near_ref[:, first + mine : first + mine + width].astype(F32)
            total = total + far_ref[:, first + theirs : first + theirs + width].astype(F32)
            at = LOCAL + first + mine
            out_ref[:, at : at + width] = total.astype(BF)
        first += 2 * width


def mix(near, far):
    return pl.pallas_call(
        mix_kernel,
        in_specs=[VMEM_SPEC] * 2,
        out_specs=VMEM_SPEC,
        out_shape=jax.ShapeDtypeStruct((RANK, BOTH), BF),
        name="mix",
    )(near, far)


def inputs_kernel(info_ref, dqkv_ref, rank_ref, w_ref, down_ref, *rows_refs):
    rows = dot_nt(dqkv_ref[...], w_ref[...]) + dot(rank_ref[...], down_ref[0])
    rows = rows.astype(BF)
    for m, ref in enumerate(rows_refs):

        @pl.when(pl.program_id(0) == m)
        def _():
            ref[...] = rows


def inputs_back(info, count, d_qkv, d_rank, cols_all, down_t):
    length = d_qkv.shape[0]
    tokens = length // count
    per_block = lambda width: pl.BlockSpec((tokens, width), lambda i, info: (i, 0))
    whole = lambda shape: pl.BlockSpec(shape, lambda i, info: (0, 0))
    return pl.pallas_call(
        inputs_kernel,
        grid_spec=pltpu.PrefetchScalarGridSpec(
            num_scalar_prefetch=1,
            grid=(count,),
            in_specs=[
                per_block(LOCAL),
                per_block(3 * RANK),
                whole((D, LOCAL)),
                by_adapter(down_t),
            ],
            out_specs=[whole((tokens, D))] * count,
        ),
        out_shape=[jax.ShapeDtypeStruct((tokens, D), BF)] * count,
        cost_estimate=pl.CostEstimate(
            flops=2 * length * D * LOCAL, bytes_accessed=4 * length * (D + LOCAL), transcendentals=0
        ),
        name="inputs_back",
    )(info, d_qkv, d_rank, cols_all, down_t)


def place_kernel(info_ref, *refs):
    up_ref, down_ref, gu_ref, da_ref, db_ref, od_ref, ou_ref, gd_ref, sum_s, parts, sems = refs[2:]
    sources = parts.shape[1]
    copies = start_copies(refs[:2], parts, sems)
    for ref in (up_ref, down_ref, db_ref, od_ref, ou_ref, gd_ref, sum_s):
        ref[...] = jnp.zeros(ref.shape, F32)
    for copy in copies:
        copy.wait()
    for j in range(GROUPS):
        group = info_ref[1] ^ j
        keys = lambda first: pl.ds(pl.multiple_of(first + group * KG, LANES), KG)
        far = j // 2
        down_at = 2 * LOCAL + far * 3 * QG
        early_at = 2 * LOCAL + 6 * QG + far * 6 * QG
        for m in range(sources):
            a = info_ref[SLOTS_AT + sources + m]
            take = lambda first, width: parts[j % 2, m, :, first : first + width].astype(F32)
            up_ref[a, :, lanes_of(group)] += take(far * LOCAL, QG)
            up_ref[a, :, keys(QW)] += take(far * LOCAL + QG, KG)
            up_ref[a, :, keys(QW + KVW)] += take(far * LOCAL + QG + KG, KG)
            for i in range(3):
                at = slice(i * RANK, (i + 1) * RANK)
                down_ref[a, at, lanes_of(group)] += take(down_at + i * QG, QG)
            for i, ref in enumerate((sum_s, db_ref, od_ref, ou_ref, gd_ref, gd_ref)):
                at = slice(RANK, 2 * RANK) if i == 5 else slice(0, RANK)
                ref[a, at, lanes_of(group)] += take(early_at + i * QG, QG)
    for a in range(ADAPT):
        gu_ref[a, 0] = sum_s[a, :, :FF]
        gu_ref[a, 1] = sum_s[a, :, FF : 2 * FF]
        da_ref[a] = sum_s[a, :, 2 * FF :]


def place_grads(info, near, far):
    shapes = [(RANK, QW + 2 * KVW), (3 * RANK, D), (2, RANK, FF), (RANK, FF), (RANK, D)]
    shapes += [(RANK, QW), (RANK, D), (2 * RANK, D)]
    return pl.pallas_call(
        place_kernel,
        in_specs=[SMEM_SPEC] + [pl.BlockSpec(memory_space=pl.ANY)] * 2,
        out_specs=[VMEM_SPEC] * len(shapes),
        out_shape=[jax.ShapeDtypeStruct((ADAPT,) + shape, F32) for shape in shapes],
        scratch_shapes=[
            pltpu.VMEM((ADAPT, RANK, D), F32),
            pltpu.VMEM((2,) + near.shape, BF),
            pltpu.SemaphoreType.DMA((2,)),
        ],
        name="place_grads",
    )(info, near, far)


def norm_backward(values, inverse, gain_vec, upstream):
    scaled = gain_vec * upstream
    return inverse * scaled - values * inverse**3 * jnp.mean(
        values * scaled, axis=-1, keepdims=True
    )


def local_columns(table, group):
    lead = table.shape[:-1]
    cut = lambda first, width: lax.dynamic_slice_in_dim(
        table, first + group * width, width, table.ndim - 1
    )
    return cut(0, QG), cut(QW, KG), cut(QW + KVW, KG)


def on_device(
    inputs,
    cotangent,
    segment_ids,
    expert_ids,
    adapter_ids,
    gain_one,
    w_qkv,
    w_out,
    gain_two,
    router,
    w_gate_up,
    w_down,
    qkv_down,
    qkv_up,
    out_down,
    out_up,
    gu_down,
    gu_up,
    down_a,
    down_b,
):
    ctx_count = lax.axis_size("ctx")
    seq_count = lax.axis_size("seq")
    ctx_index = lax.axis_index("ctx")
    seq_index = lax.axis_index("seq")
    tokens = inputs.shape[1]
    length = tokens * ctx_count
    experts_all = router.shape[1]
    copies = ctx_count // GROUPS
    group = ctx_index // copies
    half = tokens // 2
    ctx_masks = doublings(ctx_count)[::-1]
    seq_slots = (seq_index ^ jnp.arange(seq_count)).astype(jnp.int32)
    ctx_slots = ctx_index ^ jnp.arange(ctx_count)
    own_rows = inputs[0]

    moving_rows = [swap(own_rows, "ctx", mask) for mask in ctx_masks]
    own_q, own_k, own_v = local_columns(w_qkv, group)
    own_out = lax.dynamic_slice_in_dim(w_out, group * QG, QG, 1)
    col_slots = []
    cols = Steps(
        gather_line(
            jnp.concatenate([own_q, own_k, own_v, own_out], axis=1), col_slots
        )
    )
    chosen = expert_ids[0]
    hot = jnp.any(chosen[:, :, None] == jnp.arange(experts_all)[None, None, :], axis=1)
    hot_low = hot.astype(BF).T
    before = (jnp.arange(tokens)[:, None] <= jnp.arange(tokens)[None, :]).astype(BF)
    ranks = dot(hot_low, before).astype(BF) * hot_low
    per = D // tokens
    rank_rows = turned_rows(experts_all, tokens)
    ranks = jnp.pad(ranks, ((0, rank_rows * per - experts_all), (0, 0)))
    ranks = ranks.reshape(rank_rows // TURN, per, TURN, tokens)
    ranks = jnp.transpose(ranks, (0, 2, 1, 3)).reshape(rank_rows, D)
    pack = jnp.concatenate([cotangent[0], ranks], axis=0)
    cols.beside()
    seg_row = segment_ids[0]
    position = jnp.arange(length)
    start = jnp.sum((seg_row[None, :] < seg_row[:, None]).astype(jnp.int32), axis=1)
    block_id = jnp.stack([ctx_slots, 2 * ctx_count - 1 - ctx_slots], axis=1).reshape(-1)
    block_of = jnp.arange(2 * ctx_count)
    owner = jnp.minimum(block_of, 2 * ctx_count - 1 - block_of)
    place = (2 * (owner ^ ctx_index) + (block_of >= ctx_count)).astype(jnp.int32)
    first = (start[::BLK] // BLK).astype(jnp.int32)
    offset = (position - start).reshape(2 * ctx_count, half)[block_id].reshape(-1)
    lane = jnp.arange(LANES) % HEAD_DIM
    frequency = 10000.0 ** (-2.0 * (lane % (HEAD_DIM // 2)).astype(F32) / HEAD_DIM)
    angles = offset.astype(F32)[:, None] * frequency[None, :]
    cosine = jnp.cos(angles)
    sine = jnp.sin(angles) * jnp.where(lane < HEAD_DIM // 2, -1.0, 1.0)[None, :]
    start_row = start[None, :]
    adapter = adapter_ids[seq_index]
    slot_adapters = adapter_ids[seq_slots]
    info = jnp.concatenate(
        [jnp.stack([adapter, group, ctx_index, E_DEV * seq_index]), seq_slots, slot_adapters]
    ).astype(jnp.int32)

    def pick(table):
        return lax.dynamic_index_in_dim(table, adapter, 0, keepdims=False)

    qkv_down_sel = pick(qkv_down)
    out_down_t = jnp.swapaxes(out_down, 1, 2)
    aux_w = jnp.concatenate(
        [
            jnp.swapaxes(gu_down, 1, 2),
            jnp.broadcast_to(router.T[None], (ADAPT, experts_all, D)),
            jnp.zeros((ADAPT, LANES - 2 * RANK - experts_all, D), BF),
        ],
        axis=1,
    )
    down_a_t = jnp.swapaxes(down_a, 1, 2)

    pack, start_row, cosine, sine, place, first, info, *moving_rows = cols.beside(
        pack, start_row, cosine, sine, place, first, info, *moving_rows
    )
    row_slots = gather_rest(own_rows, moving_rows, ctx_masks)
    all_rows = jnp.concatenate(row_slots, axis=0).astype(F32)
    inv_all = lax.rsqrt(jnp.mean(all_rows * all_rows, axis=-1, keepdims=True) + NORM_EPS)
    h_one = (all_rows * inv_all * gain_one).astype(BF)
    rank_qkv = dot(h_one, qkv_down_sel).astype(BF)
    h_one, rank_qkv, pack = cols.beside(h_one, rank_qkv, pack)
    pack_slots = []
    packs = Steps(gather_line(pack, pack_slots))
    cols.finish()
    outs = Steps(gather_groups(order_rows(info, col_slots), copies))
    qkv, cols_all, up_diag = packs.beside(
        *project(info, h_one, rank_qkv, qkv_up, cosine, sine, col_slots)
    )
    heads_out, lse, *pieces = packs.beside(
        *outs.beside(*attend(place, first, qkv, start_row, copies))
    )
    heads_here = packs.beside(
        *[swap(piece, "ctx", j * copies) if j else piece for j, piece in enumerate(pieces)]
    )
    out_parts = outs.finish()
    attended, rank_out, y_one, h_two = project_out(
        info, own_rows, gain_two[None], out_down_t, out_up, heads_here, out_parts
    )

    def compute(m, rows):
        return experts(
            experts_all,
            info,
            SLOTS_AT + seq_count + m,
            rows,
            pack_slots[m : m + len(rows)],
            w_gate_up,
            w_down,
            aux_w,
            gu_up,
            down_a_t,
            down_b,
        )

    y_sums, d_terms = exchange_experts(h_two, packs, compute)

    d_y_one, d_heads, early = middle_back(
        info,
        ctx_count,
        experts_all,
        d_terms,
        pack,
        y_one,
        h_two,
        gain_two[None],
        aux_w,
        attended,
        rank_out,
        out_down_t,
        out_up,
        out_parts,
    )
    (d_y_one,) = y_sums.beside(d_y_one)
    d_heads = [swap(piece, "ctx", m) if m else piece for m, piece in enumerate(d_heads)]
    d_heads = y_sums.beside(*d_heads)

    (d_qkv,) = y_sums.beside(
        attend_back(place, first, qkv, start_row, heads_out, lse, cosine, sine, d_heads)
    )
    d_rank_qkv, keep, sent = ranks_back(info, d_qkv, up_diag, rank_qkv, h_one, early)

    halves = add_low(keep, swap(sent, "ctx", copies))
    for mask in doublings(copies):
        shared = halves[:, HALF - 12 * QG :]
        shared = add_low(shared, swap(shared, "ctx", mask))
        halves = jnp.concatenate([halves[:, : HALF - 12 * QG], shared], axis=1)
    halves, d_rank_qkv = lax.optimization_barrier((halves, d_rank_qkv))
    arrived, *d_rows = y_sums.beside(
        swap(halves, "ctx", 2 * copies),
        *inputs_back(info, ctx_count, d_qkv, d_rank_qkv, cols_all, jnp.swapaxes(qkv_down, 1, 2)),
    )
    d_rows = d_rows[::copies]
    near = add_low(d_rows[0], swap(d_rows[1], "ctx", copies))
    far = add_low(d_rows[2], swap(d_rows[3], "ctx", copies))
    slots = []
    grads = Steps(gather_line(mix(halves, arrived), slots))
    near, far = grads.beside(near, far)
    d_h_one = near.astype(F32) + swap(far, "ctx", 2 * copies).astype(F32)
    features = own_rows.astype(F32)
    inv_one = lax.rsqrt(jnp.mean(features * features, axis=-1, keepdims=True) + NORM_EPS)
    input_grad = d_y_one + norm_backward(features, inv_one, gain_one, d_h_one)
    layer_output = y_one
    for term in y_sums.finish():
        layer_output = layer_output + term.astype(F32)
    layer_output = layer_output.astype(BF)
    grads.beside()
    grads.beside()
    input_grad, layer_output = grads.beside(input_grad, layer_output)
    grads.finish()
    grads = join(slots)
    (
        grad_qkv_up,
        grad_qkv_down,
        grad_gu_up,
        grad_down_a,
        grad_down_b,
        grad_out_down,
        grad_out_up,
        grad_gu_down,
    ) = place_grads(info, grads, swap(grads, "ctx", copies))

    return (
        layer_output[None],
        input_grad[None],
        jnp.swapaxes(grad_qkv_down, 1, 2),
        grad_qkv_up,
        jnp.swapaxes(grad_out_down, 1, 2),
        grad_out_up,
        jnp.swapaxes(grad_gu_down, 1, 2),
        grad_gu_up,
        jnp.swapaxes(grad_down_a, 1, 2),
        grad_down_b,
    )


def solution(mesh):
    over_seq = P("seq", None)
    placed = (
        P("seq", "ctx", None),
        P("seq", "ctx", None),
        over_seq,
        P("seq", "ctx", None),
        P(),
        P(),
        over_seq,
        over_seq,
        P(),
        P(),
        P("seq", None, None),
        P("seq", None, None),
    ) + (P(),) * 8
    return jax.shard_map(
        on_device,
        mesh=mesh,
        in_specs=placed,
        out_specs=(P("seq", "ctx", None), P("seq", "ctx", None)) + (P(),) * 8,
        check_vma=False,
    )
```

```python
import functools

import jax
import jax.numpy as jnp
from jax import lax
from jax.experimental import pallas as pl
from jax.experimental.pallas import tpu as pltpu
from jax.sharding import PartitionSpec as P

D = 1536
HEADS = 24
KV_HEADS = 8
HEAD_DIM = 64
FF = 512
RANK = 16
ADAPT = 8
E_DEV = 2
CAP = 128
QW = 1536
KVW = 512
NORM_EPS = 1e-05

GROUPS = KV_HEADS // 2
PAIRS = HEADS // KV_HEADS
QG = QW // GROUPS
KG = KVW // GROUPS
LOCAL = QG + 2 * KG
BLK = 256
LANES = 128
EXP_AT = 2 * RANK
GATE_AT = 96
SLOTS_AT = 4
EXT = D + LANES
TURN = 8
NEG = -1e30

BF = jnp.bfloat16
F32 = jnp.float32
NT = (((1,), (1,)), ((), ()))
TN = (((0,), (0,)), ((), ()))


def turned_rows(columns, tokens):
    return TURN * -(-columns * tokens // (TURN * D))


def dot(left_arr, right_arr):
    return jnp.dot(left_arr, right_arr, preferred_element_type=F32)


def dot_nt(left_arr, right_arr):
    return lax.dot_general(left_arr, right_arr, NT, preferred_element_type=F32)


def dot_tn(left_arr, right_arr):
    return lax.dot_general(left_arr, right_arr, TN, preferred_element_type=F32)


def swap(block, axis, mask):
    count = lax.axis_size(axis)
    return lax.ppermute(block, axis, [(i, i ^ mask) for i in range(count)])


def gather_slots(block, axis, masks):
    slots = {0: block}
    for mask in masks:
        for have in list(slots):
            slots[have ^ mask] = swap(slots[have], axis, mask)
    return [slots[m] for m in sorted(slots)]


def together(*arrays):
    return lax.optimization_barrier(arrays)


def gather_rest(block, arrived, masks):
    slots = {0: block}
    for mask, first in zip(masks, arrived):
        for have in list(slots):
            slots[have ^ mask] = swap(slots[have], "ctx", mask) if have else first
    return [slots[m] for m in sorted(slots)]


def line_swap(block, pairs):
    return lax.ppermute(block, "seq", [(2 * i + j, 2 * k + j) for i, k in pairs for j in (0, 1)])


def outward(block):
    return line_swap(block, [(1, 0), (2, 3)])


def inward(block):
    return line_swap(block, [(0, 1), (3, 2)])


def middle(block):
    return line_swap(block, [(1, 2), (2, 1)])


class Steps:
    def __init__(self, work):
        self.work = work
        self.moving = self.result = None
        self.resume(None)

    def resume(self, arrived):
        try:
            self.moving = self.work.send(arrived)
        except StopIteration as end:
            self.moving, self.result = None, end.value

    def beside(self, *others):
        if self.moving is None:
            return others
        arrived, others = lax.optimization_barrier((tuple(self.moving), others))
        self.resume(arrived)
        return others

    def join(self, other, *others):
        if self.moving is None or other.moving is None:
            return self.beside(*other.beside(*others))
        mine, theirs, others = lax.optimization_barrier(
            (tuple(self.moving), tuple(other.moving), others)
        )
        self.resume(mine)
        other.resume(theirs)
        return others

    def finish(self):
        while self.moving is not None:
            self.beside()
        return self.result


def gather_line(block, slots):
    count = lax.axis_size("seq")
    if count != 8:
        slots += gather_slots(block, "seq", doublings(count))
        return slots
    slots.append(block)
    two, six, one = yield swap(block, "seq", 2), middle(block), swap(block, "seq", 1)
    slots += [one, two]
    four, far, three = yield middle(two), outward(six), swap(two, "seq", 1)
    four = four + far
    slots += [three, four]
    far, five = yield outward(four), swap(four, "seq", 1)
    six = six + far
    slots += [five, six]
    (seven,) = yield (swap(six, "seq", 1),)
    slots.append(seven)
    return slots


def gather_far(block, slots):
    count = lax.axis_size("seq")
    if count != 8:
        slots += gather_slots(block, "seq", doublings(count))
        return slots
    two, four, six, one = [swap(block, "seq", m) for m in (2, 4, 6, 1)]
    two, one = yield two, one
    four, three = yield four, swap(two, "seq", 1)
    six, five = yield six, swap(four, "seq", 1)
    (seven,) = yield (swap(six, "seq", 1),)
    slots += [block, one, two, three, four, five, six, seven]
    return slots


def gather_seq(block):
    return Steps(gather_line(block, [])).finish()


def reduce_line(parts, one=None):
    count = lax.axis_size("seq")
    if count != 8:
        return [reduce_slots(parts, "seq", doublings(count))]
    (seven,) = yield (swap(parts[7], "seq", 1),)
    six = add_low(parts[6], seven)
    near, five = yield inward(six), swap(parts[5], "seq", 1)
    four = add_low(parts[4], five, near)
    near, far, three = yield inward(four), middle(four), swap(parts[3], "seq", 1)
    six = add_low(six, near)
    two = add_low(parts[2], three, far)
    last = [swap(two, "seq", 2), middle(six)]
    if one is None:
        last.append(swap(parts[1], "seq", 1))
    last = yield last
    return [parts[0], *last] + ([] if one is None else [one])


def exchange_experts(block, packs, compute):
    count = lax.axis_size("seq")
    slots, y_parts, d_parts = [], [], []
    rows = Steps(gather_line(block, slots))

    def slots_of(m, some):
        some_y, some_d = compute(m, slots[m : m + some])
        return [*some_y, *some_d]

    def keep(done, some):
        y_parts.extend(done[:some])
        d_parts.extend(done[some:])

    if count != 8:
        packs.finish()
        for m in range(0, count, 2):
            keep(slots_of(m, 2), 2)
        return Steps(reduce_line(y_parts)), Steps(reduce_line(d_parts)).finish()
    keep(rows.join(packs, *slots_of(0, 1)), 1)
    for m in (1, 3, 5):
        keep(rows.beside(*slots_of(m, 2)), 2)
    one = swap(d_parts[1], "seq", 1)
    *done, one = lax.optimization_barrier((*slots_of(7, 1), one))
    keep(done, 1)
    terms = Steps(reduce_line(d_parts, one))
    terms.beside()
    terms.beside()
    y_sums = Steps(reduce_line(list(terms.beside(*y_parts))))
    return y_sums, terms.finish()


def doublings(count):
    return [1 << bit for bit in range(count.bit_length() - 1)]


def add_low(*terms):
    total = terms[0].astype(F32)
    for term in terms[1:]:
        total = total + term.astype(F32)
    return lax.optimization_barrier(total.astype(BF))


def gather_groups(block, copies):
    two, one = yield swap(block, "ctx", 2 * copies), swap(block, "ctx", copies)
    return [block, one, two, swap(two, "ctx", copies)]


def reduce_slots(parts, axis, masks):
    parts = dict(enumerate(parts))
    for step, mask in enumerate(masks):
        last = step == len(masks) - 1
        for m in [m for m in parts if m & mask]:
            arrived = swap(parts.pop(m), axis, mask)
            mine = parts[m ^ mask]
            parts[m ^ mask] = (
                mine.astype(F32) + arrived.astype(F32) if last else add_low(mine, arrived)
            )
    return parts[0]


def rotate(values, cosine, sine, sign):
    lane = lax.broadcasted_iota(jnp.int32, values.shape, 1)
    ahead = pltpu.roll(values, LANES - HEAD_DIM // 2, 1)
    behind = pltpu.roll(values, HEAD_DIM // 2, 1)
    other = jnp.where(lane % HEAD_DIM < HEAD_DIM // 2, ahead, behind)
    return values * cosine + (sign * other) * sine


def by_adapter(table):
    return pl.BlockSpec((1,) + table.shape[1:], lambda i, info: (info[0], 0, 0))


def project_kernel(info_ref, h_ref, t_ref, table_ref, cos_ref, sin_ref, *rest):
    shards = rest[:-3]
    qkv_ref, w_ref, up_ref = rest[-3:]
    rows = shards[0].shape[0]
    group = info_ref[1]

    @pl.when(pl.program_id(0) == 0)
    def _():
        for m, shard in enumerate(shards):
            start = pl.multiple_of(info_ref[SLOTS_AT + m] * rows, rows)
            w_ref[pl.ds(start, rows), :] = shard[:, :LOCAL]
        up_ref[...] = jnp.zeros(up_ref.shape, BF)
        columns = lambda first, width: table_ref[
            0, :, pl.ds(pl.multiple_of(first + group * width, LANES), width)
        ]
        up_ref[:RANK, :QG] = columns(0, QG)
        up_ref[RANK : 2 * RANK, QG : QG + KG] = columns(QW, KG)
        up_ref[2 * RANK :, QG + KG :] = columns(QW + KVW, KG)

    pre = dot(h_ref[...], w_ref[...]) + dot(t_ref[...], up_ref[...])
    cosine, sine = cos_ref[...], sin_ref[...]
    tiles = [rotate(tile, cosine, sine, 1.0) * 0.125 for tile in lane_tiles(pre)]
    tiles = paired_heads(tiles)
    tiles.append(rotate(pre[:, QG : QG + KG], cosine, sine, 1.0))
    tiles.append(pre[:, QG + KG :])
    for j, tile in enumerate(tiles):
        qkv_ref[:, j * LANES : (j + 1) * LANES] = tile.astype(BF)


def project(info, h_one, rank_qkv, table, cosine, sine, shards):
    length = h_one.shape[0]
    rows = shards[0].shape[0]
    count = len(shards)
    per_block = lambda width: pl.BlockSpec((BLK, width), lambda i, info: (i, 0))
    whole = lambda shape: pl.BlockSpec(shape, lambda i, info: (0, 0))
    return pl.pallas_call(
        project_kernel,
        grid_spec=pltpu.PrefetchScalarGridSpec(
            num_scalar_prefetch=1,
            grid=(length // BLK,),
            in_specs=[
                per_block(D),
                per_block(3 * RANK),
                by_adapter(table),
                per_block(LANES),
                per_block(LANES),
            ]
            + [whole((rows, LOCAL + QG))] * count,
            out_specs=[per_block(LOCAL), whole((D, LOCAL)), whole((3 * RANK, LOCAL))],
        ),
        out_shape=[
            jax.ShapeDtypeStruct((length, LOCAL), BF),
            jax.ShapeDtypeStruct((D, LOCAL), BF),
            jax.ShapeDtypeStruct((3 * RANK, LOCAL), BF),
        ],
        cost_estimate=pl.CostEstimate(
            flops=2 * length * D * LOCAL, bytes_accessed=2 * length * (D + LOCAL), transcendentals=0
        ),
        name="project",
    )(info, h_one, rank_qkv, table, cosine, sine, *shards)


def half_mask(shape, half):
    lane = lax.broadcasted_iota(jnp.int32, shape, 1)
    return (lane < HEAD_DIM) if half == 0 else (lane >= HEAD_DIM)


def turned(tile):
    return pltpu.roll(tile.astype(F32), HEAD_DIM, 1).astype(tile.dtype)


def paired_heads(tiles):
    is_low = half_mask(tiles[0].shape, 0)
    return [
        jnp.where(is_low, tiles[0], tiles[1]),
        jnp.where(is_low, turned(tiles[0]), turned(tiles[2])),
        jnp.where(is_low, tiles[1], tiles[2]),
    ]


def natural_heads(tiles):
    is_low = half_mask(tiles[0].shape, 0)
    return [
        jnp.where(is_low, tiles[0], turned(tiles[1])),
        jnp.where(is_low, tiles[2], tiles[0]),
        jnp.where(is_low, turned(tiles[1]), tiles[2]),
    ]


def lane_tiles(block):
    return [block[:, i * LANES : (i + 1) * LANES] for i in range(PAIRS)]


def stack_rows(place_ref, source_ref, target_ref, paired):
    half = BLK // 2
    for b in range(source_ref.shape[0] // half):
        rows = pl.ds(pl.multiple_of(place_ref[b] * half, half), half)
        tiles = lane_tiles(source_ref[rows, :QG])
        for pair, tile in enumerate(tiles if paired else paired_heads(tiles)):
            at = (b // 2) * PAIRS * BLK + pair * BLK + (b % 2) * half
            target_ref[at : at + half, :] = tile


def read_turned(block, columns, tokens, first):
    per = D // tokens
    parts = []
    for b in range(columns // TURN):
        at = slice((b // per) * TURN, (b // per + 1) * TURN)
        parts.append(block[at, (b % per) * tokens : (b % per + 1) * tokens])
    before = [jnp.zeros((first, tokens), F32)] if first else []
    after = [jnp.zeros((LANES - first - columns, tokens), F32)]
    return jnp.concatenate(before + parts + after, axis=0)


def split_keys(place_ref, qkv_ref, first_lane, target_ref, ones):
    half = BLK // 2
    for b in range(qkv_ref.shape[0] // half):
        rows = pl.ds(pl.multiple_of(place_ref[b] * half, half), half)
        both = qkv_ref[rows, first_lane : first_lane + LANES]
        for side in range(2):
            other = jnp.zeros_like(both)
            if ones:
                lane = lax.broadcasted_iota(jnp.int32, both.shape, 1)
                spare = HEAD_DIM if side == 0 else 0
                other = jnp.where(lane == spare, 1.0, 0.0).astype(BF)
            target_ref[side, b * half : (b + 1) * half, :] = jnp.where(
                half_mask(both.shape, side), both, other
            )


def as_column(row):
    return jnp.broadcast_to(row.astype(F32), (TURN, row.shape[1])).T[:, :1].astype(jnp.int32)


def tile_bias(start_col, q_first, k_first):
    shape = (BLK, BLK)
    key = k_first + lax.broadcasted_iota(jnp.int32, shape, 1)
    query = q_first + lax.broadcasted_iota(jnp.int32, shape, 0)
    bias = jnp.where((key >= start_col) & (key <= query), 0.0, NEG)
    return jnp.concatenate([bias] * PAIRS, axis=0)


def attend_kernel(copies, place_ref, first_ref, qkv_ref, start_ref, o_ref, lse_ref, *refs):
    piece_refs, (q_s, k_s, v_s, score_s, m_s, acc_s) = refs[:GROUPS], refs[GROUPS:]
    stack_rows(place_ref, qkv_ref, q_s, True)
    split_keys(place_ref, qkv_ref, QG, k_s, False)
    split_keys(place_ref, qkv_ref, QG + KG, v_s, True)
    half = BLK // 2
    tall = PAIRS * BLK

    def query_block(qb, unused):
        q_first = pl.multiple_of(qb * BLK, BLK)
        q_rows = pl.ds(pl.multiple_of(qb * tall, tall), tall)
        start_col = as_column(start_ref[:, pl.ds(q_first, BLK)])
        queries = q_s[q_rows, :]
        m_s[...] = jnp.full(m_s.shape, NEG, F32)
        acc_s[...] = jnp.zeros(acc_s.shape, F32)

        def score_block(kb, unused):
            k_first = pl.multiple_of(kb * BLK, BLK)
            bias = tile_bias(start_col, q_first, k_first)
            for side in range(2):
                scores = dot_nt(queries, k_s[side, pl.ds(k_first, BLK), :]) + bias
                score_s[kb, side] = scores
                m_s[side] = jnp.maximum(
                    m_s[side], jnp.maximum(scores[:, :LANES], scores[:, LANES:])
                )
            return unused

        lax.fori_loop(first_ref[qb], qb + 1, score_block, 0)
        peaks = [jnp.max(m_s[side], axis=1, keepdims=True) for side in range(2)]

        def value_block(kb, unused):
            k_first = pl.multiple_of(kb * BLK, BLK)
            for side in range(2):
                prob = jnp.exp(score_s[kb, side] - peaks[side]).astype(BF)
                acc_s[side] += dot(prob, v_s[side, pl.ds(k_first, BLK), :])
            return unused

        lax.fori_loop(first_ref[qb], qb + 1, value_block, 0)
        low, high = acc_s[0], acc_s[1]
        low_sum = low[:, HEAD_DIM : HEAD_DIM + 1]
        high_sum = high[:, 0:1]
        is_low = half_mask(low.shape, 0)
        out = jnp.where(is_low, low / low_sum, high / high_sum).astype(BF)
        lse_ref[q_rows, :] = jnp.where(
            is_low, peaks[0] + jnp.log(low_sum), peaks[1] + jnp.log(high_sum)
        )
        for i in range(2):
            rows = pl.ds(pl.multiple_of(place_ref[2 * qb + i] * half, half), half)
            tiles = [out[pair * BLK + i * half :][:half] for pair in range(PAIRS)]
            for pair, tile in enumerate(natural_heads(tiles)):
                o_ref[rows, pair * LANES : (pair + 1) * LANES] = tile
        return unused

    lax.fori_loop(0, qkv_ref.shape[0] // BLK, query_block, 0)
    for j, piece in enumerate(piece_refs):
        tokens = piece.shape[0]
        piece[...] = o_ref[j * copies * tokens : (j * copies + 1) * tokens, :]


SMEM_SPEC = pl.BlockSpec(memory_space=pltpu.SMEM)
VMEM_SPEC = pl.BlockSpec(memory_space=pltpu.VMEM)


def attend(place, first, qkv, start_row, copies):
    length = qkv.shape[0]
    tall = PAIRS * BLK
    return pl.pallas_call(
        functools.partial(attend_kernel, copies),
        in_specs=[SMEM_SPEC, SMEM_SPEC, VMEM_SPEC, VMEM_SPEC],
        out_specs=[VMEM_SPEC] * (2 + GROUPS),
        out_shape=[
            jax.ShapeDtypeStruct((length, QG), BF),
            jax.ShapeDtypeStruct((PAIRS * length, LANES), F32),
        ]
        + [jax.ShapeDtypeStruct((length // (GROUPS * copies), QG), BF)] * GROUPS,
        scratch_shapes=[
            pltpu.VMEM((PAIRS * length, LANES), BF),
            pltpu.VMEM((2, length, LANES), BF),
            pltpu.VMEM((2, length, LANES), BF),
            pltpu.VMEM((length // BLK, 2, tall, BLK), F32),
            pltpu.VMEM((2, tall, LANES), F32),
            pltpu.VMEM((2, tall, LANES), F32),
        ],
        cost_estimate=pl.CostEstimate(
            flops=4 * length * length * QG, bytes_accessed=8 * length * QG, transcendentals=0
        ),
        name="attend",
    )(place, first, qkv, start_row)


def attend_back_kernel(
    place_ref,
    first_ref,
    qkv_ref,
    start_ref,
    o_ref,
    lse_ref,
    cos_ref,
    sin_ref,
    *refs,
):
    do_refs = refs[:-10]
    dqkv_ref, join_s, q_s, o_s, do_s, k_s, v_s, dk_s, dv_s, dq_s = refs[-10:]
    for m, piece in enumerate(do_refs):
        join_s[m * piece.shape[0] : (m + 1) * piece.shape[0], :] = piece[...]
    stack_rows(place_ref, qkv_ref, q_s, True)
    stack_rows(place_ref, o_ref, o_s, False)
    stack_rows(place_ref, join_s, do_s, False)
    split_keys(place_ref, qkv_ref, QG, k_s, False)
    split_keys(place_ref, qkv_ref, QG + KG, v_s, False)
    dk_s[...] = jnp.zeros(dk_s.shape, F32)
    dv_s[...] = jnp.zeros(dv_s.shape, F32)
    half = BLK // 2
    tall = PAIRS * BLK

    def query_block(qb, unused):
        q_first = pl.multiple_of(qb * BLK, BLK)
        q_rows = pl.ds(pl.multiple_of(qb * tall, tall), tall)
        start_col = as_column(start_ref[:, pl.ds(q_first, BLK)])
        dq_s[...] = jnp.zeros(dq_s.shape, F32)
        product = do_s[q_rows, :].astype(F32) * o_s[q_rows, :].astype(F32)
        lse = lse_ref[q_rows, :]
        lse_of = (lse[:, 0:1], lse[:, HEAD_DIM : HEAD_DIM + 1])
        delta_of = [
            jnp.sum(jnp.where(half_mask(product.shape, side), product, 0.0), axis=1, keepdims=True)
            for side in range(2)
        ]

        def key_block(kb, unused):
            k_first = pl.multiple_of(kb * BLK, BLK)
            k_rows = pl.ds(k_first, BLK)
            bias = tile_bias(start_col, q_first, k_first)
            queries = q_s[q_rows, :]
            d_out = do_s[q_rows, :]
            for side in range(2):
                keys = k_s[side, k_rows, :]
                scores = dot_nt(queries, keys) + bias
                prob = jnp.exp(scores - lse_of[side])
                d_prob = dot_nt(d_out, v_s[side, k_rows, :])
                d_score = (prob * (d_prob - delta_of[side])).astype(BF)
                dv_s[side, k_rows, :] += dot_tn(prob.astype(BF), d_out)
                dk_s[side, k_rows, :] += dot_tn(d_score, queries)
                dq_s[...] += dot(d_score, keys)
            return unused

        lax.fori_loop(first_ref[qb], qb + 1, key_block, 0)
        for i in range(2):
            rows = pl.ds(pl.multiple_of(place_ref[2 * qb + i] * half, half), half)
            cosine, sine = cos_ref[rows, :], sin_ref[rows, :]
            tiles = []
            for pair in range(PAIRS):
                at = pair * BLK + i * half
                tiles.append(rotate(dq_s[at : at + half, :] * 0.125, cosine, sine, -1.0))
            for pair, tile in enumerate(natural_heads(tiles)):
                dqkv_ref[rows, pair * LANES : (pair + 1) * LANES] = tile.astype(BF)
        return unused

    lax.fori_loop(0, qkv_ref.shape[0] // BLK, query_block, 0)
    for b in range(qkv_ref.shape[0] // half):
        rows = pl.ds(pl.multiple_of(place_ref[b] * half, half), half)
        at = slice(b * half, (b + 1) * half)
        is_low = half_mask((half, LANES), 0)
        back = jnp.where(is_low, dk_s[0, at, :], dk_s[1, at, :])
        back = rotate(back, cos_ref[rows, :], sin_ref[rows, :], -1.0)
        dqkv_ref[rows, QG : QG + KG] = back.astype(BF)
        dqkv_ref[rows, QG + KG : LOCAL] = jnp.where(is_low, dv_s[0, at, :], dv_s[1, at, :]).astype(BF)


def attend_back(place, first, qkv, start_row, out, lse, cosine, sine, d_out):
    length = qkv.shape[0]
    tall = PAIRS * BLK
    stacked = pltpu.VMEM((PAIRS * length, LANES), BF)
    return pl.pallas_call(
        attend_back_kernel,
        in_specs=[SMEM_SPEC, SMEM_SPEC] + [VMEM_SPEC] * (6 + len(d_out)),
        out_specs=VMEM_SPEC,
        out_shape=jax.ShapeDtypeStruct((length, LOCAL), BF),
        scratch_shapes=[
            pltpu.VMEM((length, QG), BF),
            stacked,
            stacked,
            stacked,
            pltpu.VMEM((2, length, LANES), BF),
            pltpu.VMEM((2, length, LANES), BF),
            pltpu.VMEM((2, length, LANES), F32),
            pltpu.VMEM((2, length, LANES), F32),
            pltpu.VMEM((tall, LANES), F32),
        ],
        cost_estimate=pl.CostEstimate(
            flops=10 * length * length * QG, bytes_accessed=16 * length * QG, transcendentals=0
        ),
        name="attend_back",
    )(place, first, qkv, start_row, out, lse, cosine, sine, *d_out)


def expert_kernel(experts_all, ids_ref, h_refs, p_refs, wgu_ref, wd_ref, tables, y_refs, d_refs, scratch):
    aux_w, gu_refs, da_refs, db_refs = tables
    wgu_s, wd_s, gu_s, put_s, x_s, g_s, extra_s, yrow_s, drow_s, grad_s, sems = scratch
    count = len(h_refs)
    tokens = h_refs[0].shape[0]

    def fetch(e):
        return [
            pltpu.make_async_copy(wgu_ref.at[e], wgu_s.at[e], sems.at[0, e]),
            pltpu.make_async_copy(wd_ref.at[e], wd_s.at[e], sems.at[1, e]),
        ]

    for e in range(E_DEV):
        for copy in fetch(e):
            copy.start()
    wide = lax.broadcasted_iota(jnp.int32, (tokens, LANES), 1)
    narrow = lax.broadcasted_iota(jnp.int32, (CAP, LANES), 1)
    base = EXP_AT + ids_ref[3]
    grad_s[...] = jnp.zeros(grad_s.shape, F32)
    gu_s[...] = jnp.zeros(gu_s.shape, BF)
    part = lambda arr, j: arr[j * CAP : (j + 1) * CAP]
    for j in range(count):
        gu_s[j, 0, 0:RANK, :] = gu_refs[j][0, 0]
        gu_s[j, 1, RANK : 2 * RANK, :] = gu_refs[j][0, 1]
        both = dot_nt(h_refs[j][...], aux_w[j][0])
        tall = read_turned(p_refs[j][tokens:, :].astype(F32), experts_all, tokens, EXP_AT)
        ranks = tall.T
        chosen = ranks > 0.0
        picked = jnp.where(chosen, both, NEG)
        weights = jnp.exp(picked - jnp.max(picked, axis=1, keepdims=True))
        gates = weights / jnp.sum(weights, axis=1, keepdims=True)
        aux = jnp.where(wide < EXP_AT, both, 0.0)
        which = lax.broadcasted_iota(jnp.int32, tall.shape, 0)
        slot = lax.broadcasted_iota(jnp.int32, (CAP, tokens), 0).astype(F32) + 1.0
        takes = []
        for e in range(E_DEV):
            column = jnp.sum(jnp.where(wide == base + e, ranks, 0.0), axis=1, keepdims=True)
            row = jnp.sum(jnp.where(which == base + e, tall, 0.0), axis=0, keepdims=True)
            takes.append(jnp.where(slot == row, 1.0, 0.0).astype(BF))
            put_s[j, :, e * CAP : (e + 1) * CAP] = jnp.where(
                wide.astype(F32) + 1.0 == column, 1.0, 0.0
            ).astype(BF)
            gate = jnp.sum(jnp.where(wide == base + e, gates, 0.0), axis=1, keepdims=True)
            gate_one = gate.astype(BF).astype(F32)
            gate_two = (gate - gate_one).astype(BF).astype(F32)
            first = GATE_AT + 3 * e
            aux = jnp.where(wide == first, gate_one, aux)
            aux = jnp.where(wide == first + 1, gate_two, aux)
            aux = jnp.where(wide == first + 2, gate - gate_one - gate_two, aux)
        take = jnp.concatenate(takes, axis=0)
        at = slice(j * CAP, (j + 1) * CAP)
        rows = dot(take, h_refs[j][...]).astype(BF)
        upstream = dot(take, p_refs[j][:tokens, :]).astype(BF)
        extra = dot(take, aux.astype(BF))
        for e in range(E_DEV):
            x_s[e, at, :] = part(rows, e)
            g_s[e, at, :] = part(upstream, e)
            extra_s[e, at, :] = part(extra, e)

    def each(make):
        return jnp.concatenate([make(j) for j in range(count)], axis=0)

    def expert(e, unused):
        for copy in fetch(e):
            copy.wait()
        extra = extra_s[e]
        low_extra = extra.astype(BF)
        place = lax.broadcasted_iota(jnp.int32, extra.shape, 1) - (GATE_AT + 3 * e)
        gate = jnp.sum(jnp.where((place >= 0) & (place < 3), extra, 0.0), axis=1, keepdims=True)
        both = dot(x_s[e], wgu_s[e])
        gate_pre = both[:, :FF] + each(lambda j: dot(part(low_extra, j), gu_s[j, 0]))
        up_pre = both[:, FF:] + each(lambda j: dot(part(low_extra, j), gu_s[j, 1]))
        sigmoid = jax.nn.sigmoid(gate_pre)
        silu = gate_pre * sigmoid
        active = (silu * up_pre).astype(BF)
        down = [dot_nt(part(active, j), da_refs[j][0]).astype(BF) for j in range(count)]
        result = dot(active, wd_s[e]) + each(lambda j: dot(down[j], db_refs[j][0]))
        result = result.astype(BF).astype(F32)
        grad_in = g_s[e].astype(F32)
        d_gate_val = jnp.sum(grad_in * result, axis=1, keepdims=True)
        weighted = (gate * result).astype(BF)
        d_result = (gate * grad_in).astype(BF)
        d_down = [dot_nt(part(d_result, j), db_refs[j][0]).astype(BF) for j in range(count)]
        d_active = dot_nt(d_result, wd_s[e]) + each(lambda j: dot(d_down[j], da_refs[j][0]))
        d_gate = (d_active * up_pre * sigmoid * (1.0 + gate_pre * (1.0 - sigmoid))).astype(BF)
        d_up = (d_active * silu).astype(BF)
        d_rows = dot_nt(jnp.concatenate([d_gate, d_up], axis=1), wgu_s[e]).astype(BF)
        at = pl.ds(pl.multiple_of(e * CAP, CAP), CAP)
        for j in range(count):
            yrow_s[j, at, :] = part(weighted, j)
            drow_s[j, at, :D] = part(d_rows, j)
            d_extra = dot_nt(part(d_gate, j), gu_s[j, 0]) + dot_nt(part(d_up, j), gu_s[j, 1])
            d_extra = d_extra + jnp.where(narrow == base + e, part(d_gate_val, j), 0.0)
            drow_s[j, at, D:] = d_extra.astype(BF)
            ranks_in = part(low_extra, j)
            grad_s[j, 0:RANK, 0:FF] += dot_tn(ranks_in, part(d_gate, j))[0:RANK]
            grad_s[j, 0:RANK, FF : 2 * FF] += dot_tn(ranks_in, part(d_up, j))[RANK : 2 * RANK]
            grad_s[j, 0:RANK, 2 * FF :] += dot_tn(d_down[j], part(active, j))
            grad_s[j, RANK:, :] += dot_tn(down[j], part(d_result, j))
        return unused

    lax.fori_loop(0, E_DEV, expert, 0)
    for j in range(count):
        put = put_s[j]
        y_refs[j][...] = dot(put, yrow_s[j]).astype(BF)
        d_refs[j][:tokens, :] = dot(put, drow_s[j, :, :D]).astype(BF)
        d_refs[j][tokens : tokens + 2 * RANK, :] = grad_s[j].astype(BF)
        turned_ext = dot(put, drow_s[j, :, D:]).T.astype(BF)
        per = D // tokens
        for b in range(-(-(EXP_AT + experts_all) // TURN)):
            at = tokens + 2 * RANK + (b // per) * TURN
            lanes = slice((b % per) * tokens, (b % per + 1) * tokens)
            d_refs[j][at : at + TURN, lanes] = turned_ext[b * TURN : (b + 1) * TURN]


def experts(experts_all, info, first, rows, packs, w_gate_up, w_down, aux_w, gu_up, down_a, down_b):
    count = len(rows)
    tokens = rows[0].shape[0]
    whole = lambda arr: pl.BlockSpec(arr.shape, lambda e, ids: (0, 0))
    d_rows = tokens + 2 * RANK + turned_rows(EXP_AT + experts_all, tokens)

    def table(shape, j):
        at = first + j
        return pl.BlockSpec((1,) + shape, lambda e, ids: (ids[at],) + (0,) * len(shape))

    def body(ids_ref, *refs):
        refs = list(refs)
        take = lambda n: [refs.pop(0) for _ in range(n)]
        h_refs, p_refs = take(count), take(count)
        wgu_ref, wd_ref = take(2)
        tables = [take(count) for _ in range(4)]
        y_refs, d_refs = take(count), take(count)
        expert_kernel(experts_all, ids_ref, h_refs, p_refs, wgu_ref, wd_ref, tables, y_refs, d_refs, refs)

    picked = [(LANES, D), (2, RANK, FF), (RANK, FF), (RANK, D)]
    shapes = [(tokens, D)] * count + [(d_rows, D)] * count
    height = count * CAP
    outs = pl.pallas_call(
        body,
        grid_spec=pltpu.PrefetchScalarGridSpec(
            num_scalar_prefetch=1,
            grid=(1,),
            in_specs=[whole(arr) for arr in [*rows, *packs]]
            + [pl.BlockSpec(memory_space=pl.ANY)] * 2
            + [table(shape, j) for shape in picked for j in range(count)],
            out_specs=[pl.BlockSpec(shape, lambda e, ids: (0, 0)) for shape in shapes],
            scratch_shapes=[
                pltpu.VMEM((E_DEV, D, 2 * FF), BF),
                pltpu.VMEM((E_DEV, FF, D), BF),
                pltpu.VMEM((count, 2, LANES, FF), BF),
                pltpu.VMEM((count, tokens, E_DEV * CAP), BF),
                pltpu.VMEM((E_DEV, height, D), BF),
                pltpu.VMEM((E_DEV, height, D), BF),
                pltpu.VMEM((E_DEV, height, LANES), F32),
                pltpu.VMEM((count, E_DEV * CAP, D), BF),
                pltpu.VMEM((count, E_DEV * CAP, EXT), BF),
                pltpu.VMEM((count, 2 * RANK, D), F32),
                pltpu.SemaphoreType.DMA((2, E_DEV)),
            ],
        ),
        out_shape=[jax.ShapeDtypeStruct(shape, BF) for shape in shapes],
        cost_estimate=pl.CostEstimate(
            flops=16 * count * E_DEV * CAP * D * FF,
            bytes_accessed=2 * E_DEV * 3 * D * FF + 8 * count * tokens * D,
            transcendentals=0,
        ),
        name="experts",
    )(
        info,
        *rows,
        *packs,
        w_gate_up,
        w_down,
        *([aux_w] * count),
        *([gu_up] * count),
        *([down_a] * count),
        *([down_b] * count),
    )
    return list(outs[:count]), list(outs[count:])


def join_kernel(*refs):
    parts, (out_ref, sems) = refs[:-2], refs[-2:]
    for copy in start_copies(parts, out_ref, sems):
        copy.wait()


def join(parts):
    return pl.pallas_call(
        join_kernel,
        in_specs=[pl.BlockSpec(memory_space=pl.ANY)] * len(parts),
        out_specs=VMEM_SPEC,
        out_shape=jax.ShapeDtypeStruct((len(parts),) + parts[0].shape, parts[0].dtype),
        scratch_shapes=[pltpu.SemaphoreType.DMA((len(parts),))],
        name="join",
    )(*parts)


def order_rows_kernel(info_ref, *refs):
    parts, out_ref = refs[:-1], refs[-1]
    rows = parts[0].shape[0]
    for m, part in enumerate(parts):
        start = pl.multiple_of(info_ref[SLOTS_AT + m] * rows, rows)
        out_ref[pl.ds(start, rows), :] = part[:, LOCAL:]


def order_rows(order, parts):
    return pl.pallas_call(
        order_rows_kernel,
        in_specs=[SMEM_SPEC] + [VMEM_SPEC] * len(parts),
        out_specs=VMEM_SPEC,
        out_shape=jax.ShapeDtypeStruct((QW, QG), BF),
        name="order_rows",
    )(order, *parts)


def lanes_of(index):
    return pl.ds(pl.multiple_of(index * QG, LANES), QG)


def start_copies(sources, target, sems):
    copies = [
        pltpu.make_async_copy(source, target.at[j], sems.at[j]) for j, source in enumerate(sources)
    ]
    for copy in copies:
        copy.start()
    return copies


def out_kernel(info_ref, x_ref, gain_ref, down_ref, up_ref, *refs):
    o_refs, w_hbm = refs[:GROUPS], refs[GROUPS : 2 * GROUPS]
    att_ref, rank_ref, y_ref, h_ref, w_s, sems = refs[2 * GROUPS :]
    w_copies = start_copies(w_hbm, w_s, sems)
    group = info_ref[1]
    for j in range(GROUPS):
        att_ref[:, lanes_of(group ^ j)] = o_refs[j][...]
    attended = att_ref[...]
    for j in range(GROUPS):
        w_copies[j].wait()
        y_ref[:, lanes_of(group ^ j)] = dot(attended, w_s[j])
    rank_out = dot_nt(attended, down_ref[0]).astype(BF)
    rank_ref[...] = rank_out
    y_one = x_ref[...].astype(F32) + y_ref[...] + dot(rank_out, up_ref[0])
    y_ref[...] = y_one
    inverse = lax.rsqrt(jnp.mean(y_one * y_one, axis=1, keepdims=True) + NORM_EPS)
    h_ref[...] = (y_one * inverse * gain_ref[...]).astype(BF)


def project_out(info, rows, gain, down_t, up, outs, w_parts):
    tokens = rows.shape[0]
    return pl.pallas_call(
        out_kernel,
        grid_spec=pltpu.PrefetchScalarGridSpec(
            num_scalar_prefetch=1,
            grid=(1,),
            in_specs=[VMEM_SPEC] * 2
            + [by_adapter(down_t), by_adapter(up)]
            + [VMEM_SPEC] * GROUPS
            + [pl.BlockSpec(memory_space=pl.ANY)] * GROUPS,
            out_specs=[VMEM_SPEC] * 4,
            scratch_shapes=[
                pltpu.VMEM((GROUPS, QW, QG), BF),
                pltpu.SemaphoreType.DMA((GROUPS,)),
            ],
        ),
        out_shape=[
            jax.ShapeDtypeStruct((tokens, QW), BF),
            jax.ShapeDtypeStruct((tokens, RANK), BF),
            jax.ShapeDtypeStruct((tokens, D), F32),
            jax.ShapeDtypeStruct((tokens, D), BF),
        ],
        cost_estimate=pl.CostEstimate(
            flops=2 * tokens * QW * D, bytes_accessed=2 * QW * D + 12 * tokens * D, transcendentals=0
        ),
        name="project_out",
    )(info, rows, gain, down_t, up, *outs, *w_parts)


def middle_kernel(count, terms, experts_all, info_ref, *refs):
    refs = list(refs)
    take = lambda n: [refs.pop(0) for _ in range(n)]
    d_refs = take(terms)
    pack_ref, y_ref, h_ref, gain_ref, aux_ref, att_ref, rank_ref, down_ref, up_ref = take(9)
    w_hbm = take(GROUPS)
    (dy_ref,) = take(1)
    do_refs, early_refs = take(count), take(GROUPS)
    do_s, early_s, w_s, sems = refs
    w_refs = start_copies(w_hbm, w_s, sems)
    group, ctx_index, copies = info_ref[1], info_ref[2], count // GROUPS
    tokens = y_ref.shape[0]
    d_sum = d_refs[0][...].astype(F32)
    for ref in d_refs[1:]:
        d_sum = d_sum + ref[...].astype(F32)
    early_s[0 : 2 * RANK, :] = d_sum[tokens : tokens + 2 * RANK]
    d_ext = read_turned(d_sum[tokens + 2 * RANK :], EXP_AT + experts_all, tokens, 0).T
    h_two = h_ref[...]
    lane = lax.broadcasted_iota(jnp.int32, (tokens, LANES), 1)
    chosen = read_turned(pack_ref[tokens:, :].astype(F32), experts_all, tokens, EXP_AT).T > 0.0
    picked = jnp.where(chosen, dot_nt(h_two, aux_ref[0]), NEG)
    weights = jnp.exp(picked - jnp.max(picked, axis=1, keepdims=True))
    gates = weights / jnp.sum(weights, axis=1, keepdims=True)
    mixed = jnp.sum(jnp.where(chosen, gates * d_ext, 0.0), axis=1, keepdims=True)
    d_logits = jnp.where(chosen, gates * (d_ext - mixed), 0.0)
    d_ext = jnp.where(lane < EXP_AT, d_ext, d_logits).astype(BF)
    d_h = d_sum[:tokens] + dot(d_ext, aux_ref[0])
    y_one = y_ref[...]
    inverse = lax.rsqrt(jnp.mean(y_one * y_one, axis=1, keepdims=True) + NORM_EPS)
    scaled = gain_ref[...] * d_h
    d_y = pack_ref[:tokens, :].astype(F32) + inverse * scaled
    d_y = d_y - y_one * inverse**3 * jnp.mean(y_one * scaled, axis=1, keepdims=True)
    dy_ref[...] = d_y
    d_attn = d_y.astype(BF)
    d_rank = dot_nt(d_attn, up_ref[0]).astype(BF)
    do_s[...] = dot(d_rank, down_ref[0])
    for j in range(GROUPS):
        at = lanes_of(group ^ j)
        early_s[3 * RANK : 4 * RANK, at] = dot_tn(rank_ref[...], dy_ref[:, at].astype(BF))
        w_refs[j].wait()
        do_s[...] += dot_nt(dy_ref[:, at].astype(BF), w_s[j])
    for m in range(count):
        do_refs[m][...] = do_s[:, lanes_of((ctx_index ^ m) // copies)].astype(BF)
    early_s[2 * RANK : 3 * RANK, :] = dot_tn(d_rank, att_ref[...])
    early_s[4 * RANK :, :] = dot_tn(d_ext, h_two)[: 2 * RANK]
    for j in range(GROUPS):
        for i in range(6):
            block = early_s[i * RANK : (i + 1) * RANK, lanes_of(group ^ j)]
            early_refs[j][:, i * QG : (i + 1) * QG] = block.astype(BF)


def middle_back(info, count, experts_all, terms, pack, y_one, h_two, gain, aux, attended, rank_out, down_t, up, w_parts):
    tokens = y_one.shape[0]
    outs = pl.pallas_call(
        functools.partial(middle_kernel, count, len(terms), experts_all),
        grid_spec=pltpu.PrefetchScalarGridSpec(
            num_scalar_prefetch=1,
            grid=(1,),
            in_specs=[VMEM_SPEC] * (len(terms) + 4)
            + [by_adapter(aux)]
            + [VMEM_SPEC] * 2
            + [by_adapter(down_t), by_adapter(up)]
            + [pl.BlockSpec(memory_space=pl.ANY)] * GROUPS,
            out_specs=[VMEM_SPEC] * (1 + count + GROUPS),
            scratch_shapes=[
                pltpu.VMEM((tokens, QW), F32),
                pltpu.VMEM((6 * RANK, D), F32),
                pltpu.VMEM((GROUPS, QW, QG), BF),
                pltpu.SemaphoreType.DMA((GROUPS,)),
            ],
        ),
        out_shape=[jax.ShapeDtypeStruct((tokens, D), F32)]
        + [jax.ShapeDtypeStruct((tokens, QG), BF)] * count
        + [jax.ShapeDtypeStruct((RANK, 6 * QG), BF)] * GROUPS,
        cost_estimate=pl.CostEstimate(
            flops=2 * tokens * QW * D, bytes_accessed=2 * QW * D + 20 * tokens * D, transcendentals=0
        ),
        name="middle_back",
    )(info, *terms, pack, y_one, h_two, gain, aux, attended, rank_out, down_t, up, *w_parts)
    return outs[0], list(outs[1 : 1 + count]), list(outs[1 + count :])


def ranks_kernel(info_ref, dqkv_ref, up_ref, t_ref, h_ref, *refs):
    early_refs, (rank_ref, keep_ref, send_ref, h_s, sems) = refs[:GROUPS], refs[GROUPS:]
    (rows,) = start_copies([h_ref], h_s, sems)
    d_qkv = dqkv_ref[...]
    d_rank = dot_nt(d_qkv, up_ref[...]).astype(BF)
    rank_ref[...] = d_rank
    grad = dot_tn(t_ref[...], d_qkv)
    keep_ref[:, :QG] = grad[:RANK, :QG].astype(BF)
    keep_ref[:, QG : QG + KG] = grad[RANK : 2 * RANK, QG : QG + KG].astype(BF)
    keep_ref[:, QG + KG : LOCAL] = grad[2 * RANK :, QG + KG :].astype(BF)
    send_ref[:, :LOCAL] = jnp.zeros((RANK, LOCAL), BF)
    rows.wait()
    for j in range(GROUPS):
        target = send_ref if j % 2 else keep_ref
        down = dot_tn(d_rank, h_s[0, :, lanes_of(info_ref[1] ^ j)]).astype(BF)
        first = LOCAL + (j // 2) * 3 * QG
        for i in range(3):
            target[:, first + i * QG : first + (i + 1) * QG] = down[i * RANK : (i + 1) * RANK]
        first = LOCAL + 6 * QG + (j // 2) * 6 * QG
        target[:, first : first + 6 * QG] = early_refs[j][...]


HALF = LOCAL + 18 * QG
BOTH = HALF + LOCAL


def ranks_back(info, d_qkv, up_diag, rank_qkv, h_one, early):
    length = d_qkv.shape[0]
    return pl.pallas_call(
        ranks_kernel,
        in_specs=[SMEM_SPEC]
        + [VMEM_SPEC] * 3
        + [pl.BlockSpec(memory_space=pl.ANY)]
        + [VMEM_SPEC] * GROUPS,
        out_specs=[VMEM_SPEC] * 3,
        scratch_shapes=[pltpu.VMEM((1,) + h_one.shape, BF), pltpu.SemaphoreType.DMA((1,))],
        out_shape=[
            jax.ShapeDtypeStruct((length, 3 * RANK), BF),
            jax.ShapeDtypeStruct((RANK, HALF), BF),
            jax.ShapeDtypeStruct((RANK, HALF), BF),
        ],
        name="ranks_back",
    )(info, d_qkv, up_diag, rank_qkv, h_one, *early)


def mix_kernel(near_ref, far_ref, out_ref):
    out_ref[:, :LOCAL] = near_ref[:, :LOCAL]
    out_ref[:, LOCAL : 2 * LOCAL] = far_ref[:, :LOCAL]
    first = LOCAL
    for width in (3 * QG, 6 * QG):
        for mine, theirs in ((0, width), (width, 0)):
            total = near_ref[:, first + mine : first + mine + width].astype(F32)
            total = total + far_ref[:, first + theirs : first + theirs + width].astype(F32)
            at = LOCAL + first + mine
            out_ref[:, at : at + width] = total.astype(BF)
        first += 2 * width


def mix(near, far):
    return pl.pallas_call(
        mix_kernel,
        in_specs=[VMEM_SPEC] * 2,
        out_specs=VMEM_SPEC,
        out_shape=jax.ShapeDtypeStruct((RANK, BOTH), BF),
        name="mix",
    )(near, far)


def inputs_kernel(info_ref, dqkv_ref, rank_ref, w_ref, down_ref, *rows_refs):
    rows = dot_nt(dqkv_ref[...], w_ref[...]) + dot(rank_ref[...], down_ref[0])
    rows = rows.astype(BF)
    for m, ref in enumerate(rows_refs):

        @pl.when(pl.program_id(0) == m)
        def _():
            ref[...] = rows


def inputs_back(info, count, d_qkv, d_rank, cols_all, down_t):
    length = d_qkv.shape[0]
    tokens = length // count
    per_block = lambda width: pl.BlockSpec((tokens, width), lambda i, info: (i, 0))
    whole = lambda shape: pl.BlockSpec(shape, lambda i, info: (0, 0))
    return pl.pallas_call(
        inputs_kernel,
        grid_spec=pltpu.PrefetchScalarGridSpec(
            num_scalar_prefetch=1,
            grid=(count,),
            in_specs=[
                per_block(LOCAL),
                per_block(3 * RANK),
                whole((D, LOCAL)),
                by_adapter(down_t),
            ],
            out_specs=[whole((tokens, D))] * count,
        ),
        out_shape=[jax.ShapeDtypeStruct((tokens, D), BF)] * count,
        cost_estimate=pl.CostEstimate(
            flops=2 * length * D * LOCAL, bytes_accessed=4 * length * (D + LOCAL), transcendentals=0
        ),
        name="inputs_back",
    )(info, d_qkv, d_rank, cols_all, down_t)


def place_kernel(info_ref, *refs):
    up_ref, down_ref, gu_ref, da_ref, db_ref, od_ref, ou_ref, gd_ref, sum_s, parts, sems = refs[2:]
    sources = parts.shape[1]
    copies = start_copies(refs[:2], parts, sems)
    for ref in (up_ref, down_ref, db_ref, od_ref, ou_ref, gd_ref, sum_s):
        ref[...] = jnp.zeros(ref.shape, F32)
    for copy in copies:
        copy.wait()
    for j in range(GROUPS):
        group = info_ref[1] ^ j
        keys = lambda first: pl.ds(pl.multiple_of(first + group * KG, LANES), KG)
        far = j // 2
        down_at = 2 * LOCAL + far * 3 * QG
        early_at = 2 * LOCAL + 6 * QG + far * 6 * QG
        for m in range(sources):
            a = info_ref[SLOTS_AT + sources + m]
            take = lambda first, width: parts[j % 2, m, :, first : first + width].astype(F32)
            up_ref[a, :, lanes_of(group)] += take(far * LOCAL, QG)
            up_ref[a, :, keys(QW)] += take(far * LOCAL + QG, KG)
            up_ref[a, :, keys(QW + KVW)] += take(far * LOCAL + QG + KG, KG)
            for i in range(3):
                at = slice(i * RANK, (i + 1) * RANK)
                down_ref[a, at, lanes_of(group)] += take(down_at + i * QG, QG)
            for i, ref in enumerate((sum_s, db_ref, od_ref, ou_ref, gd_ref, gd_ref)):
                at = slice(RANK, 2 * RANK) if i == 5 else slice(0, RANK)
                ref[a, at, lanes_of(group)] += take(early_at + i * QG, QG)
    for a in range(ADAPT):
        gu_ref[a, 0] = sum_s[a, :, :FF]
        gu_ref[a, 1] = sum_s[a, :, FF : 2 * FF]
        da_ref[a] = sum_s[a, :, 2 * FF :]


def place_grads(info, near, far):
    shapes = [(RANK, QW + 2 * KVW), (3 * RANK, D), (2, RANK, FF), (RANK, FF), (RANK, D)]
    shapes += [(RANK, QW), (RANK, D), (2 * RANK, D)]
    return pl.pallas_call(
        place_kernel,
        in_specs=[SMEM_SPEC] + [pl.BlockSpec(memory_space=pl.ANY)] * 2,
        out_specs=[VMEM_SPEC] * len(shapes),
        out_shape=[jax.ShapeDtypeStruct((ADAPT,) + shape, F32) for shape in shapes],
        scratch_shapes=[
            pltpu.VMEM((ADAPT, RANK, D), F32),
            pltpu.VMEM((2,) + near.shape, BF),
            pltpu.SemaphoreType.DMA((2,)),
        ],
        name="place_grads",
    )(info, near, far)


def norm_backward(values, inverse, gain_vec, upstream):
    scaled = gain_vec * upstream
    return inverse * scaled - values * inverse**3 * jnp.mean(
        values * scaled, axis=-1, keepdims=True
    )


def local_columns(table, group):
    lead = table.shape[:-1]
    cut = lambda first, width: lax.dynamic_slice_in_dim(
        table, first + group * width, width, table.ndim - 1
    )
    return cut(0, QG), cut(QW, KG), cut(QW + KVW, KG)


def on_device(
    inputs,
    cotangent,
    segment_ids,
    expert_ids,
    adapter_ids,
    gain_one,
    w_qkv,
    w_out,
    gain_two,
    router,
    w_gate_up,
    w_down,
    qkv_down,
    qkv_up,
    out_down,
    out_up,
    gu_down,
    gu_up,
    down_a,
    down_b,
):
    ctx_count = lax.axis_size("ctx")
    seq_count = lax.axis_size("seq")
    ctx_index = lax.axis_index("ctx")
    seq_index = lax.axis_index("seq")
    tokens = inputs.shape[1]
    length = tokens * ctx_count
    experts_all = router.shape[1]
    copies = ctx_count // GROUPS
    group = ctx_index // copies
    half = tokens // 2
    ctx_masks = doublings(ctx_count)[::-1]
    seq_slots = (seq_index ^ jnp.arange(seq_count)).astype(jnp.int32)
    ctx_slots = ctx_index ^ jnp.arange(ctx_count)
    own_rows = inputs[0]

    moving_rows = [swap(own_rows, "ctx", mask) for mask in ctx_masks]
    own_q, own_k, own_v = local_columns(w_qkv, group)
    own_out = lax.dynamic_slice_in_dim(w_out, group * QG, QG, 1)
    col_slots = []
    cols = Steps(
        gather_far(jnp.concatenate([own_q, own_k, own_v, own_out], axis=1), col_slots)
    )
    chosen = expert_ids[0]
    hot = jnp.any(chosen[:, :, None] == jnp.arange(experts_all)[None, None, :], axis=1)
    hot_low = hot.astype(BF).T
    before = (jnp.arange(tokens)[:, None] <= jnp.arange(tokens)[None, :]).astype(BF)
    ranks = dot(hot_low, before).astype(BF) * hot_low
    per = D // tokens
    rank_rows = turned_rows(experts_all, tokens)
    ranks = jnp.pad(ranks, ((0, rank_rows * per - experts_all), (0, 0)))
    ranks = ranks.reshape(rank_rows // TURN, per, TURN, tokens)
    ranks = jnp.transpose(ranks, (0, 2, 1, 3)).reshape(rank_rows, D)
    pack = jnp.concatenate([cotangent[0], ranks], axis=0)
    cols.beside()
    seg_row = segment_ids[0]
    position = jnp.arange(length)
    start = jnp.sum((seg_row[None, :] < seg_row[:, None]).astype(jnp.int32), axis=1)
    block_id = jnp.stack([ctx_slots, 2 * ctx_count - 1 - ctx_slots], axis=1).reshape(-1)
    block_of = jnp.arange(2 * ctx_count)
    owner = jnp.minimum(block_of, 2 * ctx_count - 1 - block_of)
    place = (2 * (owner ^ ctx_index) + (block_of >= ctx_count)).astype(jnp.int32)
    first = (start[::BLK] // BLK).astype(jnp.int32)
    offset = (position - start).reshape(2 * ctx_count, half)[block_id].reshape(-1)
    lane = jnp.arange(LANES) % HEAD_DIM
    frequency = 10000.0 ** (-2.0 * (lane % (HEAD_DIM // 2)).astype(F32) / HEAD_DIM)
    angles = offset.astype(F32)[:, None] * frequency[None, :]
    cosine = jnp.cos(angles)
    sine = jnp.sin(angles) * jnp.where(lane < HEAD_DIM // 2, -1.0, 1.0)[None, :]
    start_row = start[None, :]
    adapter = adapter_ids[seq_index]
    slot_adapters = adapter_ids[seq_slots]
    info = jnp.concatenate(
        [jnp.stack([adapter, group, ctx_index, E_DEV * seq_index]), seq_slots, slot_adapters]
    ).astype(jnp.int32)

    def pick(table):
        return lax.dynamic_index_in_dim(table, adapter, 0, keepdims=False)

    qkv_down_sel = pick(qkv_down)
    out_down_t = jnp.swapaxes(out_down, 1, 2)
    aux_w = jnp.concatenate(
        [
            jnp.swapaxes(gu_down, 1, 2),
            jnp.broadcast_to(router.T[None], (ADAPT, experts_all, D)),
            jnp.zeros((ADAPT, LANES - 2 * RANK - experts_all, D), BF),
        ],
        axis=1,
    )
    down_a_t = jnp.swapaxes(down_a, 1, 2)

    pack, start_row, cosine, sine, place, first, info, *moving_rows = cols.beside(
        pack, start_row, cosine, sine, place, first, info, *moving_rows
    )
    row_slots = gather_rest(own_rows, moving_rows, ctx_masks)
    all_rows = jnp.concatenate(row_slots, axis=0).astype(F32)
    inv_all = lax.rsqrt(jnp.mean(all_rows * all_rows, axis=-1, keepdims=True) + NORM_EPS)
    h_one = (all_rows * inv_all * gain_one).astype(BF)
    rank_qkv = dot(h_one, qkv_down_sel).astype(BF)
    h_one, rank_qkv, pack = cols.beside(h_one, rank_qkv, pack)
    pack_slots = []
    packs = Steps(gather_line(pack, pack_slots))
    cols.finish()
    outs = Steps(gather_groups(order_rows(info, col_slots), copies))
    qkv, cols_all, up_diag = packs.beside(
        *project(info, h_one, rank_qkv, qkv_up, cosine, sine, col_slots)
    )
    heads_out, lse, *pieces = packs.beside(
        *outs.beside(*attend(place, first, qkv, start_row, copies))
    )
    heads_here = packs.beside(
        *[swap(piece, "ctx", j * copies) if j else piece for j, piece in enumerate(pieces)]
    )
    out_parts = outs.finish()
    attended, rank_out, y_one, h_two = project_out(
        info, own_rows, gain_two[None], out_down_t, out_up, heads_here, out_parts
    )

    def compute(m, rows):
        return experts(
            experts_all,
            info,
            SLOTS_AT + seq_count + m,
            rows,
            pack_slots[m : m + len(rows)],
            w_gate_up,
            w_down,
            aux_w,
            gu_up,
            down_a_t,
            down_b,
        )

    y_sums, d_terms = exchange_experts(h_two, packs, compute)

    d_y_one, d_heads, early = middle_back(
        info,
        ctx_count,
        experts_all,
        d_terms,
        pack,
        y_one,
        h_two,
        gain_two[None],
        aux_w,
        attended,
        rank_out,
        out_down_t,
        out_up,
        out_parts,
    )
    (d_y_one,) = y_sums.beside(d_y_one)
    d_heads = [swap(piece, "ctx", m) if m else piece for m, piece in enumerate(d_heads)]
    d_heads = y_sums.beside(*d_heads)

    (d_qkv,) = y_sums.beside(
        attend_back(place, first, qkv, start_row, heads_out, lse, cosine, sine, d_heads)
    )
    d_rank_qkv, keep, sent = ranks_back(info, d_qkv, up_diag, rank_qkv, h_one, early)

    halves = add_low(keep, swap(sent, "ctx", copies))
    for mask in doublings(copies):
        shared = halves[:, HALF - 12 * QG :]
        shared = add_low(shared, swap(shared, "ctx", mask))
        halves = jnp.concatenate([halves[:, : HALF - 12 * QG], shared], axis=1)
    halves, d_rank_qkv = lax.optimization_barrier((halves, d_rank_qkv))
    arrived, *d_rows = y_sums.beside(
        swap(halves, "ctx", 2 * copies),
        *inputs_back(info, ctx_count, d_qkv, d_rank_qkv, cols_all, jnp.swapaxes(qkv_down, 1, 2)),
    )
    d_rows = d_rows[::copies]
    near = add_low(d_rows[0], swap(d_rows[1], "ctx", copies))
    far = add_low(d_rows[2], swap(d_rows[3], "ctx", copies))
    slots = []
    grads = Steps(gather_line(mix(halves, arrived), slots))
    near, far = grads.beside(near, far)
    d_h_one = near.astype(F32) + swap(far, "ctx", 2 * copies).astype(F32)
    features = own_rows.astype(F32)
    inv_one = lax.rsqrt(jnp.mean(features * features, axis=-1, keepdims=True) + NORM_EPS)
    input_grad = d_y_one + norm_backward(features, inv_one, gain_one, d_h_one)
    layer_output = y_one
    for term in y_sums.finish():
        layer_output = layer_output + term.astype(F32)
    layer_output = layer_output.astype(BF)
    grads.beside()
    grads.beside()
    input_grad, layer_output = grads.beside(input_grad, layer_output)
    grads.finish()
    grads = join(slots)
    (
        grad_qkv_up,
        grad_qkv_down,
        grad_gu_up,
        grad_down_a,
        grad_down_b,
        grad_out_down,
        grad_out_up,
        grad_gu_down,
    ) = place_grads(info, grads, swap(grads, "ctx", copies))

    return (
        layer_output[None],
        input_grad[None],
        jnp.swapaxes(grad_qkv_down, 1, 2),
        grad_qkv_up,
        jnp.swapaxes(grad_out_down, 1, 2),
        grad_out_up,
        jnp.swapaxes(grad_gu_down, 1, 2),
        grad_gu_up,
        jnp.swapaxes(grad_down_a, 1, 2),
        grad_down_b,
    )


def solution(mesh):
    over_seq = P("seq", None)
    placed = (
        P("seq", "ctx", None),
        P("seq", "ctx", None),
        over_seq,
        P("seq", "ctx", None),
        P(),
        P(),
        over_seq,
        over_seq,
        P(),
        P(),
        P("seq", None, None),
        P("seq", None, None),
    ) + (P(),) * 8
    return jax.shard_map(
        on_device,
        mesh=mesh,
        in_specs=placed,
        out_specs=(P("seq", "ctx", None), P("seq", "ctx", None)) + (P(),) * 8,
        check_vma=False,
    )
```
